32 devices in a mesh: dp: 8 (over y, x, core), ctx: 4 (over z).
Axes of the slice: x: 2, y: 2, z: 4, core: 2. Of those that a mesh axis runs over, the one named last changes fastest.
Arguments:
- inputs: bfloat16 [8, 512, 2048], P('dp', 'ctx'), may hold values from -6 to 6
- segment: int32 [8, 512], P('dp', 'ctx'), may hold values from 0 to 3, as said below
- w_qkv: bfloat16 [2048, 6144], P(('dp', 'ctx')), may hold values from -0.125 to 0.125
- w_out: bfloat16 [2048, 2048], P(('dp', 'ctx')), may hold values from -0.125 to 0.125
- w_gate: bfloat16 [2048, 8192], P('dp', 'ctx'), may hold values from -0.125 to 0.125
- w_up: bfloat16 [2048, 8192], P('dp', 'ctx'), may hold values from -0.125 to 0.125
- w_down_t: bfloat16 [2048, 8192], P('dp', 'ctx'), may hold values from -0.0625 to 0.0625
- gains: float32 [4, 2048], replicated, may hold values from 0.25 to 1.75
- cotangent: bfloat16 [8, 512, 2048], P('dp', 'ctx'), may hold values from -6 to 6
Outputs:
- output: bfloat16 [8, 512, 2048], P('dp', 'ctx')
- input_grad: float32 [8, 512, 2048], P('dp', 'ctx')
- grad_qkv: float32 [2048, 6144], P(('dp', 'ctx'))
- grad_out: float32 [2048, 2048], P(('dp', 'ctx'))
- grad_gate: float32 [2048, 8192], P('dp', 'ctx')
- grad_up: float32 [2048, 8192], P('dp', 'ctx')
- grad_down_t: float32 [2048, 8192], P('dp', 'ctx')
- grad_gains: float32 [4, 2048], replicated
The draws below stay inside these ranges and needn't reach their ends.
Inputs may be any that keep to these rules, and one draw needn't show every extreme that they name: `segment`: in every sequence ids 1, 2 and 3 mark three documents in this order, each of one position or more, and 0 marks padding, one position or more at the sequence's end.
All inputs are finite; a program needn't handle non-finite values.
Results may differ from the reference program's by a relative error of at most 0.015.
Values may be sent and summed in bfloat16 or wider, within the bound.
A program may use at most 704 MiB of HBM per device.

```python
import jax
import jax.numpy as jnp
from jax import lax

D = 2048
HEADS = 16
HEAD_DIM = 128
FF = 8192
LEN = 512
SEQS = 8


def draw_segment(key, part):
    base = jax.random.fold_in(key, 11)
    first_key, pad_key, split_key = jax.random.split(base, 3)
    first = jax.random.randint(first_key, (SEQS, 1), LEN // 2 + LEN // 16, LEN * 3 // 4)
    pad_start = jax.random.randint(pad_key, (SEQS, 1), LEN * 7 // 8, LEN)
    spread = jax.random.randint(split_key, (SEQS, 1), 0, 1 << 20)
    second = first + 1 + spread % (pad_start - first - 1)
    places = jnp.arange(LEN, dtype=jnp.int32)[None, :]
    ids = 1 + (places >= first).astype(jnp.int32) + (places >= second).astype(jnp.int32)
    return jnp.where(places >= pad_start, 0, ids).astype(jnp.int32)


def steps_of(rng, shape, pieces, least, top_value):
    factor_of = 1.0
    for position, parts in pieces:
        draws = jax.random.uniform(jax.random.fold_in(jax.random.fold_in(rng, 6), position), (parts,), jnp.float32, least / len(pieces), top_value / len(pieces))
        factor_of = factor_of * jnp.repeat(jnp.exp(draws), shape[position] // parts).reshape((-1,) + (1,) * (len(shape) - 1 - position))
    return factor_of


def noise(rng, shape, width, bound, cuts=(), kind=jnp.bfloat16):
    loudness = steps_of(rng, shape, cuts, -0.22, 0.18) if cuts else 1.0
    values = jax.random.normal(rng, shape, jnp.float32) * width * loudness
    return jnp.minimum(jnp.maximum(values, -bound), bound).astype(kind)


def setup_inputs(seed: int = 0) -> dict:
    key_list = jax.random.split(jax.random.key(seed), 10)
    inputs = noise(key_list[0], (SEQS, LEN, D), 1.0, 6.0, ((0, 8), (1, 4)))
    segment = draw_segment(jax.random.fold_in(key_list[9], 71), 0)
    w_qkv = noise(key_list[2], (D, 3 * D), D ** -0.5, 0.125, ((0, 32),))
    w_out = noise(key_list[3], (D, D), D ** -0.5, 0.125, ((0, 32),))
    w_gate = noise(key_list[4], (D, FF), D ** -0.5, 0.125, ((0, 8), (1, 4)))
    w_up = noise(key_list[5], (D, FF), D ** -0.5, 0.125, ((0, 8), (1, 4)))
    w_down_t = noise(key_list[6], (D, FF), FF ** -0.5, 0.0625, ((0, 8), (1, 4)))
    gains = jnp.clip(1.0 + 0.15 * jax.random.normal(key_list[7], (4, D), jnp.float32), 0.25, 1.75)
    cotangent = noise(key_list[8], (SEQS, LEN, D), 1.0, 6.0, ((0, 8), (1, 4)))
    return {"inputs": inputs, "segment": segment, "w_qkv": w_qkv, "w_out": w_out, "w_gate": w_gate, "w_up": w_up, "w_down_t": w_down_t, "gains": gains, "cotangent": cotangent}


EPS = 1e-06
ROPE_BASE = 500000.0
HIGH = lax.Precision.HIGHEST

@jax.custom_vjp
def low(v):
    return lax.optimization_barrier(v.astype(jnp.bfloat16)).astype(jnp.float32)

@jax.custom_vjp
def low_back(v):
    return v

def low_keep(v):
    return (low(v), None)

def low_pass(kept, grad):
    return (grad,)

def back_keep(v):
    return (v, None)

def back_low(kept, grad):
    return (low(grad),)
low.defvjp(low_keep, low_pass)
low_back.defvjp(back_keep, back_low)

def matmul(left, right):
    return jnp.dot(left, right, precision=HIGH, preferred_element_type=jnp.float32)

def rope_tables(positions):
    half = HEAD_DIM // 2
    frequency = ROPE_BASE ** (-(jnp.arange(half, dtype=jnp.float32) * 2.0 / HEAD_DIM))
    angles = positions[:, None] * frequency[None, :]
    cosine = jnp.cos(angles)
    sine = jnp.sin(angles)
    return (jnp.concatenate([cosine, cosine], 1), jnp.concatenate([sine, sine], 1))

def rotate(values, cosine, sine):
    half = HEAD_DIM // 2
    turned = jnp.concatenate([-values[..., half:], values[..., :half]], -1)
    return values * cosine[:, None, :] + turned * sine[:, None, :]

def norm_rope(values, gain, cosine, sine):
    factor = lax.rsqrt(lax.optimization_barrier(jnp.mean(values * values, axis=-1, keepdims=True)) + EPS)
    normed = (values * factor * gain).reshape(values.shape[0], HEADS, HEAD_DIM)
    return rotate(normed, cosine, sine).reshape(values.shape[0], HEADS * HEAD_DIM)

def post_norm(values, gain):
    return values * lax.rsqrt(lax.optimization_barrier(jnp.mean(values * values, axis=-1, keepdims=True)) + EPS) * gain

def attention(queries, key_rows, value_rows, segment):
    length = queries.shape[0]
    block = min(512, length)
    count = length // block
    places = jnp.arange(length, dtype=jnp.int32)
    scale = HEAD_DIM ** (-0.5)
    blocks = queries.reshape(count, block, HEADS, HEAD_DIM)
    starts = jnp.arange(count, dtype=jnp.int32) * block

    @jax.checkpoint
    def one_block(item):
        query_block, start = item
        query_place = start + jnp.arange(block, dtype=jnp.int32)
        query_segment = lax.dynamic_slice_in_dim(segment, start, block)
        allowed = (query_segment[:, None] == segment[None, :]) & (places[None, :] <= query_place[:, None]) & ((segment[None, :] != 0) | (places[None, :] == query_place[:, None]))
        scores = low_back(jnp.einsum('qhd,khd->hqk', query_block, key_rows, precision=HIGH) * scale)
        masked = jnp.where(allowed[None], scores, -1e+30)
        row_max = lax.optimization_barrier(jnp.max(masked, axis=-1, keepdims=True))
        weights = jnp.where(allowed[None], jnp.exp(masked - row_max), 0.0)
        shares = low(weights / lax.optimization_barrier(jnp.sum(weights, axis=-1, keepdims=True)))
        return jnp.einsum('hqk,khd->qhd', shares, value_rows, precision=HIGH)
    result = lax.map(one_block, (blocks, starts))
    return result.reshape(length, HEADS * HEAD_DIM)

def layer(tokens, segment, w_qkv, w_out, w_gate, w_up, w_down_t, gains):
    length = tokens.shape[0]
    cosine, sine = rope_tables(jnp.arange(length, dtype=jnp.float32))
    mixed = low_back(matmul(tokens, w_qkv))
    query = low(norm_rope(mixed[:, :D], gains[0], cosine, sine))
    key_part = low(norm_rope(mixed[:, D:2 * D], gains[1], cosine, sine))
    value = low(mixed[:, 2 * D:])
    attended = attention(query.reshape(length, HEADS, HEAD_DIM), key_part.reshape(length, HEADS, HEAD_DIM), value.reshape(length, HEADS, HEAD_DIM), segment)
    attended = low(low_back(attended))
    projected = low_back(matmul(attended, w_out))
    residual = tokens + post_norm(projected, gains[2])
    residual_low = low(residual)
    gate = low_back(matmul(residual_low, w_gate))
    up_part = low_back(matmul(residual_low, w_up))
    activated = low(jax.nn.silu(gate) * up_part)
    feed = low_back(matmul(activated, w_down_t.T))
    return residual + post_norm(feed, gains[3])

def reference(inputs, segment, w_qkv, w_out, w_gate, w_up, w_down_t, gains, cotangent):
    weights = (w_qkv.astype(jnp.float32), w_out.astype(jnp.float32), w_gate.astype(jnp.float32), w_up.astype(jnp.float32), w_down_t.astype(jnp.float32), gains.astype(jnp.float32))
    initial = tuple((jnp.zeros(w.shape, jnp.float32) for w in weights))

    def one_sequence(totals, item):
        tokens, seq_ids, upstream = item

        def forward(token_rows, a_qkv, a_out, a_gate, a_up, a_down, a_gains):
            return layer(token_rows, seq_ids, a_qkv, a_out, a_gate, a_up, a_down, a_gains)
        result, pull = jax.vjp(forward, tokens.astype(jnp.float32), *weights)
        grads = pull(upstream.astype(jnp.float32))
        summed = tuple((t + g for t, g in zip(totals, grads[1:])))
        return (summed, (result.astype(jnp.bfloat16), grads[0]))
    totals, (outputs, input_grads) = lax.scan(one_sequence, initial, (inputs, segment, cotangent))
    return (outputs, input_grads, totals[0], totals[1], totals[2], totals[3], totals[4], totals[5])
```

```python
import jax
import jax.numpy as jnp
from jax import lax
from jax.sharding import Mesh
from jax.sharding import PartitionSpec as P

HEAD_DIM = 128
EPS = 1e-06
ROPE_BASE = 500000.0
F32 = jnp.float32
BF16 = jnp.bfloat16
GROUP = ("core", "ctx")
ALL = ("chip", "core", "ctx")


def rope_tables(positions):
    half = HEAD_DIM // 2
    frequency = ROPE_BASE ** (-(jnp.arange(half, dtype=F32) * 2.0 / HEAD_DIM))
    angles = positions[:, None] * frequency[None, :]
    cosine = jnp.cos(angles)
    sine = jnp.sin(angles)
    return (jnp.concatenate([cosine, cosine], 1), jnp.concatenate([sine, sine], 1))


def rotate(values, cosine, sine):
    half = HEAD_DIM // 2
    turned = jnp.concatenate([-values[..., half:], values[..., :half]], -1)
    return values * cosine + turned * sine


def rotate_back(values, cosine, sine):
    half = HEAD_DIM // 2
    scaled = values * sine
    turned = jnp.concatenate([scaled[..., half:], -scaled[..., :half]], -1)
    return values * cosine + turned


def dot(left, right):
    return jnp.dot(left, right, preferred_element_type=F32)


def dot_rows(left, right):
    return lax.dot_general(left, right, (((1,), (1,)), ((), ())), preferred_element_type=F32)


def dot_first(left, right):
    return lax.dot_general(left, right, (((0,), (0,)), ((), ())), preferred_element_type=F32)


def gather(values, axes):
    return lax.all_gather(values, axes, axis=0, tiled=True)


def scatter_sum(values, axes):
    return lax.psum_scatter(values, axes, scatter_dimension=0, tiled=True)


def norm_factor(values):
    return lax.rsqrt(jnp.mean(values * values, axis=-1, keepdims=True) + EPS)


def norm_back(values, factor, gain, grad):
    normed = values * factor
    scaled = gain * grad
    back = factor * (scaled - normed * jnp.mean(scaled * normed, axis=-1, keepdims=True))
    return back, jnp.sum(grad * normed, axis=0)


def per_device(inputs, segment, w_qkv, w_out, w_gate, w_up, w_down_t, gains, cotangent):
    rows, width = inputs.shape[1:]
    cores = lax.axis_size("core")
    spans = lax.axis_size("ctx")
    members = cores * spans
    length = rows * spans
    total_rows = cores * length
    part = width // members
    heads = part // HEAD_DIM
    member = lax.axis_index(GROUP)
    tokens = inputs[0]

    qkv_rows = w_qkv.shape[0]
    qkv_cut = w_qkv.reshape(qkv_rows, 3, members, part).transpose(2, 0, 1, 3)
    qkv_cut = qkv_cut.reshape(members, qkv_rows, 3 * part)
    qkv_cut = lax.all_to_all(qkv_cut, GROUP, 0, 0, tiled=True)
    qkv_w = gather(qkv_cut.reshape(members * qkv_rows, 3 * part), "chip")
    tokens_all = gather(tokens, GROUP)
    out_full = gather(w_out, ALL)
    out_w = lax.dynamic_slice_in_dim(out_full, member * part, part, 0)

    hidden = w_gate.shape[1] // cores
    gate_up = jnp.concatenate(
        [w_gate.reshape(-1, cores, 1, hidden), w_up.reshape(-1, cores, 1, hidden)], 2
    ).reshape(-1, cores * 2 * hidden)
    gate_up = lax.all_to_all(gate_up, "core", 1, 0, tiled=True)
    gate_up_w = gather(gate_up, "chip")
    down_w = gather(lax.all_to_all(w_down_t, "core", 1, 0, tiled=True), "chip")

    mixed = dot(tokens_all, qkv_w)
    query_raw = mixed[:, :part]
    key_raw = mixed[:, part : 2 * part]
    value_low = mixed[:, 2 * part :].astype(BF16)
    squares = jnp.stack([jnp.sum(query_raw * query_raw, 1), jnp.sum(key_raw * key_raw, 1)])
    squares = lax.psum(squares, GROUP)
    factors = lax.rsqrt(squares / width + EPS)
    gain_q = lax.dynamic_slice_in_dim(gains[0], member * part, part)
    gain_k = lax.dynamic_slice_in_dim(gains[1], member * part, part)
    places = jnp.arange(length, dtype=jnp.int32)
    cosine, sine = rope_tables(places.astype(F32))
    cosine, sine = cosine[None, :, None, :], sine[None, :, None, :]
    shape = (cores, length, heads, HEAD_DIM)
    query_factor, key_factor = factors[0][:, None], factors[1][:, None]
    query_low = rotate((query_raw * query_factor * gain_q).reshape(shape), cosine, sine).astype(BF16)
    key_low = rotate((key_raw * key_factor * gain_k).reshape(shape), cosine, sine).astype(BF16)
    value_low = value_low.reshape(shape)

    ids = gather(segment[0], GROUP).reshape(cores, length)
    allowed = (
        (ids[:, :, None] == ids[:, None, :])
        & (places[None, None, :] <= places[None, :, None])
        & ((ids[:, None, :] != 0) | (places[None, None, :] == places[None, :, None]))
    )[:, None]
    scale = HEAD_DIM ** (-0.5)
    scores = jnp.einsum("bqhd,bkhd->bhqk", query_low, key_low, preferred_element_type=F32) * scale
    masked = jnp.where(allowed, scores, -1e30)
    row_max = jnp.max(masked, axis=-1, keepdims=True)
    weights = jnp.where(allowed, jnp.exp(masked - row_max), 0.0)
    shares = weights / jnp.sum(weights, axis=-1, keepdims=True)
    shares_low = shares.astype(BF16)
    attended = jnp.einsum("bhqk,bkhd->bqhd", shares_low, value_low, preferred_element_type=F32)
    attended_low = attended.reshape(total_rows, part).astype(BF16)
    projected = scatter_sum(dot(attended_low, out_w).astype(BF16), GROUP).astype(F32)

    tokens_wide = tokens.astype(F32)
    proj_factor = norm_factor(projected)
    residual = tokens_wide + projected * proj_factor * gains[2]
    residual_all = gather(residual.astype(BF16), GROUP)

    gate_up_out = dot(residual_all, gate_up_w)
    gate, up_part = gate_up_out[:, :hidden], gate_up_out[:, hidden:]
    sigmoid = 1.0 / (1.0 + jnp.exp(-gate))
    activated = (gate * sigmoid * up_part).astype(BF16)
    feed = scatter_sum(dot_rows(activated, down_w).astype(BF16), GROUP).astype(F32)
    feed_factor = norm_factor(feed)
    output = (residual + feed * feed_factor * gains[3]).astype(BF16)
    upstream = cotangent[0].astype(F32)
    feed_grad, gain_feed = norm_back(feed, feed_factor, gains[3], upstream)
    feed_grad_all = gather(feed_grad.astype(BF16), GROUP)

    act_grad = dot(feed_grad_all, down_w)
    gate_grad = act_grad * up_part * sigmoid * (1.0 + gate * (1.0 - sigmoid))
    up_grad = act_grad * (gate * sigmoid)
    gate_up_grad = jnp.concatenate([gate_grad.astype(BF16), up_grad.astype(BF16)], 1)
    back_feed = scatter_sum(dot_rows(gate_up_grad, gate_up_w).astype(BF16), GROUP).astype(F32)
    residual_grad = upstream + back_feed

    grad_gate_up = scatter_sum(dot_first(residual_all, gate_up_grad).astype(BF16), "chip")
    grad_gate_up = lax.all_to_all(grad_gate_up, "core", 0, 1, tiled=True)
    grad_gate_up = grad_gate_up.reshape(-1, cores, 2, hidden).astype(F32)
    grad_gate = grad_gate_up[:, :, 0].reshape(-1, cores * hidden)
    grad_up = grad_gate_up[:, :, 1].reshape(-1, cores * hidden)
    grad_down = scatter_sum(dot_first(feed_grad_all, activated).astype(BF16), "chip")
    grad_down = lax.all_to_all(grad_down, "core", 0, 1, tiled=True).astype(F32)

    projected_grad, gain_attn = norm_back(projected, proj_factor, gains[2], residual_grad)
    projected_all = gather(projected_grad.astype(BF16), GROUP)
    attended_grad = dot_rows(projected_all, out_w).astype(BF16).reshape(shape)

    share_grad = jnp.einsum("bqhd,bkhd->bhqk", attended_grad, value_low, preferred_element_type=F32)
    inner = jnp.sum(shares * share_grad, axis=-1, keepdims=True)
    score_grad = (shares * (share_grad - inner)).astype(BF16)
    query_grad = jnp.einsum("bhqk,bkhd->bqhd", score_grad, key_low, preferred_element_type=F32)
    key_grad = jnp.einsum("bhqk,bqhd->bkhd", score_grad, query_low, preferred_element_type=F32)
    value_grad = jnp.einsum("bhqk,bqhd->bkhd", shares_low, attended_grad, preferred_element_type=F32)
    query_turn = rotate_back(query_grad * scale, cosine, sine).reshape(total_rows, part)
    key_turn = rotate_back(key_grad * scale, cosine, sine).reshape(total_rows, part)
    query_norm, key_norm = query_raw * query_factor, key_raw * key_factor
    sums = jnp.stack(
        [jnp.sum(gain_q * query_turn * query_norm, 1), jnp.sum(gain_k * key_turn * key_norm, 1)]
    )
    means = lax.psum(sums, GROUP) / width
    query_mixed = query_factor * (gain_q * query_turn - query_norm * means[0][:, None])
    key_mixed = key_factor * (gain_k * key_turn - key_norm * means[1][:, None])
    gain_query = jnp.sum(query_turn * query_norm, 0)
    gain_key = jnp.sum(key_turn * key_norm, 0)
    mixed_grad = jnp.concatenate(
        [query_mixed, key_mixed, value_grad.reshape(total_rows, part)], 1
    ).astype(BF16)
    input_part = dot_rows(mixed_grad, qkv_w).astype(BF16)
    input_grad = residual_grad + scatter_sum(input_part, GROUP).astype(F32)

    grad_qkv = scatter_sum(dot_first(tokens_all, mixed_grad).astype(BF16), "chip")
    grad_qkv = grad_qkv.reshape(members, qkv_rows, 3 * part)
    grad_qkv = lax.all_to_all(grad_qkv, GROUP, 0, 0, tiled=True)
    grad_qkv = grad_qkv.reshape(members, qkv_rows, 3, part).transpose(1, 2, 0, 3)
    grad_qkv = grad_qkv.reshape(qkv_rows, 3 * width).astype(F32)

    out_part = dot_first(attended_low, projected_all).astype(BF16)
    out_part = lax.dynamic_update_slice_in_dim(
        jnp.zeros((width, width), BF16), out_part, member * part, 0
    )
    grad_out = scatter_sum(out_part, ALL).astype(F32)

    wide = jnp.zeros((2, width), F32)
    wide = lax.dynamic_update_slice(wide, jnp.stack([gain_query, gain_key]), (0, member * part))
    grad_gains = lax.psum(jnp.concatenate([wide, gain_attn[None], gain_feed[None]]), ALL)
    return (
        output[None],
        input_grad[None],
        grad_qkv,
        grad_out,
        grad_gate,
        grad_up,
        grad_down,
        grad_gains,
    )


def solution(mesh):
    cores = 2
    chips = mesh.shape["dp"] // cores
    split = Mesh(mesh.devices.reshape(chips, cores, mesh.shape["ctx"]), ALL)
    dp = ("chip", "core")
    every = P((*dp, "ctx"), None)
    in_specs = (
        P(dp, "ctx", None),
        P(dp, "ctx"),
        every,
        every,
        P(dp, "ctx"),
        P(dp, "ctx"),
        P(dp, "ctx"),
        P(),
        P(dp, "ctx", None),
    )
    out_specs = (
        P(dp, "ctx", None),
        P(dp, "ctx", None),
        every,
        every,
        P(dp, "ctx"),
        P(dp, "ctx"),
        P(dp, "ctx"),
        P(),
    )
    return jax.shard_map(
        per_device, mesh=split, in_specs=in_specs, out_specs=out_specs, check_vma=False
    )
```

```python
import jax
import jax.numpy as jnp
from jax import lax
from jax.experimental import pallas as pl
from jax.experimental.pallas import tpu as pltpu
from jax.sharding import Mesh
from jax.sharding import PartitionSpec as P

HEAD_DIM = 128
EPS = 1e-06
ROPE_BASE = 500000.0
F32 = jnp.float32
BF16 = jnp.bfloat16
GROUP = ("core", "ctx")
ALL = ("chip", "core", "ctx")


PIECE = 32
LAGB = 1
LAGJ = 1
MESH_ID = pl.DeviceIdType.MESH


def row_factor(values):
    return lax.rsqrt(jnp.mean(values * values, axis=-1, keepdims=True) + EPS)


def row_norm_back(values, gain, grad):
    factor = row_factor(values)
    normed = values * factor
    scaled = gain * grad
    back = factor * (scaled - normed * jnp.mean(scaled * normed, axis=-1, keepdims=True))
    return back, jnp.sum(grad * normed, axis=0, keepdims=True)


def after_projected(total, ins, outs, rows):
    tokens, gains = ins
    residual_out, projected_out = outs
    projected_out[rows, :] = total
    gain = gains[2:3, :]
    residual = tokens[rows, :].astype(F32) + total * row_factor(total) * gain
    residual_out[rows, :] = residual
    return residual


def after_feed(total, ins, outs, rows):
    residual, cotangent, gains = ins
    output, gain_out = outs
    gain = gains[3:4, :]
    normed = total * row_factor(total) * gain
    output[rows, :] = (residual[rows, :] + normed).astype(BF16)
    back, term = row_norm_back(total, gain, cotangent[rows, :].astype(F32))
    gain_out[...] += term
    return back


def after_back(total, ins, outs, rows):
    projected, cotangent, gains = ins
    grad_out, gain_out = outs
    grad = cotangent[rows, :].astype(F32) + total
    grad_out[rows, :] = grad
    back, term = row_norm_back(projected[rows, :], gains[2:3, :], grad)
    gain_out[...] += term
    return back


def after_input(total, ins, outs, rows):
    (grad,), (result,) = ins, outs
    result[rows, :] = grad[rows, :] + total
    return None


def pass_tokens(total, ins, outs, rows):
    return ins[0][rows, :]


class Exchange:
    def __init__(self, spans, rows, width, piece, reduce, spread, row_fn, n_in, n_out, gain):
        self.spans, self.rows, self.width, self.piece = spans, rows, width, piece
        self.reduce, self.spread, self.row_fn = reduce, spread, row_fn
        self.n_in, self.n_out, self.gain = n_in, n_out, gain
        self.count = rows // piece

    def scratch(self):
        spans, count = self.spans, self.count
        block = pltpu.VMEM((spans * self.rows, self.width), BF16)
        sems = pltpu.SemaphoreType.DMA((spans, count))
        items = []
        if self.reduce:
            items += [block] * 4 + [pltpu.SemaphoreType.DMA] + [sems] * 6
        if self.spread:
            items += [pltpu.VMEM((2 * spans * self.rows, self.width), BF16)]
            items += [sems] * 7 + [pltpu.SemaphoreType.DMA]
        return items

    def body(self, *refs):
        spans, rows, piece, count = self.spans, self.rows, self.piece, self.count
        refs = list(refs)
        take = lambda n: [refs.pop(0) for _ in range(n)]
        partial = take(1)[0] if self.reduce else None
        ins = take(self.n_in)
        outs = take(self.n_out)
        gathered = take(1)[0] if self.spread else None
        if self.reduce:
            own, near, from_left, from_right = take(4)
            (load_sem,) = take(1)
            near_send, near_recv, right_send, right_recv, left_send, left_recv = take(6)
        if self.spread:
            (held,) = take(1)
            fwd_send, fwd_recv, bwd_send, bwd_recv, own_send, side_send, side_recv = take(7)
            (store_sem,) = take(1)
        core = lax.axis_index("core")
        place = lax.axis_index("ctx")
        other = 1 - core
        has_left = place > 0
        has_right = place < spans - 1

        def at(block, k):
            return pl.ds(pl.multiple_of(block * rows + k * piece, piece), piece)

        def held_at(seq, block, k):
            return pl.ds(pl.multiple_of((seq * spans + block) * rows + k * piece, piece), piece)

        def remote(src, dst, send, recv, **device):
            return pltpu.make_async_remote_copy(
                src_ref=src, dst_ref=dst, send_sem=send, recv_sem=recv,
                device_id=device, device_id_type=MESH_ID,
            )

        barrier = pltpu.get_barrier_semaphore()
        pl.semaphore_signal(barrier, 1, device_id={"core": other}, device_id_type=MESH_ID)

        @pl.when(has_left)
        def _():
            pl.semaphore_signal(barrier, 1, device_id={"ctx": place - 1}, device_id_type=MESH_ID)

        @pl.when(has_right)
        def _():
            pl.semaphore_signal(barrier, 1, device_id={"ctx": place + 1}, device_id_type=MESH_ID)

        pl.semaphore_wait(barrier, 1 + has_left.astype(jnp.int32) + has_right.astype(jnp.int32))

        if self.gain is not None:
            outs[self.gain][...] = jnp.zeros_like(outs[self.gain])

        def near_copy(d, k):
            return remote(
                partial.at[held_at(other, d, k)], near.at[at(d, k)],
                near_send.at[d, k], near_recv.at[d, k], core=other,
            )

        def right_copy(d, k):
            return remote(
                own.at[at(d, k)], from_left.at[at(d, k)],
                right_send.at[d, k], right_recv.at[d, k], ctx=place + 1,
            )

        def left_copy(d, k):
            return remote(
                own.at[at(d, k)], from_right.at[at(d, k)],
                left_send.at[d, k], left_recv.at[d, k], ctx=place - 1,
            )

        def fwd_copy(o, k, send):
            where = held_at(core, o, k)
            return remote(held.at[where], held.at[where], send, fwd_recv.at[o, k], ctx=place + 1)

        def bwd_copy(o, k, send):
            where = held_at(core, o, k)
            return remote(held.at[where], held.at[where], send, bwd_recv.at[o, k], ctx=place - 1)

        def side_copy(o, k):
            where = held_at(core, o, k)
            return remote(held.at[where], held.at[where], side_send.at[o, k], side_recv.at[o, k], core=other)

        if self.reduce:
            load = pltpu.make_async_copy(
                partial.at[pl.ds(pl.multiple_of(core * spans * rows, rows), spans * rows)], own, load_sem
            )
            load.start()

            @pl.loop(0, count)
            def _(k):
                for j in range(spans):
                    near_copy(j, k).start()

            load.wait()

        def base(d, k):
            near_copy(d, k).wait_recv()
            return own[at(d, k), :].astype(F32) + near[at(d, k), :].astype(F32)

        def reduce_step(k):
            for j in range(spans - 1):
                right, left = spans - 1 - j, j

                @pl.when(jnp.logical_and(right > place, has_left))
                def _():
                    value = base(right, k)
                    right_copy(right, k).wait_recv()
                    own[at(right, k), :] = (value + from_left[at(right, k), :].astype(F32)).astype(BF16)
                    right_copy(right, k).start()

                @pl.when(jnp.logical_and(right > place, jnp.logical_not(has_left)))
                def _():
                    own[at(right, k), :] = base(right, k).astype(BF16)
                    right_copy(right, k).start()

                @pl.when(jnp.logical_and(left < place, has_right))
                def _():
                    value = base(left, k)
                    left_copy(left, k).wait_recv()
                    own[at(left, k), :] = (value + from_right[at(left, k), :].astype(F32)).astype(BF16)
                    left_copy(left, k).start()

                @pl.when(jnp.logical_and(left < place, jnp.logical_not(has_right)))
                def _():
                    own[at(left, k), :] = base(left, k).astype(BF16)
                    left_copy(left, k).start()

        def finish_step(k):
            total = None
            if self.reduce:
                total = base(place, k)

                @pl.when(has_left)
                def _():
                    right_copy(place, k).wait_recv()

                @pl.when(has_right)
                def _():
                    left_copy(place, k).wait_recv()

                zero = jnp.zeros_like(total)
                total = total + jnp.where(has_left, from_left[at(place, k), :].astype(F32), zero)
                total = total + jnp.where(has_right, from_right[at(place, k), :].astype(F32), zero)
            own_rows = pl.ds(pl.multiple_of(k * piece, piece), piece)
            result = self.row_fn(total, ins, outs, own_rows)
            if self.spread:
                held[held_at(core, place, k), :] = result.astype(BF16)

                @pl.when(has_right)
                def _():
                    fwd_copy(place, k, fwd_send.at[place, k]).start()

                @pl.when(has_left)
                def _():
                    bwd_copy(place, k, bwd_send.at[place, k]).start()

                side_copy(place, k).start()

        def relay_step(k, j):
            if True:

                @pl.when(place - j >= 0)
                def _():
                    fwd_copy(place - j, k, fwd_send.at[place - j, k]).wait_recv()

                    @pl.when(has_right)
                    def _():
                        fwd_copy(place - j, k, fwd_send.at[place - j, k]).start()

                    side_copy(place - j, k).start()

                @pl.when(place + j < spans)
                def _():
                    bwd_copy(place + j, k, bwd_send.at[place + j, k]).wait_recv()

                    @pl.when(has_left)
                    def _():
                        bwd_copy(place + j, k, bwd_send.at[place + j, k]).start()

                    side_copy(place + j, k).start()

        lag = LAGB if self.reduce else 0

        @pl.loop(0, count + lag + (LAGJ * (spans - 1) if self.spread else 0))
        def _(t):
            if self.reduce:

                @pl.when(t < count)
                def _():
                    reduce_step(t)

            @pl.when(jnp.logical_and(t >= lag, t < count + lag))
            def _():
                finish_step(t - lag)

            if self.spread:
                for j in range(1, spans):
                    after = t - lag - j * LAGJ

                    @pl.when(jnp.logical_and(after >= 0, after < count))
                    def _():
                        relay_step(after, j)

        if self.spread:

            @pl.loop(0, count)
            def _(k):
                for o in range(spans):
                    side_copy(o, k).wait_recv()

            store = pltpu.make_async_copy(held, gathered, store_sem)
            store.start()

        @pl.loop(0, count)
        def _(k):
            for d in range(spans):
                if self.reduce:
                    near_copy(d, k).wait_send()

                    @pl.when(d > place)
                    def _():
                        right_copy(d, k).wait_send()

                    @pl.when(d < place)
                    def _():
                        left_copy(d, k).wait_send()

                if self.spread:
                    side_copy(d, k).wait_send()

                    @pl.when(jnp.logical_and(d <= place, has_right))
                    def _():
                        fwd_copy(d, k, fwd_send.at[d, k]).wait_send()

                    @pl.when(jnp.logical_and(d >= place, has_left))
                    def _():
                        bwd_copy(d, k, bwd_send.at[d, k]).wait_send()

        if self.spread:
            store.wait()

    def call(self, name, collective_id, partial, ins, outs):
        vmem = pl.BlockSpec(memory_space=pltpu.VMEM)
        hbm = pl.BlockSpec(memory_space=pl.ANY)
        shapes = list(outs)
        specs = [vmem] * len(outs)
        if self.spread:
            shapes.append(jax.ShapeDtypeStruct((2 * self.spans * self.rows, self.width), BF16))
            specs.append(hbm)
        operands = ([partial] if self.reduce else []) + list(ins)
        return pl.pallas_call(
            self.body,
            out_shape=shapes,
            in_specs=([hbm] if self.reduce else []) + [vmem] * len(ins),
            out_specs=specs,
            scratch_shapes=self.scratch(),
            compiler_params=pltpu.CompilerParams(
                collective_id=collective_id, has_side_effects=True, vmem_limit_bytes=40 << 20
            ),
            name=name,
        )(*operands)


def rope_tables(positions):
    half = HEAD_DIM // 2
    frequency = ROPE_BASE ** (-(jnp.arange(half, dtype=F32) * 2.0 / HEAD_DIM))
    angles = positions[:, None] * frequency[None, :]
    cosine = jnp.cos(angles)
    sine = jnp.sin(angles)
    return (jnp.concatenate([cosine, cosine], 1), jnp.concatenate([sine, sine], 1))


def rotate(values, cosine, sine):
    half = HEAD_DIM // 2
    turned = jnp.concatenate([-values[..., half:], values[..., :half]], -1)
    return values * cosine + turned * sine


def rotate_back(values, cosine, sine):
    half = HEAD_DIM // 2
    scaled = values * sine
    turned = jnp.concatenate([scaled[..., half:], -scaled[..., :half]], -1)
    return values * cosine + turned


def dot(left, right):
    return jnp.dot(left, right, preferred_element_type=F32)


def dot_rows(left, right):
    return lax.dot_general(left, right, (((1,), (1,)), ((), ())), preferred_element_type=F32)


def dot_first(left, right):
    return lax.dot_general(left, right, (((0,), (0,)), ((), ())), preferred_element_type=F32)


def gather(values, axes):
    return lax.all_gather(values, axes, axis=0, tiled=True)


def scatter_sum(values, axes):
    return lax.psum_scatter(values, axes, scatter_dimension=0, tiled=True)


def per_device(inputs, segment, w_qkv, w_out, w_gate, w_up, w_down_t, gains, cotangent):
    rows, width = inputs.shape[1:]
    cores = lax.axis_size("core")
    spans = lax.axis_size("ctx")
    members = cores * spans
    length = rows * spans
    total_rows = cores * length
    part = width // members
    heads = part // HEAD_DIM
    member = lax.axis_index(GROUP)
    tokens = inputs[0]

    qkv_rows = w_qkv.shape[0]
    qkv_cut = w_qkv.reshape(qkv_rows, 3, members, part).transpose(2, 0, 1, 3)
    qkv_cut = qkv_cut.reshape(members, qkv_rows, 3 * part)
    qkv_cut = lax.all_to_all(qkv_cut, GROUP, 0, 0, tiled=True)
    qkv_w = gather(qkv_cut.reshape(members * qkv_rows, 3 * part), "chip")
    spread = lambda reduce, row_fn, n_in, n_out, gain: Exchange(
        spans, rows, width, PIECE, reduce, True, row_fn, n_in, n_out, gain
    )
    own = jax.ShapeDtypeStruct((rows, width), F32)
    own_low = jax.ShapeDtypeStruct((rows, width), BF16)
    one = jax.ShapeDtypeStruct((1, width), F32)
    (tokens_all,) = spread(False, pass_tokens, 1, 0, None).call("gather_tokens", 1, None, [tokens], [])
    out_full = gather(w_out, ALL)
    out_w = lax.dynamic_slice_in_dim(out_full, member * part, part, 0)

    hidden = w_gate.shape[1] // cores
    gate_up = jnp.concatenate(
        [w_gate.reshape(-1, cores, 1, hidden), w_up.reshape(-1, cores, 1, hidden)], 2
    ).reshape(-1, cores * 2 * hidden)
    gate_up = lax.all_to_all(gate_up, "core", 1, 0, tiled=True)
    gate_up_w = gather(gate_up, "chip")
    down_w = gather(lax.all_to_all(w_down_t, "core", 1, 0, tiled=True), "chip")

    mixed = dot(tokens_all, qkv_w)
    query_raw = mixed[:, :part]
    key_raw = mixed[:, part : 2 * part]
    value_low = mixed[:, 2 * part :].astype(BF16)
    squares = jnp.stack([jnp.sum(query_raw * query_raw, 1), jnp.sum(key_raw * key_raw, 1)])
    squares = lax.psum(squares, GROUP)
    factors = lax.rsqrt(squares / width + EPS)
    gain_q = lax.dynamic_slice_in_dim(gains[0], member * part, part)
    gain_k = lax.dynamic_slice_in_dim(gains[1], member * part, part)
    places = jnp.arange(length, dtype=jnp.int32)
    cosine, sine = rope_tables(places.astype(F32))
    cosine, sine = cosine[None, :, None, :], sine[None, :, None, :]
    shape = (cores, length, heads, HEAD_DIM)
    query_factor, key_factor = factors[0][:, None], factors[1][:, None]
    query_low = rotate((query_raw * query_factor * gain_q).reshape(shape), cosine, sine).astype(BF16)
    key_low = rotate((key_raw * key_factor * gain_k).reshape(shape), cosine, sine).astype(BF16)
    value_low = value_low.reshape(shape)

    ids = gather(segment[0], GROUP).reshape(cores, length)
    allowed = (
        (ids[:, :, None] == ids[:, None, :])
        & (places[None, None, :] <= places[None, :, None])
        & ((ids[:, None, :] != 0) | (places[None, None, :] == places[None, :, None]))
    )[:, None]
    scale = HEAD_DIM ** (-0.5)
    scores = jnp.einsum("bqhd,bkhd->bhqk", query_low, key_low, preferred_element_type=F32) * scale
    masked = jnp.where(allowed, scores, -1e30)
    row_max = jnp.max(masked, axis=-1, keepdims=True)
    weights = jnp.where(allowed, jnp.exp(masked - row_max), 0.0)
    shares = weights / jnp.sum(weights, axis=-1, keepdims=True)
    shares_low = shares.astype(BF16)
    attended = jnp.einsum("bhqk,bkhd->bqhd", shares_low, value_low, preferred_element_type=F32)
    attended_low = attended.reshape(total_rows, part).astype(BF16)
    residual, projected, residual_all = spread(True, after_projected, 2, 2, None).call(
        "sum_projected", 2, dot(attended_low, out_w).astype(BF16), [tokens, gains], [own, own]
    )

    gate_up_out = dot(residual_all, gate_up_w)
    gate, up_part = gate_up_out[:, :hidden], gate_up_out[:, hidden:]
    sigmoid = 1.0 / (1.0 + jnp.exp(-gate))
    activated = (gate * sigmoid * up_part).astype(BF16)
    output, gain_feed, feed_grad_all = spread(True, after_feed, 3, 2, 1).call(
        "sum_feed",
        3,
        dot_rows(activated, down_w).astype(BF16),
        [residual, cotangent[0], gains],
        [own_low, one],
    )

    act_grad = dot(feed_grad_all, down_w)
    gate_grad = act_grad * up_part * sigmoid * (1.0 + gate * (1.0 - sigmoid))
    up_grad = act_grad * (gate * sigmoid)
    gate_up_grad = jnp.concatenate([gate_grad.astype(BF16), up_grad.astype(BF16)], 1)
    residual_grad, gain_attn, projected_all = spread(True, after_back, 3, 2, 1).call(
        "sum_back",
        4,
        dot_rows(gate_up_grad, gate_up_w).astype(BF16),
        [projected, cotangent[0], gains],
        [own, one],
    )

    grad_gate_up = scatter_sum(dot_first(residual_all, gate_up_grad).astype(BF16), "chip")
    grad_gate_up = lax.all_to_all(grad_gate_up, "core", 0, 1, tiled=True)
    grad_gate_up = grad_gate_up.reshape(-1, cores, 2, hidden).astype(F32)
    grad_gate = grad_gate_up[:, :, 0].reshape(-1, cores * hidden)
    grad_up = grad_gate_up[:, :, 1].reshape(-1, cores * hidden)
    grad_down = scatter_sum(dot_first(feed_grad_all, activated).astype(BF16), "chip")
    grad_down = lax.all_to_all(grad_down, "core", 0, 1, tiled=True).astype(F32)

    attended_grad = dot_rows(projected_all, out_w).astype(BF16).reshape(shape)

    share_grad = jnp.einsum("bqhd,bkhd->bhqk", attended_grad, value_low, preferred_element_type=F32)
    inner = jnp.sum(shares * share_grad, axis=-1, keepdims=True)
    score_grad = (shares * (share_grad - inner)).astype(BF16)
    query_grad = jnp.einsum("bhqk,bkhd->bqhd", score_grad, key_low, preferred_element_type=F32)
    key_grad = jnp.einsum("bhqk,bqhd->bkhd", score_grad, query_low, preferred_element_type=F32)
    value_grad = jnp.einsum("bhqk,bqhd->bkhd", shares_low, attended_grad, preferred_element_type=F32)
    query_turn = rotate_back(query_grad * scale, cosine, sine).reshape(total_rows, part)
    key_turn = rotate_back(key_grad * scale, cosine, sine).reshape(total_rows, part)
    query_norm, key_norm = query_raw * query_factor, key_raw * key_factor
    sums = jnp.stack(
        [jnp.sum(gain_q * query_turn * query_norm, 1), jnp.sum(gain_k * key_turn * key_norm, 1)]
    )
    means = lax.psum(sums, GROUP) / width
    query_mixed = query_factor * (gain_q * query_turn - query_norm * means[0][:, None])
    key_mixed = key_factor * (gain_k * key_turn - key_norm * means[1][:, None])
    gain_query = jnp.sum(query_turn * query_norm, 0)
    gain_key = jnp.sum(key_turn * key_norm, 0)
    mixed_grad = jnp.concatenate(
        [query_mixed, key_mixed, value_grad.reshape(total_rows, part)], 1
    ).astype(BF16)
    input_part = dot_rows(mixed_grad, qkv_w).astype(BF16)
    (input_grad,) = Exchange(
        spans, rows, width, PIECE, True, False, after_input, 1, 1, None
    ).call("sum_input", 5, input_part, [residual_grad], [own])

    grad_qkv = scatter_sum(dot_first(tokens_all, mixed_grad).astype(BF16), "chip")
    grad_qkv = grad_qkv.reshape(members, qkv_rows, 3 * part)
    grad_qkv = lax.all_to_all(grad_qkv, GROUP, 0, 0, tiled=True)
    grad_qkv = grad_qkv.reshape(members, qkv_rows, 3, part).transpose(1, 2, 0, 3)
    grad_qkv = grad_qkv.reshape(qkv_rows, 3 * width).astype(F32)

    out_part = dot_first(attended_low, projected_all).astype(BF16)
    out_part = lax.dynamic_update_slice_in_dim(
        jnp.zeros((width, width), BF16), out_part, member * part, 0
    )
    grad_out = scatter_sum(out_part, ALL).astype(F32)

    wide = jnp.zeros((2, width), F32)
    wide = lax.dynamic_update_slice(wide, jnp.stack([gain_query, gain_key]), (0, member * part))
    grad_gains = lax.psum(jnp.concatenate([wide, gain_attn, gain_feed]), ALL)
    return (
        output[None],
        input_grad[None],
        grad_qkv,
        grad_out,
        grad_gate,
        grad_up,
        grad_down,
        grad_gains,
    )


def solution(mesh):
    cores = 2
    chips = mesh.shape["dp"] // cores
    split = Mesh(mesh.devices.reshape(chips, cores, mesh.shape["ctx"]), ALL)
    dp = ("chip", "core")
    every = P((*dp, "ctx"), None)
    in_specs = (
        P(dp, "ctx", None),
        P(dp, "ctx"),
        every,
        every,
        P(dp, "ctx"),
        P(dp, "ctx"),
        P(dp, "ctx"),
        P(),
        P(dp, "ctx", None),
    )
    out_specs = (
        P(dp, "ctx", None),
        P(dp, "ctx", None),
        every,
        every,
        P(dp, "ctx"),
        P(dp, "ctx"),
        P(dp, "ctx"),
        P(),
    )
    return jax.shard_map(
        per_device, mesh=split, in_specs=in_specs, out_specs=out_specs, check_vma=False
    )
```

```python
import jax
import jax.numpy as jnp
from jax import lax
from jax.experimental import pallas as pl
from jax.experimental.pallas import tpu as pltpu
from jax.sharding import Mesh
from jax.sharding import PartitionSpec as P

HEAD_DIM = 128
EPS = 1e-06
ROPE_BASE = 500000.0
F32 = jnp.float32
BF16 = jnp.bfloat16
GROUP = ("core", "ctx")
ALL = ("chip", "core", "ctx")


PIECE = 32
LAGB = 1
LAGJ = 1
MESH_ID = pl.DeviceIdType.MESH


def row_factor(values):
    return lax.rsqrt(jnp.mean(values * values, axis=-1, keepdims=True) + EPS)


def row_norm_back(values, gain, grad):
    factor = row_factor(values)
    normed = values * factor
    scaled = gain * grad
    back = factor * (scaled - normed * jnp.mean(scaled * normed, axis=-1, keepdims=True))
    return back, jnp.sum(grad * normed, axis=0, keepdims=True)


def after_projected(total, ins, outs, rows):
    tokens, gains = ins
    residual_out, projected_out = outs
    projected_out[rows, :] = total
    gain = gains[2:3, :]
    residual = tokens[rows, :].astype(F32) + total * row_factor(total) * gain
    residual_out[rows, :] = residual
    return residual


def after_feed(total, ins, outs, rows):
    residual, cotangent, gains = ins
    output, gain_out = outs
    gain = gains[3:4, :]
    normed = total * row_factor(total) * gain
    output[rows, :] = (residual[rows, :] + normed).astype(BF16)
    back, term = row_norm_back(total, gain, cotangent[rows, :].astype(F32))
    gain_out[...] += term
    return back


def after_back(total, ins, outs, rows):
    projected, cotangent, gains = ins
    grad_out, gain_out = outs
    grad = cotangent[rows, :].astype(F32) + total
    grad_out[rows, :] = grad
    back, term = row_norm_back(projected[rows, :], gains[2:3, :], grad)
    gain_out[...] += term
    return back


def after_input(total, ins, outs, rows):
    (grad,), (result,) = ins, outs
    result[rows, :] = grad[rows, :] + total
    return None


def pass_tokens(total, ins, outs, rows):
    return ins[0][rows, :]


class Exchange:
    def __init__(self, spans, rows, width, piece, reduce, spread, row_fn, n_in, n_out, gain, extra=None):
        self.extra = extra
        self.spans, self.rows, self.width, self.piece = spans, rows, width, piece
        self.reduce, self.spread, self.row_fn = reduce, spread, row_fn
        self.n_in, self.n_out, self.gain = n_in, n_out, gain
        self.count = rows // piece

    def scratch(self):
        spans, count = self.spans, self.count
        block = pltpu.VMEM((spans * self.rows, self.width), BF16)
        sems = pltpu.SemaphoreType.DMA((spans, count))
        items = []
        if self.reduce:
            items += [block] * 4 + [pltpu.SemaphoreType.DMA] + [sems] * 6
        if self.spread:
            items += [pltpu.VMEM((2 * spans * self.rows, self.width), BF16)]
            items += [sems] * 7 + [pltpu.SemaphoreType.DMA]
        if self.extra is not None:
            items += self.extra.scratch()
        return items

    def body(self, *refs):
        spans, rows, piece, count = self.spans, self.rows, self.piece, self.count
        refs = list(refs)
        take = lambda n: [refs.pop(0) for _ in range(n)]
        partial = take(1)[0] if self.reduce else None
        ins = take(self.n_in)
        extra = self.extra
        if extra is not None:
            extra.ins = take(extra.n_in)
        outs = take(self.n_out)
        if extra is not None:
            extra.outs = take(extra.n_out)
        gathered = take(1)[0] if self.spread else None
        if self.reduce:
            own, near, from_left, from_right = take(4)
            (load_sem,) = take(1)
            near_send, near_recv, right_send, right_recv, left_send, left_recv = take(6)
        if self.spread:
            (held,) = take(1)
            fwd_send, fwd_recv, bwd_send, bwd_recv, own_send, side_send, side_recv = take(7)
            (store_sem,) = take(1)
        if extra is not None:
            extra.held = refs
        core = lax.axis_index("core")
        place = lax.axis_index("ctx")
        other = 1 - core
        has_left = place > 0
        has_right = place < spans - 1

        def at(block, k):
            return pl.ds(pl.multiple_of(block * rows + k * piece, piece), piece)

        def held_at(seq, block, k):
            return pl.ds(pl.multiple_of((seq * spans + block) * rows + k * piece, piece), piece)

        def remote(src, dst, send, recv, **device):
            return pltpu.make_async_remote_copy(
                src_ref=src, dst_ref=dst, send_sem=send, recv_sem=recv,
                device_id=device, device_id_type=MESH_ID,
            )

        barrier = pltpu.get_barrier_semaphore()
        if extra is not None:
            meet_all(spans)
        else:
            pl.semaphore_signal(barrier, 1, device_id={"core": other}, device_id_type=MESH_ID)

            @pl.when(has_left)
            def _():
                pl.semaphore_signal(barrier, 1, device_id={"ctx": place - 1}, device_id_type=MESH_ID)

            @pl.when(has_right)
            def _():
                pl.semaphore_signal(barrier, 1, device_id={"ctx": place + 1}, device_id_type=MESH_ID)

            pl.semaphore_wait(barrier, 1 + has_left.astype(jnp.int32) + has_right.astype(jnp.int32))

        if self.gain is not None:
            outs[self.gain][...] = jnp.zeros_like(outs[self.gain])

        def near_copy(d, k):
            return remote(
                partial.at[held_at(other, d, k)], near.at[at(d, k)],
                near_send.at[d, k], near_recv.at[d, k], core=other,
            )

        def right_copy(d, k):
            return remote(
                own.at[at(d, k)], from_left.at[at(d, k)],
                right_send.at[d, k], right_recv.at[d, k], ctx=place + 1,
            )

        def left_copy(d, k):
            return remote(
                own.at[at(d, k)], from_right.at[at(d, k)],
                left_send.at[d, k], left_recv.at[d, k], ctx=place - 1,
            )

        def fwd_copy(o, k, send):
            where = held_at(core, o, k)
            return remote(held.at[where], held.at[where], send, fwd_recv.at[o, k], ctx=place + 1)

        def bwd_copy(o, k, send):
            where = held_at(core, o, k)
            return remote(held.at[where], held.at[where], send, bwd_recv.at[o, k], ctx=place - 1)

        def side_copy(o, k):
            where = held_at(core, o, k)
            return remote(held.at[where], held.at[where], side_send.at[o, k], side_recv.at[o, k], core=other)

        if extra is not None:
            extra.start()
        if self.reduce:
            load = pltpu.make_async_copy(
                partial.at[pl.ds(pl.multiple_of(core * spans * rows, rows), spans * rows)], own, load_sem
            )
            load.start()

            @pl.loop(0, count)
            def _(k):
                for j in range(spans):
                    near_copy(j, k).start()

            load.wait()

        def base(d, k):
            near_copy(d, k).wait_recv()
            return own[at(d, k), :].astype(F32) + near[at(d, k), :].astype(F32)

        def reduce_step(k):
            for j in range(spans - 1):
                right, left = spans - 1 - j, j

                @pl.when(jnp.logical_and(right > place, has_left))
                def _():
                    value = base(right, k)
                    right_copy(right, k).wait_recv()
                    own[at(right, k), :] = (value + from_left[at(right, k), :].astype(F32)).astype(BF16)
                    right_copy(right, k).start()

                @pl.when(jnp.logical_and(right > place, jnp.logical_not(has_left)))
                def _():
                    own[at(right, k), :] = base(right, k).astype(BF16)
                    right_copy(right, k).start()

                @pl.when(jnp.logical_and(left < place, has_right))
                def _():
                    value = base(left, k)
                    left_copy(left, k).wait_recv()
                    own[at(left, k), :] = (value + from_right[at(left, k), :].astype(F32)).astype(BF16)
                    left_copy(left, k).start()

                @pl.when(jnp.logical_and(left < place, jnp.logical_not(has_right)))
                def _():
                    own[at(left, k), :] = base(left, k).astype(BF16)
                    left_copy(left, k).start()

        def finish_step(k):
            total = None
            if self.reduce:
                total = base(place, k)

                @pl.when(has_left)
                def _():
                    right_copy(place, k).wait_recv()

                @pl.when(has_right)
                def _():
                    left_copy(place, k).wait_recv()

                zero = jnp.zeros_like(total)
                total = total + jnp.where(has_left, from_left[at(place, k), :].astype(F32), zero)
                total = total + jnp.where(has_right, from_right[at(place, k), :].astype(F32), zero)
            own_rows = pl.ds(pl.multiple_of(k * piece, piece), piece)
            result = self.row_fn(total, ins, outs, own_rows)
            if self.spread:
                held[held_at(core, place, k), :] = result.astype(BF16)

                @pl.when(has_right)
                def _():
                    fwd_copy(place, k, fwd_send.at[place, k]).start()

                @pl.when(has_left)
                def _():
                    bwd_copy(place, k, bwd_send.at[place, k]).start()

                side_copy(place, k).start()

        def relay_step(k, j):
            if True:

                @pl.when(place - j >= 0)
                def _():
                    fwd_copy(place - j, k, fwd_send.at[place - j, k]).wait_recv()

                    @pl.when(has_right)
                    def _():
                        fwd_copy(place - j, k, fwd_send.at[place - j, k]).start()

                    side_copy(place - j, k).start()

                @pl.when(place + j < spans)
                def _():
                    bwd_copy(place + j, k, bwd_send.at[place + j, k]).wait_recv()

                    @pl.when(has_left)
                    def _():
                        bwd_copy(place + j, k, bwd_send.at[place + j, k]).start()

                    side_copy(place + j, k).start()

        lag = LAGB if self.reduce else 0

        @pl.loop(0, count + lag + (LAGJ * (spans - 1) if self.spread else 0))
        def _(t):
            if self.reduce:

                @pl.when(t < count)
                def _():
                    reduce_step(t)

            if self.reduce:

                @pl.when(jnp.logical_and(t >= lag, t < count + lag))
                def _():
                    finish_step(t - lag)
            else:

                @pl.when(t == 0)
                def _():
                    for k in range(count):
                        finish_step(k)

            if self.spread:
                for j in range(1, spans):
                    after = t - lag - j * LAGJ

                    @pl.when(jnp.logical_and(after >= 0, after < count))
                    def _():
                        relay_step(after, j)
            if extra is not None:
                extra.tick(t)

        if extra is not None:
            extra.finish(count + lag + (LAGJ * (spans - 1) if self.spread else 0))
        if self.spread:

            @pl.loop(0, count)
            def _(k):
                for o in range(spans):
                    side_copy(o, k).wait_recv()

            store = pltpu.make_async_copy(held, gathered, store_sem)
            store.start()

        @pl.loop(0, count)
        def _(k):
            for d in range(spans):
                if self.reduce:
                    near_copy(d, k).wait_send()

                    @pl.when(d > place)
                    def _():
                        right_copy(d, k).wait_send()

                    @pl.when(d < place)
                    def _():
                        left_copy(d, k).wait_send()

                if self.spread:
                    side_copy(d, k).wait_send()

                    @pl.when(jnp.logical_and(d <= place, has_right))
                    def _():
                        fwd_copy(d, k, fwd_send.at[d, k]).wait_send()

                    @pl.when(jnp.logical_and(d >= place, has_left))
                    def _():
                        bwd_copy(d, k, bwd_send.at[d, k]).wait_send()

        if self.spread:
            store.wait()

    def call(self, name, collective_id, partial, ins, outs):
        vmem = pl.BlockSpec(memory_space=pltpu.VMEM)
        hbm = pl.BlockSpec(memory_space=pl.ANY)
        operands = ([partial] if self.reduce else []) + list(ins)
        in_specs = ([hbm] if self.reduce else []) + [vmem] * len(ins)
        shapes = list(outs)
        specs = [vmem] * len(outs)
        if self.extra is not None:
            operands += self.extra.operands
            in_specs += self.extra.in_specs
            shapes += self.extra.out_shapes
            specs += self.extra.out_specs
        if self.spread:
            shapes.append(jax.ShapeDtypeStruct((2 * self.spans * self.rows, self.width), BF16))
            specs.append(hbm)
        return pl.pallas_call(
            self.body,
            out_shape=shapes,
            in_specs=in_specs,
            out_specs=specs,
            scratch_shapes=self.scratch(),
            compiler_params=pltpu.CompilerParams(
                collective_id=collective_id, has_side_effects=True, vmem_limit_bytes=48 << 20
            ),
            cost_estimate=pl.CostEstimate(
                flops=0,
                bytes_accessed=(50 if self.reduce else 30) * self.width * self.width,
                transcendentals=0,
            ),
            name=name,
        )(*operands)


def meet_all(spans):
    chips = lax.axis_size("chip")
    barrier = pltpu.get_barrier_semaphore()
    chip = lax.axis_index("chip")
    core = lax.axis_index("core")
    place = lax.axis_index("ctx")
    for s in range(1, chips):
        pl.semaphore_signal(
            barrier, 1, device_id={"chip": lax.rem(chip + s, chips)}, device_id_type=MESH_ID
        )
    for s in range(1, 2 * spans):
        to_core, to_place = step_member(core, place, s, spans)
        pl.semaphore_signal(
            barrier, 1, device_id={"core": to_core, "ctx": to_place}, device_id_type=MESH_ID
        )
    pl.semaphore_wait(barrier, chips - 1 + 2 * spans - 1)


def step_member(core, place, s, spans):
    return lax.rem(core + s % 2, 2), lax.rem(place + s // 2, spans)


class Extra:
    def remote(self, src, dst, send, recv, **device):
        return pltpu.make_async_remote_copy(
            src_ref=src, dst_ref=dst, send_sem=send, recv_sem=recv,
            device_id=device, device_id_type=MESH_ID,
        )

    def locate(self):
        self.chip = lax.axis_index("chip")
        self.core = lax.axis_index("core")
        self.place = lax.axis_index("ctx")
        self.me = self.core * self.spans + self.place


class QkvWeights(Extra):
    n_in, n_out = 2, 2

    def __init__(self, spans, chips, cut, ids):
        self.spans, self.chips = spans, chips
        self.members, self.block, self.columns = cut.shape
        self.operands = [cut, ids]
        self.ids_shape = ids.shape
        vmem = pl.BlockSpec(memory_space=pltpu.VMEM)
        self.in_specs = [vmem, vmem]
        self.out_shapes = [
            jax.ShapeDtypeStruct((chips * self.members * self.block, self.columns), BF16),
            jax.ShapeDtypeStruct((self.members * ids.shape[0], ids.shape[1]), jnp.int32),
        ]
        self.out_specs = [vmem, vmem]

    def scratch(self):
        rows = self.chips * self.members * self.block
        sems = pltpu.SemaphoreType.DMA((self.members,))
        cross = pltpu.SemaphoreType.DMA((self.chips, self.members))
        ids = (self.members * self.ids_shape[0], self.ids_shape[1])
        return [pltpu.VMEM((rows, self.columns), BF16), pltpu.VMEM(ids, jnp.int32)] + [sems] * 4 + [cross] * 2

    def at(self, chip, m):
        return pl.ds(pl.multiple_of((chip * self.members + m) * self.block, self.block), self.block)

    def ids_at(self, m):
        return pl.ds(pl.multiple_of(m * self.ids_shape[0], self.ids_shape[0]), self.ids_shape[0])

    def block_copy(self, s):
        full, _, send, recv = self.held[:4]
        core, place = step_member(self.core, self.place, s, self.spans)
        return self.remote(
            self.ins[0].at[core * self.spans + place], full.at[self.at(self.chip, self.me)],
            send.at[s], recv.at[s], core=core, ctx=place,
        )

    def ids_copy(self, s):
        all_ids, send, recv = self.held[1], self.held[4], self.held[5]
        core, place = step_member(self.core, self.place, s, self.spans)
        return self.remote(
            self.ins[1], all_ids.at[self.ids_at(self.me)], send.at[s], recv.at[s], core=core, ctx=place
        )

    def source(self, s):
        core = lax.rem(self.core + s % 2, 2)
        return core * self.spans + lax.rem(self.place + self.spans - s // 2, self.spans)

    def chip_copy(self, s, m):
        full, _, _, _, _, _, send, recv = self.held
        where = self.at(self.chip, m)
        return self.remote(
            full.at[where], full.at[where], send.at[s, m], recv.at[s, m], chip=lax.rem(self.chip + s, self.chips)
        )

    def start(self):
        self.locate()
        cut, ids = self.ins
        full, all_ids = self.held[:2]
        for s in range(1, self.members):
            self.block_copy(s).start()
        for s in range(1, self.members):
            self.ids_copy(s).start()
        full[self.at(self.chip, self.me), :] = cut[self.me]
        all_ids[self.ids_at(self.me), :] = ids[...]

    def send_block(self, s):
        m = self.me if s == 0 else self.source(s)
        if s > 0:
            self.block_copy(s).wait_recv()
        for step in range(1, self.chips):
            self.chip_copy(step, m).start()

    def tick(self, t):
        @pl.when(t == 0)
        def _():
            for s in range(self.members):
                self.send_block(s)

    def finish(self, ticks):
        full, all_ids = self.held[:2]
        for s in range(1, self.members):
            self.ids_copy(s).wait_recv()
            self.block_copy(s).wait_send()
            self.ids_copy(s).wait_send()

        @pl.loop(0, self.members)
        def _(m):
            for s in range(1, self.chips):
                self.chip_copy(s, m).wait()

        self.outs[0][...] = full[...]
        self.outs[1][...] = all_ids[...]


class QkvGrads(Extra):
    n_in, n_out = 2, 2

    def __init__(self, spans, chips, members, grads, sums):
        self.spans, self.chips, self.members = spans, chips, members
        self.block, self.columns = grads.shape[0] // (chips * members), grads.shape[1]
        self.part = self.columns // 3
        self.width = self.part * members
        self.own_rows = self.part // 128
        self.sum_rows = sums.shape[0]
        self.operands = [grads, sums]
        vmem = pl.BlockSpec(memory_space=pltpu.VMEM)
        self.in_specs = [vmem, vmem]
        self.out_shapes = [
            jax.ShapeDtypeStruct((self.block, 3 * self.width), F32),
            jax.ShapeDtypeStruct((4, self.width // 128, 128), F32),
        ]
        self.out_specs = [vmem, vmem]

    def scratch(self):
        sems = pltpu.SemaphoreType.DMA((self.members,))
        chip_sems = pltpu.SemaphoreType.DMA((self.chips,))
        cross = pltpu.SemaphoreType.DMA((self.chips, self.members))
        return [
            pltpu.VMEM((self.chips, self.members, self.block, self.columns), BF16),
            pltpu.VMEM((self.members, self.block, self.columns), BF16),
            pltpu.VMEM((self.members, self.block, self.columns), BF16),
            pltpu.VMEM((self.chips, self.sum_rows, 128), F32),
            pltpu.VMEM((self.sum_rows, 128), F32),
            pltpu.VMEM((self.members, self.sum_rows, 128), F32),
        ] + [cross] * 2 + [sems] * 2 + [chip_sems] * 2 + [sems] * 2

    def at(self, chip, m):
        return pl.ds(pl.multiple_of((chip * self.members + m) * self.block, self.block), self.block)

    def chip_copy(self, s, m):
        other = lax.rem(self.chip + s, self.chips)
        return self.remote(
            self.ins[0].at[self.at(other, m)], self.arrived.at[s, m],
            self.cross_send.at[s, m], self.cross_recv.at[s, m], chip=other,
        )

    def member_copy(self, s):
        core, place = step_member(self.core, self.place, s, self.spans)
        return self.remote(
            self.summed.at[core * self.spans + place], self.columns_in.at[self.me],
            self.member_send.at[s], self.member_recv.at[s], core=core, ctx=place,
        )

    def sums_chip(self, s):
        return self.remote(
            self.ins[1], self.sums_in.at[s], self.sums_send.at[s], self.sums_recv.at[s],
            chip=lax.rem(self.chip + s, self.chips),
        )

    def sums_member(self, s):
        core, place = step_member(self.core, self.place, s, self.spans)
        return self.remote(
            self.sums_chips, self.sums_members.at[self.me], self.last_send.at[s], self.last_recv.at[s],
            core=core, ctx=place,
        )

    def start(self):
        self.locate()
        (
            self.arrived, self.summed, self.columns_in, self.sums_in, self.sums_chips, self.sums_members,
            self.cross_send, self.cross_recv, self.member_send, self.member_recv,
            self.sums_send, self.sums_recv, self.last_send, self.last_recv,
        ) = self.held
        for s in range(1, self.chips):
            self.sums_chip(s).start()

        @pl.loop(0, self.members)
        def _(i):
            m = lax.rem(self.me + 1 + i, self.members)
            for s in range(1, self.chips):
                self.chip_copy(s, m).start()

    def add_block(self, m):
        total = self.ins[0][self.at(self.chip, m), :].astype(F32)
        for s in range(1, self.chips):
            self.chip_copy(s, m).wait_recv()
            total = total + self.arrived[s, m].astype(F32)
        self.summed[m] = total.astype(BF16)

    def send_blocks(self, first, last):
        for s in range(first, last):
            core, place = step_member(self.core, self.place, s, self.spans)
            self.add_block(core * self.spans + place)
            self.member_copy(s).start()

    def tick(self, t):
        @pl.when(t == 1)
        def _():
            total = self.ins[1][...]
            for s in range(1, self.chips):
                self.sums_chip(s).wait_recv()
                total = total + self.sums_in[s]
            self.sums_chips[...] = total
            self.sums_members[self.me] = total
            for s in range(1, self.members):
                self.sums_member(s).start()

    def finish(self, ticks):
        self.send_blocks(1, self.members)
        self.add_block(self.me)
        self.columns_in[self.me] = self.summed[self.me]
        for s in range(1, self.members):
            self.sums_member(s).wait()
        wide = self.width // 128
        for i in range(2):
            total = self.sums_members[0, i * wide : (i + 1) * wide, :]
            for m in range(1, self.members):
                total = total + self.sums_members[m, i * wide : (i + 1) * wide, :]
            self.outs[1][2 + i] = total
            base = 2 * wide + i * self.own_rows
            for m in range(self.members):
                self.outs[1][i, m * self.own_rows : (m + 1) * self.own_rows, :] = self.sums_members[
                    m, base : base + self.own_rows, :
                ]
        for s in range(1, self.members):
            self.member_copy(s).wait()
        for m in range(self.members):
            for i in range(3):
                self.outs[0][:, i * self.width + m * self.part : i * self.width + (m + 1) * self.part] = (
                    self.columns_in[m, :, i * self.part : (i + 1) * self.part].astype(F32)
                )
        for s in range(1, self.chips):
            self.sums_chip(s).wait_send()

        @pl.loop(0, self.members)
        def _(m):
            for s in range(1, self.chips):
                self.chip_copy(s, m).wait_send()


def rope_tables(positions):
    half = HEAD_DIM // 2
    frequency = ROPE_BASE ** (-(jnp.arange(half, dtype=F32) * 2.0 / HEAD_DIM))
    angles = positions[:, None] * frequency[None, :]
    cosine = jnp.cos(angles)
    sine = jnp.sin(angles)
    return (jnp.concatenate([cosine, cosine], 1), jnp.concatenate([sine, sine], 1))


def rotate(values, cosine, sine):
    half = HEAD_DIM // 2
    turned = jnp.concatenate([-values[..., half:], values[..., :half]], -1)
    return values * cosine + turned * sine


def rotate_back(values, cosine, sine):
    half = HEAD_DIM // 2
    scaled = values * sine
    turned = jnp.concatenate([scaled[..., half:], -scaled[..., :half]], -1)
    return values * cosine + turned


def dot(left, right):
    return jnp.dot(left, right, preferred_element_type=F32)


def dot_rows(left, right):
    return lax.dot_general(left, right, (((1,), (1,)), ((), ())), preferred_element_type=F32)


def dot_first(left, right):
    return lax.dot_general(left, right, (((0,), (0,)), ((), ())), preferred_element_type=F32)


def gather(values, axes):
    return lax.all_gather(values, axes, axis=0, tiled=True)


def scatter_sum(values, axes):
    return lax.psum_scatter(values, axes, scatter_dimension=0, tiled=True)


def per_device(inputs, segment, w_qkv, w_out, w_gate, w_up, w_down_t, gains, cotangent):
    rows, width = inputs.shape[1:]
    cores = lax.axis_size("core")
    spans = lax.axis_size("ctx")
    members = cores * spans
    length = rows * spans
    total_rows = cores * length
    part = width // members
    heads = part // HEAD_DIM
    member = lax.axis_index(GROUP)
    tokens = inputs[0]

    qkv_rows = w_qkv.shape[0]
    qkv_cut = w_qkv.reshape(qkv_rows, 3, members, part).transpose(2, 0, 1, 3)
    qkv_cut = qkv_cut.reshape(members, qkv_rows, 3 * part)
    chips = lax.axis_size("chip")
    assert chips == spans
    spread = lambda reduce, row_fn, n_in, n_out, gain: Exchange(
        spans, rows, width, PIECE, reduce, True, row_fn, n_in, n_out, gain
    )
    own = jax.ShapeDtypeStruct((rows, width), F32)
    own_low = jax.ShapeDtypeStruct((rows, width), BF16)
    one = jax.ShapeDtypeStruct((1, width), F32)
    qkv_w, ids, tokens_all = Exchange(
        spans, rows, width, PIECE, False, True, pass_tokens, 1, 0, None,
        QkvWeights(spans, chips, qkv_cut, jnp.broadcast_to(segment, (8, rows))),
    ).call("gather_tokens", 1, None, [tokens], [])
    swaps = [
        (m * spans + a, a * members + m) for m in range(members) for a in range(chips)
    ]
    out_w = gather(lax.ppermute(w_out, ALL, swaps), "chip")

    hidden = w_gate.shape[1] // cores
    gate_up = jnp.concatenate(
        [w_gate.reshape(-1, cores, 1, hidden), w_up.reshape(-1, cores, 1, hidden)], 2
    ).reshape(-1, cores * 2 * hidden)
    gate_up = lax.all_to_all(gate_up, "core", 1, 0, tiled=True)
    gate_up_w = gather(gate_up, "chip")
    down_w = gather(lax.all_to_all(w_down_t, "core", 1, 0, tiled=True), "chip")

    mixed = dot(tokens_all, qkv_w)
    query_raw = mixed[:, :part]
    key_raw = mixed[:, part : 2 * part]
    value_low = mixed[:, 2 * part :].astype(BF16)
    squares = jnp.stack([jnp.sum(query_raw * query_raw, 1), jnp.sum(key_raw * key_raw, 1)])
    squares = lax.psum(squares, GROUP)
    factors = lax.rsqrt(squares / width + EPS)
    gain_q = lax.dynamic_slice_in_dim(gains[0], member * part, part)
    gain_k = lax.dynamic_slice_in_dim(gains[1], member * part, part)
    places = jnp.arange(length, dtype=jnp.int32)
    cosine, sine = rope_tables(places.astype(F32))
    cosine, sine = cosine[None, :, None, :], sine[None, :, None, :]
    shape = (cores, length, heads, HEAD_DIM)
    query_factor, key_factor = factors[0][:, None], factors[1][:, None]
    query_low = rotate((query_raw * query_factor * gain_q).reshape(shape), cosine, sine).astype(BF16)
    key_low = rotate((key_raw * key_factor * gain_k).reshape(shape), cosine, sine).astype(BF16)
    value_low = value_low.reshape(shape)

    ids = ids.reshape(members, 8, rows)[:, 0].reshape(cores, length)
    allowed = (
        (ids[:, :, None] == ids[:, None, :])
        & (places[None, None, :] <= places[None, :, None])
        & ((ids[:, None, :] != 0) | (places[None, None, :] == places[None, :, None]))
    )[:, None]
    scale = HEAD_DIM ** (-0.5)
    scores = jnp.einsum("bqhd,bkhd->bhqk", query_low, key_low, preferred_element_type=F32) * scale
    masked = jnp.where(allowed, scores, -1e30)
    row_max = jnp.max(masked, axis=-1, keepdims=True)
    weights = jnp.where(allowed, jnp.exp(masked - row_max), 0.0)
    shares = weights / jnp.sum(weights, axis=-1, keepdims=True)
    shares_low = shares.astype(BF16)
    attended = jnp.einsum("bhqk,bkhd->bqhd", shares_low, value_low, preferred_element_type=F32)
    attended_low = attended.reshape(total_rows, part).astype(BF16)
    residual, projected, residual_all = spread(True, after_projected, 2, 2, None).call(
        "sum_projected", 2, dot(attended_low, out_w).astype(BF16), [tokens, gains], [own, own]
    )

    gate_up_out = dot(residual_all, gate_up_w)
    gate, up_part = gate_up_out[:, :hidden], gate_up_out[:, hidden:]
    sigmoid = 1.0 / (1.0 + jnp.exp(-gate))
    activated = (gate * sigmoid * up_part).astype(BF16)
    output, gain_feed, feed_grad_all = spread(True, after_feed, 3, 2, 1).call(
        "sum_feed",
        3,
        dot_rows(activated, down_w).astype(BF16),
        [residual, cotangent[0], gains],
        [own_low, one],
    )

    act_grad = dot(feed_grad_all, down_w)
    gate_grad = act_grad * up_part * sigmoid * (1.0 + gate * (1.0 - sigmoid))
    up_grad = act_grad * (gate * sigmoid)
    gate_up_grad = jnp.concatenate([gate_grad.astype(BF16), up_grad.astype(BF16)], 1)
    back_part = dot_rows(gate_up_grad, gate_up_w).astype(BF16)
    down_part = dot_first(feed_grad_all, activated).astype(BF16)
    gate_up_part = dot_first(residual_all, gate_up_grad).astype(BF16)
    back_part, down_part, gate_up_part = lax.optimization_barrier((back_part, down_part, gate_up_part))
    grad_gate_up = scatter_sum(gate_up_part, "chip")
    grad_gate_up = lax.all_to_all(grad_gate_up, "core", 0, 1, tiled=True)
    grad_gate_up = grad_gate_up.reshape(-1, cores, 2, hidden).astype(F32)
    grad_gate = grad_gate_up[:, :, 0].reshape(-1, cores * hidden)
    grad_up = grad_gate_up[:, :, 1].reshape(-1, cores * hidden)
    grad_down = scatter_sum(down_part, "chip")
    grad_down = lax.all_to_all(grad_down, "core", 0, 1, tiled=True).astype(F32)

    residual_grad, gain_attn, projected_all = spread(True, after_back, 3, 2, 1).call(
        "sum_back",
        4,
        back_part,
        [projected, cotangent[0], gains],
        [own, one],
    )

    attended_grad = dot_rows(projected_all, out_w).astype(BF16).reshape(shape)

    share_grad = jnp.einsum("bqhd,bkhd->bhqk", attended_grad, value_low, preferred_element_type=F32)
    inner = jnp.sum(shares * share_grad, axis=-1, keepdims=True)
    score_grad = (shares * (share_grad - inner)).astype(BF16)
    query_grad = jnp.einsum("bhqk,bkhd->bqhd", score_grad, key_low, preferred_element_type=F32)
    key_grad = jnp.einsum("bhqk,bqhd->bkhd", score_grad, query_low, preferred_element_type=F32)
    value_grad = jnp.einsum("bhqk,bqhd->bkhd", shares_low, attended_grad, preferred_element_type=F32)
    query_turn = rotate_back(query_grad * scale, cosine, sine).reshape(total_rows, part)
    key_turn = rotate_back(key_grad * scale, cosine, sine).reshape(total_rows, part)
    query_norm, key_norm = query_raw * query_factor, key_raw * key_factor
    sums = jnp.stack(
        [jnp.sum(gain_q * query_turn * query_norm, 1), jnp.sum(gain_k * key_turn * key_norm, 1)]
    )
    means = lax.psum(sums, GROUP) / width
    query_mixed = query_factor * (gain_q * query_turn - query_norm * means[0][:, None])
    key_mixed = key_factor * (gain_k * key_turn - key_norm * means[1][:, None])
    gain_query = jnp.sum(query_turn * query_norm, 0)
    gain_key = jnp.sum(key_turn * key_norm, 0)
    mixed_grad = jnp.concatenate(
        [query_mixed, key_mixed, value_grad.reshape(total_rows, part)], 1
    ).astype(BF16)
    input_part = dot_rows(mixed_grad, qkv_w).astype(BF16)
    sums = jnp.concatenate(
        [a.reshape(-1, 128) for a in (gain_attn, gain_feed, gain_query, gain_key)]
        + [jnp.zeros((-2 * part // 128 % 8, 128), F32)]
    )
    input_grad, grad_qkv, grad_gains = Exchange(
        spans, rows, width, PIECE, True, False, after_input, 1, 1, None,
        QkvGrads(spans, chips, members, dot_first(tokens_all, mixed_grad).astype(BF16), sums),
    ).call("sum_input", 5, input_part, [residual_grad], [own])

    out_part = scatter_sum(dot_first(attended_low, projected_all).astype(BF16), "chip")
    grad_out = lax.ppermute(out_part, ALL, [(b, a) for a, b in swaps]).astype(F32)

    return (
        output[None],
        input_grad[None],
        grad_qkv,
        grad_out,
        grad_gate,
        grad_up,
        grad_down,
        grad_gains.reshape(4, width),
    )


def solution(mesh):
    cores = 2
    chips = mesh.shape["dp"] // cores
    split = Mesh(mesh.devices.reshape(chips, cores, mesh.shape["ctx"]), ALL)
    dp = ("chip", "core")
    every = P((*dp, "ctx"), None)
    in_specs = (
        P(dp, "ctx", None),
        P(dp, "ctx"),
        every,
        every,
        P(dp, "ctx"),
        P(dp, "ctx"),
        P(dp, "ctx"),
        P(),
        P(dp, "ctx", None),
    )
    out_specs = (
        P(dp, "ctx", None),
        P(dp, "ctx", None),
        every,
        every,
        P(dp, "ctx"),
        P(dp, "ctx"),
        P(dp, "ctx"),
        P(),
    )
    return jax.shard_map(
        per_device, mesh=split, in_specs=in_specs, out_specs=out_specs, check_vma=False
    )
```

```python
import jax
import jax.numpy as jnp
from jax import lax
from jax.experimental import pallas as pl
from jax.experimental.pallas import tpu as pltpu
from jax.sharding import Mesh
from jax.sharding import PartitionSpec as P

HEAD_DIM = 128
EPS = 1e-06
ROPE_BASE = 500000.0
F32 = jnp.float32
BF16 = jnp.bfloat16
GROUP = ("core", "ctx")
ALL = ("chip", "core", "ctx")


PIECE = 32
LAGB = 1
LAGJ = 1
MESH_ID = pl.DeviceIdType.MESH


def row_factor(values):
    return lax.rsqrt(jnp.mean(values * values, axis=-1, keepdims=True) + EPS)


def row_norm_back(values, gain, grad):
    factor = row_factor(values)
    normed = values * factor
    scaled = gain * grad
    back = factor * (scaled - normed * jnp.mean(scaled * normed, axis=-1, keepdims=True))
    return back, jnp.sum(grad * normed, axis=0, keepdims=True)


def after_projected(total, ins, outs, rows):
    tokens, gains = ins
    residual_out, projected_out = outs
    projected_out[rows, :] = total
    gain = gains[2:3, :]
    residual = tokens[rows, :].astype(F32) + total * row_factor(total) * gain
    residual_out[rows, :] = residual
    return residual


def after_feed(total, ins, outs, rows):
    residual, cotangent, gains = ins
    output, gain_out = outs
    gain = gains[3:4, :]
    normed = total * row_factor(total) * gain
    output[rows, :] = (residual[rows, :] + normed).astype(BF16)
    back, term = row_norm_back(total, gain, cotangent[rows, :].astype(F32))
    gain_out[...] += term
    return back


def after_back(total, ins, outs, rows):
    projected, cotangent, gains = ins
    grad_out, gain_out = outs
    grad = cotangent[rows, :].astype(F32) + total
    grad_out[rows, :] = grad
    back, term = row_norm_back(projected[rows, :], gains[2:3, :], grad)
    gain_out[...] += term
    return back


def after_input(total, ins, outs, rows):
    (grad,), (result,) = ins, outs
    result[rows, :] = grad[rows, :] + total
    return None


def pass_tokens(total, ins, outs, rows):
    return ins[0][rows, :]


class Exchange:
    def __init__(self, spans, rows, width, piece, reduce, spread, row_fn, n_in, n_out, gain, extra=None):
        self.extra = extra
        self.spans, self.rows, self.width, self.piece = spans, rows, width, piece
        self.reduce, self.spread, self.row_fn = reduce, spread, row_fn
        self.n_in, self.n_out, self.gain = n_in, n_out, gain
        self.count = rows // piece

    def scratch(self):
        spans, count = self.spans, self.count
        block = pltpu.VMEM((spans * self.rows, self.width), BF16)
        sems = pltpu.SemaphoreType.DMA((spans, count))
        items = []
        if self.reduce:
            items += [block] * 4 + [pltpu.SemaphoreType.DMA] + [sems] * 6
        if self.spread:
            items += [pltpu.VMEM((2 * spans * self.rows, self.width), BF16)]
            items += [sems] * 7 + [pltpu.SemaphoreType.DMA]
        if self.extra is not None:
            items += self.extra.scratch()
        return items

    def body(self, *refs):
        spans, rows, piece, count = self.spans, self.rows, self.piece, self.count
        refs = list(refs)
        take = lambda n: [refs.pop(0) for _ in range(n)]
        partial = take(1)[0] if self.reduce else None
        ins = take(self.n_in)
        extra = self.extra
        if extra is not None:
            extra.ins = take(extra.n_in)
        outs = take(self.n_out)
        if extra is not None:
            extra.outs = take(extra.n_out)
        gathered = take(1)[0] if self.spread else None
        if self.reduce:
            own, near, from_left, from_right = take(4)
            (load_sem,) = take(1)
            near_send, near_recv, right_send, right_recv, left_send, left_recv = take(6)
        if self.spread:
            (held,) = take(1)
            fwd_send, fwd_recv, bwd_send, bwd_recv, own_send, side_send, side_recv = take(7)
            (store_sem,) = take(1)
        if extra is not None:
            extra.held = refs
        core = lax.axis_index("core")
        place = lax.axis_index("ctx")
        other = 1 - core
        has_left = place > 0
        has_right = place < spans - 1

        def at(block, k):
            return pl.ds(pl.multiple_of(block * rows + k * piece, piece), piece)

        def held_at(seq, block, k):
            return pl.ds(pl.multiple_of((seq * spans + block) * rows + k * piece, piece), piece)

        def remote(src, dst, send, recv, **device):
            return pltpu.make_async_remote_copy(
                src_ref=src, dst_ref=dst, send_sem=send, recv_sem=recv,
                device_id=device, device_id_type=MESH_ID,
            )

        barrier = pltpu.get_barrier_semaphore()
        if extra is not None:
            meet_all(spans, getattr(extra, "moves", False))
        else:
            pl.semaphore_signal(barrier, 1, device_id={"core": other}, device_id_type=MESH_ID)

            @pl.when(has_left)
            def _():
                pl.semaphore_signal(barrier, 1, device_id={"ctx": place - 1}, device_id_type=MESH_ID)

            @pl.when(has_right)
            def _():
                pl.semaphore_signal(barrier, 1, device_id={"ctx": place + 1}, device_id_type=MESH_ID)

            pl.semaphore_wait(barrier, 1 + has_left.astype(jnp.int32) + has_right.astype(jnp.int32))

        if self.gain is not None:
            outs[self.gain][...] = jnp.zeros_like(outs[self.gain])

        def near_copy(d, k):
            return remote(
                partial.at[held_at(other, d, k)], near.at[at(d, k)],
                near_send.at[d, k], near_recv.at[d, k], core=other,
            )

        def right_copy(d, k):
            return remote(
                own.at[at(d, k)], from_left.at[at(d, k)],
                right_send.at[d, k], right_recv.at[d, k], ctx=place + 1,
            )

        def left_copy(d, k):
            return remote(
                own.at[at(d, k)], from_right.at[at(d, k)],
                left_send.at[d, k], left_recv.at[d, k], ctx=place - 1,
            )

        def fwd_copy(o, k, send):
            where = held_at(core, o, k)
            return remote(held.at[where], held.at[where], send, fwd_recv.at[o, k], ctx=place + 1)

        def bwd_copy(o, k, send):
            where = held_at(core, o, k)
            return remote(held.at[where], held.at[where], send, bwd_recv.at[o, k], ctx=place - 1)

        def side_copy(o, k):
            where = held_at(core, o, k)
            return remote(held.at[where], held.at[where], side_send.at[o, k], side_recv.at[o, k], core=other)

        if extra is not None:
            extra.start()
        if self.reduce:
            load = pltpu.make_async_copy(
                partial.at[pl.ds(pl.multiple_of(core * spans * rows, rows), spans * rows)], own, load_sem
            )
            load.start()

            @pl.loop(0, count)
            def _(k):
                for j in range(spans):
                    near_copy(j, k).start()

            load.wait()

        def base(d, k):
            near_copy(d, k).wait_recv()
            return own[at(d, k), :].astype(F32) + near[at(d, k), :].astype(F32)

        def reduce_step(k):
            for j in range(spans - 1):
                right, left = spans - 1 - j, j

                @pl.when(jnp.logical_and(right > place, has_left))
                def _():
                    value = base(right, k)
                    right_copy(right, k).wait_recv()
                    own[at(right, k), :] = (value + from_left[at(right, k), :].astype(F32)).astype(BF16)
                    right_copy(right, k).start()

                @pl.when(jnp.logical_and(right > place, jnp.logical_not(has_left)))
                def _():
                    own[at(right, k), :] = base(right, k).astype(BF16)
                    right_copy(right, k).start()

                @pl.when(jnp.logical_and(left < place, has_right))
                def _():
                    value = base(left, k)
                    left_copy(left, k).wait_recv()
                    own[at(left, k), :] = (value + from_right[at(left, k), :].astype(F32)).astype(BF16)
                    left_copy(left, k).start()

                @pl.when(jnp.logical_and(left < place, jnp.logical_not(has_right)))
                def _():
                    own[at(left, k), :] = base(left, k).astype(BF16)
                    left_copy(left, k).start()

        def finish_step(k):
            total = None
            if self.reduce:
                total = base(place, k)

                @pl.when(has_left)
                def _():
                    right_copy(place, k).wait_recv()

                @pl.when(has_right)
                def _():
                    left_copy(place, k).wait_recv()

                zero = jnp.zeros_like(total)
                total = total + jnp.where(has_left, from_left[at(place, k), :].astype(F32), zero)
                total = total + jnp.where(has_right, from_right[at(place, k), :].astype(F32), zero)
            own_rows = pl.ds(pl.multiple_of(k * piece, piece), piece)
            result = self.row_fn(total, ins, outs, own_rows)
            if self.spread:
                held[held_at(core, place, k), :] = result.astype(BF16)

                @pl.when(has_right)
                def _():
                    fwd_copy(place, k, fwd_send.at[place, k]).start()

                @pl.when(has_left)
                def _():
                    bwd_copy(place, k, bwd_send.at[place, k]).start()

                side_copy(place, k).start()

        def relay_step(k, j):
            if True:

                @pl.when(place - j >= 0)
                def _():
                    fwd_copy(place - j, k, fwd_send.at[place - j, k]).wait_recv()

                    @pl.when(has_right)
                    def _():
                        fwd_copy(place - j, k, fwd_send.at[place - j, k]).start()

                    side_copy(place - j, k).start()

                @pl.when(place + j < spans)
                def _():
                    bwd_copy(place + j, k, bwd_send.at[place + j, k]).wait_recv()

                    @pl.when(has_left)
                    def _():
                        bwd_copy(place + j, k, bwd_send.at[place + j, k]).start()

                    side_copy(place + j, k).start()

        lag = LAGB if self.reduce else 0

        @pl.loop(0, count + lag + (LAGJ * (spans - 1) if self.spread else 0))
        def _(t):
            if self.reduce:

                @pl.when(t < count)
                def _():
                    reduce_step(t)

            if self.reduce:

                @pl.when(jnp.logical_and(t >= lag, t < count + lag))
                def _():
                    finish_step(t - lag)
            else:

                @pl.when(t == 0)
                def _():
                    for k in range(count):
                        finish_step(k)

            if self.spread:
                for j in range(1, spans):
                    after = t - lag - j * LAGJ

                    @pl.when(jnp.logical_and(after >= 0, after < count))
                    def _():
                        relay_step(after, j)
            if extra is not None:
                extra.tick(t)

        if extra is not None:
            extra.finish(count + lag + (LAGJ * (spans - 1) if self.spread else 0))
        if self.spread:

            @pl.loop(0, count)
            def _(k):
                for o in range(spans):
                    side_copy(o, k).wait_recv()

            store = pltpu.make_async_copy(held, gathered, store_sem)
            store.start()

        @pl.loop(0, count)
        def _(k):
            for d in range(spans):
                if self.reduce:
                    near_copy(d, k).wait_send()

                    @pl.when(d > place)
                    def _():
                        right_copy(d, k).wait_send()

                    @pl.when(d < place)
                    def _():
                        left_copy(d, k).wait_send()

                if self.spread:
                    side_copy(d, k).wait_send()

                    @pl.when(jnp.logical_and(d <= place, has_right))
                    def _():
                        fwd_copy(d, k, fwd_send.at[d, k]).wait_send()

                    @pl.when(jnp.logical_and(d >= place, has_left))
                    def _():
                        bwd_copy(d, k, bwd_send.at[d, k]).wait_send()

        if self.spread:
            store.wait()

    def call(self, name, collective_id, partial, ins, outs):
        vmem = pl.BlockSpec(memory_space=pltpu.VMEM)
        hbm = pl.BlockSpec(memory_space=pl.ANY)
        operands = ([partial] if self.reduce else []) + list(ins)
        in_specs = ([hbm] if self.reduce else []) + [vmem] * len(ins)
        shapes = list(outs)
        specs = [vmem] * len(outs)
        if self.extra is not None:
            operands += self.extra.operands
            in_specs += self.extra.in_specs
            shapes += self.extra.out_shapes
            specs += self.extra.out_specs
        if self.spread:
            shapes.append(jax.ShapeDtypeStruct((2 * self.spans * self.rows, self.width), BF16))
            specs.append(hbm)
        return pl.pallas_call(
            self.body,
            out_shape=shapes,
            in_specs=in_specs,
            out_specs=specs,
            scratch_shapes=self.scratch(),
            compiler_params=pltpu.CompilerParams(
                collective_id=collective_id, has_side_effects=True, vmem_limit_bytes=48 << 20
            ),
            cost_estimate=pl.CostEstimate(
                flops=0,
                bytes_accessed=(50 if self.reduce else 30) * self.width * self.width,
                transcendentals=0,
            ),
            name=name,
        )(*operands)


def owner_of(chip, core, place, spans):
    member = core * spans + place
    return member // 2, lax.rem(member, 2), chip


def summer_of(chip, core, place, spans):
    member = chip * 2 + core
    return place, member // spans, lax.rem(member, spans)


def stays(chip, core, place, spans):
    to_chip, to_core, to_place = owner_of(chip, core, place, spans)
    return jnp.logical_and(to_chip == chip, jnp.logical_and(to_core == core, to_place == place))


def meet_all(spans, moves):
    chips = lax.axis_size("chip")
    barrier = pltpu.get_barrier_semaphore()
    chip = lax.axis_index("chip")
    core = lax.axis_index("core")
    place = lax.axis_index("ctx")
    for s in range(1, chips):
        pl.semaphore_signal(
            barrier, 1, device_id={"chip": lax.rem(chip + s, chips)}, device_id_type=MESH_ID
        )
    for s in range(1, 2 * spans):
        to_core, to_place = step_member(core, place, s, spans)
        pl.semaphore_signal(
            barrier, 1, device_id={"core": to_core, "ctx": to_place}, device_id_type=MESH_ID
        )
    count = chips - 1 + 2 * spans - 1
    if moves:
        away = jnp.logical_not(stays(chip, core, place, spans))

        @pl.when(away)
        def _():
            for find in (owner_of, summer_of):
                to_chip, to_core, to_place = find(chip, core, place, spans)
                pl.semaphore_signal(
                    barrier, 1, device_id={"chip": to_chip, "core": to_core, "ctx": to_place}, device_id_type=MESH_ID
                )

        count = count + 2 * away.astype(jnp.int32)
    pl.semaphore_wait(barrier, count)


def step_member(core, place, s, spans):
    return lax.rem(core + s % 2, 2), lax.rem(place + s // 2, spans)


def meet_other_core():
    barrier = pltpu.get_barrier_semaphore()
    other = 1 - lax.axis_index("core")
    pl.semaphore_signal(barrier, 1, device_id={"core": other}, device_id_type=MESH_ID)
    pl.semaphore_wait(barrier, 1)


def split_body(gate, up, down, gate_up_out, down_out, held, load_sem, store_sem, send_sem, recv_sem):
    core = lax.axis_index("core")
    other = 1 - core
    rows, width = gate.shape
    half = width // 2
    where = pl.ds(pl.multiple_of(core * rows, rows), rows)
    places = [gate_up_out.at[where, :half], gate_up_out.at[where, half:], down_out.at[where, :]]
    mine = pl.ds(pl.multiple_of(core * half, half), half)
    theirs = pl.ds(pl.multiple_of(other * half, half), half)
    loads = [
        pltpu.make_async_copy(a.at[:, mine], held.at[i], load_sem.at[i]) for i, a in enumerate((gate, up, down))
    ]
    for load in loads:
        load.start()
    meet_other_core()
    sends = [
        pltpu.make_async_remote_copy(
            src_ref=a.at[:, theirs], dst_ref=places[i], send_sem=send_sem.at[i], recv_sem=recv_sem.at[i],
            device_id={"core": other}, device_id_type=MESH_ID,
        )
        for i, a in enumerate((gate, up, down))
    ]
    for send in sends:
        send.start()
    stores = [pltpu.make_async_copy(held.at[i], places[i], store_sem.at[i]) for i in range(3)]
    for load, store in zip(loads, stores):
        load.wait()
        store.start()
    for store, send in zip(stores, sends):
        store.wait()
        send.wait()


def split_columns(gate, up, down):
    rows, width = gate.shape
    hbm = pl.BlockSpec(memory_space=pl.ANY)
    three = pltpu.SemaphoreType.DMA((3,))
    return pl.pallas_call(
        split_body,
        out_shape=[
            jax.ShapeDtypeStruct((2 * rows, width), BF16),
            jax.ShapeDtypeStruct((2 * rows, width // 2), BF16),
        ],
        in_specs=[hbm] * 3,
        out_specs=[hbm] * 2,
        scratch_shapes=[pltpu.VMEM((3, rows, width // 2), BF16)] + [three] * 4,
        compiler_params=pltpu.CompilerParams(collective_id=6, has_side_effects=True, vmem_limit_bytes=8 << 20),
        name="split_columns",
    )(gate, up, down)


def join_body(gate_up, down, gate_out, up_out, down_out, gate_up_in, down_in, send_sem, recv_sem):
    core = lax.axis_index("core")
    other = 1 - core
    rows, width = gate_out.shape
    half = width // 2
    meet_other_core()
    theirs = pl.ds(pl.multiple_of(other * rows, rows), rows)
    sends = [
        pltpu.make_async_remote_copy(
            src_ref=a.at[theirs], dst_ref=b, send_sem=send_sem.at[i], recv_sem=recv_sem.at[i],
            device_id={"core": other}, device_id_type=MESH_ID,
        )
        for i, (a, b) in enumerate(((gate_up, gate_up_in), (down, down_in)))
    ]
    for send in sends:
        send.start()
    mine = pl.ds(pl.multiple_of(core * half, half), half)
    far = pl.ds(pl.multiple_of(other * half, half), half)
    step = 16

    def rows_at(i, base):
        return pl.ds(pl.multiple_of(base + i * step, step), step)

    @pl.loop(0, rows // step)
    def _(i):
        here, there = rows_at(i, core * rows), rows_at(i, 0)
        gate_out[there, mine] = gate_up[here, :half].astype(F32)
        up_out[there, mine] = gate_up[here, half:].astype(F32)
        down_out[there, mine] = down[here, :].astype(F32)

    for send in sends:
        send.wait()

    @pl.loop(0, rows // step)
    def _(i):
        there = rows_at(i, 0)
        gate_out[there, far] = gate_up_in[there, :half].astype(F32)
        up_out[there, far] = gate_up_in[there, half:].astype(F32)
        down_out[there, far] = down_in[there, :].astype(F32)


def join_columns(gate_up, down):
    rows, width = gate_up.shape[0] // 2, gate_up.shape[1]
    vmem = pl.BlockSpec(memory_space=pltpu.VMEM)
    two = pltpu.SemaphoreType.DMA((2,))
    return pl.pallas_call(
        join_body,
        out_shape=[jax.ShapeDtypeStruct((rows, width), F32)] * 3,
        in_specs=[vmem] * 2,
        out_specs=[vmem] * 3,
        scratch_shapes=[pltpu.VMEM((rows, width), BF16), pltpu.VMEM((rows, width // 2), BF16), two, two],
        compiler_params=pltpu.CompilerParams(collective_id=7, has_side_effects=True, vmem_limit_bytes=32 << 20),
        name="join_columns",
    )(gate_up, down)


class Extra:
    def remote(self, src, dst, send, recv, **device):
        return pltpu.make_async_remote_copy(
            src_ref=src, dst_ref=dst, send_sem=send, recv_sem=recv,
            device_id=device, device_id_type=MESH_ID,
        )

    def locate(self):
        self.chip = lax.axis_index("chip")
        self.core = lax.axis_index("core")
        self.place = lax.axis_index("ctx")
        self.me = self.core * self.spans + self.place


class QkvWeights(Extra):
    n_in, n_out = 2, 2

    def __init__(self, spans, chips, cut, ids):
        self.spans, self.chips = spans, chips
        self.members, self.block, self.columns = cut.shape
        self.operands = [cut, ids]
        self.ids_shape = ids.shape
        vmem = pl.BlockSpec(memory_space=pltpu.VMEM)
        self.in_specs = [vmem, vmem]
        self.out_shapes = [
            jax.ShapeDtypeStruct((chips * self.members * self.block, self.columns), BF16),
            jax.ShapeDtypeStruct((self.members * ids.shape[0], ids.shape[1]), jnp.int32),
        ]
        self.out_specs = [vmem, vmem]

    def scratch(self):
        rows = self.chips * self.members * self.block
        sems = pltpu.SemaphoreType.DMA((self.members,))
        cross = pltpu.SemaphoreType.DMA((self.chips, self.members))
        ids = (self.members * self.ids_shape[0], self.ids_shape[1])
        return [pltpu.VMEM((rows, self.columns), BF16), pltpu.VMEM(ids, jnp.int32)] + [sems] * 4 + [cross] * 2

    def at(self, chip, m):
        return pl.ds(pl.multiple_of((chip * self.members + m) * self.block, self.block), self.block)

    def ids_at(self, m):
        return pl.ds(pl.multiple_of(m * self.ids_shape[0], self.ids_shape[0]), self.ids_shape[0])

    def block_copy(self, s):
        full, _, send, recv = self.held[:4]
        core, place = step_member(self.core, self.place, s, self.spans)
        return self.remote(
            self.ins[0].at[core * self.spans + place], full.at[self.at(self.chip, self.me)],
            send.at[s], recv.at[s], core=core, ctx=place,
        )

    def ids_copy(self, s):
        all_ids, send, recv = self.held[1], self.held[4], self.held[5]
        core, place = step_member(self.core, self.place, s, self.spans)
        return self.remote(
            self.ins[1], all_ids.at[self.ids_at(self.me)], send.at[s], recv.at[s], core=core, ctx=place
        )

    def source(self, s):
        core = lax.rem(self.core + s % 2, 2)
        return core * self.spans + lax.rem(self.place + self.spans - s // 2, self.spans)

    def chip_copy(self, s, m):
        full, _, _, _, _, _, send, recv = self.held
        where = self.at(self.chip, m)
        return self.remote(
            full.at[where], full.at[where], send.at[s, m], recv.at[s, m], chip=lax.rem(self.chip + s, self.chips)
        )

    def start(self):
        self.locate()
        cut, ids = self.ins
        full, all_ids = self.held[:2]
        for s in range(1, self.members):
            self.block_copy(s).start()
        for s in range(1, self.members):
            self.ids_copy(s).start()
        full[self.at(self.chip, self.me), :] = cut[self.me]
        all_ids[self.ids_at(self.me), :] = ids[...]

    def send_block(self, s):
        m = self.me if s == 0 else self.source(s)
        if s > 0:
            self.block_copy(s).wait_recv()
        for step in range(1, self.chips):
            self.chip_copy(step, m).start()

    def tick(self, t):
        @pl.when(t == 0)
        def _():
            for s in range(self.members):
                self.send_block(s)

    def finish(self, ticks):
        full, all_ids = self.held[:2]
        for s in range(1, self.members):
            self.ids_copy(s).wait_recv()
            self.block_copy(s).wait_send()
            self.ids_copy(s).wait_send()

        @pl.loop(0, self.members)
        def _(m):
            for s in range(1, self.chips):
                self.chip_copy(s, m).wait()

        self.outs[0][...] = full[...]
        self.outs[1][...] = all_ids[...]


class QkvGrads(Extra):
    n_in, n_out = 3, 3
    moves = True

    def __init__(self, spans, chips, members, grads, sums, out_grads):
        self.spans, self.chips, self.members = spans, chips, members
        self.out_rows = out_grads.shape[0] // chips
        self.block, self.columns = grads.shape[0] // (chips * members), grads.shape[1]
        self.part = self.columns // 3
        self.width = self.part * members
        self.own_rows = self.part // 128
        self.sum_rows = sums.shape[0]
        self.operands = [grads, sums, out_grads]
        vmem = pl.BlockSpec(memory_space=pltpu.VMEM)
        self.in_specs = [vmem] * 3
        self.out_shapes = [
            jax.ShapeDtypeStruct((self.block, 3 * self.width), F32),
            jax.ShapeDtypeStruct((4, self.width // 128, 128), F32),
            jax.ShapeDtypeStruct((self.out_rows, self.width), F32),
        ]
        self.out_specs = [vmem] * 3

    def scratch(self):
        sems = pltpu.SemaphoreType.DMA((self.members,))
        chip_sems = pltpu.SemaphoreType.DMA((self.chips,))
        cross = pltpu.SemaphoreType.DMA((self.chips, self.members))
        return [
            pltpu.VMEM((self.chips, self.members, self.block, self.columns), BF16),
            pltpu.VMEM((self.members, self.block, self.columns), BF16),
            pltpu.VMEM((self.members, self.block, self.columns), BF16),
            pltpu.VMEM((self.chips, self.sum_rows, 128), F32),
            pltpu.VMEM((self.sum_rows, 128), F32),
            pltpu.VMEM((self.members, self.sum_rows, 128), F32),
            pltpu.VMEM((self.chips, self.out_rows, self.width), BF16),
            pltpu.VMEM((self.out_rows, self.width), BF16),
            pltpu.VMEM((self.out_rows, self.width), BF16),
        ] + [cross] * 2 + [sems] * 2 + [chip_sems] * 2 + [sems] * 2 + [chip_sems] * 2 + [pltpu.SemaphoreType.DMA] * 2

    def at(self, chip, m):
        return pl.ds(pl.multiple_of((chip * self.members + m) * self.block, self.block), self.block)

    def chip_copy(self, s, m):
        other = lax.rem(self.chip + s, self.chips)
        return self.remote(
            self.ins[0].at[self.at(other, m)], self.arrived.at[s, m],
            self.cross_send.at[s, m], self.cross_recv.at[s, m], chip=other,
        )

    def member_copy(self, s):
        core, place = step_member(self.core, self.place, s, self.spans)
        return self.remote(
            self.summed.at[core * self.spans + place], self.columns_in.at[self.me],
            self.member_send.at[s], self.member_recv.at[s], core=core, ctx=place,
        )

    def sums_chip(self, s):
        return self.remote(
            self.ins[1], self.sums_in.at[s], self.sums_send.at[s], self.sums_recv.at[s],
            chip=lax.rem(self.chip + s, self.chips),
        )

    def sums_member(self, s):
        core, place = step_member(self.core, self.place, s, self.spans)
        return self.remote(
            self.sums_chips, self.sums_members.at[self.me], self.last_send.at[s], self.last_recv.at[s],
            core=core, ctx=place,
        )

    def out_copy(self, s):
        other = lax.rem(self.chip + s, self.chips)
        rows = pl.ds(pl.multiple_of(other * self.out_rows, self.out_rows), self.out_rows)
        return self.remote(
            self.ins[2].at[rows], self.out_in.at[s], self.out_send.at[s], self.out_recv.at[s], chip=other
        )

    def move_copy(self):
        chip, core, place = owner_of(self.chip, self.core, self.place, self.spans)
        return self.remote(
            self.out_sum, self.out_final, self.move_send, self.move_recv, chip=chip, core=core, ctx=place
        )

    def start(self):
        self.locate()
        (
            self.arrived, self.summed, self.columns_in, self.sums_in, self.sums_chips, self.sums_members,
            self.out_in, self.out_sum, self.out_final,
            self.cross_send, self.cross_recv, self.member_send, self.member_recv,
            self.sums_send, self.sums_recv, self.last_send, self.last_recv,
            self.out_send, self.out_recv, self.move_send, self.move_recv,
        ) = self.held
        for s in range(1, self.chips):
            self.sums_chip(s).start()
            self.out_copy(s).start()

        @pl.loop(0, self.members)
        def _(i):
            m = lax.rem(self.me + 1 + i, self.members)
            for s in range(1, self.chips):
                self.chip_copy(s, m).start()

    def add_block(self, m):
        total = self.ins[0][self.at(self.chip, m), :].astype(F32)
        for s in range(1, self.chips):
            self.chip_copy(s, m).wait_recv()
            total = total + self.arrived[s, m].astype(F32)
        self.summed[m] = total.astype(BF16)

    def send_blocks(self, first, last):
        for s in range(first, last):
            core, place = step_member(self.core, self.place, s, self.spans)
            self.add_block(core * self.spans + place)
            self.member_copy(s).start()

    def tick(self, t):
        @pl.when(t == 1)
        def _():
            total = self.ins[1][...]
            for s in range(1, self.chips):
                self.sums_chip(s).wait_recv()
                total = total + self.sums_in[s]
            self.sums_chips[...] = total
            self.sums_members[self.me] = total
            for s in range(1, self.members):
                self.sums_member(s).start()

        @pl.when(t == 2)
        def _():
            rows = pl.ds(pl.multiple_of(self.chip * self.out_rows, self.out_rows), self.out_rows)
            total = self.ins[2][rows, :].astype(F32)
            for s in range(1, self.chips):
                self.out_copy(s).wait_recv()
                total = total + self.out_in[s].astype(F32)
            self.out_sum[...] = total.astype(BF16)

            @pl.when(stays(self.chip, self.core, self.place, self.spans))
            def _():
                self.out_final[...] = total.astype(BF16)

            @pl.when(jnp.logical_not(stays(self.chip, self.core, self.place, self.spans)))
            def _():
                self.move_copy().start()

    def finish(self, ticks):
        self.send_blocks(1, self.members)
        self.add_block(self.me)
        self.columns_in[self.me] = self.summed[self.me]
        for s in range(1, self.members):
            self.sums_member(s).wait()
        wide = self.width // 128
        for i in range(2):
            total = self.sums_members[0, i * wide : (i + 1) * wide, :]
            for m in range(1, self.members):
                total = total + self.sums_members[m, i * wide : (i + 1) * wide, :]
            self.outs[1][2 + i] = total
            base = 2 * wide + i * self.own_rows
            for m in range(self.members):
                self.outs[1][i, m * self.own_rows : (m + 1) * self.own_rows, :] = self.sums_members[
                    m, base : base + self.own_rows, :
                ]
        for s in range(1, self.members):
            self.member_copy(s).wait()
        for m in range(self.members):
            for i in range(3):
                self.outs[0][:, i * self.width + m * self.part : i * self.width + (m + 1) * self.part] = (
                    self.columns_in[m, :, i * self.part : (i + 1) * self.part].astype(F32)
                )
        @pl.when(jnp.logical_not(stays(self.chip, self.core, self.place, self.spans)))
        def _():
            self.move_copy().wait()

        self.outs[2][...] = self.out_final[...].astype(F32)
        for s in range(1, self.chips):
            self.sums_chip(s).wait_send()
            self.out_copy(s).wait_send()

        @pl.loop(0, self.members)
        def _(m):
            for s in range(1, self.chips):
                self.chip_copy(s, m).wait_send()


def rope_tables(positions):
    half = HEAD_DIM // 2
    frequency = ROPE_BASE ** (-(jnp.arange(half, dtype=F32) * 2.0 / HEAD_DIM))
    angles = positions[:, None] * frequency[None, :]
    cosine = jnp.cos(angles)
    sine = jnp.sin(angles)
    return (jnp.concatenate([cosine, cosine], 1), jnp.concatenate([sine, sine], 1))


def rotate(values, cosine, sine):
    half = HEAD_DIM // 2
    turned = jnp.concatenate([-values[..., half:], values[..., :half]], -1)
    return values * cosine + turned * sine


def rotate_back(values, cosine, sine):
    half = HEAD_DIM // 2
    scaled = values * sine
    turned = jnp.concatenate([scaled[..., half:], -scaled[..., :half]], -1)
    return values * cosine + turned


def dot(left, right):
    return jnp.dot(left, right, preferred_element_type=F32)


def dot_rows(left, right):
    return lax.dot_general(left, right, (((1,), (1,)), ((), ())), preferred_element_type=F32)


def dot_first(left, right):
    return lax.dot_general(left, right, (((0,), (0,)), ((), ())), preferred_element_type=F32)


def gather(values, axes):
    return lax.all_gather(values, axes, axis=0, tiled=True)


def scatter_sum(values, axes):
    return lax.psum_scatter(values, axes, scatter_dimension=0, tiled=True)


def per_device(inputs, segment, w_qkv, w_out, w_gate, w_up, w_down_t, gains, cotangent):
    rows, width = inputs.shape[1:]
    cores = lax.axis_size("core")
    spans = lax.axis_size("ctx")
    members = cores * spans
    length = rows * spans
    total_rows = cores * length
    part = width // members
    heads = part // HEAD_DIM
    member = lax.axis_index(GROUP)
    tokens = inputs[0]

    qkv_rows = w_qkv.shape[0]
    qkv_cut = w_qkv.reshape(qkv_rows, 3, members, part).transpose(2, 0, 1, 3)
    qkv_cut = qkv_cut.reshape(members, qkv_rows, 3 * part)
    chips = lax.axis_size("chip")
    assert chips == spans
    spread = lambda reduce, row_fn, n_in, n_out, gain: Exchange(
        spans, rows, width, PIECE, reduce, True, row_fn, n_in, n_out, gain
    )
    own = jax.ShapeDtypeStruct((rows, width), F32)
    own_low = jax.ShapeDtypeStruct((rows, width), BF16)
    one = jax.ShapeDtypeStruct((1, width), F32)
    qkv_w, ids, tokens_all = Exchange(
        spans, rows, width, PIECE, False, True, pass_tokens, 1, 0, None,
        QkvWeights(spans, chips, qkv_cut, jnp.broadcast_to(segment, (8, rows))),
    ).call("gather_tokens", 1, None, [tokens], [])
    swaps = [
        (m * spans + a, a * members + m) for m in range(members) for a in range(chips)
    ]
    out_w = gather(lax.ppermute(w_out, ALL, swaps), "chip")

    hidden = w_gate.shape[1] // cores
    gate_up, down = split_columns(w_gate, w_up, w_down_t)
    gate_up_w, down_w = gather(gate_up, "chip"), gather(down, "chip")

    mixed = dot(tokens_all, qkv_w)
    query_raw = mixed[:, :part]
    key_raw = mixed[:, part : 2 * part]
    value_low = mixed[:, 2 * part :].astype(BF16)
    squares = jnp.stack([jnp.sum(query_raw * query_raw, 1), jnp.sum(key_raw * key_raw, 1)])
    squares = lax.psum(squares, GROUP)
    factors = lax.rsqrt(squares / width + EPS)
    gain_q = lax.dynamic_slice_in_dim(gains[0], member * part, part)
    gain_k = lax.dynamic_slice_in_dim(gains[1], member * part, part)
    places = jnp.arange(length, dtype=jnp.int32)
    cosine, sine = rope_tables(places.astype(F32))
    cosine, sine = cosine[None, :, None, :], sine[None, :, None, :]
    shape = (cores, length, heads, HEAD_DIM)
    query_factor, key_factor = factors[0][:, None], factors[1][:, None]
    query_low = rotate((query_raw * query_factor * gain_q).reshape(shape), cosine, sine).astype(BF16)
    key_low = rotate((key_raw * key_factor * gain_k).reshape(shape), cosine, sine).astype(BF16)
    value_low = value_low.reshape(shape)

    ids = ids.reshape(members, 8, rows)[:, 0].reshape(cores, length)
    allowed = (
        (ids[:, :, None] == ids[:, None, :])
        & (places[None, None, :] <= places[None, :, None])
        & ((ids[:, None, :] != 0) | (places[None, None, :] == places[None, :, None]))
    )[:, None]
    scale = HEAD_DIM ** (-0.5)
    scores = jnp.einsum("bqhd,bkhd->bhqk", query_low, key_low, preferred_element_type=F32) * scale
    masked = jnp.where(allowed, scores, -1e30)
    row_max = jnp.max(masked, axis=-1, keepdims=True)
    weights = jnp.where(allowed, jnp.exp(masked - row_max), 0.0)
    shares = weights / jnp.sum(weights, axis=-1, keepdims=True)
    shares_low = shares.astype(BF16)
    attended = jnp.einsum("bhqk,bkhd->bqhd", shares_low, value_low, preferred_element_type=F32)
    attended_low = attended.reshape(total_rows, part).astype(BF16)
    residual, projected, residual_all = spread(True, after_projected, 2, 2, None).call(
        "sum_projected", 2, dot(attended_low, out_w).astype(BF16), [tokens, gains], [own, own]
    )

    gate_up_out = dot(residual_all, gate_up_w)
    gate, up_part = gate_up_out[:, :hidden], gate_up_out[:, hidden:]
    sigmoid = 1.0 / (1.0 + jnp.exp(-gate))
    activated = (gate * sigmoid * up_part).astype(BF16)
    output, gain_feed, feed_grad_all = spread(True, after_feed, 3, 2, 1).call(
        "sum_feed",
        3,
        dot_rows(activated, down_w).astype(BF16),
        [residual, cotangent[0], gains],
        [own_low, one],
    )

    act_grad = dot(feed_grad_all, down_w)
    gate_grad = act_grad * up_part * sigmoid * (1.0 + gate * (1.0 - sigmoid))
    up_grad = act_grad * (gate * sigmoid)
    gate_up_grad = jnp.concatenate([gate_grad.astype(BF16), up_grad.astype(BF16)], 1)
    back_part = dot_rows(gate_up_grad, gate_up_w).astype(BF16)
    down_part = dot_first(feed_grad_all, activated).astype(BF16)
    gate_up_part = dot_first(residual_all, gate_up_grad).astype(BF16)
    back_part, down_part, gate_up_part = lax.optimization_barrier((back_part, down_part, gate_up_part))
    gate_up_sum, down_sum = scatter_sum(gate_up_part, "chip"), scatter_sum(down_part, "chip")
    residual_grad, gain_attn, projected_all = spread(True, after_back, 3, 2, 1).call(
        "sum_back",
        4,
        back_part,
        [projected, cotangent[0], gains],
        [own, one],
    )

    attended_grad = dot_rows(projected_all, out_w).astype(BF16).reshape(shape)

    share_grad = jnp.einsum("bqhd,bkhd->bhqk", attended_grad, value_low, preferred_element_type=F32)
    inner = jnp.sum(shares * share_grad, axis=-1, keepdims=True)
    score_grad = (shares * (share_grad - inner)).astype(BF16)
    query_grad = jnp.einsum("bhqk,bkhd->bqhd", score_grad, key_low, preferred_element_type=F32)
    key_grad = jnp.einsum("bhqk,bqhd->bkhd", score_grad, query_low, preferred_element_type=F32)
    value_grad = jnp.einsum("bhqk,bqhd->bkhd", shares_low, attended_grad, preferred_element_type=F32)
    query_turn = rotate_back(query_grad * scale, cosine, sine).reshape(total_rows, part)
    key_turn = rotate_back(key_grad * scale, cosine, sine).reshape(total_rows, part)
    query_norm, key_norm = query_raw * query_factor, key_raw * key_factor
    sums = jnp.stack(
        [jnp.sum(gain_q * query_turn * query_norm, 1), jnp.sum(gain_k * key_turn * key_norm, 1)]
    )
    means = lax.psum(sums, GROUP) / width
    query_mixed = query_factor * (gain_q * query_turn - query_norm * means[0][:, None])
    key_mixed = key_factor * (gain_k * key_turn - key_norm * means[1][:, None])
    gain_query = jnp.sum(query_turn * query_norm, 0)
    gain_key = jnp.sum(key_turn * key_norm, 0)
    mixed_grad = jnp.concatenate(
        [query_mixed, key_mixed, value_grad.reshape(total_rows, part)], 1
    ).astype(BF16)
    input_part = dot_rows(mixed_grad, qkv_w).astype(BF16)
    sums = jnp.concatenate(
        [a.reshape(-1, 128) for a in (gain_attn, gain_feed, gain_query, gain_key)]
        + [jnp.zeros((-2 * part // 128 % 8, 128), F32)]
    )
    input_grad, grad_qkv, grad_gains, grad_out = Exchange(
        spans, rows, width, PIECE, True, False, after_input, 1, 1, None,
        QkvGrads(
            spans, chips, members, dot_first(tokens_all, mixed_grad).astype(BF16), sums,
            dot_first(attended_low, projected_all).astype(BF16),
        ),
    ).call("sum_input", 5, input_part, [residual_grad], [own])

    grad_gate, grad_up, grad_down = join_columns(gate_up_sum, down_sum)
    return (
        output[None],
        input_grad[None],
        grad_qkv,
        grad_out,
        grad_gate,
        grad_up,
        grad_down,
        grad_gains.reshape(4, width),
    )


def solution(mesh):
    cores = 2
    chips = mesh.shape["dp"] // cores
    split = Mesh(mesh.devices.reshape(chips, cores, mesh.shape["ctx"]), ALL)
    dp = ("chip", "core")
    every = P((*dp, "ctx"), None)
    in_specs = (
        P(dp, "ctx", None),
        P(dp, "ctx"),
        every,
        every,
        P(dp, "ctx"),
        P(dp, "ctx"),
        P(dp, "ctx"),
        P(),
        P(dp, "ctx", None),
    )
    out_specs = (
        P(dp, "ctx", None),
        P(dp, "ctx", None),
        every,
        every,
        P(dp, "ctx"),
        P(dp, "ctx"),
        P(dp, "ctx"),
        P(),
    )
    return jax.shard_map(
        per_device, mesh=split, in_specs=in_specs, out_specs=out_specs, check_vma=False
    )
```

```python
import functools

import jax
import jax.numpy as jnp
from jax import lax
from jax.experimental import pallas as pl
from jax.experimental.pallas import tpu as pltpu
from jax.sharding import Mesh
from jax.sharding import PartitionSpec as P

HEAD_DIM = 128
EPS = 1e-06
ROPE_BASE = 500000.0
F32 = jnp.float32
BF16 = jnp.bfloat16
GROUP = ("core", "ctx")
ALL = ("chip", "core", "ctx")


PIECE = 32
LAGB = 1
LAGJ = 1
MESH_ID = pl.DeviceIdType.MESH


def row_factor(values):
    return lax.rsqrt(jnp.mean(values * values, axis=-1, keepdims=True) + EPS)


def row_norm_back(values, gain, grad):
    factor = row_factor(values)
    normed = values * factor
    scaled = gain * grad
    back = factor * (scaled - normed * jnp.mean(scaled * normed, axis=-1, keepdims=True))
    return back, jnp.sum(grad * normed, axis=0, keepdims=True)


def after_projected(total, ins, outs, rows):
    tokens, gains = ins
    residual_out, projected_out = outs
    projected_out[rows, :] = total
    gain = gains[2:3, :]
    residual = tokens[rows, :].astype(F32) + total * row_factor(total) * gain
    residual_out[rows, :] = residual
    return residual


def after_feed(total, ins, outs, rows):
    residual, cotangent, gains = ins
    output, gain_out = outs
    gain = gains[3:4, :]
    normed = total * row_factor(total) * gain
    output[rows, :] = (residual[rows, :] + normed).astype(BF16)
    back, term = row_norm_back(total, gain, cotangent[rows, :].astype(F32))
    gain_out[...] += term
    return back


def after_back(total, ins, outs, rows):
    projected, cotangent, gains = ins
    grad_out, gain_out = outs
    grad = cotangent[rows, :].astype(F32) + total
    grad_out[rows, :] = grad
    back, term = row_norm_back(projected[rows, :], gains[2:3, :], grad)
    gain_out[...] += term
    return back


def after_input(total, ins, outs, rows):
    (grad,), (result,) = ins, outs
    result[rows, :] = grad[rows, :] + total
    return None


def pass_tokens(total, ins, outs, rows):
    return ins[0][rows, :]


class Exchange:
    def __init__(self, spans, rows, width, piece, reduce, spread, row_fn, n_in, n_out, gain, extra=None):
        self.extra = extra
        self.spans, self.rows, self.width, self.piece = spans, rows, width, piece
        self.reduce, self.spread, self.row_fn = reduce, spread, row_fn
        self.n_in, self.n_out, self.gain = n_in, n_out, gain
        self.count = rows // piece

    def scratch(self):
        spans, count = self.spans, self.count
        block = pltpu.VMEM((spans * self.rows, self.width), BF16)
        sems = pltpu.SemaphoreType.DMA((spans, count))
        items = []
        if self.reduce:
            items += [block] * 4 + [pltpu.SemaphoreType.DMA] + [sems] * 6
        if self.spread:
            items += [pltpu.VMEM((2 * spans * self.rows, self.width), BF16)]
            items += [sems] * 7 + [pltpu.SemaphoreType.DMA]
        if self.extra is not None:
            items += self.extra.scratch()
        return items

    def body(self, *refs):
        spans, rows, piece, count = self.spans, self.rows, self.piece, self.count
        refs = list(refs)
        take = lambda n: [refs.pop(0) for _ in range(n)]
        partial = take(1)[0] if self.reduce else None
        ins = take(self.n_in)
        extra = self.extra
        if extra is not None:
            extra.ins = take(extra.n_in)
        outs = take(self.n_out)
        if extra is not None:
            extra.outs = take(extra.n_out)
        gathered = take(1)[0] if self.spread else None
        if self.reduce:
            own, near, from_left, from_right = take(4)
            (load_sem,) = take(1)
            near_send, near_recv, right_send, right_recv, left_send, left_recv = take(6)
        if self.spread:
            (held,) = take(1)
            fwd_send, fwd_recv, bwd_send, bwd_recv, own_send, side_send, side_recv = take(7)
            (store_sem,) = take(1)
        if extra is not None:
            extra.held = refs
        core = lax.axis_index("core")
        place = lax.axis_index("ctx")
        other = 1 - core
        has_left = place > 0
        has_right = place < spans - 1

        def at(block, k):
            return pl.ds(pl.multiple_of(block * rows + k * piece, piece), piece)

        def held_at(seq, block, k):
            return pl.ds(pl.multiple_of((seq * spans + block) * rows + k * piece, piece), piece)

        def remote(src, dst, send, recv, **device):
            return pltpu.make_async_remote_copy(
                src_ref=src, dst_ref=dst, send_sem=send, recv_sem=recv,
                device_id=device, device_id_type=MESH_ID,
            )

        barrier = pltpu.get_barrier_semaphore()
        if extra is not None:
            meet_all(spans, getattr(extra, "moves", False))
        else:
            pl.semaphore_signal(barrier, 1, device_id={"core": other}, device_id_type=MESH_ID)

            @pl.when(has_left)
            def _():
                pl.semaphore_signal(barrier, 1, device_id={"ctx": place - 1}, device_id_type=MESH_ID)

            @pl.when(has_right)
            def _():
                pl.semaphore_signal(barrier, 1, device_id={"ctx": place + 1}, device_id_type=MESH_ID)

            pl.semaphore_wait(barrier, 1 + has_left.astype(jnp.int32) + has_right.astype(jnp.int32))

        if self.gain is not None:
            outs[self.gain][...] = jnp.zeros_like(outs[self.gain])

        def near_copy(d, k):
            return remote(
                partial.at[held_at(other, d, k)], near.at[at(d, k)],
                near_send.at[d, k], near_recv.at[d, k], core=other,
            )

        def right_copy(d, k):
            return remote(
                own.at[at(d, k)], from_left.at[at(d, k)],
                right_send.at[d, k], right_recv.at[d, k], ctx=place + 1,
            )

        def left_copy(d, k):
            return remote(
                own.at[at(d, k)], from_right.at[at(d, k)],
                left_send.at[d, k], left_recv.at[d, k], ctx=place - 1,
            )

        def fwd_copy(o, k, send):
            where = held_at(core, o, k)
            return remote(held.at[where], held.at[where], send, fwd_recv.at[o, k], ctx=place + 1)

        def bwd_copy(o, k, send):
            where = held_at(core, o, k)
            return remote(held.at[where], held.at[where], send, bwd_recv.at[o, k], ctx=place - 1)

        def side_copy(o, k):
            where = held_at(core, o, k)
            return remote(held.at[where], held.at[where], side_send.at[o, k], side_recv.at[o, k], core=other)

        if extra is not None:
            extra.start()
        if self.reduce:
            load = pltpu.make_async_copy(
                partial.at[pl.ds(pl.multiple_of(core * spans * rows, rows), spans * rows)], own, load_sem
            )
            load.start()

            @pl.loop(0, count)
            def _(k):
                for j in range(spans):
                    near_copy(j, k).start()

            load.wait()

        def base(d, k):
            near_copy(d, k).wait_recv()
            return own[at(d, k), :].astype(F32) + near[at(d, k), :].astype(F32)

        def reduce_step(k):
            for j in range(spans - 1):
                right, left = spans - 1 - j, j

                @pl.when(jnp.logical_and(right > place, has_left))
                def _():
                    value = base(right, k)
                    right_copy(right, k).wait_recv()
                    own[at(right, k), :] = (value + from_left[at(right, k), :].astype(F32)).astype(BF16)
                    right_copy(right, k).start()

                @pl.when(jnp.logical_and(right > place, jnp.logical_not(has_left)))
                def _():
                    own[at(right, k), :] = base(right, k).astype(BF16)
                    right_copy(right, k).start()

                @pl.when(jnp.logical_and(left < place, has_right))
                def _():
                    value = base(left, k)
                    left_copy(left, k).wait_recv()
                    own[at(left, k), :] = (value + from_right[at(left, k), :].astype(F32)).astype(BF16)
                    left_copy(left, k).start()

                @pl.when(jnp.logical_and(left < place, jnp.logical_not(has_right)))
                def _():
                    own[at(left, k), :] = base(left, k).astype(BF16)
                    left_copy(left, k).start()

        def finish_step(k):
            total = None
            if self.reduce:
                total = base(place, k)

                @pl.when(has_left)
                def _():
                    right_copy(place, k).wait_recv()

                @pl.when(has_right)
                def _():
                    left_copy(place, k).wait_recv()

                zero = jnp.zeros_like(total)
                total = total + jnp.where(has_left, from_left[at(place, k), :].astype(F32), zero)
                total = total + jnp.where(has_right, from_right[at(place, k), :].astype(F32), zero)
            own_rows = pl.ds(pl.multiple_of(k * piece, piece), piece)
            result = self.row_fn(total, ins, outs, own_rows)
            if self.spread:
                held[held_at(core, place, k), :] = result.astype(BF16)

                @pl.when(has_right)
                def _():
                    fwd_copy(place, k, fwd_send.at[place, k]).start()

                @pl.when(has_left)
                def _():
                    bwd_copy(place, k, bwd_send.at[place, k]).start()

                side_copy(place, k).start()

        def relay_step(k, j):
            if True:

                @pl.when(place - j >= 0)
                def _():
                    fwd_copy(place - j, k, fwd_send.at[place - j, k]).wait_recv()

                    @pl.when(has_right)
                    def _():
                        fwd_copy(place - j, k, fwd_send.at[place - j, k]).start()

                    side_copy(place - j, k).start()

                @pl.when(place + j < spans)
                def _():
                    bwd_copy(place + j, k, bwd_send.at[place + j, k]).wait_recv()

                    @pl.when(has_left)
                    def _():
                        bwd_copy(place + j, k, bwd_send.at[place + j, k]).start()

                    side_copy(place + j, k).start()

        lag = LAGB if self.reduce else 0

        @pl.loop(0, count + lag + (LAGJ * (spans - 1) if self.spread else 0))
        def _(t):
            if self.reduce:

                @pl.when(t < count)
                def _():
                    reduce_step(t)

            if self.reduce:

                @pl.when(jnp.logical_and(t >= lag, t < count + lag))
                def _():
                    finish_step(t - lag)
            else:

                @pl.when(t == 0)
                def _():
                    for k in range(count):
                        finish_step(k)

            if self.spread:
                for j in range(1, spans):
                    after = t - lag - j * LAGJ

                    @pl.when(jnp.logical_and(after >= 0, after < count))
                    def _():
                        relay_step(after, j)
            if extra is not None:
                extra.tick(t)

        if extra is not None:
            extra.finish(count + lag + (LAGJ * (spans - 1) if self.spread else 0))
        if self.spread:

            @pl.loop(0, count)
            def _(k):
                for o in range(spans):
                    side_copy(o, k).wait_recv()

            store = pltpu.make_async_copy(held, gathered, store_sem)
            store.start()

        @pl.loop(0, count)
        def _(k):
            for d in range(spans):
                if self.reduce:
                    near_copy(d, k).wait_send()

                    @pl.when(d > place)
                    def _():
                        right_copy(d, k).wait_send()

                    @pl.when(d < place)
                    def _():
                        left_copy(d, k).wait_send()

                if self.spread:
                    side_copy(d, k).wait_send()

                    @pl.when(jnp.logical_and(d <= place, has_right))
                    def _():
                        fwd_copy(d, k, fwd_send.at[d, k]).wait_send()

                    @pl.when(jnp.logical_and(d >= place, has_left))
                    def _():
                        bwd_copy(d, k, bwd_send.at[d, k]).wait_send()

        if self.spread:
            store.wait()

    def call(self, name, collective_id, partial, ins, outs):
        vmem = pl.BlockSpec(memory_space=pltpu.VMEM)
        hbm = pl.BlockSpec(memory_space=pl.ANY)
        operands = ([partial] if self.reduce else []) + list(ins)
        in_specs = ([hbm] if self.reduce else []) + [vmem] * len(ins)
        shapes = list(outs)
        specs = [vmem] * len(outs)
        if self.extra is not None:
            operands += self.extra.operands
            in_specs += self.extra.in_specs
            shapes += self.extra.out_shapes
            specs += self.extra.out_specs
        if self.spread:
            shapes.append(jax.ShapeDtypeStruct((2 * self.spans * self.rows, self.width), BF16))
            specs.append(hbm)
        return pl.pallas_call(
            self.body,
            out_shape=shapes,
            in_specs=in_specs,
            out_specs=specs,
            scratch_shapes=self.scratch(),
            compiler_params=pltpu.CompilerParams(
                collective_id=collective_id, has_side_effects=True, vmem_limit_bytes=48 << 20
            ),
            cost_estimate=pl.CostEstimate(
                flops=0,
                bytes_accessed=(50 if self.reduce else 30) * self.width * self.width,
                transcendentals=0,
            ),
            name=name,
        )(*operands)


def owner_of(chip, core, place, spans):
    member = core * spans + place
    return member // 2, lax.rem(member, 2), chip


def summer_of(chip, core, place, spans):
    member = chip * 2 + core
    return place, member // spans, lax.rem(member, spans)


def stays(chip, core, place, spans):
    to_chip, to_core, to_place = owner_of(chip, core, place, spans)
    return jnp.logical_and(to_chip == chip, jnp.logical_and(to_core == core, to_place == place))


def meet_all(spans, moves):
    chips = lax.axis_size("chip")
    barrier = pltpu.get_barrier_semaphore()
    chip = lax.axis_index("chip")
    core = lax.axis_index("core")
    place = lax.axis_index("ctx")
    for s in range(1, chips):
        pl.semaphore_signal(
            barrier, 1, device_id={"chip": lax.rem(chip + s, chips)}, device_id_type=MESH_ID
        )
    for s in range(1, 2 * spans):
        to_core, to_place = step_member(core, place, s, spans)
        pl.semaphore_signal(
            barrier, 1, device_id={"core": to_core, "ctx": to_place}, device_id_type=MESH_ID
        )
    count = chips - 1 + 2 * spans - 1
    if moves:
        away = jnp.logical_not(stays(chip, core, place, spans))

        @pl.when(away)
        def _():
            for find in (owner_of, summer_of):
                to_chip, to_core, to_place = find(chip, core, place, spans)
                pl.semaphore_signal(
                    barrier, 1, device_id={"chip": to_chip, "core": to_core, "ctx": to_place}, device_id_type=MESH_ID
                )

        count = count + 2 * away.astype(jnp.int32)
    pl.semaphore_wait(barrier, count)


def step_member(core, place, s, spans):
    return lax.rem(core + s % 2, 2), lax.rem(place + s // 2, spans)


def meet_other_core():
    barrier = pltpu.get_barrier_semaphore()
    other = 1 - lax.axis_index("core")
    pl.semaphore_signal(barrier, 1, device_id={"core": other}, device_id_type=MESH_ID)
    pl.semaphore_wait(barrier, 1)


def split_body(gate, up, down, gate_up_out, down_out, held, load_sem, store_sem, send_sem, recv_sem):
    core = lax.axis_index("core")
    other = 1 - core
    rows, width = gate.shape
    half = width // 2
    where = pl.ds(pl.multiple_of(core * rows, rows), rows)
    places = [gate_up_out.at[where, :half], gate_up_out.at[where, half:], down_out.at[where, :]]
    mine = pl.ds(pl.multiple_of(core * half, half), half)
    theirs = pl.ds(pl.multiple_of(other * half, half), half)
    loads = [
        pltpu.make_async_copy(a.at[:, mine], held.at[i], load_sem.at[i]) for i, a in enumerate((gate, up, down))
    ]
    for load in loads:
        load.start()
    meet_other_core()
    sends = [
        pltpu.make_async_remote_copy(
            src_ref=a.at[:, theirs], dst_ref=places[i], send_sem=send_sem.at[i], recv_sem=recv_sem.at[i],
            device_id={"core": other}, device_id_type=MESH_ID,
        )
        for i, a in enumerate((gate, up, down))
    ]
    for send in sends:
        send.start()
    stores = [pltpu.make_async_copy(held.at[i], places[i], store_sem.at[i]) for i in range(3)]
    for load, store in zip(loads, stores):
        load.wait()
        store.start()
    for store, send in zip(stores, sends):
        store.wait()
        send.wait()


def split_columns(gate, up, down):
    rows, width = gate.shape
    hbm = pl.BlockSpec(memory_space=pl.ANY)
    three = pltpu.SemaphoreType.DMA((3,))
    return pl.pallas_call(
        split_body,
        out_shape=[
            jax.ShapeDtypeStruct((2 * rows, width), BF16),
            jax.ShapeDtypeStruct((2 * rows, width // 2), BF16),
        ],
        in_specs=[hbm] * 3,
        out_specs=[hbm] * 2,
        scratch_shapes=[pltpu.VMEM((3, rows, width // 2), BF16)] + [three] * 4,
        compiler_params=pltpu.CompilerParams(collective_id=6, has_side_effects=True, vmem_limit_bytes=8 << 20),
        name="split_columns",
    )(gate, up, down)


def join_body(gate_up, down, gate_out, up_out, down_out, gate_up_in, down_in, send_sem, recv_sem):
    core = lax.axis_index("core")
    other = 1 - core
    rows, width = gate_out.shape
    half = width // 2
    meet_other_core()
    theirs = pl.ds(pl.multiple_of(other * rows, rows), rows)
    sends = [
        pltpu.make_async_remote_copy(
            src_ref=a.at[theirs], dst_ref=b, send_sem=send_sem.at[i], recv_sem=recv_sem.at[i],
            device_id={"core": other}, device_id_type=MESH_ID,
        )
        for i, (a, b) in enumerate(((gate_up, gate_up_in), (down, down_in)))
    ]
    for send in sends:
        send.start()
    mine = pl.ds(pl.multiple_of(core * half, half), half)
    far = pl.ds(pl.multiple_of(other * half, half), half)
    step = 16

    def rows_at(i, base):
        return pl.ds(pl.multiple_of(base + i * step, step), step)

    @pl.loop(0, rows // step)
    def _(i):
        here, there = rows_at(i, core * rows), rows_at(i, 0)
        gate_out[there, mine] = gate_up[here, :half].astype(F32)
        up_out[there, mine] = gate_up[here, half:].astype(F32)
        down_out[there, mine] = down[here, :].astype(F32)

    for send in sends:
        send.wait()

    @pl.loop(0, rows // step)
    def _(i):
        there = rows_at(i, 0)
        gate_out[there, far] = gate_up_in[there, :half].astype(F32)
        up_out[there, far] = gate_up_in[there, half:].astype(F32)
        down_out[there, far] = down_in[there, :].astype(F32)


def join_columns(gate_up, down):
    rows, width = gate_up.shape[0] // 2, gate_up.shape[1]
    vmem = pl.BlockSpec(memory_space=pltpu.VMEM)
    two = pltpu.SemaphoreType.DMA((2,))
    return pl.pallas_call(
        join_body,
        out_shape=[jax.ShapeDtypeStruct((rows, width), F32)] * 3,
        in_specs=[vmem] * 2,
        out_specs=[vmem] * 3,
        scratch_shapes=[pltpu.VMEM((rows, width), BF16), pltpu.VMEM((rows, width // 2), BF16), two, two],
        compiler_params=pltpu.CompilerParams(collective_id=7, has_side_effects=True, vmem_limit_bytes=32 << 20),
        name="join_columns",
    )(gate_up, down)


class Extra:
    def remote(self, src, dst, send, recv, **device):
        return pltpu.make_async_remote_copy(
            src_ref=src, dst_ref=dst, send_sem=send, recv_sem=recv,
            device_id=device, device_id_type=MESH_ID,
        )

    def locate(self):
        self.chip = lax.axis_index("chip")
        self.core = lax.axis_index("core")
        self.place = lax.axis_index("ctx")
        self.me = self.core * self.spans + self.place


class QkvWeights(Extra):
    n_in, n_out = 2, 2

    def __init__(self, spans, chips, cut, ids):
        self.spans, self.chips = spans, chips
        self.members, self.block, self.columns = cut.shape
        self.operands = [cut, ids]
        self.ids_shape = ids.shape
        vmem = pl.BlockSpec(memory_space=pltpu.VMEM)
        self.in_specs = [vmem, vmem]
        self.out_shapes = [
            jax.ShapeDtypeStruct((chips * self.members * self.block, self.columns), BF16),
            jax.ShapeDtypeStruct((self.members * ids.shape[0], ids.shape[1]), jnp.int32),
        ]
        self.out_specs = [vmem, vmem]

    def scratch(self):
        rows = self.chips * self.members * self.block
        sems = pltpu.SemaphoreType.DMA((self.members,))
        cross = pltpu.SemaphoreType.DMA((self.chips, self.members))
        ids = (self.members * self.ids_shape[0], self.ids_shape[1])
        return [pltpu.VMEM((rows, self.columns), BF16), pltpu.VMEM(ids, jnp.int32)] + [sems] * 4 + [cross] * 2

    def at(self, chip, m):
        return pl.ds(pl.multiple_of((chip * self.members + m) * self.block, self.block), self.block)

    def ids_at(self, m):
        return pl.ds(pl.multiple_of(m * self.ids_shape[0], self.ids_shape[0]), self.ids_shape[0])

    def block_copy(self, s):
        full, _, send, recv = self.held[:4]
        core, place = step_member(self.core, self.place, s, self.spans)
        return self.remote(
            self.ins[0].at[core * self.spans + place], full.at[self.at(self.chip, self.me)],
            send.at[s], recv.at[s], core=core, ctx=place,
        )

    def ids_copy(self, s):
        all_ids, send, recv = self.held[1], self.held[4], self.held[5]
        core, place = step_member(self.core, self.place, s, self.spans)
        return self.remote(
            self.ins[1], all_ids.at[self.ids_at(self.me)], send.at[s], recv.at[s], core=core, ctx=place
        )

    def source(self, s):
        core = lax.rem(self.core + s % 2, 2)
        return core * self.spans + lax.rem(self.place + self.spans - s // 2, self.spans)

    def chip_copy(self, s, m):
        full, _, _, _, _, _, send, recv = self.held
        where = self.at(self.chip, m)
        return self.remote(
            full.at[where], full.at[where], send.at[s, m], recv.at[s, m], chip=lax.rem(self.chip + s, self.chips)
        )

    def start(self):
        self.locate()
        cut, ids = self.ins
        full, all_ids = self.held[:2]
        for s in range(1, self.members):
            self.block_copy(s).start()
        for s in range(1, self.members):
            self.ids_copy(s).start()
        full[self.at(self.chip, self.me), :] = cut[self.me]
        all_ids[self.ids_at(self.me), :] = ids[...]

    def send_block(self, s):
        m = self.me if s == 0 else self.source(s)
        if s > 0:
            self.block_copy(s).wait_recv()
        for step in range(1, self.chips):
            self.chip_copy(step, m).start()

    def tick(self, t):
        @pl.when(t == 0)
        def _():
            for s in range(self.members):
                self.send_block(s)

    def finish(self, ticks):
        full, all_ids = self.held[:2]
        for s in range(1, self.members):
            self.ids_copy(s).wait_recv()
            self.block_copy(s).wait_send()
            self.ids_copy(s).wait_send()

        @pl.loop(0, self.members)
        def _(m):
            for s in range(1, self.chips):
                self.chip_copy(s, m).wait()

        self.outs[0][...] = full[...]
        self.outs[1][...] = all_ids[...]


class QkvGrads(Extra):
    n_in, n_out = 3, 3
    moves = True

    def __init__(self, spans, chips, members, grads, sums, out_grads):
        self.spans, self.chips, self.members = spans, chips, members
        self.out_rows = out_grads.shape[0] // chips
        self.block, self.columns = grads.shape[0] // (chips * members), grads.shape[1]
        self.part = self.columns // 3
        self.width = self.part * members
        self.own_rows = self.part // 128
        self.sum_rows = sums.shape[0]
        self.operands = [grads, sums, out_grads]
        vmem = pl.BlockSpec(memory_space=pltpu.VMEM)
        self.in_specs = [vmem] * 3
        self.out_shapes = [
            jax.ShapeDtypeStruct((self.block, 3 * self.width), F32),
            jax.ShapeDtypeStruct((4, self.width // 128, 128), F32),
            jax.ShapeDtypeStruct((self.out_rows, self.width), F32),
        ]
        self.out_specs = [vmem] * 3

    def scratch(self):
        sems = pltpu.SemaphoreType.DMA((self.members,))
        chip_sems = pltpu.SemaphoreType.DMA((self.chips,))
        cross = pltpu.SemaphoreType.DMA((self.chips, self.members))
        return [
            pltpu.VMEM((self.chips, self.members, self.block, self.columns), BF16),
            pltpu.VMEM((self.members, self.block, self.columns), BF16),
            pltpu.VMEM((self.members, self.block, self.columns), BF16),
            pltpu.VMEM((self.chips, self.sum_rows, 128), F32),
            pltpu.VMEM((self.sum_rows, 128), F32),
            pltpu.VMEM((self.members, self.sum_rows, 128), F32),
            pltpu.VMEM((self.chips, self.out_rows, self.width), BF16),
            pltpu.VMEM((self.out_rows, self.width), BF16),
            pltpu.VMEM((self.out_rows, self.width), BF16),
        ] + [cross] * 2 + [sems] * 2 + [chip_sems] * 2 + [sems] * 2 + [chip_sems] * 2 + [pltpu.SemaphoreType.DMA] * 2

    def at(self, chip, m):
        return pl.ds(pl.multiple_of((chip * self.members + m) * self.block, self.block), self.block)

    def chip_copy(self, s, m):
        other = lax.rem(self.chip + s, self.chips)
        return self.remote(
            self.ins[0].at[self.at(other, m)], self.arrived.at[s, m],
            self.cross_send.at[s, m], self.cross_recv.at[s, m], chip=other,
        )

    def member_copy(self, s):
        core, place = step_member(self.core, self.place, s, self.spans)
        return self.remote(
            self.summed.at[core * self.spans + place], self.columns_in.at[self.me],
            self.member_send.at[s], self.member_recv.at[s], core=core, ctx=place,
        )

    def sums_chip(self, s):
        return self.remote(
            self.ins[1], self.sums_in.at[s], self.sums_send.at[s], self.sums_recv.at[s],
            chip=lax.rem(self.chip + s, self.chips),
        )

    def sums_member(self, s):
        core, place = step_member(self.core, self.place, s, self.spans)
        return self.remote(
            self.sums_chips, self.sums_members.at[self.me], self.last_send.at[s], self.last_recv.at[s],
            core=core, ctx=place,
        )

    def out_copy(self, s):
        other = lax.rem(self.chip + s, self.chips)
        rows = pl.ds(pl.multiple_of(other * self.out_rows, self.out_rows), self.out_rows)
        return self.remote(
            self.ins[2].at[rows], self.out_in.at[s], self.out_send.at[s], self.out_recv.at[s], chip=other
        )

    def move_copy(self):
        chip, core, place = owner_of(self.chip, self.core, self.place, self.spans)
        return self.remote(
            self.out_sum, self.out_final, self.move_send, self.move_recv, chip=chip, core=core, ctx=place
        )

    def start(self):
        self.locate()
        (
            self.arrived, self.summed, self.columns_in, self.sums_in, self.sums_chips, self.sums_members,
            self.out_in, self.out_sum, self.out_final,
            self.cross_send, self.cross_recv, self.member_send, self.member_recv,
            self.sums_send, self.sums_recv, self.last_send, self.last_recv,
            self.out_send, self.out_recv, self.move_send, self.move_recv,
        ) = self.held
        for s in range(1, self.chips):
            self.sums_chip(s).start()
            self.out_copy(s).start()

        @pl.loop(0, self.members)
        def _(i):
            m = lax.rem(self.me + 1 + i, self.members)
            for s in range(1, self.chips):
                self.chip_copy(s, m).start()

    def add_block(self, m):
        total = self.ins[0][self.at(self.chip, m), :].astype(F32)
        for s in range(1, self.chips):
            self.chip_copy(s, m).wait_recv()
            total = total + self.arrived[s, m].astype(F32)
        self.summed[m] = total.astype(BF16)

    def send_blocks(self, first, last):
        for s in range(first, last):
            core, place = step_member(self.core, self.place, s, self.spans)
            self.add_block(core * self.spans + place)
            self.member_copy(s).start()

    def tick(self, t):
        @pl.when(t == 1)
        def _():
            total = self.ins[1][...]
            for s in range(1, self.chips):
                self.sums_chip(s).wait_recv()
                total = total + self.sums_in[s]
            self.sums_chips[...] = total
            self.sums_members[self.me] = total
            for s in range(1, self.members):
                self.sums_member(s).start()

        @pl.when(t == 2)
        def _():
            rows = pl.ds(pl.multiple_of(self.chip * self.out_rows, self.out_rows), self.out_rows)
            total = self.ins[2][rows, :].astype(F32)
            for s in range(1, self.chips):
                self.out_copy(s).wait_recv()
                total = total + self.out_in[s].astype(F32)
            self.out_sum[...] = total.astype(BF16)

            @pl.when(stays(self.chip, self.core, self.place, self.spans))
            def _():
                self.out_final[...] = total.astype(BF16)

            @pl.when(jnp.logical_not(stays(self.chip, self.core, self.place, self.spans)))
            def _():
                self.move_copy().start()

    def finish(self, ticks):
        self.send_blocks(1, self.members)
        self.add_block(self.me)
        self.columns_in[self.me] = self.summed[self.me]
        for s in range(1, self.members):
            self.sums_member(s).wait()
        wide = self.width // 128
        for i in range(2):
            total = self.sums_members[0, i * wide : (i + 1) * wide, :]
            for m in range(1, self.members):
                total = total + self.sums_members[m, i * wide : (i + 1) * wide, :]
            self.outs[1][2 + i] = total
            base = 2 * wide + i * self.own_rows
            for m in range(self.members):
                self.outs[1][i, m * self.own_rows : (m + 1) * self.own_rows, :] = self.sums_members[
                    m, base : base + self.own_rows, :
                ]
        for s in range(1, self.members):
            self.member_copy(s).wait()
        for m in range(self.members):
            for i in range(3):
                self.outs[0][:, i * self.width + m * self.part : i * self.width + (m + 1) * self.part] = (
                    self.columns_in[m, :, i * self.part : (i + 1) * self.part].astype(F32)
                )
        @pl.when(jnp.logical_not(stays(self.chip, self.core, self.place, self.spans)))
        def _():
            self.move_copy().wait()

        self.outs[2][...] = self.out_final[...].astype(F32)
        for s in range(1, self.chips):
            self.sums_chip(s).wait_send()
            self.out_copy(s).wait_send()

        @pl.loop(0, self.members)
        def _(m):
            for s in range(1, self.chips):
                self.chip_copy(s, m).wait_send()


def rope_tables(positions):
    half = HEAD_DIM // 2
    frequency = ROPE_BASE ** (-(jnp.arange(half, dtype=F32) * 2.0 / HEAD_DIM))
    angles = positions[:, None] * frequency[None, :]
    cosine = jnp.cos(angles)
    sine = jnp.sin(angles)
    return (jnp.concatenate([cosine, cosine], 1), jnp.concatenate([sine, sine], 1))


def dot(left, right):
    return jnp.dot(left, right, preferred_element_type=F32)


def dot_rows(left, right):
    return lax.dot_general(left, right, (((1,), (1,)), ((), ())), preferred_element_type=F32)


def dot_first(left, right):
    return lax.dot_general(left, right, (((0,), (0,)), ((), ())), preferred_element_type=F32)


def gather(values, axes):
    return lax.all_gather(values, axes, axis=0, tiled=True)


def scatter_sum(values, axes):
    return lax.psum_scatter(values, axes, scatter_dimension=0, tiled=True)


def turn(values, cosine, sine):
    return values * cosine + pltpu.roll(values, HEAD_DIM // 2, 1) * sine


def member_rows(part):
    row = lax.broadcasted_iota(jnp.int32, (8, 2 * part), 0)
    column = lax.broadcasted_iota(jnp.int32, (8, 2 * part), 1)
    return jnp.where(row == column // part, 1.0, 0.0).astype(F32)


def row_sums(pick, values):
    return lax.dot_general(
        pick, values, (((1,), (1,)), ((), ())), precision=lax.Precision.HIGHEST, preferred_element_type=F32
    )


def over_columns(pick, sums):
    return lax.dot_general(
        sums, pick, (((0,), (0,)), ((), ())), precision=lax.Precision.HIGHEST, preferred_element_type=F32
    )


class Stats:
    def __init__(self, spans, own, arrived, send, recv):
        self.spans, self.own, self.arrived, self.send, self.recv = spans, own, arrived, send, recv
        self.core, self.place = lax.axis_index("core"), lax.axis_index("ctx")
        self.me = self.core * spans + self.place

    def member(self, s):
        core, place = step_member(self.core, self.place, s, self.spans)
        return {"core": core, "ctx": place}

    def greet(self):
        for s in range(1, 2 * self.spans):
            pl.semaphore_signal(
                pltpu.get_barrier_semaphore(), 1, device_id=self.member(s), device_id_type=MESH_ID
            )

    def meet(self):
        pl.semaphore_wait(pltpu.get_barrier_semaphore(), 2 * self.spans - 1)

    def copy(self, s):
        return pltpu.make_async_remote_copy(
            src_ref=self.own, dst_ref=self.arrived.at[s], send_sem=self.send.at[s], recv_sem=self.recv.at[s],
            device_id=self.member(s), device_id_type=MESH_ID,
        )

    def start(self):
        for s in range(1, 2 * self.spans):
            self.copy(s).start()

    def total(self):
        total = self.own[...]
        for s in range(1, 2 * self.spans):
            self.copy(s).wait()
            total = total + self.arrived[s]
        return total


def stats_scratch(spans, total_rows):
    sems = pltpu.SemaphoreType.DMA((2 * spans,))
    return [
        pltpu.VMEM((8, total_rows), F32),
        pltpu.VMEM((2 * spans, 8, total_rows), F32),
        sems,
        sems,
    ]


def allowed_at(ids, seq, block, count, spans):
    rows = ids.shape[1]
    per = block // rows
    ids_of = lambda z: ids[(seq * spans + z) * 8 : (seq * spans + z) * 8 + 8, :].astype(F32)
    first = count * per
    keys = jnp.concatenate([ids_of(z)[:1] for z in range(first + per)], 1)
    queries = jnp.concatenate([jnp.transpose(ids_of(z))[:, :1] for z in range(first, first + per)], 0)
    shape = (block, (count + 1) * block)
    query_at = lax.broadcasted_iota(jnp.int32, shape, 0) + count * block
    key_at = lax.broadcasted_iota(jnp.int32, shape, 1)
    same = queries == keys
    seen = jnp.logical_and(same, key_at <= query_at)
    return jnp.logical_and(seen, jnp.logical_or(keys != 0.0, key_at == query_at))


def softmax_parts(query, key, allowed):
    scores = jnp.where(allowed, dot_rows(query, key) * HEAD_DIM ** (-0.5), -1e30)
    weights = jnp.exp(scores - jnp.max(scores, axis=1, keepdims=True))
    return weights / jnp.sum(weights, axis=1, keepdims=True)


QUERY_BLOCK = 256
ROW_TILE = 256


def attend_body(
    spans, tokens, weights, out_w, gains, ids, cosine, sine,
    partial_out, query_out, key_out, value_out, normed_out, factor_out, attended_out,
    held, held_w, raw, given, own, arrived, load_sem, store_sem, send, recv,
):
    part = out_w.shape[0]
    total_rows = raw.shape[0]
    length = total_rows // 2
    width = tokens.shape[1]
    tiles = total_rows // ROW_TILE
    stats = Stats(spans, own, arrived, send, recv)
    stats.greet()

    def at(i):
        return pl.ds(pl.multiple_of(i * ROW_TILE, ROW_TILE), ROW_TILE)

    def load_rows(i):
        return pltpu.make_async_copy(tokens.at[at(i)], held.at[at(i)], load_sem.at[i])

    load_w = pltpu.make_async_copy(weights, held_w, load_sem.at[tiles])
    load_w.start()

    @pl.loop(0, tiles)
    def _(i):
        load_rows(i).start()

    pick = member_rows(part)
    load_w.wait()

    @pl.loop(0, tiles)
    def _(i):
        load_rows(i).wait()
        values = dot(held[at(i), :], held_w[...])
        raw[at(i), :] = values
        both = values[:, : 2 * part]
        own[:, at(i)] = row_sums(pick, both * both)

    stats.meet()
    stats.start()

    @pl.loop(0, tiles)
    def _(i):
        value_out[at(i), :] = raw[at(i), 2 * part :].astype(BF16)

    factor_out[...] = lax.rsqrt(stats.total() / width + EPS)
    me = stats.me
    columns = pl.ds(pl.multiple_of(me * part, part), part)
    gain = jnp.concatenate([gains[0:1, columns], gains[1:2, columns]], 1)

    @pl.loop(0, tiles)
    def _(i):
        normed = raw[at(i), : 2 * part] * over_columns(pick, factor_out[:, at(i)])
        normed_out[at(i), :] = normed
        scaled = normed * gain
        place = pl.ds(pl.multiple_of(lax.rem(i, length // ROW_TILE) * ROW_TILE, ROW_TILE), ROW_TILE)
        for h in range(part // HEAD_DIM):
            head = slice(h * HEAD_DIM, (h + 1) * HEAD_DIM)
            low = slice(part + h * HEAD_DIM, part + (h + 1) * HEAD_DIM)
            query_out[at(i), head] = turn(scaled[:, head], cosine[place, :], sine[place, :]).astype(BF16)
            key_out[at(i), head] = turn(scaled[:, low], cosine[place, :], sine[place, :]).astype(BF16)

    block = QUERY_BLOCK
    for seq in range(2):
        for count in range(length // block):
            allowed = allowed_at(ids, seq, block, count, spans)
            rows = slice(seq * length + count * block, seq * length + (count + 1) * block)
            keys = slice(seq * length, seq * length + (count + 1) * block)
            for h in range(part // HEAD_DIM):
                head = slice(h * HEAD_DIM, (h + 1) * HEAD_DIM)
                shares = softmax_parts(query_out[rows, head], key_out[keys, head], allowed)
                attended_out[rows, head] = dot(shares.astype(BF16), value_out[keys, head]).astype(BF16)
            i = rows.start // ROW_TILE
            if i >= 2:
                pltpu.make_async_copy(given.at[i % 2], partial_out.at[at(i - 2)], store_sem.at[i - 2]).wait()
            given[i % 2] = dot(attended_out[rows, :], out_w[...]).astype(BF16)
            pltpu.make_async_copy(given.at[i % 2], partial_out.at[at(i)], store_sem.at[i]).start()
    for i in range(tiles - 2, tiles):
        pltpu.make_async_copy(given.at[i % 2], partial_out.at[at(i)], store_sem.at[i]).wait()


def attend(spans, tokens, weights, out_w, gains, ids, cosine, sine):
    total_rows, width = tokens.shape
    part = out_w.shape[0]
    tiles = total_rows // ROW_TILE
    vmem = pl.BlockSpec(memory_space=pltpu.VMEM)
    hbm = pl.BlockSpec(memory_space=pl.ANY)
    shape = jax.ShapeDtypeStruct
    return pl.pallas_call(
        functools.partial(attend_body, spans),
        out_shape=[
            shape((total_rows, width), BF16),
            shape((total_rows, part), BF16),
            shape((total_rows, part), BF16),
            shape((total_rows, part), BF16),
            shape((total_rows, 2 * part), F32),
            shape((8, total_rows), F32),
            shape((total_rows, part), BF16),
        ],
        in_specs=[hbm, hbm] + [vmem] * 5,
        out_specs=[hbm] + [vmem] * 6,
        scratch_shapes=[
            pltpu.VMEM((total_rows, width), BF16),
            pltpu.VMEM(weights.shape, BF16),
            pltpu.VMEM((total_rows, 3 * part), F32),
            pltpu.VMEM((2, ROW_TILE, width), BF16),
            *stats_scratch(spans, total_rows)[:2],
            pltpu.SemaphoreType.DMA((tiles + 1,)),
            pltpu.SemaphoreType.DMA((tiles,)),
            *stats_scratch(spans, total_rows)[2:],
        ],
        compiler_params=pltpu.CompilerParams(collective_id=8, has_side_effects=True, vmem_limit_bytes=56 << 20),
        cost_estimate=pl.CostEstimate(flops=2 * total_rows * width * 5 * part, bytes_accessed=0, transcendentals=0),
        name="attend",
    )(tokens, weights, out_w, gains, ids, cosine, sine)


def attend_back_body(
    spans, grads, tokens, weights, out_w, gains, ids, cosine, sine,
    query, key, value, normed, factor, attended,
    input_out, qkv_out, out_out, gains_out,
    held, held_tokens, held_w, raw, mixed, attended_grad, given, own, arrived, load_sem, store_sem, send, recv,
):
    part = out_w.shape[0]
    total_rows = raw.shape[0]
    length = total_rows // 2
    width = grads.shape[1]
    tiles = total_rows // ROW_TILE
    scale = HEAD_DIM ** (-0.5)
    stats = Stats(spans, own, arrived, send, recv)
    stats.greet()

    def at(i):
        return pl.ds(pl.multiple_of(i * ROW_TILE, ROW_TILE), ROW_TILE)

    def load_rows(i):
        return pltpu.make_async_copy(grads.at[at(i)], held.at[at(i)], load_sem.at[i])

    @pl.loop(0, tiles)
    def _(i):
        load_rows(i).start()

    load_w = pltpu.make_async_copy(weights, held_w, load_sem.at[tiles])
    load_tokens = pltpu.make_async_copy(tokens, held_tokens, load_sem.at[tiles + 1])
    load_w.start()
    load_tokens.start()
    pick = member_rows(part)
    me = stats.me
    columns = pl.ds(pl.multiple_of(me * part, part), part)
    gain = jnp.concatenate([gains[0:1, columns], gains[1:2, columns]], 1)

    @pl.loop(0, tiles)
    def _(i):
        load_rows(i).wait()
        attended_grad[at(i), :] = dot_rows(held[at(i), :], out_w[...]).astype(BF16)

    block = QUERY_BLOCK
    blocks = length // block
    for seq in range(2):
        for h in range(part // HEAD_DIM):
            head = slice(h * HEAD_DIM, (h + 1) * HEAD_DIM)
            key_at = slice(part + h * HEAD_DIM, part + (h + 1) * HEAD_DIM)
            value_at = slice(2 * part + h * HEAD_DIM, 2 * part + (h + 1) * HEAD_DIM)
            for count in reversed(range(blocks)):
                allowed = allowed_at(ids, seq, block, count, spans)
                rows = slice(seq * length + count * block, seq * length + (count + 1) * block)
                keys = slice(seq * length, seq * length + (count + 1) * block)
                shares = softmax_parts(query[rows, head], key[keys, head], allowed)
                share_grad = dot_rows(attended_grad[rows, head], value[keys, head])
                inner = jnp.sum(shares * share_grad, axis=1, keepdims=True)
                score_grad = (shares * (share_grad - inner)).astype(BF16)
                raw[rows, head] = dot(score_grad, key[keys, head]) * scale
                key_grad = dot_first(score_grad, query[rows, head]) * scale
                value_grad = dot_first(shares.astype(BF16), attended_grad[rows, head])
                if count == blocks - 1:
                    raw[keys, key_at] = key_grad
                    raw[keys, value_at] = value_grad
                else:
                    raw[keys, key_at] += key_grad
                    raw[keys, value_at] += value_grad

    gains_out[...] = jnp.zeros_like(gains_out)

    @pl.loop(0, tiles)
    def _(i):
        place = pl.ds(pl.multiple_of(lax.rem(i, length // ROW_TILE) * ROW_TILE, ROW_TILE), ROW_TILE)
        for h in range(2 * part // HEAD_DIM):
            head = slice(h * HEAD_DIM, (h + 1) * HEAD_DIM)
            raw[at(i), head] = turn(raw[at(i), head], cosine[place, :], -sine[place, :])
        terms = raw[at(i), : 2 * part] * normed[at(i), :]
        gains_out[0:1, :] += jnp.sum(terms, axis=0, keepdims=True)
        own[:, at(i)] = row_sums(pick, terms * gain)
        mixed[at(i), 2 * part :] = raw[at(i), 2 * part :].astype(BF16)

    stats.meet()
    stats.start()
    out_out[...] = dot_first(attended[...], held[...]).astype(BF16)
    own[...] = stats.total() / width

    @pl.loop(0, tiles)
    def _(i):
        mean = over_columns(pick, own[:, at(i)])
        back = gain * raw[at(i), : 2 * part] - normed[at(i), :] * mean
        mixed[at(i), : 2 * part] = (over_columns(pick, factor[:, at(i)]) * back).astype(BF16)

    load_w.wait()

    def store(i):
        return pltpu.make_async_copy(given.at[lax.rem(i, 2)], input_out.at[at(i)], store_sem.at[lax.rem(i, 2)])

    @pl.loop(0, tiles)
    def _(i):
        @pl.when(i >= 2)
        def _():
            store(i - 2).wait()

        given[lax.rem(i, 2)] = dot_rows(mixed[at(i), :], held_w[...]).astype(BF16)
        store(i).start()

    load_tokens.wait()

    @pl.loop(0, width // ROW_TILE)
    def _(i):
        qkv_out[at(i), :] = dot_first(held_tokens[:, at(i)], mixed[...]).astype(BF16)

    for i in range(tiles - 2, tiles):
        store(i).wait()


def attend_back(spans, grads, tokens, weights, out_w, gains, ids, cosine, sine, saved):
    total_rows, width = tokens.shape
    part = out_w.shape[0]
    tiles = total_rows // ROW_TILE
    vmem = pl.BlockSpec(memory_space=pltpu.VMEM)
    hbm = pl.BlockSpec(memory_space=pl.ANY)
    shape = jax.ShapeDtypeStruct
    return pl.pallas_call(
        functools.partial(attend_back_body, spans),
        out_shape=[
            shape((total_rows, width), BF16),
            shape((width, 3 * part), BF16),
            shape((part, width), BF16),
            shape((8, 2 * part), F32),
        ],
        in_specs=[hbm] * 3 + [vmem] * (5 + len(saved)),
        out_specs=[hbm] + [vmem] * 3,
        scratch_shapes=[
            pltpu.VMEM((total_rows, width), BF16),
            pltpu.VMEM((total_rows, width), BF16),
            pltpu.VMEM(weights.shape, BF16),
            pltpu.VMEM((total_rows, 3 * part), F32),
            pltpu.VMEM((total_rows, 3 * part), BF16),
            pltpu.VMEM((total_rows, part), BF16),
            pltpu.VMEM((2, ROW_TILE, width), BF16),
            *stats_scratch(spans, total_rows)[:2],
            pltpu.SemaphoreType.DMA((tiles + 2,)),
            pltpu.SemaphoreType.DMA((2,)),
            *stats_scratch(spans, total_rows)[2:],
        ],
        compiler_params=pltpu.CompilerParams(collective_id=9, has_side_effects=True, vmem_limit_bytes=58 << 20),
        cost_estimate=pl.CostEstimate(flops=2 * total_rows * width * 8 * part, bytes_accessed=0, transcendentals=0),
        name="attend_back",
    )(grads, tokens, weights, out_w, gains, ids, cosine, sine, *saved)


def per_device(inputs, segment, w_qkv, w_out, w_gate, w_up, w_down_t, gains, cotangent):
    rows, width = inputs.shape[1:]
    cores = lax.axis_size("core")
    spans = lax.axis_size("ctx")
    members = cores * spans
    length = rows * spans
    part = width // members
    tokens = inputs[0]

    qkv_rows = w_qkv.shape[0]
    qkv_cut = w_qkv.reshape(qkv_rows, 3, members, part).transpose(2, 0, 1, 3)
    qkv_cut = qkv_cut.reshape(members, qkv_rows, 3 * part)
    chips = lax.axis_size("chip")
    assert chips == spans
    spread = lambda reduce, row_fn, n_in, n_out, gain: Exchange(
        spans, rows, width, PIECE, reduce, True, row_fn, n_in, n_out, gain
    )
    own = jax.ShapeDtypeStruct((rows, width), F32)
    own_low = jax.ShapeDtypeStruct((rows, width), BF16)
    one = jax.ShapeDtypeStruct((1, width), F32)
    qkv_w, ids, tokens_all = Exchange(
        spans, rows, width, PIECE, False, True, pass_tokens, 1, 0, None,
        QkvWeights(spans, chips, qkv_cut, jnp.broadcast_to(segment, (8, rows))),
    ).call("gather_tokens", 1, None, [tokens], [])
    swaps = [
        (m * spans + a, a * members + m) for m in range(members) for a in range(chips)
    ]
    out_w = gather(lax.ppermute(w_out, ALL, swaps), "chip")

    hidden = w_gate.shape[1] // cores
    gate_up, down = split_columns(w_gate, w_up, w_down_t)
    gate_up_w, down_w = gather(gate_up, "chip"), gather(down, "chip")

    cosine, sine = rope_tables(jnp.arange(length, dtype=F32))
    half = jnp.arange(HEAD_DIM) < HEAD_DIM // 2
    sine = jnp.where(half[None, :], -sine, sine)
    out_part, *saved = attend(spans, tokens_all, qkv_w, out_w, gains, ids, cosine, sine)
    residual, projected, residual_all = spread(True, after_projected, 2, 2, None).call(
        "sum_projected", 2, out_part, [tokens, gains], [own, own]
    )

    gate_up_out = dot(residual_all, gate_up_w)
    gate, up_part = gate_up_out[:, :hidden], gate_up_out[:, hidden:]
    sigmoid = 1.0 / (1.0 + jnp.exp(-gate))
    activated = (gate * sigmoid * up_part).astype(BF16)
    output, gain_feed, feed_grad_all = spread(True, after_feed, 3, 2, 1).call(
        "sum_feed",
        3,
        dot_rows(activated, down_w).astype(BF16),
        [residual, cotangent[0], gains],
        [own_low, one],
    )

    act_grad = dot(feed_grad_all, down_w)
    gate_grad = act_grad * up_part * sigmoid * (1.0 + gate * (1.0 - sigmoid))
    up_grad = act_grad * (gate * sigmoid)
    gate_up_grad = jnp.concatenate([gate_grad.astype(BF16), up_grad.astype(BF16)], 1)
    back_part = dot_rows(gate_up_grad, gate_up_w).astype(BF16)
    down_part = dot_first(feed_grad_all, activated).astype(BF16)
    gate_up_part = dot_first(residual_all, gate_up_grad).astype(BF16)
    back_part, down_part, gate_up_part = lax.optimization_barrier((back_part, down_part, gate_up_part))
    gate_up_sum, down_sum = scatter_sum(gate_up_part, "chip"), scatter_sum(down_part, "chip")
    residual_grad, gain_attn, projected_all = spread(True, after_back, 3, 2, 1).call(
        "sum_back",
        4,
        back_part,
        [projected, cotangent[0], gains],
        [own, one],
    )

    input_part, qkv_part, out_grads, gain_sums = attend_back(
        spans, projected_all, tokens_all, qkv_w, out_w, gains, ids, cosine, sine, saved
    )
    gain_query, gain_key = gain_sums[0, :part], gain_sums[0, part:]
    sums = jnp.concatenate(
        [a.reshape(-1, 128) for a in (gain_attn, gain_feed, gain_query, gain_key)]
        + [jnp.zeros((-2 * part // 128 % 8, 128), F32)]
    )
    input_grad, grad_qkv, grad_gains, grad_out = Exchange(
        spans, rows, width, PIECE, True, False, after_input, 1, 1, None,
        QkvGrads(
            spans, chips, members, qkv_part, sums, out_grads,
        ),
    ).call("sum_input", 5, input_part, [residual_grad], [own])

    grad_gate, grad_up, grad_down = join_columns(gate_up_sum, down_sum)
    return (
        output[None],
        input_grad[None],
        grad_qkv,
        grad_out,
        grad_gate,
        grad_up,
        grad_down,
        grad_gains.reshape(4, width),
    )


def solution(mesh):
    cores = 2
    chips = mesh.shape["dp"] // cores
    split = Mesh(mesh.devices.reshape(chips, cores, mesh.shape["ctx"]), ALL)
    dp = ("chip", "core")
    every = P((*dp, "ctx"), None)
    in_specs = (
        P(dp, "ctx", None),
        P(dp, "ctx"),
        every,
        every,
        P(dp, "ctx"),
        P(dp, "ctx"),
        P(dp, "ctx"),
        P(),
        P(dp, "ctx", None),
    )
    out_specs = (
        P(dp, "ctx", None),
        P(dp, "ctx", None),
        every,
        every,
        P(dp, "ctx"),
        P(dp, "ctx"),
        P(dp, "ctx"),
        P(),
    )
    return jax.shard_map(
        per_device, mesh=split, in_specs=in_specs, out_specs=out_specs, check_vma=False
    )
```

```python
import functools

import jax
import jax.numpy as jnp
from jax import lax
from jax.experimental import pallas as pl
from jax.experimental.pallas import tpu as pltpu
from jax.sharding import Mesh
from jax.sharding import PartitionSpec as P

HEAD_DIM = 128
EPS = 1e-06
ROPE_BASE = 500000.0
F32 = jnp.float32
BF16 = jnp.bfloat16
GROUP = ("core", "ctx")
ALL = ("chip", "core", "ctx")


PIECE = 32
LAGB = 1
LAGJ = 1
MESH_ID = pl.DeviceIdType.MESH


def row_factor(values):
    return lax.rsqrt(jnp.mean(values * values, axis=-1, keepdims=True) + EPS)


def row_norm_back(values, gain, grad):
    factor = row_factor(values)
    normed = values * factor
    scaled = gain * grad
    back = factor * (scaled - normed * jnp.mean(scaled * normed, axis=-1, keepdims=True))
    return back, jnp.sum(grad * normed, axis=0, keepdims=True)


def after_projected(total, ins, outs, rows):
    tokens, gains = ins
    residual_out, projected_out = outs
    projected_out[rows, :] = total
    gain = gains[2:3, :]
    residual = tokens[rows, :].astype(F32) + total * row_factor(total) * gain
    residual_out[rows, :] = residual
    return residual


def after_feed(total, ins, outs, rows):
    residual, cotangent, gains = ins
    output, gain_out = outs
    gain = gains[3:4, :]
    normed = total * row_factor(total) * gain
    output[rows, :] = (residual[rows, :] + normed).astype(BF16)
    back, term = row_norm_back(total, gain, cotangent[rows, :].astype(F32))
    gain_out[...] += term
    return back


def after_back(total, ins, outs, rows):
    projected, cotangent, gains = ins
    grad_out, gain_out = outs
    grad = cotangent[rows, :].astype(F32) + total
    grad_out[rows, :] = grad
    back, term = row_norm_back(projected[rows, :], gains[2:3, :], grad)
    gain_out[...] += term
    return back


def after_input(total, ins, outs, rows):
    (grad,), (result,) = ins, outs
    result[rows, :] = grad[rows, :] + total
    return None


def pass_tokens(total, ins, outs, rows):
    return ins[0][rows, :]


class Exchange:
    def __init__(self, spans, rows, width, piece, reduce, spread, row_fn, n_in, n_out, gain, extra=None):
        self.extra = extra
        self.spans, self.rows, self.width, self.piece = spans, rows, width, piece
        self.reduce, self.spread, self.row_fn = reduce, spread, row_fn
        self.n_in, self.n_out, self.gain = n_in, n_out, gain
        self.count = rows // piece

    def scratch(self):
        spans, count = self.spans, self.count
        block = pltpu.VMEM((spans * self.rows, self.width), BF16)
        sems = pltpu.SemaphoreType.DMA((spans, count))
        items = []
        if self.reduce:
            items += [block] * 4 + [pltpu.SemaphoreType.DMA] + [sems] * 6
        if self.spread:
            items += [pltpu.VMEM((2 * spans * self.rows, self.width), BF16)]
            items += [sems] * 7 + [pltpu.SemaphoreType.DMA]
        if self.extra is not None:
            items += self.extra.scratch()
        return items

    def body(self, *refs):
        spans, rows, piece, count = self.spans, self.rows, self.piece, self.count
        refs = list(refs)
        take = lambda n: [refs.pop(0) for _ in range(n)]
        partial = take(1)[0] if self.reduce else None
        ins = take(self.n_in)
        extra = self.extra
        if extra is not None:
            extra.ins = take(extra.n_in)
        outs = take(self.n_out)
        if extra is not None:
            extra.outs = take(extra.n_out)
        gathered = take(1)[0] if self.spread else None
        if self.reduce:
            own, near, from_left, from_right = take(4)
            (load_sem,) = take(1)
            near_send, near_recv, right_send, right_recv, left_send, left_recv = take(6)
        if self.spread:
            (held,) = take(1)
            fwd_send, fwd_recv, bwd_send, bwd_recv, own_send, side_send, side_recv = take(7)
            (store_sem,) = take(1)
        if extra is not None:
            extra.held = refs
        core = lax.axis_index("core")
        place = lax.axis_index("ctx")
        other = 1 - core
        has_left = place > 0
        has_right = place < spans - 1

        def at(block, k):
            return pl.ds(pl.multiple_of(block * rows + k * piece, piece), piece)

        def held_at(seq, block, k):
            return pl.ds(pl.multiple_of((seq * spans + block) * rows + k * piece, piece), piece)

        def remote(src, dst, send, recv, **device):
            return pltpu.make_async_remote_copy(
                src_ref=src, dst_ref=dst, send_sem=send, recv_sem=recv,
                device_id=device, device_id_type=MESH_ID,
            )

        barrier = pltpu.get_barrier_semaphore()
        if extra is not None:
            meet_all(spans, getattr(extra, "moves", False))
        else:
            pl.semaphore_signal(barrier, 1, device_id={"core": other}, device_id_type=MESH_ID)

            @pl.when(has_left)
            def _():
                pl.semaphore_signal(barrier, 1, device_id={"ctx": place - 1}, device_id_type=MESH_ID)

            @pl.when(has_right)
            def _():
                pl.semaphore_signal(barrier, 1, device_id={"ctx": place + 1}, device_id_type=MESH_ID)

            pl.semaphore_wait(barrier, 1 + has_left.astype(jnp.int32) + has_right.astype(jnp.int32))

        if self.gain is not None:
            outs[self.gain][...] = jnp.zeros_like(outs[self.gain])

        def near_copy(d, k):
            return remote(
                partial.at[held_at(other, d, k)], near.at[at(d, k)],
                near_send.at[d, k], near_recv.at[d, k], core=other,
            )

        def right_copy(d, k):
            return remote(
                own.at[at(d, k)], from_left.at[at(d, k)],
                right_send.at[d, k], right_recv.at[d, k], ctx=place + 1,
            )

        def left_copy(d, k):
            return remote(
                own.at[at(d, k)], from_right.at[at(d, k)],
                left_send.at[d, k], left_recv.at[d, k], ctx=place - 1,
            )

        def fwd_copy(o, k, send):
            where = held_at(core, o, k)
            return remote(held.at[where], held.at[where], send, fwd_recv.at[o, k], ctx=place + 1)

        def bwd_copy(o, k, send):
            where = held_at(core, o, k)
            return remote(held.at[where], held.at[where], send, bwd_recv.at[o, k], ctx=place - 1)

        def side_copy(o, k):
            where = held_at(core, o, k)
            return remote(held.at[where], held.at[where], side_send.at[o, k], side_recv.at[o, k], core=other)

        if extra is not None:
            extra.start()
        if self.reduce:
            load = pltpu.make_async_copy(
                partial.at[pl.ds(pl.multiple_of(core * spans * rows, rows), spans * rows)], own, load_sem
            )
            load.start()

            @pl.loop(0, count)
            def _(k):
                for j in range(spans):
                    near_copy(j, k).start()

            load.wait()

        def base(d, k):
            near_copy(d, k).wait_recv()
            return own[at(d, k), :].astype(F32) + near[at(d, k), :].astype(F32)

        def reduce_step(k):
            for j in range(spans - 1):
                right, left = spans - 1 - j, j

                @pl.when(jnp.logical_and(right > place, has_left))
                def _():
                    value = base(right, k)
                    right_copy(right, k).wait_recv()
                    own[at(right, k), :] = (value + from_left[at(right, k), :].astype(F32)).astype(BF16)
                    right_copy(right, k).start()

                @pl.when(jnp.logical_and(right > place, jnp.logical_not(has_left)))
                def _():
                    own[at(right, k), :] = base(right, k).astype(BF16)
                    right_copy(right, k).start()

                @pl.when(jnp.logical_and(left < place, has_right))
                def _():
                    value = base(left, k)
                    left_copy(left, k).wait_recv()
                    own[at(left, k), :] = (value + from_right[at(left, k), :].astype(F32)).astype(BF16)
                    left_copy(left, k).start()

                @pl.when(jnp.logical_and(left < place, jnp.logical_not(has_right)))
                def _():
                    own[at(left, k), :] = base(left, k).astype(BF16)
                    left_copy(left, k).start()

        def finish_step(k):
            total = None
            if self.reduce:
                total = base(place, k)

                @pl.when(has_left)
                def _():
                    right_copy(place, k).wait_recv()

                @pl.when(has_right)
                def _():
                    left_copy(place, k).wait_recv()

                zero = jnp.zeros_like(total)
                total = total + jnp.where(has_left, from_left[at(place, k), :].astype(F32), zero)
                total = total + jnp.where(has_right, from_right[at(place, k), :].astype(F32), zero)
            own_rows = pl.ds(pl.multiple_of(k * piece, piece), piece)
            result = self.row_fn(total, ins, outs, own_rows)
            if self.spread:
                held[held_at(core, place, k), :] = result.astype(BF16)

                @pl.when(has_right)
                def _():
                    fwd_copy(place, k, fwd_send.at[place, k]).start()

                @pl.when(has_left)
                def _():
                    bwd_copy(place, k, bwd_send.at[place, k]).start()

                side_copy(place, k).start()

        def relay_step(k, j):
            if True:

                @pl.when(place - j >= 0)
                def _():
                    fwd_copy(place - j, k, fwd_send.at[place - j, k]).wait_recv()

                    @pl.when(has_right)
                    def _():
                        fwd_copy(place - j, k, fwd_send.at[place - j, k]).start()

                    side_copy(place - j, k).start()

                @pl.when(place + j < spans)
                def _():
                    bwd_copy(place + j, k, bwd_send.at[place + j, k]).wait_recv()

                    @pl.when(has_left)
                    def _():
                        bwd_copy(place + j, k, bwd_send.at[place + j, k]).start()

                    side_copy(place + j, k).start()

        lag = LAGB if self.reduce else 0

        @pl.loop(0, count + lag + (LAGJ * (spans - 1) if self.spread else 0))
        def _(t):
            if self.reduce:

                @pl.when(t < count)
                def _():
                    reduce_step(t)

            if self.reduce:

                @pl.when(jnp.logical_and(t >= lag, t < count + lag))
                def _():
                    finish_step(t - lag)
            else:

                @pl.when(t == 0)
                def _():
                    for k in range(count):
                        finish_step(k)

            if self.spread:
                for j in range(1, spans):
                    after = t - lag - j * LAGJ

                    @pl.when(jnp.logical_and(after >= 0, after < count))
                    def _():
                        relay_step(after, j)
            if extra is not None:
                extra.tick(t)

        if extra is not None:
            extra.finish(count + lag + (LAGJ * (spans - 1) if self.spread else 0))
        if self.spread:

            @pl.loop(0, count)
            def _(k):
                for o in range(spans):
                    side_copy(o, k).wait_recv()

            store = pltpu.make_async_copy(held, gathered, store_sem)
            store.start()

        @pl.loop(0, count)
        def _(k):
            for d in range(spans):
                if self.reduce:
                    near_copy(d, k).wait_send()

                    @pl.when(d > place)
                    def _():
                        right_copy(d, k).wait_send()

                    @pl.when(d < place)
                    def _():
                        left_copy(d, k).wait_send()

                if self.spread:
                    side_copy(d, k).wait_send()

                    @pl.when(jnp.logical_and(d <= place, has_right))
                    def _():
                        fwd_copy(d, k, fwd_send.at[d, k]).wait_send()

                    @pl.when(jnp.logical_and(d >= place, has_left))
                    def _():
                        bwd_copy(d, k, bwd_send.at[d, k]).wait_send()

        if self.spread:
            store.wait()

    def call(self, name, collective_id, partial, ins, outs):
        vmem = pl.BlockSpec(memory_space=pltpu.VMEM)
        hbm = pl.BlockSpec(memory_space=pl.ANY)
        operands = ([partial] if self.reduce else []) + list(ins)
        in_specs = ([hbm] if self.reduce else []) + [vmem] * len(ins)
        shapes = list(outs)
        specs = [vmem] * len(outs)
        if self.extra is not None:
            operands += self.extra.operands
            in_specs += self.extra.in_specs
            shapes += self.extra.out_shapes
            specs += self.extra.out_specs
        if self.spread:
            shapes.append(jax.ShapeDtypeStruct((2 * self.spans * self.rows, self.width), BF16))
            specs.append(hbm)
        return pl.pallas_call(
            self.body,
            out_shape=shapes,
            in_specs=in_specs,
            out_specs=specs,
            scratch_shapes=self.scratch(),
            compiler_params=pltpu.CompilerParams(
                collective_id=collective_id, has_side_effects=True, vmem_limit_bytes=48 << 20
            ),
            cost_estimate=pl.CostEstimate(
                flops=0,
                bytes_accessed=(50 if self.reduce else 30) * self.width * self.width,
                transcendentals=0,
            ),
            name=name,
        )(*operands)


def owner_of(chip, core, place, spans):
    member = core * spans + place
    return member // 2, lax.rem(member, 2), chip


def summer_of(chip, core, place, spans):
    member = chip * 2 + core
    return place, member // spans, lax.rem(member, spans)


def stays(chip, core, place, spans):
    to_chip, to_core, to_place = owner_of(chip, core, place, spans)
    return jnp.logical_and(to_chip == chip, jnp.logical_and(to_core == core, to_place == place))


def meet_all(spans, moves):
    chips = lax.axis_size("chip")
    barrier = pltpu.get_barrier_semaphore()
    chip = lax.axis_index("chip")
    core = lax.axis_index("core")
    place = lax.axis_index("ctx")
    for s in range(1, chips):
        pl.semaphore_signal(
            barrier, 1, device_id={"chip": lax.rem(chip + s, chips)}, device_id_type=MESH_ID
        )
    for s in range(1, 2 * spans):
        to_core, to_place = step_member(core, place, s, spans)
        pl.semaphore_signal(
            barrier, 1, device_id={"core": to_core, "ctx": to_place}, device_id_type=MESH_ID
        )
    count = chips - 1 + 2 * spans - 1
    if moves:
        away = jnp.logical_not(stays(chip, core, place, spans))

        @pl.when(away)
        def _():
            for find in (owner_of, summer_of):
                to_chip, to_core, to_place = find(chip, core, place, spans)
                pl.semaphore_signal(
                    barrier, 1, device_id={"chip": to_chip, "core": to_core, "ctx": to_place}, device_id_type=MESH_ID
                )

        count = count + 2 * away.astype(jnp.int32)
    pl.semaphore_wait(barrier, count)


def step_member(core, place, s, spans):
    return lax.rem(core + s % 2, 2), lax.rem(place + s // 2, spans)


def meet_other_core():
    barrier = pltpu.get_barrier_semaphore()
    other = 1 - lax.axis_index("core")
    pl.semaphore_signal(barrier, 1, device_id={"core": other}, device_id_type=MESH_ID)
    pl.semaphore_wait(barrier, 1)


def split_body(gate, up, down, gate_up_out, down_out, held, load_sem, store_sem, send_sem, recv_sem):
    core = lax.axis_index("core")
    other = 1 - core
    rows, width = gate.shape
    half = width // 2
    where = pl.ds(pl.multiple_of(core * rows, rows), rows)
    places = [gate_up_out.at[where, :half], gate_up_out.at[where, half:], down_out.at[where, :]]
    mine = pl.ds(pl.multiple_of(core * half, half), half)
    theirs = pl.ds(pl.multiple_of(other * half, half), half)
    loads = [
        pltpu.make_async_copy(a.at[:, mine], held.at[i], load_sem.at[i]) for i, a in enumerate((gate, up, down))
    ]
    for load in loads:
        load.start()
    meet_other_core()
    sends = [
        pltpu.make_async_remote_copy(
            src_ref=a.at[:, theirs], dst_ref=places[i], send_sem=send_sem.at[i], recv_sem=recv_sem.at[i],
            device_id={"core": other}, device_id_type=MESH_ID,
        )
        for i, a in enumerate((gate, up, down))
    ]
    for send in sends:
        send.start()
    stores = [pltpu.make_async_copy(held.at[i], places[i], store_sem.at[i]) for i in range(3)]
    for load, store in zip(loads, stores):
        load.wait()
        store.start()
    for store, send in zip(stores, sends):
        store.wait()
        send.wait()


def split_columns(gate, up, down):
    rows, width = gate.shape
    hbm = pl.BlockSpec(memory_space=pl.ANY)
    three = pltpu.SemaphoreType.DMA((3,))
    return pl.pallas_call(
        split_body,
        out_shape=[
            jax.ShapeDtypeStruct((2 * rows, width), BF16),
            jax.ShapeDtypeStruct((2 * rows, width // 2), BF16),
        ],
        in_specs=[hbm] * 3,
        out_specs=[hbm] * 2,
        scratch_shapes=[pltpu.VMEM((3, rows, width // 2), BF16)] + [three] * 4,
        compiler_params=pltpu.CompilerParams(collective_id=6, has_side_effects=True, vmem_limit_bytes=8 << 20),
        name="split_columns",
    )(gate, up, down)


def join_body(gate_up, down, gate_out, up_out, down_out, gate_up_in, down_in, send_sem, recv_sem):
    core = lax.axis_index("core")
    other = 1 - core
    rows, width = gate_out.shape
    half = width // 2
    meet_other_core()
    theirs = pl.ds(pl.multiple_of(other * rows, rows), rows)
    sends = [
        pltpu.make_async_remote_copy(
            src_ref=a.at[theirs], dst_ref=b, send_sem=send_sem.at[i], recv_sem=recv_sem.at[i],
            device_id={"core": other}, device_id_type=MESH_ID,
        )
        for i, (a, b) in enumerate(((gate_up, gate_up_in), (down, down_in)))
    ]
    for send in sends:
        send.start()
    mine = pl.ds(pl.multiple_of(core * half, half), half)
    far = pl.ds(pl.multiple_of(other * half, half), half)
    step = 16

    def rows_at(i, base):
        return pl.ds(pl.multiple_of(base + i * step, step), step)

    @pl.loop(0, rows // step)
    def _(i):
        here, there = rows_at(i, core * rows), rows_at(i, 0)
        gate_out[there, mine] = gate_up[here, :half].astype(F32)
        up_out[there, mine] = gate_up[here, half:].astype(F32)
        down_out[there, mine] = down[here, :].astype(F32)

    for send in sends:
        send.wait()

    @pl.loop(0, rows // step)
    def _(i):
        there = rows_at(i, 0)
        gate_out[there, far] = gate_up_in[there, :half].astype(F32)
        up_out[there, far] = gate_up_in[there, half:].astype(F32)
        down_out[there, far] = down_in[there, :].astype(F32)


def join_columns(gate_up, down):
    rows, width = gate_up.shape[0] // 2, gate_up.shape[1]
    vmem = pl.BlockSpec(memory_space=pltpu.VMEM)
    two = pltpu.SemaphoreType.DMA((2,))
    return pl.pallas_call(
        join_body,
        out_shape=[jax.ShapeDtypeStruct((rows, width), F32)] * 3,
        in_specs=[vmem] * 2,
        out_specs=[vmem] * 3,
        scratch_shapes=[pltpu.VMEM((rows, width), BF16), pltpu.VMEM((rows, width // 2), BF16), two, two],
        compiler_params=pltpu.CompilerParams(collective_id=7, has_side_effects=True, vmem_limit_bytes=32 << 20),
        name="join_columns",
    )(gate_up, down)


class Extra:
    def remote(self, src, dst, send, recv, **device):
        return pltpu.make_async_remote_copy(
            src_ref=src, dst_ref=dst, send_sem=send, recv_sem=recv,
            device_id=device, device_id_type=MESH_ID,
        )

    def locate(self):
        self.chip = lax.axis_index("chip")
        self.core = lax.axis_index("core")
        self.place = lax.axis_index("ctx")
        self.me = self.core * self.spans + self.place


class QkvWeights(Extra):
    n_in, n_out = 2, 2

    def __init__(self, spans, chips, cut, ids):
        self.spans, self.chips = spans, chips
        self.members, self.block, self.columns = cut.shape
        self.operands = [cut, ids]
        self.ids_shape = ids.shape
        vmem = pl.BlockSpec(memory_space=pltpu.VMEM)
        self.in_specs = [vmem, vmem]
        self.out_shapes = [
            jax.ShapeDtypeStruct((chips * self.members * self.block, self.columns), BF16),
            jax.ShapeDtypeStruct((self.members * ids.shape[0], ids.shape[1]), jnp.int32),
        ]
        self.out_specs = [vmem, vmem]

    def scratch(self):
        rows = self.chips * self.members * self.block
        sems = pltpu.SemaphoreType.DMA((self.members,))
        cross = pltpu.SemaphoreType.DMA((self.chips, self.members))
        ids = (self.members * self.ids_shape[0], self.ids_shape[1])
        return [pltpu.VMEM((rows, self.columns), BF16), pltpu.VMEM(ids, jnp.int32)] + [sems] * 4 + [cross] * 2

    def at(self, chip, m):
        return pl.ds(pl.multiple_of((chip * self.members + m) * self.block, self.block), self.block)

    def ids_at(self, m):
        return pl.ds(pl.multiple_of(m * self.ids_shape[0], self.ids_shape[0]), self.ids_shape[0])

    def block_copy(self, s):
        full, _, send, recv = self.held[:4]
        core, place = step_member(self.core, self.place, s, self.spans)
        return self.remote(
            self.ins[0].at[core * self.spans + place], full.at[self.at(self.chip, self.me)],
            send.at[s], recv.at[s], core=core, ctx=place,
        )

    def ids_copy(self, s):
        all_ids, send, recv = self.held[1], self.held[4], self.held[5]
        core, place = step_member(self.core, self.place, s, self.spans)
        return self.remote(
            self.ins[1], all_ids.at[self.ids_at(self.me)], send.at[s], recv.at[s], core=core, ctx=place
        )

    def source(self, s):
        core = lax.rem(self.core + s % 2, 2)
        return core * self.spans + lax.rem(self.place + self.spans - s // 2, self.spans)

    def chip_copy(self, s, m):
        full, _, _, _, _, _, send, recv = self.held
        where = self.at(self.chip, m)
        return self.remote(
            full.at[where], full.at[where], send.at[s, m], recv.at[s, m], chip=lax.rem(self.chip + s, self.chips)
        )

    def start(self):
        self.locate()
        cut, ids = self.ins
        full, all_ids = self.held[:2]
        for s in range(1, self.members):
            self.block_copy(s).start()
        for s in range(1, self.members):
            self.ids_copy(s).start()
        full[self.at(self.chip, self.me), :] = cut[self.me]
        all_ids[self.ids_at(self.me), :] = ids[...]

    def send_block(self, s):
        m = self.me if s == 0 else self.source(s)
        if s > 0:
            self.block_copy(s).wait_recv()
        for step in range(1, self.chips):
            self.chip_copy(step, m).start()

    def tick(self, t):
        @pl.when(t == 0)
        def _():
            for s in range(self.members):
                self.send_block(s)

    def finish(self, ticks):
        full, all_ids = self.held[:2]
        for s in range(1, self.members):
            self.ids_copy(s).wait_recv()
            self.block_copy(s).wait_send()
            self.ids_copy(s).wait_send()

        @pl.loop(0, self.members)
        def _(m):
            for s in range(1, self.chips):
                self.chip_copy(s, m).wait()

        self.outs[0][...] = full[...]
        self.outs[1][...] = all_ids[...]


class QkvGrads(Extra):
    n_in, n_out = 3, 3
    moves = True

    def __init__(self, spans, chips, members, grads, sums, out_grads):
        self.spans, self.chips, self.members = spans, chips, members
        self.out_rows = out_grads.shape[0] // chips
        self.block, self.columns = grads.shape[0] // (chips * members), grads.shape[1]
        self.part = self.columns // 3
        self.width = self.part * members
        self.own_rows = self.part // 128
        self.sum_rows = sums.shape[0]
        self.operands = [grads, sums, out_grads]
        vmem = pl.BlockSpec(memory_space=pltpu.VMEM)
        self.in_specs = [vmem] * 3
        self.out_shapes = [
            jax.ShapeDtypeStruct((self.block, 3 * self.width), F32),
            jax.ShapeDtypeStruct((4, self.width // 128, 128), F32),
            jax.ShapeDtypeStruct((self.out_rows, self.width), F32),
        ]
        self.out_specs = [vmem] * 3

    def scratch(self):
        sems = pltpu.SemaphoreType.DMA((self.members,))
        chip_sems = pltpu.SemaphoreType.DMA((self.chips,))
        cross = pltpu.SemaphoreType.DMA((self.chips, self.members))
        return [
            pltpu.VMEM((self.chips, self.members, self.block, self.columns), BF16),
            pltpu.VMEM((self.members, self.block, self.columns), BF16),
            pltpu.VMEM((self.members, self.block, self.columns), BF16),
            pltpu.VMEM((self.chips, self.sum_rows, 128), F32),
            pltpu.VMEM((self.sum_rows, 128), F32),
            pltpu.VMEM((self.members, self.sum_rows, 128), F32),
            pltpu.VMEM((self.chips, self.out_rows, self.width), BF16),
            pltpu.VMEM((self.out_rows, self.width), BF16),
            pltpu.VMEM((self.out_rows, self.width), BF16),
        ] + [cross] * 2 + [sems] * 2 + [chip_sems] * 2 + [sems] * 2 + [chip_sems] * 2 + [pltpu.SemaphoreType.DMA] * 2

    def at(self, chip, m):
        return pl.ds(pl.multiple_of((chip * self.members + m) * self.block, self.block), self.block)

    def chip_copy(self, s, m):
        other = lax.rem(self.chip + s, self.chips)
        return self.remote(
            self.ins[0].at[self.at(other, m)], self.arrived.at[s, m],
            self.cross_send.at[s, m], self.cross_recv.at[s, m], chip=other,
        )

    def member_copy(self, s):
        core, place = step_member(self.core, self.place, s, self.spans)
        return self.remote(
            self.summed.at[core * self.spans + place], self.columns_in.at[self.me],
            self.member_send.at[s], self.member_recv.at[s], core=core, ctx=place,
        )

    def sums_chip(self, s):
        return self.remote(
            self.ins[1], self.sums_in.at[s], self.sums_send.at[s], self.sums_recv.at[s],
            chip=lax.rem(self.chip + s, self.chips),
        )

    def sums_member(self, s):
        core, place = step_member(self.core, self.place, s, self.spans)
        return self.remote(
            self.sums_chips, self.sums_members.at[self.me], self.last_send.at[s], self.last_recv.at[s],
            core=core, ctx=place,
        )

    def out_copy(self, s):
        other = lax.rem(self.chip + s, self.chips)
        rows = pl.ds(pl.multiple_of(other * self.out_rows, self.out_rows), self.out_rows)
        return self.remote(
            self.ins[2].at[rows], self.out_in.at[s], self.out_send.at[s], self.out_recv.at[s], chip=other
        )

    def move_copy(self):
        chip, core, place = owner_of(self.chip, self.core, self.place, self.spans)
        return self.remote(
            self.out_sum, self.out_final, self.move_send, self.move_recv, chip=chip, core=core, ctx=place
        )

    def start(self):
        self.locate()
        (
            self.arrived, self.summed, self.columns_in, self.sums_in, self.sums_chips, self.sums_members,
            self.out_in, self.out_sum, self.out_final,
            self.cross_send, self.cross_recv, self.member_send, self.member_recv,
            self.sums_send, self.sums_recv, self.last_send, self.last_recv,
            self.out_send, self.out_recv, self.move_send, self.move_recv,
        ) = self.held
        for s in range(1, self.chips):
            self.sums_chip(s).start()
            self.out_copy(s).start()

        @pl.loop(0, self.members)
        def _(i):
            m = lax.rem(self.me + 1 + i, self.members)
            for s in range(1, self.chips):
                self.chip_copy(s, m).start()

    def add_block(self, m):
        total = self.ins[0][self.at(self.chip, m), :].astype(F32)
        for s in range(1, self.chips):
            self.chip_copy(s, m).wait_recv()
            total = total + self.arrived[s, m].astype(F32)
        self.summed[m] = total.astype(BF16)

    def send_blocks(self, first, last):
        for s in range(first, last):
            core, place = step_member(self.core, self.place, s, self.spans)
            self.add_block(core * self.spans + place)
            self.member_copy(s).start()

    def tick(self, t):
        @pl.when(t == 1)
        def _():
            total = self.ins[1][...]
            for s in range(1, self.chips):
                self.sums_chip(s).wait_recv()
                total = total + self.sums_in[s]
            self.sums_chips[...] = total
            self.sums_members[self.me] = total
            for s in range(1, self.members):
                self.sums_member(s).start()

        @pl.when(t == 2)
        def _():
            rows = pl.ds(pl.multiple_of(self.chip * self.out_rows, self.out_rows), self.out_rows)
            total = self.ins[2][rows, :].astype(F32)
            for s in range(1, self.chips):
                self.out_copy(s).wait_recv()
                total = total + self.out_in[s].astype(F32)
            self.out_sum[...] = total.astype(BF16)

            @pl.when(stays(self.chip, self.core, self.place, self.spans))
            def _():
                self.out_final[...] = total.astype(BF16)

            @pl.when(jnp.logical_not(stays(self.chip, self.core, self.place, self.spans)))
            def _():
                self.move_copy().start()

    def finish(self, ticks):
        self.send_blocks(1, self.members)
        self.add_block(self.me)
        self.columns_in[self.me] = self.summed[self.me]
        for s in range(1, self.members):
            self.sums_member(s).wait()
        wide = self.width // 128
        for i in range(2):
            total = self.sums_members[0, i * wide : (i + 1) * wide, :]
            for m in range(1, self.members):
                total = total + self.sums_members[m, i * wide : (i + 1) * wide, :]
            self.outs[1][2 + i] = total
            base = 2 * wide + i * self.own_rows
            for m in range(self.members):
                self.outs[1][i, m * self.own_rows : (m + 1) * self.own_rows, :] = self.sums_members[
                    m, base : base + self.own_rows, :
                ]
        for s in range(1, self.members):
            self.member_copy(s).wait()
        for m in range(self.members):
            for i in range(3):
                self.outs[0][:, i * self.width + m * self.part : i * self.width + (m + 1) * self.part] = (
                    self.columns_in[m, :, i * self.part : (i + 1) * self.part].astype(F32)
                )
        @pl.when(jnp.logical_not(stays(self.chip, self.core, self.place, self.spans)))
        def _():
            self.move_copy().wait()

        self.outs[2][...] = self.out_final[...].astype(F32)
        for s in range(1, self.chips):
            self.sums_chip(s).wait_send()
            self.out_copy(s).wait_send()

        @pl.loop(0, self.members)
        def _(m):
            for s in range(1, self.chips):
                self.chip_copy(s, m).wait_send()


def rope_tables(positions):
    half = HEAD_DIM // 2
    frequency = ROPE_BASE ** (-(jnp.arange(half, dtype=F32) * 2.0 / HEAD_DIM))
    angles = positions[:, None] * frequency[None, :]
    cosine = jnp.cos(angles)
    sine = jnp.sin(angles)
    return (jnp.concatenate([cosine, cosine], 1), jnp.concatenate([sine, sine], 1))


def dot(left, right):
    return jnp.dot(left, right, preferred_element_type=F32)


def dot_rows(left, right):
    return lax.dot_general(left, right, (((1,), (1,)), ((), ())), preferred_element_type=F32)


def dot_first(left, right):
    return lax.dot_general(left, right, (((0,), (0,)), ((), ())), preferred_element_type=F32)


def gather(values, axes):
    return lax.all_gather(values, axes, axis=0, tiled=True)


def scatter_sum(values, axes):
    return lax.psum_scatter(values, axes, scatter_dimension=0, tiled=True)


FF_TILE = 512
SUM_TILE = 1024
BATCH_PIECE = 16


class Middle:
    def __init__(self, spans, rows, width, hidden, piece):
        self.spans, self.rows, self.width, self.hidden, self.piece = spans, rows, width, hidden, piece
        self.count = rows // piece
        self.block = spans * piece
        self.batch = 2 * self.block

    def body(
        self, chips, partial, tokens, cotangent, gains, gate_up_w, down,
        output, residual_grad, gain_feed, gain_attn, residual_all, feed_grad_all, gate_up_grad, activated, projected_all,
        residual, projected, own, near, from_left, from_right, held, wide, act, back, up_weights, down_weights,
        load_sem, weight_sem, store_sem, act_sem, near_send, near_recv, right_send, right_recv, left_send, left_recv,
        fwd_send, fwd_recv, bwd_send, bwd_recv, side_send, side_recv, down_send, down_recv,
    ):
        spans, rows, piece, count = self.spans, self.rows, self.piece, self.count
        width, hidden, block, batch = self.width, self.hidden, self.block, self.batch
        core = lax.axis_index("core")
        place = lax.axis_index("ctx")
        other = 1 - core
        last = spans - 1
        has_left = place > 0
        has_right = place < last

        def turn_of(o):
            return jnp.maximum(o, last - o)

        def at(d, k):
            return pl.ds(pl.multiple_of((k * spans + d) * piece, piece), piece)

        def at_seq(seq, d, k):
            return pl.ds(pl.multiple_of(((k * 2 + seq) * spans + d) * piece, piece), piece)

        def batch_at(k):
            return pl.ds(pl.multiple_of(k * batch, batch), batch)

        def natural(seq, d, k):
            return pl.ds(pl.multiple_of((seq * spans + d) * rows + k * piece, piece), piece)

        def remote(src, dst, send, recv, **device):
            return pltpu.make_async_remote_copy(
                src_ref=src, dst_ref=dst, send_sem=send, recv_sem=recv, device_id=device, device_id_type=MESH_ID
            )

        barrier = pltpu.get_barrier_semaphore()
        pl.semaphore_signal(barrier, 1, device_id={"core": other}, device_id_type=MESH_ID)

        @pl.when(has_left)
        def _():
            pl.semaphore_signal(barrier, 1, device_id={"ctx": place - 1}, device_id_type=MESH_ID)

        @pl.when(has_right)
        def _():
            pl.semaphore_signal(barrier, 1, device_id={"ctx": place + 1}, device_id_type=MESH_ID)

        def near_copy(e, d, k):
            src = partial.at[natural(other, d, k)] if e == 0 else own.at[at_seq(other, d, k)]
            return remote(src, near.at[at(d, k)], near_send.at[d, k], near_recv.at[d, k], core=other)

        def right_copy(d, k):
            return remote(
                own.at[at_seq(core, d, k)], from_left.at[at(d, k)], right_send.at[d, k], right_recv.at[d, k],
                ctx=place + 1,
            )

        def left_copy(d, k):
            return remote(
                own.at[at_seq(core, d, k)], from_right.at[at(d, k)], left_send.at[d, k], left_recv.at[d, k],
                ctx=place - 1,
            )

        def spread_copy(o, k, send, recv, **device):
            where = held.at[at_seq(core, o, k)]
            return remote(where, where, send.at[o, k], recv.at[o, k], **device)

        def fwd_copy(o, k):
            return spread_copy(o, k, fwd_send, fwd_recv, ctx=place + 1)

        def bwd_copy(o, k):
            return spread_copy(o, k, bwd_send, bwd_recv, ctx=place - 1)

        def side_copy(o, k):
            return spread_copy(o, k, side_send, side_recv, core=other)

        def load_own(d, k):
            return pltpu.make_async_copy(
                partial.at[natural(core, d, k)], own.at[at_seq(core, d, k)], load_sem.at[d, k]
            )

        @pl.loop(0, count)
        def _(k):
            for d in range(spans):
                load_own(d, k).start()

        load_up = pltpu.make_async_copy(gate_up_w, up_weights, weight_sem.at[0])
        chip = lax.axis_index("chip")
        shard = down.shape[0]
        here = pl.ds(pl.multiple_of(chip * shard, shard), shard)
        load_down = pltpu.make_async_copy(down, down_weights.at[here], weight_sem.at[1])

        def down_copy(s):
            return remote(
                down, down_weights.at[here], down_send.at[s], down_recv.at[s], chip=lax.rem(chip + s, chips)
            )

        load_up.start()
        load_down.start()
        gain_feed[...] = jnp.zeros_like(gain_feed)
        gain_attn[...] = jnp.zeros_like(gain_attn)
        for s in range(1, chips):
            pl.semaphore_signal(
                barrier, 1, device_id={"chip": lax.rem(chip + s, chips)}, device_id_type=MESH_ID
            )
        pl.semaphore_wait(barrier, chips + has_left.astype(jnp.int32) + has_right.astype(jnp.int32))
        for s in range(1, chips):
            down_copy(s).start()

        @pl.loop(0, count)
        def _(k):
            for d in range(spans):
                near_copy(0, d, k).start()

        def base(e, d, k):
            near_copy(e, d, k).wait_recv()
            if e == 0:
                load_own(d, k).wait()
            return own[at_seq(core, d, k), :].astype(F32) + near[at(d, k), :].astype(F32)

        def pass_on(e, d, k, arrived, copy, later):
            value = base(e, d, k)

            @pl.when(later)
            def _():
                copy(d, k).wait_recv()

            before = arrived[at(d, k), :].astype(F32)
            value = value + jnp.where(later, before, jnp.zeros_like(before))
            own[at_seq(core, d, k), :] = value.astype(BF16)
            copy(d, k).start()

        def pass_right(e, k):
            for d in range(last, 0, -1):

                @pl.when(d > place)
                def _():
                    pass_on(e, d, k, from_left, right_copy, has_left)

        def pass_left(e, k):
            for d in range(last):

                @pl.when(d < place)
                def _():
                    pass_on(e, d, k, from_right, left_copy, has_right)

        def finish(e, k):
            total = base(e, place, k)

            @pl.when(has_left)
            def _():
                right_copy(place, k).wait_recv()

            @pl.when(has_right)
            def _():
                left_copy(place, k).wait_recv()

            zero = jnp.zeros_like(total)
            total = total + jnp.where(has_left, from_left[at(place, k), :].astype(F32), zero)
            total = total + jnp.where(has_right, from_right[at(place, k), :].astype(F32), zero)
            mine = pl.ds(pl.multiple_of(k * piece, piece), piece)
            if e == 0:
                result = after_projected(total, (tokens, gains), (residual, projected), mine)
            elif e == 1:
                result = after_feed(total, (residual, cotangent, gains), (output, gain_feed), mine)
            else:
                result = after_back(total, (projected, cotangent, gains), (residual_grad, gain_attn), mine)
            held[at_seq(core, place, k), :] = result.astype(BF16)

            @pl.when(has_right)
            def _():
                fwd_copy(place, k).start()

            @pl.when(has_left)
            def _():
                bwd_copy(place, k).start()

            side_copy(place, k).start()

        def relay_right(o, k):
            fwd_copy(o, k).wait_recv()

            @pl.when(has_right)
            def _():
                fwd_copy(o, k).start()

            side_copy(o, k).start()

        def relay_left(o, k):
            bwd_copy(o, k).wait_recv()

            @pl.when(has_left)
            def _():
                bwd_copy(o, k).start()

            side_copy(o, k).start()

        def gathered(k):
            for o in range(spans):
                side_copy(o, k).wait_recv()

        def sums_sent(e, k):
            for d in range(spans):
                near_copy(e, d, k).wait_send()

                @pl.when(d > place)
                def _():
                    right_copy(d, k).wait_send()

                @pl.when(d < place)
                def _():
                    left_copy(d, k).wait_send()

        def spread_sent(k):
            for o in range(spans):
                side_copy(o, k).wait_send()

                @pl.when(jnp.logical_and(o <= place, has_right))
                def _():
                    fwd_copy(o, k).wait_send()

                @pl.when(jnp.logical_and(o >= place, has_left))
                def _():
                    bwd_copy(o, k).wait_send()

        def store(src, dst, k, sem):
            return pltpu.make_async_copy(src, dst.at[batch_at(k)], sem)

        def forward(k):
            @pl.when(k == 0)
            def _():
                load_up.wait()
                load_down.wait()
                for s in range(1, chips):
                    down_copy(s).wait()

            gathered(k)
            keep = store(held.at[batch_at(k)], residual_all, k, store_sem.at[0])
            keep.start()

            @pl.loop(0, hidden // FF_TILE)
            def _(n):
                low = pl.ds(pl.multiple_of(n * FF_TILE, FF_TILE), FF_TILE)
                high = pl.ds(pl.multiple_of(hidden + n * FF_TILE, FF_TILE), FF_TILE)
                gate = dot(held[batch_at(k), :], up_weights[:, low])
                up = dot(held[batch_at(k), :], up_weights[:, high])
                wide[batch_at(k), low] = gate
                wide[batch_at(k), high] = up
                act[:, low] = (gate * (1.0 / (1.0 + jnp.exp(-gate))) * up).astype(BF16)

            keep_act = store(act, activated, k, act_sem.at[0])
            keep_act.start()
            sums_sent(0, k)

            @pl.loop(0, width // SUM_TILE)
            def _(n):
                columns = pl.ds(pl.multiple_of(n * SUM_TILE, SUM_TILE), SUM_TILE)
                own[batch_at(k), columns] = dot_rows(act[...], down_weights[columns, :]).astype(BF16)

            keep_act.wait()
            keep.wait()
            spread_sent(k)
            for d in range(spans):
                near_copy(1, d, k).start()

        def backward(k):
            gathered(k)
            keep = store(held.at[batch_at(k)], feed_grad_all, k, store_sem.at[0])
            keep.start()

            @pl.loop(0, hidden // FF_TILE)
            def _(n):
                low = pl.ds(pl.multiple_of(n * FF_TILE, FF_TILE), FF_TILE)
                high = pl.ds(pl.multiple_of(hidden + n * FF_TILE, FF_TILE), FF_TILE)
                act_grad = dot(held[batch_at(k), :], down_weights[:, low])
                gate = wide[batch_at(k), low]
                up = wide[batch_at(k), high]
                sigmoid = 1.0 / (1.0 + jnp.exp(-gate))
                back[:, low] = (act_grad * up * sigmoid * (1.0 + gate * (1.0 - sigmoid))).astype(BF16)
                back[:, high] = (act_grad * (gate * sigmoid)).astype(BF16)

            keep_back = store(back, gate_up_grad, k, act_sem.at[1])
            keep_back.start()
            sums_sent(1, k)

            @pl.loop(0, width // SUM_TILE)
            def _(n):
                columns = pl.ds(pl.multiple_of(n * SUM_TILE, SUM_TILE), SUM_TILE)
                own[batch_at(k), columns] = dot_rows(back[...], up_weights[columns, :]).astype(BF16)

            keep_back.wait()
            keep.wait()
            spread_sent(k)
            for d in range(spans):
                near_copy(2, d, k).start()

        def give(seq, d, k):
            return pltpu.make_async_copy(
                held.at[at_seq(seq, d, k)], projected_all.at[natural(seq, d, k)], load_sem.at[d, k]
            )

        def hand_out(k):
            gathered(k)
            sums_sent(2, k)
            for seq in range(2):
                for d in range(spans):
                    give(seq, d, k).start()
                for d in range(spans):
                    give(seq, d, k).wait()
            spread_sent(k)

        step = 2 * last + 2

        def due(t, run):
            @pl.when(jnp.logical_and(t >= 0, t < count))
            def _():
                run(t)

        @pl.loop(0, 3 * step + count - 1)
        def _(t):
            for e in range(2, -1, -1):
                now = t - e * step
                for j in range(1, spans):
                    o = place - j

                    @pl.when(o >= 0)
                    def _():
                        due(now - turn_of(o) - j, functools.partial(relay_right, o))

                    p = place + j

                    @pl.when(p < spans)
                    def _():
                        due(now - turn_of(p) - j, functools.partial(relay_left, p))

                due(now - place, functools.partial(pass_right, e))
                due(now - (last - place), functools.partial(pass_left, e))
                due(now - turn_of(place), functools.partial(finish, e))
            for e, run in ((2, hand_out), (1, backward), (0, forward)):
                due(t - e * step - 2 * last, run)

    def call(self, chips, partial, tokens, cotangent, gains, gate_up_w, down):
        spans, rows, width, hidden, count = self.spans, self.rows, self.width, self.hidden, self.count
        total = 2 * spans * rows
        vmem = pl.BlockSpec(memory_space=pltpu.VMEM)
        hbm = pl.BlockSpec(memory_space=pl.ANY)
        shape = jax.ShapeDtypeStruct
        sems = pltpu.SemaphoreType.DMA((spans, count))
        two = pltpu.SemaphoreType.DMA((2,))
        return pl.pallas_call(
            functools.partial(self.body, chips),
            out_shape=[
                shape((rows, width), BF16),
                shape((rows, width), F32),
                shape((1, width), F32),
                shape((1, width), F32),
                shape((total, width), BF16),
                shape((total, width), BF16),
                shape((total, 2 * hidden), BF16),
                shape((total, hidden), BF16),
                shape((total, width), BF16),
            ],
            in_specs=[hbm, vmem, vmem, vmem, hbm, hbm],
            out_specs=[vmem] * 4 + [hbm] * 5,
            scratch_shapes=[
                pltpu.VMEM((rows, width), F32),
                pltpu.VMEM((rows, width), F32),
                pltpu.VMEM((total, width), BF16),
                pltpu.VMEM((total // 2, width), BF16),
                pltpu.VMEM((total // 2, width), BF16),
                pltpu.VMEM((total // 2, width), BF16),
                pltpu.VMEM((total, width), BF16),
                pltpu.VMEM((total, 2 * hidden), F32),
                pltpu.VMEM((self.batch, hidden), BF16),
                pltpu.VMEM((self.batch, 2 * hidden), BF16),
                pltpu.VMEM((width, 2 * hidden), BF16),
                pltpu.VMEM((width, hidden), BF16),
                sems,
                two,
                two,
                two,
            ]
            + [sems] * 12
            + [pltpu.SemaphoreType.DMA((chips,))] * 2,
            compiler_params=pltpu.CompilerParams(
                collective_id=2, has_side_effects=True, vmem_limit_bytes=62 << 20
            ),
            cost_estimate=pl.CostEstimate(
                flops=36 * rows * spans * width * hidden, bytes_accessed=100 * width * width, transcendentals=0
            ),
            name="feed_forward",
        )(partial, tokens, cotangent, gains, gate_up_w, down)


def turn(values, cosine, sine):
    return values * cosine + pltpu.roll(values, HEAD_DIM // 2, 1) * sine


def member_rows(part):
    row = lax.broadcasted_iota(jnp.int32, (8, 2 * part), 0)
    column = lax.broadcasted_iota(jnp.int32, (8, 2 * part), 1)
    return jnp.where(row == column // part, 1.0, 0.0).astype(F32)


def row_sums(pick, values):
    return lax.dot_general(
        pick, values, (((1,), (1,)), ((), ())), precision=lax.Precision.HIGHEST, preferred_element_type=F32
    )


def over_columns(pick, sums):
    return lax.dot_general(
        sums, pick, (((0,), (0,)), ((), ())), precision=lax.Precision.HIGHEST, preferred_element_type=F32
    )


class Stats:
    def __init__(self, spans, own, arrived, send, recv):
        self.spans, self.own, self.arrived, self.send, self.recv = spans, own, arrived, send, recv
        self.core, self.place = lax.axis_index("core"), lax.axis_index("ctx")
        self.me = self.core * spans + self.place

    def member(self, s):
        core, place = step_member(self.core, self.place, s, self.spans)
        return {"core": core, "ctx": place}

    def greet(self):
        for s in range(1, 2 * self.spans):
            pl.semaphore_signal(
                pltpu.get_barrier_semaphore(), 1, device_id=self.member(s), device_id_type=MESH_ID
            )

    def meet(self):
        pl.semaphore_wait(pltpu.get_barrier_semaphore(), 2 * self.spans - 1)

    def copy(self, s):
        return pltpu.make_async_remote_copy(
            src_ref=self.own, dst_ref=self.arrived.at[s], send_sem=self.send.at[s], recv_sem=self.recv.at[s],
            device_id=self.member(s), device_id_type=MESH_ID,
        )

    def start(self):
        for s in range(1, 2 * self.spans):
            self.copy(s).start()

    def total(self):
        total = self.own[...]
        for s in range(1, 2 * self.spans):
            self.copy(s).wait()
            total = total + self.arrived[s]
        return total


def stats_scratch(spans, total_rows):
    sems = pltpu.SemaphoreType.DMA((2 * spans,))
    return [
        pltpu.VMEM((8, total_rows), F32),
        pltpu.VMEM((2 * spans, 8, total_rows), F32),
        sems,
        sems,
    ]


def allowed_at(ids, seq, block, count, spans):
    rows = ids.shape[1]
    per = block // rows
    ids_of = lambda z: ids[(seq * spans + z) * 8 : (seq * spans + z) * 8 + 8, :].astype(F32)
    first = count * per
    keys = jnp.concatenate([ids_of(z)[:1] for z in range(first + per)], 1)
    queries = jnp.concatenate([jnp.transpose(ids_of(z))[:, :1] for z in range(first, first + per)], 0)
    shape = (block, (count + 1) * block)
    query_at = lax.broadcasted_iota(jnp.int32, shape, 0) + count * block
    key_at = lax.broadcasted_iota(jnp.int32, shape, 1)
    same = queries == keys
    seen = jnp.logical_and(same, key_at <= query_at)
    return jnp.logical_and(seen, jnp.logical_or(keys != 0.0, key_at == query_at))


def softmax_parts(query, key, allowed):
    scores = jnp.where(allowed, dot_rows(query, key) * HEAD_DIM ** (-0.5), -1e30)
    weights = jnp.exp(scores - jnp.max(scores, axis=1, keepdims=True))
    return weights / jnp.sum(weights, axis=1, keepdims=True)


QUERY_BLOCK = 256
ROW_TILE = 256


def attend_body(
    spans, chips, tokens, weights, out_rows, gains, ids, cosine, sine,
    partial_out, out_w_out, query_out, key_out, value_out, normed_out, factor_out, attended_out,
    held, held_w, raw, given, out_w, own, arrived, load_sem, store_sem, chip_send, chip_recv, send, recv,
):
    part = out_w.shape[0]
    total_rows = raw.shape[0]
    length = total_rows // 2
    width = tokens.shape[1]
    tiles = total_rows // ROW_TILE
    stats = Stats(spans, own, arrived, send, recv)
    stats.greet()
    chip = lax.axis_index("chip")
    shard = out_rows.shape[0]
    here = pl.ds(pl.multiple_of(chip * shard, shard), shard)

    def chip_copy(s):
        return pltpu.make_async_remote_copy(
            src_ref=out_rows, dst_ref=out_w.at[here], send_sem=chip_send.at[s], recv_sem=chip_recv.at[s],
            device_id={"chip": lax.rem(chip + s, chips)}, device_id_type=MESH_ID,
        )

    for s in range(1, chips):
        pl.semaphore_signal(
            pltpu.get_barrier_semaphore(), 1, device_id={"chip": lax.rem(chip + s, chips)}, device_id_type=MESH_ID
        )
    out_w[here, :] = out_rows[...]

    def at(i):
        return pl.ds(pl.multiple_of(i * ROW_TILE, ROW_TILE), ROW_TILE)

    def load_rows(i):
        return pltpu.make_async_copy(tokens.at[at(i)], held.at[at(i)], load_sem.at[i])

    load_w = pltpu.make_async_copy(weights, held_w, load_sem.at[tiles])
    load_w.start()

    @pl.loop(0, tiles)
    def _(i):
        load_rows(i).start()

    pick = member_rows(part)
    pl.semaphore_wait(pltpu.get_barrier_semaphore(), 2 * spans - 1 + chips - 1)
    for s in range(1, chips):
        chip_copy(s).start()
    load_w.wait()

    @pl.loop(0, tiles)
    def _(i):
        load_rows(i).wait()
        values = dot(held[at(i), :], held_w[...])
        raw[at(i), :] = values
        both = values[:, : 2 * part]
        own[:, at(i)] = row_sums(pick, both * both)

    stats.start()

    @pl.loop(0, tiles)
    def _(i):
        value_out[at(i), :] = raw[at(i), 2 * part :].astype(BF16)

    factor_out[...] = lax.rsqrt(stats.total() / width + EPS)
    me = stats.me
    columns = pl.ds(pl.multiple_of(me * part, part), part)
    gain = jnp.concatenate([gains[0:1, columns], gains[1:2, columns]], 1)

    @pl.loop(0, tiles)
    def _(i):
        normed = raw[at(i), : 2 * part] * over_columns(pick, factor_out[:, at(i)])
        normed_out[at(i), :] = normed
        scaled = normed * gain
        place = pl.ds(pl.multiple_of(lax.rem(i, length // ROW_TILE) * ROW_TILE, ROW_TILE), ROW_TILE)
        for h in range(part // HEAD_DIM):
            head = slice(h * HEAD_DIM, (h + 1) * HEAD_DIM)
            low = slice(part + h * HEAD_DIM, part + (h + 1) * HEAD_DIM)
            query_out[at(i), head] = turn(scaled[:, head], cosine[place, :], sine[place, :]).astype(BF16)
            key_out[at(i), head] = turn(scaled[:, low], cosine[place, :], sine[place, :]).astype(BF16)

    for s in range(1, chips):
        chip_copy(s).wait()
    out_w_out[...] = out_w[...]
    block = QUERY_BLOCK
    for seq in range(2):
        for count in range(length // block):
            allowed = allowed_at(ids, seq, block, count, spans)
            rows = slice(seq * length + count * block, seq * length + (count + 1) * block)
            keys = slice(seq * length, seq * length + (count + 1) * block)
            for h in range(part // HEAD_DIM):
                head = slice(h * HEAD_DIM, (h + 1) * HEAD_DIM)
                shares = softmax_parts(query_out[rows, head], key_out[keys, head], allowed)
                attended_out[rows, head] = dot(shares.astype(BF16), value_out[keys, head]).astype(BF16)
            i = rows.start // ROW_TILE
            if i >= 2:
                pltpu.make_async_copy(given.at[i % 2], partial_out.at[at(i - 2)], store_sem.at[i - 2]).wait()
            given[i % 2] = dot(attended_out[rows, :], out_w[...]).astype(BF16)
            pltpu.make_async_copy(given.at[i % 2], partial_out.at[at(i)], store_sem.at[i]).start()
    for i in range(tiles - 2, tiles):
        pltpu.make_async_copy(given.at[i % 2], partial_out.at[at(i)], store_sem.at[i]).wait()


def attend(spans, chips, tokens, weights, out_rows, gains, ids, cosine, sine):
    total_rows, width = tokens.shape
    part = out_rows.shape[0] * chips
    tiles = total_rows // ROW_TILE
    vmem = pl.BlockSpec(memory_space=pltpu.VMEM)
    hbm = pl.BlockSpec(memory_space=pl.ANY)
    shape = jax.ShapeDtypeStruct
    return pl.pallas_call(
        functools.partial(attend_body, spans, chips),
        out_shape=[
            shape((total_rows, width), BF16),
            shape((part, width), BF16),
            shape((total_rows, part), BF16),
            shape((total_rows, part), BF16),
            shape((total_rows, part), BF16),
            shape((total_rows, 2 * part), F32),
            shape((8, total_rows), F32),
            shape((total_rows, part), BF16),
        ],
        in_specs=[hbm, hbm] + [vmem] * 5,
        out_specs=[hbm] + [vmem] * 7,
        scratch_shapes=[
            pltpu.VMEM((total_rows, width), BF16),
            pltpu.VMEM(weights.shape, BF16),
            pltpu.VMEM((total_rows, 3 * part), F32),
            pltpu.VMEM((2, ROW_TILE, width), BF16),
            pltpu.VMEM((part, width), BF16),
            *stats_scratch(spans, total_rows)[:2],
            pltpu.SemaphoreType.DMA((tiles + 1,)),
            pltpu.SemaphoreType.DMA((tiles,)),
            pltpu.SemaphoreType.DMA((chips,)),
            pltpu.SemaphoreType.DMA((chips,)),
            *stats_scratch(spans, total_rows)[2:],
        ],
        compiler_params=pltpu.CompilerParams(collective_id=8, has_side_effects=True, vmem_limit_bytes=56 << 20),
        cost_estimate=pl.CostEstimate(flops=2 * total_rows * width * 5 * part, bytes_accessed=0, transcendentals=0),
        name="attend",
    )(tokens, weights, out_rows, gains, ids, cosine, sine)


def attend_back_body(
    spans, grads, tokens, weights, out_w, gains, ids, cosine, sine,
    query, key, value, normed, factor, attended,
    input_out, qkv_out, out_out, gains_out,
    held, held_tokens, held_w, raw, mixed, attended_grad, given, own, arrived, load_sem, store_sem, send, recv,
):
    part = out_w.shape[0]
    total_rows = raw.shape[0]
    length = total_rows // 2
    width = grads.shape[1]
    tiles = total_rows // ROW_TILE
    scale = HEAD_DIM ** (-0.5)
    stats = Stats(spans, own, arrived, send, recv)
    stats.greet()

    def at(i):
        return pl.ds(pl.multiple_of(i * ROW_TILE, ROW_TILE), ROW_TILE)

    def load_rows(i):
        return pltpu.make_async_copy(grads.at[at(i)], held.at[at(i)], load_sem.at[i])

    @pl.loop(0, tiles)
    def _(i):
        load_rows(i).start()

    load_w = pltpu.make_async_copy(weights, held_w, load_sem.at[tiles])
    load_tokens = pltpu.make_async_copy(tokens, held_tokens, load_sem.at[tiles + 1])
    load_w.start()
    load_tokens.start()
    pick = member_rows(part)
    me = stats.me
    columns = pl.ds(pl.multiple_of(me * part, part), part)
    gain = jnp.concatenate([gains[0:1, columns], gains[1:2, columns]], 1)

    @pl.loop(0, tiles)
    def _(i):
        load_rows(i).wait()
        attended_grad[at(i), :] = dot_rows(held[at(i), :], out_w[...]).astype(BF16)

    block = QUERY_BLOCK
    blocks = length // block
    for seq in range(2):
        for h in range(part // HEAD_DIM):
            head = slice(h * HEAD_DIM, (h + 1) * HEAD_DIM)
            key_at = slice(part + h * HEAD_DIM, part + (h + 1) * HEAD_DIM)
            value_at = slice(2 * part + h * HEAD_DIM, 2 * part + (h + 1) * HEAD_DIM)
            for count in reversed(range(blocks)):
                allowed = allowed_at(ids, seq, block, count, spans)
                rows = slice(seq * length + count * block, seq * length + (count + 1) * block)
                keys = slice(seq * length, seq * length + (count + 1) * block)
                shares = softmax_parts(query[rows, head], key[keys, head], allowed)
                share_grad = dot_rows(attended_grad[rows, head], value[keys, head])
                inner = jnp.sum(shares * share_grad, axis=1, keepdims=True)
                score_grad = (shares * (share_grad - inner)).astype(BF16)
                raw[rows, head] = dot(score_grad, key[keys, head]) * scale
                key_grad = dot_first(score_grad, query[rows, head]) * scale
                value_grad = dot_first(shares.astype(BF16), attended_grad[rows, head])
                if count == blocks - 1:
                    raw[keys, key_at] = key_grad
                    raw[keys, value_at] = value_grad
                else:
                    raw[keys, key_at] += key_grad
                    raw[keys, value_at] += value_grad

    gains_out[...] = jnp.zeros_like(gains_out)

    @pl.loop(0, tiles)
    def _(i):
        place = pl.ds(pl.multiple_of(lax.rem(i, length // ROW_TILE) * ROW_TILE, ROW_TILE), ROW_TILE)
        for h in range(2 * part // HEAD_DIM):
            head = slice(h * HEAD_DIM, (h + 1) * HEAD_DIM)
            raw[at(i), head] = turn(raw[at(i), head], cosine[place, :], -sine[place, :])
        terms = raw[at(i), : 2 * part] * normed[at(i), :]
        gains_out[0:1, :] += jnp.sum(terms, axis=0, keepdims=True)
        own[:, at(i)] = row_sums(pick, terms * gain)
        mixed[at(i), 2 * part :] = raw[at(i), 2 * part :].astype(BF16)

    stats.meet()
    stats.start()
    out_out[...] = dot_first(attended[...], held[...]).astype(BF16)
    own[...] = stats.total() / width

    @pl.loop(0, tiles)
    def _(i):
        mean = over_columns(pick, own[:, at(i)])
        back = gain * raw[at(i), : 2 * part] - normed[at(i), :] * mean
        mixed[at(i), : 2 * part] = (over_columns(pick, factor[:, at(i)]) * back).astype(BF16)

    load_w.wait()

    def store(i):
        return pltpu.make_async_copy(given.at[lax.rem(i, 2)], input_out.at[at(i)], store_sem.at[lax.rem(i, 2)])

    @pl.loop(0, tiles)
    def _(i):
        @pl.when(i >= 2)
        def _():
            store(i - 2).wait()

        given[lax.rem(i, 2)] = dot_rows(mixed[at(i), :], held_w[...]).astype(BF16)
        store(i).start()

    load_tokens.wait()

    @pl.loop(0, width // ROW_TILE)
    def _(i):
        qkv_out[at(i), :] = dot_first(held_tokens[:, at(i)], mixed[...]).astype(BF16)

    for i in range(tiles - 2, tiles):
        store(i).wait()


def attend_back(spans, grads, tokens, weights, out_w, gains, ids, cosine, sine, saved):
    total_rows, width = tokens.shape
    part = out_w.shape[0]
    tiles = total_rows // ROW_TILE
    vmem = pl.BlockSpec(memory_space=pltpu.VMEM)
    hbm = pl.BlockSpec(memory_space=pl.ANY)
    shape = jax.ShapeDtypeStruct
    return pl.pallas_call(
        functools.partial(attend_back_body, spans),
        out_shape=[
            shape((total_rows, width), BF16),
            shape((width, 3 * part), BF16),
            shape((part, width), BF16),
            shape((8, 2 * part), F32),
        ],
        in_specs=[hbm] * 3 + [vmem] * (5 + len(saved)),
        out_specs=[hbm] + [vmem] * 3,
        scratch_shapes=[
            pltpu.VMEM((total_rows, width), BF16),
            pltpu.VMEM((total_rows, width), BF16),
            pltpu.VMEM(weights.shape, BF16),
            pltpu.VMEM((total_rows, 3 * part), F32),
            pltpu.VMEM((total_rows, 3 * part), BF16),
            pltpu.VMEM((total_rows, part), BF16),
            pltpu.VMEM((2, ROW_TILE, width), BF16),
            *stats_scratch(spans, total_rows)[:2],
            pltpu.SemaphoreType.DMA((tiles + 2,)),
            pltpu.SemaphoreType.DMA((2,)),
            *stats_scratch(spans, total_rows)[2:],
        ],
        compiler_params=pltpu.CompilerParams(collective_id=9, has_side_effects=True, vmem_limit_bytes=58 << 20),
        cost_estimate=pl.CostEstimate(flops=2 * total_rows * width * 8 * part, bytes_accessed=0, transcendentals=0),
        name="attend_back",
    )(grads, tokens, weights, out_w, gains, ids, cosine, sine, *saved)


def per_device(inputs, segment, w_qkv, w_out, w_gate, w_up, w_down_t, gains, cotangent):
    rows, width = inputs.shape[1:]
    cores = lax.axis_size("core")
    spans = lax.axis_size("ctx")
    members = cores * spans
    length = rows * spans
    part = width // members
    tokens = inputs[0]

    qkv_rows = w_qkv.shape[0]
    qkv_cut = w_qkv.reshape(qkv_rows, 3, members, part).transpose(2, 0, 1, 3)
    qkv_cut = qkv_cut.reshape(members, qkv_rows, 3 * part)
    chips = lax.axis_size("chip")
    assert chips == spans
    own = jax.ShapeDtypeStruct((rows, width), F32)
    qkv_w, ids, tokens_all = Exchange(
        spans, rows, width, PIECE, False, True, pass_tokens, 1, 0, None,
        QkvWeights(spans, chips, qkv_cut, jnp.broadcast_to(segment, (8, rows))),
    ).call("gather_tokens", 1, None, [tokens], [])
    swaps = [
        (m * spans + a, a * members + m) for m in range(members) for a in range(chips)
    ]
    out_rows = lax.ppermute(w_out, ALL, swaps)

    gate_up, down = split_columns(w_gate, w_up, w_down_t)
    gate_up_w = gather(gate_up, "chip")

    cosine, sine = rope_tables(jnp.arange(length, dtype=F32))
    half = jnp.arange(HEAD_DIM) < HEAD_DIM // 2
    sine = jnp.where(half[None, :], -sine, sine)
    out_part, out_w, *saved = attend(spans, chips, tokens_all, qkv_w, out_rows, gains, ids, cosine, sine)
    (
        output, residual_grad, gain_feed, gain_attn, residual_all, feed_grad_all, gate_up_grad, activated, projected_all
    ) = Middle(spans, rows, width, w_gate.shape[1] // cores, BATCH_PIECE).call(
        chips, out_part, tokens, cotangent[0], gains, gate_up_w, down
    )
    down_part = dot_first(feed_grad_all, activated).astype(BF16)
    gate_up_part = dot_first(residual_all, gate_up_grad).astype(BF16)
    gate_up_sum, down_sum = scatter_sum(gate_up_part, "chip"), scatter_sum(down_part, "chip")
    input_part, qkv_part, out_grads, gain_sums = attend_back(
        spans, projected_all, tokens_all, qkv_w, out_w, gains, ids, cosine, sine, saved
    )
    gain_query, gain_key = gain_sums[0, :part], gain_sums[0, part:]
    sums = jnp.concatenate(
        [a.reshape(-1, 128) for a in (gain_attn, gain_feed, gain_query, gain_key)]
        + [jnp.zeros((-2 * part // 128 % 8, 128), F32)]
    )
    input_grad, grad_qkv, grad_gains, grad_out = Exchange(
        spans, rows, width, PIECE, True, False, after_input, 1, 1, None,
        QkvGrads(
            spans, chips, members, qkv_part, sums, out_grads,
        ),
    ).call("sum_input", 5, input_part, [residual_grad], [own])

    grad_gate, grad_up, grad_down = join_columns(gate_up_sum, down_sum)
    return (
        output[None],
        input_grad[None],
        grad_qkv,
        grad_out,
        grad_gate,
        grad_up,
        grad_down,
        grad_gains.reshape(4, width),
    )


def solution(mesh):
    cores = 2
    chips = mesh.shape["dp"] // cores
    split = Mesh(mesh.devices.reshape(chips, cores, mesh.shape["ctx"]), ALL)
    dp = ("chip", "core")
    every = P((*dp, "ctx"), None)
    in_specs = (
        P(dp, "ctx", None),
        P(dp, "ctx"),
        every,
        every,
        P(dp, "ctx"),
        P(dp, "ctx"),
        P(dp, "ctx"),
        P(),
        P(dp, "ctx", None),
    )
    out_specs = (
        P(dp, "ctx", None),
        P(dp, "ctx", None),
        every,
        every,
        P(dp, "ctx"),
        P(dp, "ctx"),
        P(dp, "ctx"),
        P(),
    )
    return jax.shard_map(
        per_device, mesh=split, in_specs=in_specs, out_specs=out_specs, check_vma=False
    )
```

```python
import functools

import jax
import jax.numpy as jnp
from jax import lax
from jax.experimental import pallas as pl
from jax.experimental.pallas import tpu as pltpu
from jax.sharding import Mesh
from jax.sharding import PartitionSpec as P

HEAD_DIM = 128
EPS = 1e-06
ROPE_BASE = 500000.0
F32 = jnp.float32
BF16 = jnp.bfloat16
GROUP = ("core", "ctx")
ALL = ("chip", "core", "ctx")


PIECE = 32
LAGB = 1
LAGJ = 1
MESH_ID = pl.DeviceIdType.MESH


def row_factor(values):
    return lax.rsqrt(jnp.mean(values * values, axis=-1, keepdims=True) + EPS)


def row_norm_back(values, gain, grad):
    factor = row_factor(values)
    normed = values * factor
    scaled = gain * grad
    back = factor * (scaled - normed * jnp.mean(scaled * normed, axis=-1, keepdims=True))
    return back, jnp.sum(grad * normed, axis=0, keepdims=True)


def after_projected(total, ins, outs, rows):
    tokens, gains = ins
    residual_out, projected_out = outs
    projected_out[rows, :] = total
    gain = gains[2:3, :]
    residual = tokens[rows, :].astype(F32) + total * row_factor(total) * gain
    residual_out[rows, :] = residual
    return residual


def after_feed(total, ins, outs, rows):
    residual, cotangent, gains = ins
    output, gain_out = outs
    gain = gains[3:4, :]
    normed = total * row_factor(total) * gain
    output[rows, :] = (residual[rows, :] + normed).astype(BF16)
    back, term = row_norm_back(total, gain, cotangent[rows, :].astype(F32))
    gain_out[...] += term
    return back


def after_back(total, ins, outs, rows):
    projected, cotangent, gains = ins
    grad_out, gain_out = outs
    grad = cotangent[rows, :].astype(F32) + total
    grad_out[rows, :] = grad
    back, term = row_norm_back(projected[rows, :], gains[2:3, :], grad)
    gain_out[...] += term
    return back


def after_input(total, ins, outs, rows):
    (grad,), (result,) = ins, outs
    result[rows, :] = grad[rows, :] + total
    return None


def pass_tokens(total, ins, outs, rows):
    return ins[0][rows, :]


class Exchange:
    def __init__(self, spans, rows, width, piece, reduce, spread, row_fn, n_in, n_out, gain, extra=None):
        self.extra = extra
        self.spans, self.rows, self.width, self.piece = spans, rows, width, piece
        self.reduce, self.spread, self.row_fn = reduce, spread, row_fn
        self.n_in, self.n_out, self.gain = n_in, n_out, gain
        self.count = rows // piece

    def scratch(self):
        spans, count = self.spans, self.count
        block = pltpu.VMEM((spans * self.rows, self.width), BF16)
        sems = pltpu.SemaphoreType.DMA((spans, count))
        items = []
        if self.reduce:
            items += [block] * 4 + [pltpu.SemaphoreType.DMA] + [sems] * 6
        if self.spread:
            items += [pltpu.VMEM((2 * spans * self.rows, self.width), BF16)]
            items += [sems] * 7 + [pltpu.SemaphoreType.DMA]
        if self.extra is not None:
            items += self.extra.scratch()
        return items

    def body(self, *refs):
        spans, rows, piece, count = self.spans, self.rows, self.piece, self.count
        refs = list(refs)
        take = lambda n: [refs.pop(0) for _ in range(n)]
        partial = take(1)[0] if self.reduce else None
        ins = take(self.n_in)
        extra = self.extra
        if extra is not None:
            extra.ins = take(extra.n_in)
        outs = take(self.n_out)
        if extra is not None:
            extra.outs = take(extra.n_out)
        gathered = take(1)[0] if self.spread else None
        if self.reduce:
            own, near, from_left, from_right = take(4)
            (load_sem,) = take(1)
            near_send, near_recv, right_send, right_recv, left_send, left_recv = take(6)
        if self.spread:
            (held,) = take(1)
            fwd_send, fwd_recv, bwd_send, bwd_recv, own_send, side_send, side_recv = take(7)
            (store_sem,) = take(1)
        if extra is not None:
            extra.held = refs
        core = lax.axis_index("core")
        place = lax.axis_index("ctx")
        other = 1 - core
        has_left = place > 0
        has_right = place < spans - 1

        def at(block, k):
            return pl.ds(pl.multiple_of(block * rows + k * piece, piece), piece)

        def held_at(seq, block, k):
            return pl.ds(pl.multiple_of((seq * spans + block) * rows + k * piece, piece), piece)

        def remote(src, dst, send, recv, **device):
            return pltpu.make_async_remote_copy(
                src_ref=src, dst_ref=dst, send_sem=send, recv_sem=recv,
                device_id=device, device_id_type=MESH_ID,
            )

        barrier = pltpu.get_barrier_semaphore()
        if extra is not None:
            meet_all(spans, getattr(extra, "moves", False))
        else:
            pl.semaphore_signal(barrier, 1, device_id={"core": other}, device_id_type=MESH_ID)

            @pl.when(has_left)
            def _():
                pl.semaphore_signal(barrier, 1, device_id={"ctx": place - 1}, device_id_type=MESH_ID)

            @pl.when(has_right)
            def _():
                pl.semaphore_signal(barrier, 1, device_id={"ctx": place + 1}, device_id_type=MESH_ID)

            pl.semaphore_wait(barrier, 1 + has_left.astype(jnp.int32) + has_right.astype(jnp.int32))

        if self.gain is not None:
            outs[self.gain][...] = jnp.zeros_like(outs[self.gain])

        def near_copy(d, k):
            return remote(
                partial.at[held_at(other, d, k)], near.at[at(d, k)],
                near_send.at[d, k], near_recv.at[d, k], core=other,
            )

        def right_copy(d, k):
            return remote(
                own.at[at(d, k)], from_left.at[at(d, k)],
                right_send.at[d, k], right_recv.at[d, k], ctx=place + 1,
            )

        def left_copy(d, k):
            return remote(
                own.at[at(d, k)], from_right.at[at(d, k)],
                left_send.at[d, k], left_recv.at[d, k], ctx=place - 1,
            )

        def fwd_copy(o, k, send):
            where = held_at(core, o, k)
            return remote(held.at[where], held.at[where], send, fwd_recv.at[o, k], ctx=place + 1)

        def bwd_copy(o, k, send):
            where = held_at(core, o, k)
            return remote(held.at[where], held.at[where], send, bwd_recv.at[o, k], ctx=place - 1)

        def side_copy(o, k):
            where = held_at(core, o, k)
            return remote(held.at[where], held.at[where], side_send.at[o, k], side_recv.at[o, k], core=other)

        if extra is not None:
            extra.start()
        if self.reduce:
            load = pltpu.make_async_copy(
                partial.at[pl.ds(pl.multiple_of(core * spans * rows, rows), spans * rows)], own, load_sem
            )
            load.start()

            @pl.loop(0, count)
            def _(k):
                for j in range(spans):
                    near_copy(j, k).start()

            load.wait()

        def base(d, k):
            near_copy(d, k).wait_recv()
            return own[at(d, k), :].astype(F32) + near[at(d, k), :].astype(F32)

        def reduce_step(k):
            for j in range(spans - 1):
                right, left = spans - 1 - j, j

                @pl.when(jnp.logical_and(right > place, has_left))
                def _():
                    value = base(right, k)
                    right_copy(right, k).wait_recv()
                    own[at(right, k), :] = (value + from_left[at(right, k), :].astype(F32)).astype(BF16)
                    right_copy(right, k).start()

                @pl.when(jnp.logical_and(right > place, jnp.logical_not(has_left)))
                def _():
                    own[at(right, k), :] = base(right, k).astype(BF16)
                    right_copy(right, k).start()

                @pl.when(jnp.logical_and(left < place, has_right))
                def _():
                    value = base(left, k)
                    left_copy(left, k).wait_recv()
                    own[at(left, k), :] = (value + from_right[at(left, k), :].astype(F32)).astype(BF16)
                    left_copy(left, k).start()

                @pl.when(jnp.logical_and(left < place, jnp.logical_not(has_right)))
                def _():
                    own[at(left, k), :] = base(left, k).astype(BF16)
                    left_copy(left, k).start()

        def finish_step(k):
            total = None
            if self.reduce:
                total = base(place, k)

                @pl.when(has_left)
                def _():
                    right_copy(place, k).wait_recv()

                @pl.when(has_right)
                def _():
                    left_copy(place, k).wait_recv()

                zero = jnp.zeros_like(total)
                total = total + jnp.where(has_left, from_left[at(place, k), :].astype(F32), zero)
                total = total + jnp.where(has_right, from_right[at(place, k), :].astype(F32), zero)
            own_rows = pl.ds(pl.multiple_of(k * piece, piece), piece)
            result = self.row_fn(total, ins, outs, own_rows)
            if self.spread:
                held[held_at(core, place, k), :] = result.astype(BF16)

                @pl.when(has_right)
                def _():
                    fwd_copy(place, k, fwd_send.at[place, k]).start()

                @pl.when(has_left)
                def _():
                    bwd_copy(place, k, bwd_send.at[place, k]).start()

                side_copy(place, k).start()

        def relay_step(k, j):
            if True:

                @pl.when(place - j >= 0)
                def _():
                    fwd_copy(place - j, k, fwd_send.at[place - j, k]).wait_recv()

                    @pl.when(has_right)
                    def _():
                        fwd_copy(place - j, k, fwd_send.at[place - j, k]).start()

                    side_copy(place - j, k).start()

                @pl.when(place + j < spans)
                def _():
                    bwd_copy(place + j, k, bwd_send.at[place + j, k]).wait_recv()

                    @pl.when(has_left)
                    def _():
                        bwd_copy(place + j, k, bwd_send.at[place + j, k]).start()

                    side_copy(place + j, k).start()

        lag = LAGB if self.reduce else 0

        @pl.loop(0, count + lag + (LAGJ * (spans - 1) if self.spread else 0))
        def _(t):
            if self.reduce:

                @pl.when(t < count)
                def _():
                    reduce_step(t)

            if self.reduce:

                @pl.when(jnp.logical_and(t >= lag, t < count + lag))
                def _():
                    finish_step(t - lag)
            else:

                @pl.when(t == 0)
                def _():
                    for k in range(count):
                        finish_step(k)

            if self.spread:
                for j in range(1, spans):
                    after = t - lag - j * LAGJ

                    @pl.when(jnp.logical_and(after >= 0, after < count))
                    def _():
                        relay_step(after, j)
            if extra is not None:
                extra.tick(t)

        if extra is not None:
            extra.finish(count + lag + (LAGJ * (spans - 1) if self.spread else 0))
        if self.spread:

            @pl.loop(0, count)
            def _(k):
                for o in range(spans):
                    side_copy(o, k).wait_recv()

            store = pltpu.make_async_copy(held, gathered, store_sem)
            store.start()

        @pl.loop(0, count)
        def _(k):
            for d in range(spans):
                if self.reduce:
                    near_copy(d, k).wait_send()

                    @pl.when(d > place)
                    def _():
                        right_copy(d, k).wait_send()

                    @pl.when(d < place)
                    def _():
                        left_copy(d, k).wait_send()

                if self.spread:
                    side_copy(d, k).wait_send()

                    @pl.when(jnp.logical_and(d <= place, has_right))
                    def _():
                        fwd_copy(d, k, fwd_send.at[d, k]).wait_send()

                    @pl.when(jnp.logical_and(d >= place, has_left))
                    def _():
                        bwd_copy(d, k, bwd_send.at[d, k]).wait_send()

        if self.spread:
            store.wait()

    def call(self, name, collective_id, partial, ins, outs):
        vmem = pl.BlockSpec(memory_space=pltpu.VMEM)
        hbm = pl.BlockSpec(memory_space=pl.ANY)
        operands = ([partial] if self.reduce else []) + list(ins)
        in_specs = ([hbm] if self.reduce else []) + [vmem] * len(ins)
        shapes = list(outs)
        specs = [vmem] * len(outs)
        if self.extra is not None:
            operands += self.extra.operands
            in_specs += self.extra.in_specs
            shapes += self.extra.out_shapes
            specs += self.extra.out_specs
        if self.spread:
            shapes.append(jax.ShapeDtypeStruct((2 * self.spans * self.rows, self.width), BF16))
            specs.append(hbm)
        return pl.pallas_call(
            self.body,
            out_shape=shapes,
            in_specs=in_specs,
            out_specs=specs,
            scratch_shapes=self.scratch(),
            compiler_params=pltpu.CompilerParams(
                collective_id=collective_id, has_side_effects=True, vmem_limit_bytes=48 << 20
            ),
            cost_estimate=pl.CostEstimate(
                flops=0,
                bytes_accessed=(50 if self.reduce else 30) * self.width * self.width,
                transcendentals=0,
            ),
            name=name,
        )(*operands)


def owner_of(chip, core, place, spans):
    member = core * spans + place
    return member // 2, lax.rem(member, 2), chip


def summer_of(chip, core, place, spans):
    member = chip * 2 + core
    return place, member // spans, lax.rem(member, spans)


def stays(chip, core, place, spans):
    to_chip, to_core, to_place = owner_of(chip, core, place, spans)
    return jnp.logical_and(to_chip == chip, jnp.logical_and(to_core == core, to_place == place))


def meet_all(spans, moves):
    chips = lax.axis_size("chip")
    barrier = pltpu.get_barrier_semaphore()
    chip = lax.axis_index("chip")
    core = lax.axis_index("core")
    place = lax.axis_index("ctx")
    for s in range(1, chips):
        pl.semaphore_signal(
            barrier, 1, device_id={"chip": lax.rem(chip + s, chips)}, device_id_type=MESH_ID
        )
    for s in range(1, 2 * spans):
        to_core, to_place = step_member(core, place, s, spans)
        pl.semaphore_signal(
            barrier, 1, device_id={"core": to_core, "ctx": to_place}, device_id_type=MESH_ID
        )
    count = chips - 1 + 2 * spans - 1
    if moves:
        away = jnp.logical_not(stays(chip, core, place, spans))

        @pl.when(away)
        def _():
            for find in (owner_of, summer_of):
                to_chip, to_core, to_place = find(chip, core, place, spans)
                pl.semaphore_signal(
                    barrier, 1, device_id={"chip": to_chip, "core": to_core, "ctx": to_place}, device_id_type=MESH_ID
                )

        count = count + 2 * away.astype(jnp.int32)
    pl.semaphore_wait(barrier, count)


def step_member(core, place, s, spans):
    return lax.rem(core + s % 2, 2), lax.rem(place + s // 2, spans)


def meet_other_core():
    barrier = pltpu.get_barrier_semaphore()
    other = 1 - lax.axis_index("core")
    pl.semaphore_signal(barrier, 1, device_id={"core": other}, device_id_type=MESH_ID)
    pl.semaphore_wait(barrier, 1)


def split_body(gate, up, down, gate_up_out, down_out, held, load_sem, store_sem, send_sem, recv_sem):
    core = lax.axis_index("core")
    other = 1 - core
    rows, width = gate.shape
    half = width // 2
    where = pl.ds(pl.multiple_of(core * rows, rows), rows)
    places = [gate_up_out.at[where, :half], gate_up_out.at[where, half:], down_out.at[where, :]]
    mine = pl.ds(pl.multiple_of(core * half, half), half)
    theirs = pl.ds(pl.multiple_of(other * half, half), half)
    loads = [
        pltpu.make_async_copy(a.at[:, mine], held.at[i], load_sem.at[i]) for i, a in enumerate((gate, up, down))
    ]
    for load in loads:
        load.start()
    meet_other_core()
    sends = [
        pltpu.make_async_remote_copy(
            src_ref=a.at[:, theirs], dst_ref=places[i], send_sem=send_sem.at[i], recv_sem=recv_sem.at[i],
            device_id={"core": other}, device_id_type=MESH_ID,
        )
        for i, a in enumerate((gate, up, down))
    ]
    for send in sends:
        send.start()
    stores = [pltpu.make_async_copy(held.at[i], places[i], store_sem.at[i]) for i in range(3)]
    for load, store in zip(loads, stores):
        load.wait()
        store.start()
    for store, send in zip(stores, sends):
        store.wait()
        send.wait()


def split_columns(gate, up, down):
    rows, width = gate.shape
    hbm = pl.BlockSpec(memory_space=pl.ANY)
    three = pltpu.SemaphoreType.DMA((3,))
    return pl.pallas_call(
        split_body,
        out_shape=[
            jax.ShapeDtypeStruct((2 * rows, width), BF16),
            jax.ShapeDtypeStruct((2 * rows, width // 2), BF16),
        ],
        in_specs=[hbm] * 3,
        out_specs=[hbm] * 2,
        scratch_shapes=[pltpu.VMEM((3, rows, width // 2), BF16)] + [three] * 4,
        compiler_params=pltpu.CompilerParams(collective_id=6, has_side_effects=True, vmem_limit_bytes=8 << 20),
        name="split_columns",
    )(gate, up, down)


def join_body(gate, up, down, gate_out, up_out, down_out, arrived, send_sem, recv_sem):
    core = lax.axis_index("core")
    other = 1 - core
    rows, width = gate_out.shape
    half = width // 2
    meet_other_core()
    theirs = pl.ds(pl.multiple_of(other * rows, rows), rows)
    pairs = ((gate, gate_out), (up, up_out), (down, down_out))
    sends = [
        pltpu.make_async_remote_copy(
            src_ref=a.at[theirs], dst_ref=arrived.at[i], send_sem=send_sem.at[i], recv_sem=recv_sem.at[i],
            device_id={"core": other}, device_id_type=MESH_ID,
        )
        for i, (a, _) in enumerate(pairs)
    ]
    for send in sends:
        send.start()
    mine = pl.ds(pl.multiple_of(core * half, half), half)
    far = pl.ds(pl.multiple_of(other * half, half), half)
    step = 16

    def rows_at(i, base):
        return pl.ds(pl.multiple_of(base + i * step, step), step)

    @pl.loop(0, rows // step)
    def _(i):
        for a, b in pairs:
            b[rows_at(i, 0), mine] = a[rows_at(i, core * rows), :].astype(F32)

    for send in sends:
        send.wait()

    @pl.loop(0, rows // step)
    def _(i):
        for n, (_, b) in enumerate(pairs):
            b[rows_at(i, 0), far] = arrived[n, rows_at(i, 0), :].astype(F32)


def join_columns(gate, up, down):
    rows, half = gate.shape[0] // 2, gate.shape[1]
    vmem = pl.BlockSpec(memory_space=pltpu.VMEM)
    three = pltpu.SemaphoreType.DMA((3,))
    return pl.pallas_call(
        join_body,
        out_shape=[jax.ShapeDtypeStruct((rows, 2 * half), F32)] * 3,
        in_specs=[vmem] * 3,
        out_specs=[vmem] * 3,
        scratch_shapes=[pltpu.VMEM((3, rows, half), BF16), three, three],
        compiler_params=pltpu.CompilerParams(collective_id=7, has_side_effects=True, vmem_limit_bytes=32 << 20),
        name="join_columns",
    )(gate, up, down)


class Extra:
    def remote(self, src, dst, send, recv, **device):
        return pltpu.make_async_remote_copy(
            src_ref=src, dst_ref=dst, send_sem=send, recv_sem=recv,
            device_id=device, device_id_type=MESH_ID,
        )

    def locate(self):
        self.chip = lax.axis_index("chip")
        self.core = lax.axis_index("core")
        self.place = lax.axis_index("ctx")
        self.me = self.core * self.spans + self.place


class QkvWeights(Extra):
    n_in, n_out = 2, 2

    def __init__(self, spans, chips, cut, ids):
        self.spans, self.chips = spans, chips
        self.members, self.block, self.columns = cut.shape
        self.operands = [cut, ids]
        self.ids_shape = ids.shape
        vmem = pl.BlockSpec(memory_space=pltpu.VMEM)
        self.in_specs = [vmem, vmem]
        self.out_shapes = [
            jax.ShapeDtypeStruct((chips * self.members * self.block, self.columns), BF16),
            jax.ShapeDtypeStruct((self.members * ids.shape[0], ids.shape[1]), jnp.int32),
        ]
        self.out_specs = [vmem, vmem]

    def scratch(self):
        rows = self.chips * self.members * self.block
        sems = pltpu.SemaphoreType.DMA((self.members,))
        cross = pltpu.SemaphoreType.DMA((self.chips, self.members))
        ids = (self.members * self.ids_shape[0], self.ids_shape[1])
        return [pltpu.VMEM((rows, self.columns), BF16), pltpu.VMEM(ids, jnp.int32)] + [sems] * 4 + [cross] * 2

    def at(self, chip, m):
        return pl.ds(pl.multiple_of((chip * self.members + m) * self.block, self.block), self.block)

    def ids_at(self, m):
        return pl.ds(pl.multiple_of(m * self.ids_shape[0], self.ids_shape[0]), self.ids_shape[0])

    def block_copy(self, s):
        full, _, send, recv = self.held[:4]
        core, place = step_member(self.core, self.place, s, self.spans)
        return self.remote(
            self.ins[0].at[core * self.spans + place], full.at[self.at(self.chip, self.me)],
            send.at[s], recv.at[s], core=core, ctx=place,
        )

    def ids_copy(self, s):
        all_ids, send, recv = self.held[1], self.held[4], self.held[5]
        core, place = step_member(self.core, self.place, s, self.spans)
        return self.remote(
            self.ins[1], all_ids.at[self.ids_at(self.me)], send.at[s], recv.at[s], core=core, ctx=place
        )

    def source(self, s):
        core = lax.rem(self.core + s % 2, 2)
        return core * self.spans + lax.rem(self.place + self.spans - s // 2, self.spans)

    def chip_copy(self, s, m):
        full, _, _, _, _, _, send, recv = self.held
        where = self.at(self.chip, m)
        return self.remote(
            full.at[where], full.at[where], send.at[s, m], recv.at[s, m], chip=lax.rem(self.chip + s, self.chips)
        )

    def start(self):
        self.locate()
        cut, ids = self.ins
        full, all_ids = self.held[:2]
        for s in range(1, self.members):
            self.block_copy(s).start()
        for s in range(1, self.members):
            self.ids_copy(s).start()
        full[self.at(self.chip, self.me), :] = cut[self.me]
        all_ids[self.ids_at(self.me), :] = ids[...]

    def send_block(self, s):
        m = self.me if s == 0 else self.source(s)
        if s > 0:
            self.block_copy(s).wait_recv()
        for step in range(1, self.chips):
            self.chip_copy(step, m).start()

    def tick(self, t):
        @pl.when(t == 0)
        def _():
            for s in range(self.members):
                self.send_block(s)

    def finish(self, ticks):
        full, all_ids = self.held[:2]
        for s in range(1, self.members):
            self.ids_copy(s).wait_recv()
            self.block_copy(s).wait_send()
            self.ids_copy(s).wait_send()

        @pl.loop(0, self.members)
        def _(m):
            for s in range(1, self.chips):
                self.chip_copy(s, m).wait()

        self.outs[0][...] = full[...]
        self.outs[1][...] = all_ids[...]


class QkvGrads(Extra):
    n_in, n_out = 3, 3
    moves = True

    def __init__(self, spans, chips, members, grads, sums, out_grads):
        self.spans, self.chips, self.members = spans, chips, members
        self.out_rows = out_grads.shape[0] // chips
        self.block, self.columns = grads.shape[0] // (chips * members), grads.shape[1]
        self.part = self.columns // 3
        self.width = self.part * members
        self.own_rows = self.part // 128
        self.sum_rows = sums.shape[0]
        self.operands = [grads, sums, out_grads]
        vmem = pl.BlockSpec(memory_space=pltpu.VMEM)
        self.in_specs = [vmem] * 3
        self.out_shapes = [
            jax.ShapeDtypeStruct((self.block, 3 * self.width), F32),
            jax.ShapeDtypeStruct((4, self.width // 128, 128), F32),
            jax.ShapeDtypeStruct((self.out_rows, self.width), F32),
        ]
        self.out_specs = [vmem] * 3

    def scratch(self):
        sems = pltpu.SemaphoreType.DMA((self.members,))
        chip_sems = pltpu.SemaphoreType.DMA((self.chips,))
        cross = pltpu.SemaphoreType.DMA((self.chips, self.members))
        return [
            pltpu.VMEM((self.chips, self.members, self.block, self.columns), BF16),
            pltpu.VMEM((self.members, self.block, self.columns), BF16),
            pltpu.VMEM((self.members, self.block, self.columns), BF16),
            pltpu.VMEM((self.chips, self.sum_rows, 128), F32),
            pltpu.VMEM((self.sum_rows, 128), F32),
            pltpu.VMEM((self.members, self.sum_rows, 128), F32),
            pltpu.VMEM((self.chips, self.out_rows, self.width), BF16),
            pltpu.VMEM((self.out_rows, self.width), BF16),
            pltpu.VMEM((self.out_rows, self.width), BF16),
        ] + [cross] * 2 + [sems] * 2 + [chip_sems] * 2 + [sems] * 2 + [chip_sems] * 2 + [pltpu.SemaphoreType.DMA] * 2

    def at(self, chip, m):
        return pl.ds(pl.multiple_of((chip * self.members + m) * self.block, self.block), self.block)

    def chip_copy(self, s, m):
        other = lax.rem(self.chip + s, self.chips)
        return self.remote(
            self.ins[0].at[self.at(other, m)], self.arrived.at[s, m],
            self.cross_send.at[s, m], self.cross_recv.at[s, m], chip=other,
        )

    def member_copy(self, s):
        core, place = step_member(self.core, self.place, s, self.spans)
        return self.remote(
            self.summed.at[core * self.spans + place], self.columns_in.at[self.me],
            self.member_send.at[s], self.member_recv.at[s], core=core, ctx=place,
        )

    def sums_chip(self, s):
        return self.remote(
            self.ins[1], self.sums_in.at[s], self.sums_send.at[s], self.sums_recv.at[s],
            chip=lax.rem(self.chip + s, self.chips),
        )

    def sums_member(self, s):
        core, place = step_member(self.core, self.place, s, self.spans)
        return self.remote(
            self.sums_chips, self.sums_members.at[self.me], self.last_send.at[s], self.last_recv.at[s],
            core=core, ctx=place,
        )

    def out_copy(self, s):
        other = lax.rem(self.chip + s, self.chips)
        rows = pl.ds(pl.multiple_of(other * self.out_rows, self.out_rows), self.out_rows)
        return self.remote(
            self.ins[2].at[rows], self.out_in.at[s], self.out_send.at[s], self.out_recv.at[s], chip=other
        )

    def move_copy(self):
        chip, core, place = owner_of(self.chip, self.core, self.place, self.spans)
        return self.remote(
            self.out_sum, self.out_final, self.move_send, self.move_recv, chip=chip, core=core, ctx=place
        )

    def start(self):
        self.locate()
        (
            self.arrived, self.summed, self.columns_in, self.sums_in, self.sums_chips, self.sums_members,
            self.out_in, self.out_sum, self.out_final,
            self.cross_send, self.cross_recv, self.member_send, self.member_recv,
            self.sums_send, self.sums_recv, self.last_send, self.last_recv,
            self.out_send, self.out_recv, self.move_send, self.move_recv,
        ) = self.held
        for s in range(1, self.chips):
            self.sums_chip(s).start()
            self.out_copy(s).start()

        @pl.loop(0, self.members)
        def _(i):
            m = lax.rem(self.me + 1 + i, self.members)
            for s in range(1, self.chips):
                self.chip_copy(s, m).start()

    def add_block(self, m):
        total = self.ins[0][self.at(self.chip, m), :].astype(F32)
        for s in range(1, self.chips):
            self.chip_copy(s, m).wait_recv()
            total = total + self.arrived[s, m].astype(F32)
        self.summed[m] = total.astype(BF16)

    def send_blocks(self, first, last):
        for s in range(first, last):
            core, place = step_member(self.core, self.place, s, self.spans)
            self.add_block(core * self.spans + place)
            self.member_copy(s).start()

    def tick(self, t):
        @pl.when(t == 1)
        def _():
            total = self.ins[1][...]
            for s in range(1, self.chips):
                self.sums_chip(s).wait_recv()
                total = total + self.sums_in[s]
            self.sums_chips[...] = total
            self.sums_members[self.me] = total
            for s in range(1, self.members):
                self.sums_member(s).start()

        @pl.when(t == 2)
        def _():
            rows = pl.ds(pl.multiple_of(self.chip * self.out_rows, self.out_rows), self.out_rows)
            total = self.ins[2][rows, :].astype(F32)
            for s in range(1, self.chips):
                self.out_copy(s).wait_recv()
                total = total + self.out_in[s].astype(F32)
            self.out_sum[...] = total.astype(BF16)

            @pl.when(stays(self.chip, self.core, self.place, self.spans))
            def _():
                self.out_final[...] = total.astype(BF16)

            @pl.when(jnp.logical_not(stays(self.chip, self.core, self.place, self.spans)))
            def _():
                self.move_copy().start()

    def finish(self, ticks):
        self.send_blocks(1, self.members)
        self.add_block(self.me)
        self.columns_in[self.me] = self.summed[self.me]
        for s in range(1, self.members):
            self.sums_member(s).wait()
        wide = self.width // 128
        for i in range(2):
            total = self.sums_members[0, i * wide : (i + 1) * wide, :]
            for m in range(1, self.members):
                total = total + self.sums_members[m, i * wide : (i + 1) * wide, :]
            self.outs[1][2 + i] = total
            base = 2 * wide + i * self.own_rows
            for m in range(self.members):
                self.outs[1][i, m * self.own_rows : (m + 1) * self.own_rows, :] = self.sums_members[
                    m, base : base + self.own_rows, :
                ]
        for s in range(1, self.members):
            self.member_copy(s).wait()
        for m in range(self.members):
            for i in range(3):
                self.outs[0][:, i * self.width + m * self.part : i * self.width + (m + 1) * self.part] = (
                    self.columns_in[m, :, i * self.part : (i + 1) * self.part].astype(F32)
                )
        @pl.when(jnp.logical_not(stays(self.chip, self.core, self.place, self.spans)))
        def _():
            self.move_copy().wait()

        self.outs[2][...] = self.out_final[...].astype(F32)
        for s in range(1, self.chips):
            self.sums_chip(s).wait_send()
            self.out_copy(s).wait_send()

        @pl.loop(0, self.members)
        def _(m):
            for s in range(1, self.chips):
                self.chip_copy(s, m).wait_send()


def rope_tables(positions):
    half = HEAD_DIM // 2
    frequency = ROPE_BASE ** (-(jnp.arange(half, dtype=F32) * 2.0 / HEAD_DIM))
    angles = positions[:, None] * frequency[None, :]
    cosine = jnp.cos(angles)
    sine = jnp.sin(angles)
    return (jnp.concatenate([cosine, cosine], 1), jnp.concatenate([sine, sine], 1))


def dot(left, right):
    return jnp.dot(left, right, preferred_element_type=F32)


def dot_rows(left, right):
    return lax.dot_general(left, right, (((1,), (1,)), ((), ())), preferred_element_type=F32)


def dot_first(left, right):
    return lax.dot_general(left, right, (((0,), (0,)), ((), ())), preferred_element_type=F32)


def gather(values, axes):
    return lax.all_gather(values, axes, axis=0, tiled=True)


def scatter_sum(values, axes):
    return lax.psum_scatter(values, axes, scatter_dimension=0, tiled=True)


FF_TILE = 512
SUM_TILE = 1024
BATCH_PIECE = 16
GRAD_TILE = 256


def square(chip):
    along_x = chip + 1 - 2 * lax.rem(chip, 2)
    return along_x, lax.rem(chip + 2, 4), lax.rem(along_x + 2, 4)


class SquareSum:
    def __init__(self, chip, block, landing, send, recv):
        self.chip, self.block, self.landing, self.send, self.recv = chip, block, landing, send, recv
        self.x, self.y, self.across = square(chip)

    def copy(self, i):
        owner = (self.across, self.across, self.x, self.y, self.y, self.x)[i]
        half = (0, 1, 0, 1, 0, 1)[i]
        to = (self.x, self.y, self.x, self.y, self.y, self.x)[i]
        return pltpu.make_async_remote_copy(
            src_ref=self.block(owner, half), dst_ref=self.landing.at[i], send_sem=self.send.at[i],
            recv_sem=self.recv.at[i], device_id={"chip": to}, device_id_type=MESH_ID,
        )

    def begin(self, first):
        self.copy(first).start()
        self.copy(first + 1).start()

    def relay(self):
        for i, owner, half in ((0, self.y, 0), (1, self.x, 1)):
            self.copy(i).wait_recv()
            ref = self.block(owner, half)
            ref[...] = (ref[...].astype(F32) + self.landing[i].astype(F32)).astype(BF16)
        self.begin(4)

    def finish(self, half):
        for i in (2 + half, 4 + half):
            self.copy(i).wait_recv()
        for i in (0 + half, 2 + half, 4 + half):
            self.copy(i).wait_send()
        total = self.block(self.chip, half)[...].astype(F32)
        return total + self.landing[2 + half].astype(F32) + self.landing[4 + half].astype(F32)


class Middle:
    def __init__(self, spans, rows, width, hidden, piece):
        self.spans, self.rows, self.width, self.hidden, self.piece = spans, rows, width, hidden, piece
        self.count = rows // piece
        self.block = spans * piece
        self.batch = 2 * self.block

    def body(
        self, chips, partial, tokens, cotangent, gains, gate_up_w, down,
        output, residual_grad, gain_feed, gain_attn, down_sum, gate_sum, residual_all, feed_grad_all, gate_part, up_part, projected_all,
        residual, projected, own, near, from_left, from_right, held, wide, act, back, up_weights, down_weights, slices, given, landed,
        load_sem, weight_sem, store_sem, slice_sem, part_sem, free_sem, near_send, near_recv, right_send, right_recv, left_send, left_recv,
        fwd_send, fwd_recv, bwd_send, bwd_recv, side_send, side_recv, down_send, down_recv, give_send, give_recv, take_send, take_recv,
    ):
        spans, rows, piece, count = self.spans, self.rows, self.piece, self.count
        width, hidden, block, batch = self.width, self.hidden, self.block, self.batch
        core = lax.axis_index("core")
        place = lax.axis_index("ctx")
        other = 1 - core
        last = spans - 1
        has_left = place > 0
        has_right = place < last

        def turn_of(o):
            return jnp.maximum(o, last - o)

        def at(d, k):
            return pl.ds(pl.multiple_of((k * spans + d) * piece, piece), piece)

        def at_seq(seq, d, k):
            return pl.ds(pl.multiple_of(((k * 2 + seq) * spans + d) * piece, piece), piece)

        def batch_at(k):
            return pl.ds(pl.multiple_of(k * batch, batch), batch)

        def natural(seq, d, k):
            return pl.ds(pl.multiple_of((seq * spans + d) * rows + k * piece, piece), piece)

        def remote(src, dst, send, recv, **device):
            return pltpu.make_async_remote_copy(
                src_ref=src, dst_ref=dst, send_sem=send, recv_sem=recv, device_id=device, device_id_type=MESH_ID
            )

        barrier = pltpu.get_barrier_semaphore()
        pl.semaphore_signal(barrier, 1, device_id={"core": other}, device_id_type=MESH_ID)

        @pl.when(has_left)
        def _():
            pl.semaphore_signal(barrier, 1, device_id={"ctx": place - 1}, device_id_type=MESH_ID)

        @pl.when(has_right)
        def _():
            pl.semaphore_signal(barrier, 1, device_id={"ctx": place + 1}, device_id_type=MESH_ID)

        def near_copy(e, d, k):
            src = partial.at[natural(other, d, k)] if e == 0 else own.at[at_seq(other, d, k)]
            return remote(src, near.at[at(d, k)], near_send.at[d, k], near_recv.at[d, k], core=other)

        def right_copy(d, k):
            return remote(
                own.at[at_seq(core, d, k)], from_left.at[at(d, k)], right_send.at[d, k], right_recv.at[d, k],
                ctx=place + 1,
            )

        def left_copy(d, k):
            return remote(
                own.at[at_seq(core, d, k)], from_right.at[at(d, k)], left_send.at[d, k], left_recv.at[d, k],
                ctx=place - 1,
            )

        def spread_copy(o, k, send, recv, **device):
            where = held.at[at_seq(core, o, k)]
            return remote(where, where, send.at[o, k], recv.at[o, k], **device)

        def fwd_copy(o, k):
            return spread_copy(o, k, fwd_send, fwd_recv, ctx=place + 1)

        def bwd_copy(o, k):
            return spread_copy(o, k, bwd_send, bwd_recv, ctx=place - 1)

        def side_copy(o, k):
            return spread_copy(o, k, side_send, side_recv, core=other)

        def load_own(d, k):
            return pltpu.make_async_copy(
                partial.at[natural(core, d, k)], own.at[at_seq(core, d, k)], load_sem.at[d, k]
            )

        @pl.loop(0, count)
        def _(k):
            for d in range(spans):
                load_own(d, k).start()

        load_up = pltpu.make_async_copy(gate_up_w, up_weights, weight_sem.at[0])
        chip = lax.axis_index("chip")
        shard = down.shape[0]
        here = pl.ds(pl.multiple_of(chip * shard, shard), shard)
        load_down = pltpu.make_async_copy(down, down_weights.at[here], weight_sem.at[1])

        if chips == 4:
            along_x, along_y, across = square(chip)

        def down_copy(s):
            if chips != 4:
                return remote(
                    down, down_weights.at[here], down_send.at[s], down_recv.at[s], chip=lax.rem(chip + s, chips)
                )
            half = (0, 1, 1, 0, 0, 1)[s]
            to = (along_x, along_y, along_x, along_y, along_y, along_x)[s]
            size = shard // 2
            if s < 4:
                src = down.at[half * size : (half + 1) * size]
                at_chip = chip
            else:
                at_chip = (along_x, along_y)[s - 4]
            dst = down_weights.at[pl.ds(pl.multiple_of(at_chip * shard + half * size, size), size)]
            return remote(src if s < 4 else dst, dst, down_send.at[s], down_recv.at[s], chip=to)

        def relay_down():
            for s in range(2):
                down_copy(s).wait_recv()
                down_copy(4 + s).start()

        load_up.start()
        load_down.start()
        gain_feed[...] = jnp.zeros_like(gain_feed)
        gain_attn[...] = jnp.zeros_like(gain_attn)
        for s in range(1, chips):
            pl.semaphore_signal(
                barrier, 1, device_id={"chip": lax.rem(chip + s, chips)}, device_id_type=MESH_ID
            )
        pl.semaphore_wait(barrier, chips + has_left.astype(jnp.int32) + has_right.astype(jnp.int32))
        for s in range(4) if chips == 4 else range(1, chips):
            down_copy(s).start()

        @pl.loop(0, count)
        def _(k):
            for d in range(spans):
                near_copy(0, d, k).start()

        def base(e, d, k):
            near_copy(e, d, k).wait_recv()
            if e == 0:
                load_own(d, k).wait()
            return own[at_seq(core, d, k), :].astype(F32) + near[at(d, k), :].astype(F32)

        def pass_on(e, d, k, arrived, copy, later):
            value = base(e, d, k)

            @pl.when(later)
            def _():
                copy(d, k).wait_recv()

            before = arrived[at(d, k), :].astype(F32)
            value = value + jnp.where(later, before, jnp.zeros_like(before))
            own[at_seq(core, d, k), :] = value.astype(BF16)
            copy(d, k).start()

        def pass_right(e, k):
            for d in range(last, 0, -1):

                @pl.when(d > place)
                def _():
                    pass_on(e, d, k, from_left, right_copy, has_left)

        def pass_left(e, k):
            for d in range(last):

                @pl.when(d < place)
                def _():
                    pass_on(e, d, k, from_right, left_copy, has_right)

        def finish(e, k):
            total = base(e, place, k)

            @pl.when(has_left)
            def _():
                right_copy(place, k).wait_recv()

            @pl.when(has_right)
            def _():
                left_copy(place, k).wait_recv()

            zero = jnp.zeros_like(total)
            total = total + jnp.where(has_left, from_left[at(place, k), :].astype(F32), zero)
            total = total + jnp.where(has_right, from_right[at(place, k), :].astype(F32), zero)
            mine = pl.ds(pl.multiple_of(k * piece, piece), piece)
            if e == 0:
                result = after_projected(total, (tokens, gains), (residual, projected), mine)
            elif e == 1:
                result = after_feed(total, (residual, cotangent, gains), (output, gain_feed), mine)
            else:
                result = after_back(total, (projected, cotangent, gains), (residual_grad, gain_attn), mine)
            held[at_seq(core, place, k), :] = result.astype(BF16)

            @pl.when(has_right)
            def _():
                fwd_copy(place, k).start()

            @pl.when(has_left)
            def _():
                bwd_copy(place, k).start()

            side_copy(place, k).start()

        def relay_right(o, k):
            fwd_copy(o, k).wait_recv()

            @pl.when(has_right)
            def _():
                fwd_copy(o, k).start()

            side_copy(o, k).start()

        def relay_left(o, k):
            bwd_copy(o, k).wait_recv()

            @pl.when(has_left)
            def _():
                bwd_copy(o, k).start()

            side_copy(o, k).start()

        def gathered(k):
            for o in range(spans):
                side_copy(o, k).wait_recv()

        def sums_sent(e, k):
            for d in range(spans):
                near_copy(e, d, k).wait_send()

                @pl.when(d > place)
                def _():
                    right_copy(d, k).wait_send()

                @pl.when(d < place)
                def _():
                    left_copy(d, k).wait_send()

        def spread_sent(k):
            for o in range(spans):
                side_copy(o, k).wait_send()

                @pl.when(jnp.logical_and(o <= place, has_right))
                def _():
                    fwd_copy(o, k).wait_send()

                @pl.when(jnp.logical_and(o >= place, has_left))
                def _():
                    bwd_copy(o, k).wait_send()

        def store(src, dst, k, sem):
            return pltpu.make_async_copy(src, dst.at[batch_at(k)], sem)

        def forward(k):
            @pl.when(k == 0)
            def _():
                load_up.wait()
                load_down.wait()
                for s in range(1, chips) if chips != 4 else range(6):
                    down_copy(s).wait_send()
                    if chips != 4 or s >= 2:
                        down_copy(s).wait_recv()

            gathered(k)
            keep = store(held.at[batch_at(k)], residual_all, k, store_sem.at[0])
            keep.start()

            @pl.loop(0, hidden // FF_TILE)
            def _(n):
                low = pl.ds(pl.multiple_of(n * FF_TILE, FF_TILE), FF_TILE)
                high = pl.ds(pl.multiple_of(hidden + n * FF_TILE, FF_TILE), FF_TILE)
                gate = dot(held[batch_at(k), :], up_weights[:, low])
                up = dot(held[batch_at(k), :], up_weights[:, high])
                wide[batch_at(k), low] = gate
                wide[batch_at(k), high] = up
                act[batch_at(k), low] = (gate * (1.0 / (1.0 + jnp.exp(-gate))) * up).astype(BF16)

            sums_sent(0, k)

            @pl.loop(0, width // SUM_TILE)
            def _(n):
                columns = pl.ds(pl.multiple_of(n * SUM_TILE, SUM_TILE), SUM_TILE)
                own[batch_at(k), columns] = dot_rows(act[batch_at(k), :], down_weights[columns, :]).astype(BF16)

            keep.wait()
            spread_sent(k)
            for d in range(spans):
                near_copy(1, d, k).start()

        down_tiles = width // GRAD_TILE
        per_chip = shard // GRAD_TILE

        def tile_rows(n):
            return pl.ds(pl.multiple_of(n * GRAD_TILE, GRAD_TILE), GRAD_TILE)

        if chips == 4:
            assert per_chip == 2
            turns = [(across, 0), (across, 1), (along_x, 0), (along_y, 1), (along_y, 0), (along_x, 1), (chip, 0), (chip, 1)]
            order = [owner * per_chip + half for owner, half in turns]
        else:
            order = [lax.rem(chip + 1 + j // per_chip, chips) * per_chip + j % per_chip for j in range(down_tiles)]
        tiles = [(m, order[j] if m < 2 else j) for m in range(3) for j in range(down_tiles)]

        def load_slice(j):
            m, n = tiles[j]
            source = feed_grad_all if m == 0 else residual_all
            return pltpu.make_async_copy(source.at[:, tile_rows(n)], slices.at[j % 4], slice_sem.at[j % 4])

        def half_at(owner, half):
            return pl.ds(pl.multiple_of((owner * per_chip + half) * GRAD_TILE, GRAD_TILE), GRAD_TILE)

        if chips == 4:
            sums = [
                SquareSum(
                    chip, lambda owner, half: given.at[half_at(owner, half)], landed.at[0], give_send, give_recv
                ),
                SquareSum(
                    chip, lambda owner, half: up_weights.at[half_at(owner, half), :hidden], landed.at[1], take_send, take_recv
                ),
            ]

        def give_copy(s):
            theirs = pl.ds(pl.multiple_of(lax.rem(chip + s, chips) * shard, shard), shard)
            return remote(
                given.at[theirs], down_weights.at[s * shard : (s + 1) * shard], give_send.at[s], give_recv.at[s],
                chip=lax.rem(chip + s, chips),
            )

        def part_copy(n, m):
            half = slice((m - 1) * hidden, m * hidden)
            return pltpu.make_async_copy(
                up_weights.at[tile_rows(n), half], (gate_part, up_part)[m - 1].at[tile_rows(n)], part_sem.at[m - 1, n]
            )

        def work_out(j):
            if j + 2 < len(tiles):
                load_slice(j + 2).start()
            load_slice(j).wait()
            m, n = tiles[j]
            if m == 0:
                given[tile_rows(n), :] = dot_first(slices[j % 4], act[...]).astype(BF16)
            else:
                half = slice((m - 1) * hidden, m * hidden)
                up_weights[tile_rows(n), half] = dot_first(slices[j % 4], back[:, half]).astype(BF16)

        def weight_grads(q):
            if chips == 4:
                m, r = q // 4, q % 4
                if m < 2:
                    for j in range(m * down_tiles + 2 * r, m * down_tiles + 2 * r + 2):
                        work_out(j)
                    if r < 2:
                        sums[m].begin(2 * r)
                    elif r == 2:
                        sums[m].relay()
                else:
                    for j in range(2 * down_tiles, 3 * down_tiles):
                        work_out(j)
                        part_copy(tiles[j][1], 2).start()
                return
            if q < chips:
                for j in range(q * per_chip, (q + 1) * per_chip):
                    work_out(j)
                if q == 0:
                    pl.semaphore_wait(free_sem, chips - 1)
                if q < chips - 1:
                    give_copy(q + 1).start()
                return
            first = down_tiles + 4 * (q - chips)
            for j in range(first, min(first + 4, len(tiles))):
                work_out(j)
                part_copy(tiles[j][1], tiles[j][0]).start()

        def backward(k):
            gathered(k)
            keep = store(held.at[batch_at(k)], feed_grad_all, k, store_sem.at[0])
            keep.start()

            @pl.loop(0, hidden // FF_TILE)
            def _(n):
                low = pl.ds(pl.multiple_of(n * FF_TILE, FF_TILE), FF_TILE)
                high = pl.ds(pl.multiple_of(hidden + n * FF_TILE, FF_TILE), FF_TILE)
                act_grad = dot(held[batch_at(k), :], down_weights[:, low])
                gate = wide[batch_at(k), low]
                up = wide[batch_at(k), high]
                sigmoid = 1.0 / (1.0 + jnp.exp(-gate))
                back[batch_at(k), low] = (act_grad * up * sigmoid * (1.0 + gate * (1.0 - sigmoid))).astype(BF16)
                back[batch_at(k), high] = (act_grad * (gate * sigmoid)).astype(BF16)

            sums_sent(1, k)

            @pl.loop(0, width // SUM_TILE)
            def _(n):
                columns = pl.ds(pl.multiple_of(n * SUM_TILE, SUM_TILE), SUM_TILE)
                own[batch_at(k), columns] = dot_rows(back[batch_at(k), :], up_weights[columns, :]).astype(BF16)

            keep.wait()
            spread_sent(k)
            for d in range(spans):
                near_copy(2, d, k).start()

            @pl.when(k == count - 1)
            def _():
                for s in range(1, chips) if chips != 4 else ():
                    pl.semaphore_signal(
                        free_sem, 1, device_id={"chip": lax.rem(chip + s, chips)}, device_id_type=MESH_ID
                    )
                load_slice(0).start()
                load_slice(1).start()

        def give(seq, d, k):
            return pltpu.make_async_copy(
                held.at[at_seq(seq, d, k)], projected_all.at[natural(seq, d, k)], load_sem.at[d, k]
            )

        def hand_out(k):
            gathered(k)
            sums_sent(2, k)
            for seq in range(2):
                for d in range(spans):
                    give(seq, d, k).start()
                for d in range(spans):
                    give(seq, d, k).wait()
            spread_sent(k)

        step = 2 * last + 2
        last_steps = 9 if chips == 4 else chips + down_tiles // 2
        assert last_steps <= step + 1

        def due(t, run):
            @pl.when(jnp.logical_and(t >= 0, t < count))
            def _():
                run(t)

        @pl.loop(0, 3 * step + count - 1)
        def _(t):
            for e in range(2, -1, -1):
                now = t - e * step
                for j in range(1, spans):
                    o = place - j

                    @pl.when(o >= 0)
                    def _():
                        due(now - turn_of(o) - j, functools.partial(relay_right, o))

                    p = place + j

                    @pl.when(p < spans)
                    def _():
                        due(now - turn_of(p) - j, functools.partial(relay_left, p))

                due(now - place, functools.partial(pass_right, e))
                due(now - (last - place), functools.partial(pass_left, e))
                due(now - turn_of(place), functools.partial(finish, e))
            if chips == 4:

                @pl.when(t == 2 * last - 2)
                def _():
                    relay_down()

            for e, run in ((2, hand_out), (1, backward), (0, forward)):
                due(t - e * step - 2 * last, run)
            for q in range(last_steps):

                @pl.when(t == count + step + 2 * last + q)
                def _():
                    weight_grads(q)

        if chips == 4:
            for group, out in zip(sums, (down_sum, gate_sum)):
                for half in range(2):
                    out[half * GRAD_TILE : (half + 1) * GRAD_TILE, :] = group.finish(half).astype(BF16)
            for n in range(down_tiles):
                part_copy(n, 2).wait()
            return
        total = given[here, :].astype(F32)
        for s in range(1, chips):
            give_copy(s).wait()
            total = total + down_weights[s * shard : (s + 1) * shard, :].astype(F32)
        down_sum[...] = total.astype(BF16)
        gate_sum[...] = jnp.zeros_like(gate_sum)
        for n in range(down_tiles):
            part_copy(n, 1).wait()
            part_copy(n, 2).wait()

    def call(self, chips, partial, tokens, cotangent, gains, gate_up_w, down):
        spans, rows, width, hidden, count = self.spans, self.rows, self.width, self.hidden, self.count
        total = 2 * spans * rows
        vmem = pl.BlockSpec(memory_space=pltpu.VMEM)
        hbm = pl.BlockSpec(memory_space=pl.ANY)
        shape = jax.ShapeDtypeStruct
        sems = pltpu.SemaphoreType.DMA((spans, count))
        two = pltpu.SemaphoreType.DMA((2,))
        return pl.pallas_call(
            functools.partial(self.body, chips),
            out_shape=[
                shape((rows, width), BF16),
                shape((rows, width), F32),
                shape((1, width), F32),
                shape((1, width), F32),
                shape(down.shape, BF16),
                shape(down.shape, BF16),
                shape((total, width), BF16),
                shape((total, width), BF16),
                shape((16, 128) if chips == 4 else (width, hidden), BF16),
                shape((width, hidden), BF16),
                shape((total, width), BF16),
            ],
            in_specs=[hbm, vmem, vmem, vmem, hbm, hbm],
            out_specs=[vmem] * 6 + [hbm] * 5,
            scratch_shapes=[
                pltpu.VMEM((rows, width), F32),
                pltpu.VMEM((rows, width), F32),
                pltpu.VMEM((total, width), BF16),
                pltpu.VMEM((total // 2, width), BF16),
                pltpu.VMEM((total // 2, width), BF16),
                pltpu.VMEM((total // 2, width), BF16),
                pltpu.VMEM((total, width), BF16),
                pltpu.VMEM((total, 2 * hidden), F32),
                pltpu.VMEM((total, hidden), BF16),
                pltpu.VMEM((total, 2 * hidden), BF16),
                pltpu.VMEM((width, 2 * hidden), BF16),
                pltpu.VMEM((width, hidden), BF16),
                pltpu.VMEM((4, total, GRAD_TILE), BF16),
                pltpu.VMEM((width, hidden), BF16),
                pltpu.VMEM((2, 6, GRAD_TILE, hidden) if chips == 4 else (2, 6, 16, 128), BF16),
                sems,
                two,
                two,
                pltpu.SemaphoreType.DMA((4,)),
                pltpu.SemaphoreType.DMA((2, width // GRAD_TILE)),
                pltpu.SemaphoreType.REGULAR,
            ]
            + [sems] * 12
            + [pltpu.SemaphoreType.DMA((max(chips, 6),))] * 6,
            compiler_params=pltpu.CompilerParams(
                collective_id=2, has_side_effects=True, vmem_limit_bytes=62 << 20
            ),
            cost_estimate=pl.CostEstimate(
                flops=36 * rows * spans * width * hidden, bytes_accessed=100 * width * width, transcendentals=0
            ),
            name="feed_forward",
        )(partial, tokens, cotangent, gains, gate_up_w, down)


def turn(values, cosine, sine):
    return values * cosine + pltpu.roll(values, HEAD_DIM // 2, 1) * sine


def member_rows(part):
    row = lax.broadcasted_iota(jnp.int32, (8, 2 * part), 0)
    column = lax.broadcasted_iota(jnp.int32, (8, 2 * part), 1)
    return jnp.where(row == column // part, 1.0, 0.0).astype(F32)


def row_sums(pick, values):
    return lax.dot_general(
        pick, values, (((1,), (1,)), ((), ())), precision=lax.Precision.HIGHEST, preferred_element_type=F32
    )


def over_columns(pick, sums):
    return lax.dot_general(
        sums, pick, (((0,), (0,)), ((), ())), precision=lax.Precision.HIGHEST, preferred_element_type=F32
    )


class Stats:
    def __init__(self, spans, own, arrived, send, recv):
        self.spans, self.own, self.arrived, self.send, self.recv = spans, own, arrived, send, recv
        self.core, self.place = lax.axis_index("core"), lax.axis_index("ctx")
        self.me = self.core * spans + self.place

    def member(self, s):
        core, place = step_member(self.core, self.place, s, self.spans)
        return {"core": core, "ctx": place}

    def greet(self):
        for s in range(1, 2 * self.spans):
            pl.semaphore_signal(
                pltpu.get_barrier_semaphore(), 1, device_id=self.member(s), device_id_type=MESH_ID
            )

    def meet(self):
        pl.semaphore_wait(pltpu.get_barrier_semaphore(), 2 * self.spans - 1)

    def copy(self, s):
        return pltpu.make_async_remote_copy(
            src_ref=self.own, dst_ref=self.arrived.at[s], send_sem=self.send.at[s], recv_sem=self.recv.at[s],
            device_id=self.member(s), device_id_type=MESH_ID,
        )

    def start(self):
        for s in range(1, 2 * self.spans):
            self.copy(s).start()

    def total(self):
        total = self.own[...]
        for s in range(1, 2 * self.spans):
            self.copy(s).wait()
            total = total + self.arrived[s]
        return total


def stats_scratch(spans, total_rows):
    sems = pltpu.SemaphoreType.DMA((2 * spans,))
    return [
        pltpu.VMEM((8, total_rows), F32),
        pltpu.VMEM((2 * spans, 8, total_rows), F32),
        sems,
        sems,
    ]


def allowed_at(ids, seq, block, count, spans):
    rows = ids.shape[1]
    per = block // rows
    ids_of = lambda z: ids[(seq * spans + z) * 8 : (seq * spans + z) * 8 + 8, :].astype(F32)
    first = count * per
    keys = jnp.concatenate([ids_of(z)[:1] for z in range(first + per)], 1)
    queries = jnp.concatenate([jnp.transpose(ids_of(z))[:, :1] for z in range(first, first + per)], 0)
    shape = (block, (count + 1) * block)
    query_at = lax.broadcasted_iota(jnp.int32, shape, 0) + count * block
    key_at = lax.broadcasted_iota(jnp.int32, shape, 1)
    same = queries == keys
    seen = jnp.logical_and(same, key_at <= query_at)
    return jnp.logical_and(seen, jnp.logical_or(keys != 0.0, key_at == query_at))


def softmax_parts(query, key, allowed):
    scores = jnp.where(allowed, dot_rows(query, key) * HEAD_DIM ** (-0.5), -1e30)
    weights = jnp.exp(scores - jnp.max(scores, axis=1, keepdims=True))
    return weights / jnp.sum(weights, axis=1, keepdims=True)


QUERY_BLOCK = 256
ROW_TILE = 256


def attend_body(
    spans, chips, tokens, weights, out_rows, gains, ids, cosine, sine,
    partial_out, out_w_out, query_out, key_out, value_out, normed_out, factor_out, attended_out,
    held, held_w, raw, given, out_w, own, arrived, load_sem, store_sem, chip_send, chip_recv, send, recv,
):
    part = out_w.shape[0]
    total_rows = raw.shape[0]
    length = total_rows // 2
    width = tokens.shape[1]
    tiles = total_rows // ROW_TILE
    stats = Stats(spans, own, arrived, send, recv)
    stats.greet()
    chip = lax.axis_index("chip")
    shard = out_rows.shape[0]
    here = pl.ds(pl.multiple_of(chip * shard, shard), shard)

    def chip_copy(s):
        return pltpu.make_async_remote_copy(
            src_ref=out_rows, dst_ref=out_w.at[here], send_sem=chip_send.at[s], recv_sem=chip_recv.at[s],
            device_id={"chip": lax.rem(chip + s, chips)}, device_id_type=MESH_ID,
        )

    for s in range(1, chips):
        pl.semaphore_signal(
            pltpu.get_barrier_semaphore(), 1, device_id={"chip": lax.rem(chip + s, chips)}, device_id_type=MESH_ID
        )
    out_w[here, :] = out_rows[...]

    def at(i):
        return pl.ds(pl.multiple_of(i * ROW_TILE, ROW_TILE), ROW_TILE)

    def load_rows(i):
        return pltpu.make_async_copy(tokens.at[at(i)], held.at[at(i)], load_sem.at[i])

    load_w = pltpu.make_async_copy(weights, held_w, load_sem.at[tiles])
    load_w.start()

    @pl.loop(0, tiles)
    def _(i):
        load_rows(i).start()

    pick = member_rows(part)
    pl.semaphore_wait(pltpu.get_barrier_semaphore(), 2 * spans - 1 + chips - 1)
    for s in range(1, chips):
        chip_copy(s).start()
    load_w.wait()

    @pl.loop(0, tiles)
    def _(i):
        load_rows(i).wait()
        values = dot(held[at(i), :], held_w[...])
        raw[at(i), :] = values
        both = values[:, : 2 * part]
        own[:, at(i)] = row_sums(pick, both * both)

    stats.start()

    @pl.loop(0, tiles)
    def _(i):
        value_out[at(i), :] = raw[at(i), 2 * part :].astype(BF16)

    factor_out[...] = lax.rsqrt(stats.total() / width + EPS)
    me = stats.me
    columns = pl.ds(pl.multiple_of(me * part, part), part)
    gain = jnp.concatenate([gains[0:1, columns], gains[1:2, columns]], 1)

    @pl.loop(0, tiles)
    def _(i):
        normed = raw[at(i), : 2 * part] * over_columns(pick, factor_out[:, at(i)])
        normed_out[at(i), :] = normed
        scaled = normed * gain
        place = pl.ds(pl.multiple_of(lax.rem(i, length // ROW_TILE) * ROW_TILE, ROW_TILE), ROW_TILE)
        for h in range(part // HEAD_DIM):
            head = slice(h * HEAD_DIM, (h + 1) * HEAD_DIM)
            low = slice(part + h * HEAD_DIM, part + (h + 1) * HEAD_DIM)
            query_out[at(i), head] = turn(scaled[:, head], cosine[place, :], sine[place, :]).astype(BF16)
            key_out[at(i), head] = turn(scaled[:, low], cosine[place, :], sine[place, :]).astype(BF16)

    for s in range(1, chips):
        chip_copy(s).wait()
    out_w_out[...] = out_w[...]
    block = QUERY_BLOCK
    for seq in range(2):
        for count in range(length // block):
            allowed = allowed_at(ids, seq, block, count, spans)
            rows = slice(seq * length + count * block, seq * length + (count + 1) * block)
            keys = slice(seq * length, seq * length + (count + 1) * block)
            for h in range(part // HEAD_DIM):
                head = slice(h * HEAD_DIM, (h + 1) * HEAD_DIM)
                shares = softmax_parts(query_out[rows, head], key_out[keys, head], allowed)
                attended_out[rows, head] = dot(shares.astype(BF16), value_out[keys, head]).astype(BF16)
            i = rows.start // ROW_TILE
            if i >= 2:
                pltpu.make_async_copy(given.at[i % 2], partial_out.at[at(i - 2)], store_sem.at[i - 2]).wait()
            given[i % 2] = dot(attended_out[rows, :], out_w[...]).astype(BF16)
            pltpu.make_async_copy(given.at[i % 2], partial_out.at[at(i)], store_sem.at[i]).start()
    for i in range(tiles - 2, tiles):
        pltpu.make_async_copy(given.at[i % 2], partial_out.at[at(i)], store_sem.at[i]).wait()


def attend(spans, chips, tokens, weights, out_rows, gains, ids, cosine, sine):
    total_rows, width = tokens.shape
    part = out_rows.shape[0] * chips
    tiles = total_rows // ROW_TILE
    vmem = pl.BlockSpec(memory_space=pltpu.VMEM)
    hbm = pl.BlockSpec(memory_space=pl.ANY)
    shape = jax.ShapeDtypeStruct
    return pl.pallas_call(
        functools.partial(attend_body, spans, chips),
        out_shape=[
            shape((total_rows, width), BF16),
            shape((part, width), BF16),
            shape((total_rows, part), BF16),
            shape((total_rows, part), BF16),
            shape((total_rows, part), BF16),
            shape((total_rows, 2 * part), F32),
            shape((8, total_rows), F32),
            shape((total_rows, part), BF16),
        ],
        in_specs=[hbm, hbm] + [vmem] * 5,
        out_specs=[hbm] + [vmem] * 7,
        scratch_shapes=[
            pltpu.VMEM((total_rows, width), BF16),
            pltpu.VMEM(weights.shape, BF16),
            pltpu.VMEM((total_rows, 3 * part), F32),
            pltpu.VMEM((2, ROW_TILE, width), BF16),
            pltpu.VMEM((part, width), BF16),
            *stats_scratch(spans, total_rows)[:2],
            pltpu.SemaphoreType.DMA((tiles + 1,)),
            pltpu.SemaphoreType.DMA((tiles,)),
            pltpu.SemaphoreType.DMA((chips,)),
            pltpu.SemaphoreType.DMA((chips,)),
            *stats_scratch(spans, total_rows)[2:],
        ],
        compiler_params=pltpu.CompilerParams(collective_id=8, has_side_effects=True, vmem_limit_bytes=56 << 20),
        cost_estimate=pl.CostEstimate(flops=2 * total_rows * width * 5 * part, bytes_accessed=0, transcendentals=0),
        name="attend",
    )(tokens, weights, out_rows, gains, ids, cosine, sine)


def attend_back_body(
    spans, grads, tokens, weights, out_w, gains, ids, cosine, sine,
    query, key, value, normed, factor, attended,
    input_out, qkv_out, out_out, gains_out,
    held, held_tokens, held_w, raw, mixed, attended_grad, given, own, arrived, load_sem, store_sem, send, recv,
):
    part = out_w.shape[0]
    total_rows = raw.shape[0]
    length = total_rows // 2
    width = grads.shape[1]
    tiles = total_rows // ROW_TILE
    scale = HEAD_DIM ** (-0.5)
    stats = Stats(spans, own, arrived, send, recv)
    stats.greet()

    def at(i):
        return pl.ds(pl.multiple_of(i * ROW_TILE, ROW_TILE), ROW_TILE)

    def load_rows(i):
        return pltpu.make_async_copy(grads.at[at(i)], held.at[at(i)], load_sem.at[i])

    @pl.loop(0, tiles)
    def _(i):
        load_rows(i).start()

    load_w = pltpu.make_async_copy(weights, held_w, load_sem.at[tiles])
    load_tokens = pltpu.make_async_copy(tokens, held_tokens, load_sem.at[tiles + 1])
    load_w.start()
    load_tokens.start()
    pick = member_rows(part)
    me = stats.me
    columns = pl.ds(pl.multiple_of(me * part, part), part)
    gain = jnp.concatenate([gains[0:1, columns], gains[1:2, columns]], 1)

    @pl.loop(0, tiles)
    def _(i):
        load_rows(i).wait()
        attended_grad[at(i), :] = dot_rows(held[at(i), :], out_w[...]).astype(BF16)

    block = QUERY_BLOCK
    blocks = length // block
    for seq in range(2):
        for h in range(part // HEAD_DIM):
            head = slice(h * HEAD_DIM, (h + 1) * HEAD_DIM)
            key_at = slice(part + h * HEAD_DIM, part + (h + 1) * HEAD_DIM)
            value_at = slice(2 * part + h * HEAD_DIM, 2 * part + (h + 1) * HEAD_DIM)
            for count in reversed(range(blocks)):
                allowed = allowed_at(ids, seq, block, count, spans)
                rows = slice(seq * length + count * block, seq * length + (count + 1) * block)
                keys = slice(seq * length, seq * length + (count + 1) * block)
                shares = softmax_parts(query[rows, head], key[keys, head], allowed)
                share_grad = dot_rows(attended_grad[rows, head], value[keys, head])
                inner = jnp.sum(shares * share_grad, axis=1, keepdims=True)
                score_grad = (shares * (share_grad - inner)).astype(BF16)
                raw[rows, head] = dot(score_grad, key[keys, head]) * scale
                key_grad = dot_first(score_grad, query[rows, head]) * scale
                value_grad = dot_first(shares.astype(BF16), attended_grad[rows, head])
                if count == blocks - 1:
                    raw[keys, key_at] = key_grad
                    raw[keys, value_at] = value_grad
                else:
                    raw[keys, key_at] += key_grad
                    raw[keys, value_at] += value_grad

    gains_out[...] = jnp.zeros_like(gains_out)

    @pl.loop(0, tiles)
    def _(i):
        place = pl.ds(pl.multiple_of(lax.rem(i, length // ROW_TILE) * ROW_TILE, ROW_TILE), ROW_TILE)
        for h in range(2 * part // HEAD_DIM):
            head = slice(h * HEAD_DIM, (h + 1) * HEAD_DIM)
            raw[at(i), head] = turn(raw[at(i), head], cosine[place, :], -sine[place, :])
        terms = raw[at(i), : 2 * part] * normed[at(i), :]
        gains_out[0:1, :] += jnp.sum(terms, axis=0, keepdims=True)
        own[:, at(i)] = row_sums(pick, terms * gain)
        mixed[at(i), 2 * part :] = raw[at(i), 2 * part :].astype(BF16)

    stats.meet()
    stats.start()
    out_out[...] = dot_first(attended[...], held[...]).astype(BF16)
    own[...] = stats.total() / width

    @pl.loop(0, tiles)
    def _(i):
        mean = over_columns(pick, own[:, at(i)])
        back = gain * raw[at(i), : 2 * part] - normed[at(i), :] * mean
        mixed[at(i), : 2 * part] = (over_columns(pick, factor[:, at(i)]) * back).astype(BF16)

    load_w.wait()

    def store(i):
        return pltpu.make_async_copy(given.at[lax.rem(i, 2)], input_out.at[at(i)], store_sem.at[lax.rem(i, 2)])

    @pl.loop(0, tiles)
    def _(i):
        @pl.when(i >= 2)
        def _():
            store(i - 2).wait()

        given[lax.rem(i, 2)] = dot_rows(mixed[at(i), :], held_w[...]).astype(BF16)
        store(i).start()

    load_tokens.wait()

    @pl.loop(0, width // ROW_TILE)
    def _(i):
        qkv_out[at(i), :] = dot_first(held_tokens[:, at(i)], mixed[...]).astype(BF16)

    for i in range(tiles - 2, tiles):
        store(i).wait()


def attend_back(spans, grads, tokens, weights, out_w, gains, ids, cosine, sine, saved):
    total_rows, width = tokens.shape
    part = out_w.shape[0]
    tiles = total_rows // ROW_TILE
    vmem = pl.BlockSpec(memory_space=pltpu.VMEM)
    hbm = pl.BlockSpec(memory_space=pl.ANY)
    shape = jax.ShapeDtypeStruct
    return pl.pallas_call(
        functools.partial(attend_back_body, spans),
        out_shape=[
            shape((total_rows, width), BF16),
            shape((width, 3 * part), BF16),
            shape((part, width), BF16),
            shape((8, 2 * part), F32),
        ],
        in_specs=[hbm] * 3 + [vmem] * (5 + len(saved)),
        out_specs=[hbm] + [vmem] * 3,
        scratch_shapes=[
            pltpu.VMEM((total_rows, width), BF16),
            pltpu.VMEM((total_rows, width), BF16),
            pltpu.VMEM(weights.shape, BF16),
            pltpu.VMEM((total_rows, 3 * part), F32),
            pltpu.VMEM((total_rows, 3 * part), BF16),
            pltpu.VMEM((total_rows, part), BF16),
            pltpu.VMEM((2, ROW_TILE, width), BF16),
            *stats_scratch(spans, total_rows)[:2],
            pltpu.SemaphoreType.DMA((tiles + 2,)),
            pltpu.SemaphoreType.DMA((2,)),
            *stats_scratch(spans, total_rows)[2:],
        ],
        compiler_params=pltpu.CompilerParams(collective_id=9, has_side_effects=True, vmem_limit_bytes=58 << 20),
        cost_estimate=pl.CostEstimate(flops=2 * total_rows * width * 8 * part, bytes_accessed=0, transcendentals=0),
        name="attend_back",
    )(grads, tokens, weights, out_w, gains, ids, cosine, sine, *saved)


def per_device(inputs, segment, w_qkv, w_out, w_gate, w_up, w_down_t, gains, cotangent):
    rows, width = inputs.shape[1:]
    cores = lax.axis_size("core")
    spans = lax.axis_size("ctx")
    members = cores * spans
    length = rows * spans
    part = width // members
    tokens = inputs[0]

    qkv_rows = w_qkv.shape[0]
    qkv_cut = w_qkv.reshape(qkv_rows, 3, members, part).transpose(2, 0, 1, 3)
    qkv_cut = qkv_cut.reshape(members, qkv_rows, 3 * part)
    chips = lax.axis_size("chip")
    assert chips == spans
    own = jax.ShapeDtypeStruct((rows, width), F32)
    qkv_w, ids, tokens_all = Exchange(
        spans, rows, width, PIECE, False, True, pass_tokens, 1, 0, None,
        QkvWeights(spans, chips, qkv_cut, jnp.broadcast_to(segment, (8, rows))),
    ).call("gather_tokens", 1, None, [tokens], [])
    swaps = [
        (m * spans + a, a * members + m) for m in range(members) for a in range(chips)
    ]
    out_rows = lax.ppermute(w_out, ALL, swaps)

    gate_up, down = split_columns(w_gate, w_up, w_down_t)
    gate_up_w = gather(gate_up, "chip")

    cosine, sine = rope_tables(jnp.arange(length, dtype=F32))
    half = jnp.arange(HEAD_DIM) < HEAD_DIM // 2
    sine = jnp.where(half[None, :], -sine, sine)
    out_part, out_w, *saved = attend(spans, chips, tokens_all, qkv_w, out_rows, gains, ids, cosine, sine)
    (
        output, residual_grad, gain_feed, gain_attn, down_sum, gate_sum, _, _, gate_part, up_part, projected_all
    ) = Middle(spans, rows, width, w_gate.shape[1] // cores, BATCH_PIECE).call(
        chips, out_part, tokens, cotangent[0], gains, gate_up_w, down
    )
    up_sum = scatter_sum(up_part, "chip")
    if chips != 4:
        gate_sum = scatter_sum(gate_part, "chip")
    input_part, qkv_part, out_grads, gain_sums = attend_back(
        spans, projected_all, tokens_all, qkv_w, out_w, gains, ids, cosine, sine, saved
    )
    gain_query, gain_key = gain_sums[0, :part], gain_sums[0, part:]
    sums = jnp.concatenate(
        [a.reshape(-1, 128) for a in (gain_attn, gain_feed, gain_query, gain_key)]
        + [jnp.zeros((-2 * part // 128 % 8, 128), F32)]
    )
    input_grad, grad_qkv, grad_gains, grad_out = Exchange(
        spans, rows, width, PIECE, True, False, after_input, 1, 1, None,
        QkvGrads(
            spans, chips, members, qkv_part, sums, out_grads,
        ),
    ).call("sum_input", 5, input_part, [residual_grad], [own])

    grad_gate, grad_up, grad_down = join_columns(gate_sum, up_sum, down_sum)
    return (
        output[None],
        input_grad[None],
        grad_qkv,
        grad_out,
        grad_gate,
        grad_up,
        grad_down,
        grad_gains.reshape(4, width),
    )


def solution(mesh):
    cores = 2
    chips = mesh.shape["dp"] // cores
    split = Mesh(mesh.devices.reshape(chips, cores, mesh.shape["ctx"]), ALL)
    dp = ("chip", "core")
    every = P((*dp, "ctx"), None)
    in_specs = (
        P(dp, "ctx", None),
        P(dp, "ctx"),
        every,
        every,
        P(dp, "ctx"),
        P(dp, "ctx"),
        P(dp, "ctx"),
        P(),
        P(dp, "ctx", None),
    )
    out_specs = (
        P(dp, "ctx", None),
        P(dp, "ctx", None),
        every,
        every,
        P(dp, "ctx"),
        P(dp, "ctx"),
        P(dp, "ctx"),
        P(),
    )
    return jax.shard_map(
        per_device, mesh=split, in_specs=in_specs, out_specs=out_specs, check_vma=False
    )
```

```python
import functools

import jax
import jax.numpy as jnp
from jax import lax
from jax.experimental import pallas as pl
from jax.experimental.pallas import tpu as pltpu
from jax.sharding import Mesh
from jax.sharding import PartitionSpec as P

HEAD_DIM = 128
EPS = 1e-06
ROPE_BASE = 500000.0
F32 = jnp.float32
BF16 = jnp.bfloat16
GROUP = ("core", "ctx")
ALL = ("chip", "core", "ctx")


PIECE = 32
SUM_PIECE = 32
LATE_TICK = 2
PASS_TICK = 4
LAGJ = 1
MESH_ID = pl.DeviceIdType.MESH


def row_factor(values):
    return lax.rsqrt(jnp.mean(values * values, axis=-1, keepdims=True) + EPS)


def row_norm_back(values, gain, grad):
    factor = row_factor(values)
    normed = values * factor
    scaled = gain * grad
    back = factor * (scaled - normed * jnp.mean(scaled * normed, axis=-1, keepdims=True))
    return back, jnp.sum(grad * normed, axis=0, keepdims=True)


def after_projected(total, ins, outs, rows):
    tokens, gains = ins
    residual_out, projected_out = outs
    projected_out[rows, :] = total
    gain = gains[2:3, :]
    residual = tokens[rows, :].astype(F32) + total * row_factor(total) * gain
    residual_out[rows, :] = residual
    return residual


def after_feed(total, ins, outs, rows):
    residual, cotangent, gains = ins
    output, gain_out = outs
    gain = gains[3:4, :]
    normed = total * row_factor(total) * gain
    output[rows, :] = (residual[rows, :] + normed).astype(BF16)
    back, term = row_norm_back(total, gain, cotangent[rows, :].astype(F32))
    gain_out[...] += term
    return back


def after_back(total, ins, outs, rows):
    projected, cotangent, gains = ins
    grad_out, gain_out = outs
    grad = cotangent[rows, :].astype(F32) + total
    grad_out[rows, :] = grad
    back, term = row_norm_back(projected[rows, :], gains[2:3, :], grad)
    gain_out[...] += term
    return back


def after_input(total, ins, outs, rows):
    (grad,), (result,) = ins, outs
    result[rows, :] = grad[rows, :] + total
    return None


def pass_tokens(total, ins, outs, rows):
    return ins[0][rows, :]


class Exchange:
    def __init__(self, spans, rows, width, piece, reduce, spread, row_fn, n_in, n_out, gain, extra=None):
        self.extra = extra
        self.spans, self.rows, self.width, self.piece = spans, rows, width, piece
        self.reduce, self.spread, self.row_fn = reduce, spread, row_fn
        self.n_in, self.n_out, self.gain = n_in, n_out, gain
        self.count = rows // piece

    def scratch(self):
        spans, count = self.spans, self.count
        block = pltpu.VMEM((spans * self.rows, self.width), BF16)
        sems = pltpu.SemaphoreType.DMA((spans, count))
        items = []
        if self.reduce:
            items += [block] * 4 + [pltpu.SemaphoreType.DMA] + [sems] * 6
        if self.spread:
            items += [pltpu.VMEM((2 * spans * self.rows, self.width), BF16)]
            items += [sems] * 7 + [pltpu.SemaphoreType.DMA]
        if self.extra is not None:
            items += self.extra.scratch()
        return items

    def body(self, *refs):
        spans, rows, piece, count = self.spans, self.rows, self.piece, self.count
        refs = list(refs)
        take = lambda n: [refs.pop(0) for _ in range(n)]
        partial = take(1)[0] if self.reduce else None
        ins = take(self.n_in)
        extra = self.extra
        if extra is not None:
            extra.ins = take(extra.n_in)
        outs = take(self.n_out)
        if extra is not None:
            extra.outs = take(extra.n_out)
        gathered = take(1)[0] if self.spread else None
        if self.reduce:
            own, near, from_left, from_right = take(4)
            (load_sem,) = take(1)
            near_send, near_recv, right_send, right_recv, left_send, left_recv = take(6)
        if self.spread:
            (held,) = take(1)
            fwd_send, fwd_recv, bwd_send, bwd_recv, own_send, side_send, side_recv = take(7)
            (store_sem,) = take(1)
        if extra is not None:
            extra.held = refs
        core = lax.axis_index("core")
        place = lax.axis_index("ctx")
        other = 1 - core
        has_left = place > 0
        has_right = place < spans - 1

        def at(block, k):
            return pl.ds(pl.multiple_of(block * rows + k * piece, piece), piece)

        def held_at(seq, block, k):
            return pl.ds(pl.multiple_of((seq * spans + block) * rows + k * piece, piece), piece)

        def remote(src, dst, send, recv, **device):
            return pltpu.make_async_remote_copy(
                src_ref=src, dst_ref=dst, send_sem=send, recv_sem=recv,
                device_id=device, device_id_type=MESH_ID,
            )

        barrier = pltpu.get_barrier_semaphore()
        if extra is not None:
            if not extra.met:
                meet_all(spans)
        else:
            pl.semaphore_signal(barrier, 1, device_id={"core": other}, device_id_type=MESH_ID)

            @pl.when(has_left)
            def _():
                pl.semaphore_signal(barrier, 1, device_id={"ctx": place - 1}, device_id_type=MESH_ID)

            @pl.when(has_right)
            def _():
                pl.semaphore_signal(barrier, 1, device_id={"ctx": place + 1}, device_id_type=MESH_ID)

            pl.semaphore_wait(barrier, 1 + has_left.astype(jnp.int32) + has_right.astype(jnp.int32))

        if self.gain is not None:
            outs[self.gain][...] = jnp.zeros_like(outs[self.gain])

        def near_copy(d, k):
            return remote(
                partial.at[held_at(other, d, k)], near.at[at(d, k)],
                near_send.at[d, k], near_recv.at[d, k], core=other,
            )

        def right_copy(d, k):
            return remote(
                own.at[at(d, k)], from_left.at[at(d, k)],
                right_send.at[d, k], right_recv.at[d, k], ctx=place + 1,
            )

        def left_copy(d, k):
            return remote(
                own.at[at(d, k)], from_right.at[at(d, k)],
                left_send.at[d, k], left_recv.at[d, k], ctx=place - 1,
            )

        def fwd_copy(o, k, send):
            where = held_at(core, o, k)
            return remote(held.at[where], held.at[where], send, fwd_recv.at[o, k], ctx=place + 1)

        def bwd_copy(o, k, send):
            where = held_at(core, o, k)
            return remote(held.at[where], held.at[where], send, bwd_recv.at[o, k], ctx=place - 1)

        def side_copy(o, k):
            where = held_at(core, o, k)
            return remote(held.at[where], held.at[where], side_send.at[o, k], side_recv.at[o, k], core=other)

        if extra is not None:
            extra.start()
        if self.reduce:
            load = pltpu.make_async_copy(
                partial.at[pl.ds(pl.multiple_of(core * spans * rows, rows), spans * rows)], own, load_sem
            )
            load.start()

            @pl.loop(0, count)
            def _(k):
                for j in range(spans):
                    near_copy(j, k).start()

            load.wait()

        def base(d, k):
            near_copy(d, k).wait_recv()
            return own[at(d, k), :].astype(F32) + near[at(d, k), :].astype(F32)

        def pass_on(d, k, arrived, copy, later):
            value = base(d, k)

            @pl.when(later)
            def _():
                copy(d, k).wait_recv()

            before = arrived[at(d, k), :].astype(F32)
            value = value + jnp.where(later, before, jnp.zeros_like(before))
            own[at(d, k), :] = value.astype(BF16)
            copy(d, k).start()

        def pass_right(k):
            for d in range(spans - 1, 0, -1):

                @pl.when(d > place)
                def _():
                    pass_on(d, k, from_left, right_copy, has_left)

        def pass_left(k):
            for d in range(spans - 1):

                @pl.when(d < place)
                def _():
                    pass_on(d, k, from_right, left_copy, has_right)

        def finish_step(k):
            total = None
            if self.reduce:
                total = base(place, k)

                @pl.when(has_left)
                def _():
                    right_copy(place, k).wait_recv()

                @pl.when(has_right)
                def _():
                    left_copy(place, k).wait_recv()

                zero = jnp.zeros_like(total)
                total = total + jnp.where(has_left, from_left[at(place, k), :].astype(F32), zero)
                total = total + jnp.where(has_right, from_right[at(place, k), :].astype(F32), zero)
            own_rows = pl.ds(pl.multiple_of(k * piece, piece), piece)
            result = self.row_fn(total, ins, outs, own_rows)
            if self.spread:
                held[held_at(core, place, k), :] = result.astype(BF16)

                @pl.when(has_right)
                def _():
                    fwd_copy(place, k, fwd_send.at[place, k]).start()

                @pl.when(has_left)
                def _():
                    bwd_copy(place, k, bwd_send.at[place, k]).start()

                side_copy(place, k).start()

        def relay_step(k, j):
            if True:

                @pl.when(place - j >= 0)
                def _():
                    fwd_copy(place - j, k, fwd_send.at[place - j, k]).wait_recv()

                    @pl.when(has_right)
                    def _():
                        fwd_copy(place - j, k, fwd_send.at[place - j, k]).start()

                    side_copy(place - j, k).start()

                @pl.when(place + j < spans)
                def _():
                    bwd_copy(place + j, k, bwd_send.at[place + j, k]).wait_recv()

                    @pl.when(has_left)
                    def _():
                        bwd_copy(place + j, k, bwd_send.at[place + j, k]).start()

                    side_copy(place + j, k).start()

        lag = spans - 1 if self.reduce else 0

        def due(k, run):
            @pl.when(jnp.logical_and(k >= 0, k < count))
            def _():
                run(k)

        @pl.loop(0, count + lag + (LAGJ * (spans - 1) if self.spread else 0))
        def _(t):
            if self.reduce:
                due(t - place, pass_right)
                due(t - (spans - 1 - place), pass_left)
                due(t - jnp.maximum(place, spans - 1 - place), finish_step)
            else:

                @pl.when(t == 0)
                def _():
                    for k in range(count):
                        finish_step(k)

            if self.spread:
                for j in range(1, spans):
                    after = t - lag - j * LAGJ

                    @pl.when(jnp.logical_and(after >= 0, after < count))
                    def _():
                        relay_step(after, j)
            if extra is not None:
                extra.tick(t)

        if extra is not None:
            extra.finish(count + lag + (LAGJ * (spans - 1) if self.spread else 0))
        if self.spread:

            @pl.loop(0, count)
            def _(k):
                for o in range(spans):
                    side_copy(o, k).wait_recv()

            store = pltpu.make_async_copy(held, gathered, store_sem)
            store.start()

        @pl.loop(0, count)
        def _(k):
            for d in range(spans):
                if self.reduce:
                    near_copy(d, k).wait_send()

                    @pl.when(d > place)
                    def _():
                        right_copy(d, k).wait_send()

                    @pl.when(d < place)
                    def _():
                        left_copy(d, k).wait_send()

                if self.spread:
                    side_copy(d, k).wait_send()

                    @pl.when(jnp.logical_and(d <= place, has_right))
                    def _():
                        fwd_copy(d, k, fwd_send.at[d, k]).wait_send()

                    @pl.when(jnp.logical_and(d >= place, has_left))
                    def _():
                        bwd_copy(d, k, bwd_send.at[d, k]).wait_send()

        if self.spread:
            store.wait()

    def call(self, name, collective_id, partial, ins, outs):
        vmem = pl.BlockSpec(memory_space=pltpu.VMEM)
        hbm = pl.BlockSpec(memory_space=pl.ANY)
        operands = ([partial] if self.reduce else []) + list(ins)
        in_specs = ([hbm] if self.reduce else []) + [vmem] * len(ins)
        shapes = list(outs)
        specs = [vmem] * len(outs)
        if self.extra is not None:
            operands += self.extra.operands
            in_specs += self.extra.in_specs
            shapes += self.extra.out_shapes
            specs += self.extra.out_specs
        if self.spread:
            shapes.append(jax.ShapeDtypeStruct((2 * self.spans * self.rows, self.width), BF16))
            specs.append(hbm)
        return pl.pallas_call(
            self.body,
            out_shape=shapes,
            in_specs=in_specs,
            out_specs=specs,
            scratch_shapes=self.scratch(),
            compiler_params=pltpu.CompilerParams(
                collective_id=collective_id, has_side_effects=True, vmem_limit_bytes=48 << 20
            ),
            cost_estimate=pl.CostEstimate(
                flops=0,
                bytes_accessed=(50 if self.reduce else 30) * self.width * self.width,
                transcendentals=0,
            ),
            name=name,
        )(*operands)


def owner_of(chip, core, place, spans):
    member = core * spans + place
    return member // 2, lax.rem(member, 2), chip


def summer_of(chip, core, place, spans):
    member = chip * 2 + core
    return place, member // spans, lax.rem(member, spans)


def stays(chip, core, place, spans):
    to_chip, to_core, to_place = owner_of(chip, core, place, spans)
    return jnp.logical_and(to_chip == chip, jnp.logical_and(to_core == core, to_place == place))


def meet_all(spans):
    greet_all(spans, False)
    wait_all(spans, False)


def greet_all(spans, moves):
    chips = lax.axis_size("chip")
    barrier = pltpu.get_barrier_semaphore()
    chip = lax.axis_index("chip")
    core = lax.axis_index("core")
    place = lax.axis_index("ctx")
    for s in range(1, chips):
        pl.semaphore_signal(
            barrier, 1, device_id={"chip": lax.rem(chip + s, chips)}, device_id_type=MESH_ID
        )
    for s in range(1, 2 * spans):
        to_core, to_place = step_member(core, place, s, spans)
        pl.semaphore_signal(
            barrier, 1, device_id={"core": to_core, "ctx": to_place}, device_id_type=MESH_ID
        )
    if moves:

        @pl.when(jnp.logical_not(stays(chip, core, place, spans)))
        def _():
            for find in (owner_of, summer_of):
                to_chip, to_core, to_place = find(chip, core, place, spans)
                pl.semaphore_signal(
                    barrier, 1, device_id={"chip": to_chip, "core": to_core, "ctx": to_place}, device_id_type=MESH_ID
                )


def wait_all(spans, moves):
    count = lax.axis_size("chip") - 1 + 2 * spans - 1
    if moves:
        here = stays(lax.axis_index("chip"), lax.axis_index("core"), lax.axis_index("ctx"), spans)
        count = count + 2 * jnp.logical_not(here).astype(jnp.int32)
    pl.semaphore_wait(pltpu.get_barrier_semaphore(), count)


def step_member(core, place, s, spans):
    return lax.rem(core + s % 2, 2), lax.rem(place + s // 2, spans)


def meet_other_core():
    barrier = pltpu.get_barrier_semaphore()
    other = 1 - lax.axis_index("core")
    pl.semaphore_signal(barrier, 1, device_id={"core": other}, device_id_type=MESH_ID)
    pl.semaphore_wait(barrier, 1)


def split_body(gate, up, down, gate_up_out, down_out, held, load_sem, store_sem, send_sem, recv_sem):
    core = lax.axis_index("core")
    other = 1 - core
    rows, width = gate.shape
    half = width // 2
    where = pl.ds(pl.multiple_of(core * rows, rows), rows)
    places = [gate_up_out.at[where, :half], gate_up_out.at[where, half:], down_out.at[where, :]]
    mine = pl.ds(pl.multiple_of(core * half, half), half)
    theirs = pl.ds(pl.multiple_of(other * half, half), half)
    loads = [
        pltpu.make_async_copy(a.at[:, mine], held.at[i], load_sem.at[i]) for i, a in enumerate((gate, up, down))
    ]
    for load in loads:
        load.start()
    meet_other_core()
    sends = [
        pltpu.make_async_remote_copy(
            src_ref=a.at[:, theirs], dst_ref=places[i], send_sem=send_sem.at[i], recv_sem=recv_sem.at[i],
            device_id={"core": other}, device_id_type=MESH_ID,
        )
        for i, a in enumerate((gate, up, down))
    ]
    for send in sends:
        send.start()
    stores = [pltpu.make_async_copy(held.at[i], places[i], store_sem.at[i]) for i in range(3)]
    for load, store in zip(loads, stores):
        load.wait()
        store.start()
    for store, send in zip(stores, sends):
        store.wait()
        send.wait()


def split_columns(gate, up, down):
    rows, width = gate.shape
    hbm = pl.BlockSpec(memory_space=pl.ANY)
    three = pltpu.SemaphoreType.DMA((3,))
    return pl.pallas_call(
        split_body,
        out_shape=[
            jax.ShapeDtypeStruct((2 * rows, width), BF16),
            jax.ShapeDtypeStruct((2 * rows, width // 2), BF16),
        ],
        in_specs=[hbm] * 3,
        out_specs=[hbm] * 2,
        scratch_shapes=[pltpu.VMEM((3, rows, width // 2), BF16)] + [three] * 4,
        compiler_params=pltpu.CompilerParams(collective_id=6, has_side_effects=True, vmem_limit_bytes=8 << 20),
        name="split_columns",
    )(gate, up, down)


def join_body(gate, up, down, gate_out, up_out, down_out, arrived, send_sem, recv_sem):
    core = lax.axis_index("core")
    other = 1 - core
    rows, width = gate_out.shape
    half = width // 2
    meet_other_core()
    theirs = pl.ds(pl.multiple_of(other * rows, rows), rows)
    pairs = ((gate, gate_out), (up, up_out), (down, down_out))
    sends = [
        pltpu.make_async_remote_copy(
            src_ref=a.at[theirs], dst_ref=arrived.at[i], send_sem=send_sem.at[i], recv_sem=recv_sem.at[i],
            device_id={"core": other}, device_id_type=MESH_ID,
        )
        for i, (a, _) in enumerate(pairs)
    ]
    for send in sends:
        send.start()
    mine = pl.ds(pl.multiple_of(core * half, half), half)
    far = pl.ds(pl.multiple_of(other * half, half), half)
    step = 16

    def rows_at(i, base):
        return pl.ds(pl.multiple_of(base + i * step, step), step)

    @pl.loop(0, rows // step)
    def _(i):
        for a, b in pairs:
            b[rows_at(i, 0), mine] = a[rows_at(i, core * rows), :].astype(F32)

    for send in sends:
        send.wait()

    @pl.loop(0, rows // step)
    def _(i):
        for n, (_, b) in enumerate(pairs):
            b[rows_at(i, 0), far] = arrived[n, rows_at(i, 0), :].astype(F32)


def join_columns(gate, up, down):
    rows, half = gate.shape[0] // 2, gate.shape[1]
    vmem = pl.BlockSpec(memory_space=pltpu.VMEM)
    three = pltpu.SemaphoreType.DMA((3,))
    return pl.pallas_call(
        join_body,
        out_shape=[jax.ShapeDtypeStruct((rows, 2 * half), F32)] * 3,
        in_specs=[vmem] * 3,
        out_specs=[vmem] * 3,
        scratch_shapes=[pltpu.VMEM((3, rows, half), BF16), three, three],
        compiler_params=pltpu.CompilerParams(collective_id=7, has_side_effects=True, vmem_limit_bytes=32 << 20),
        name="join_columns",
    )(gate, up, down)


class Extra:
    met = False

    def remote(self, src, dst, send, recv, **device):
        return pltpu.make_async_remote_copy(
            src_ref=src, dst_ref=dst, send_sem=send, recv_sem=recv,
            device_id=device, device_id_type=MESH_ID,
        )

    def locate(self):
        self.chip = lax.axis_index("chip")
        self.core = lax.axis_index("core")
        self.place = lax.axis_index("ctx")
        self.me = self.core * self.spans + self.place


class QkvWeights(Extra):
    n_in, n_out = 2, 2

    def __init__(self, spans, chips, cut, ids):
        self.spans, self.chips = spans, chips
        self.members, self.block, self.columns = cut.shape
        self.operands = [cut, ids]
        self.ids_shape = ids.shape
        vmem = pl.BlockSpec(memory_space=pltpu.VMEM)
        self.in_specs = [vmem, vmem]
        self.out_shapes = [
            jax.ShapeDtypeStruct((chips * self.members * self.block, self.columns), BF16),
            jax.ShapeDtypeStruct((self.members * ids.shape[0], ids.shape[1]), jnp.int32),
        ]
        self.out_specs = [vmem, vmem]

    def scratch(self):
        rows = self.chips * self.members * self.block
        sems = pltpu.SemaphoreType.DMA((self.members,))
        cross = pltpu.SemaphoreType.DMA((self.chips, self.members))
        ids = (self.members * self.ids_shape[0], self.ids_shape[1])
        return [pltpu.VMEM((rows, self.columns), BF16), pltpu.VMEM(ids, jnp.int32)] + [sems] * 4 + [cross] * 2

    def at(self, chip, m):
        return pl.ds(pl.multiple_of((chip * self.members + m) * self.block, self.block), self.block)

    def ids_at(self, m):
        return pl.ds(pl.multiple_of(m * self.ids_shape[0], self.ids_shape[0]), self.ids_shape[0])

    def block_copy(self, s):
        full, _, send, recv = self.held[:4]
        core, place = step_member(self.core, self.place, s, self.spans)
        return self.remote(
            self.ins[0].at[core * self.spans + place], full.at[self.at(self.chip, self.me)],
            send.at[s], recv.at[s], core=core, ctx=place,
        )

    def ids_copy(self, s):
        all_ids, send, recv = self.held[1], self.held[4], self.held[5]
        core, place = step_member(self.core, self.place, s, self.spans)
        return self.remote(
            self.ins[1], all_ids.at[self.ids_at(self.me)], send.at[s], recv.at[s], core=core, ctx=place
        )

    def source(self, s):
        core = lax.rem(self.core + s % 2, 2)
        return core * self.spans + lax.rem(self.place + self.spans - s // 2, self.spans)

    def chip_copy(self, s, m):
        full, _, _, _, _, _, send, recv = self.held
        where = self.at(self.chip, m)
        return self.remote(
            full.at[where], full.at[where], send.at[s, m], recv.at[s, m], chip=lax.rem(self.chip + s, self.chips)
        )

    def square_copy(self, kind, s):
        full, _, _, _, _, _, send, recv = self.held
        along_x, along_y, _ = square(self.chip)
        m = self.me if s == 0 else self.source(s)
        owner = self.chip if kind < 2 else (along_x if s % 2 == 0 else along_y)
        to = (along_x, along_y, along_y if s % 2 == 0 else along_x)[kind]
        where = self.at(owner, m)
        return self.remote(full.at[where], full.at[where], send.at[kind, s], recv.at[kind, s], chip=to)

    def start(self):
        self.locate()
        cut, ids = self.ins
        full, all_ids = self.held[:2]
        for s in range(1, self.members):
            self.block_copy(s).start()
        for s in range(1, self.members):
            self.ids_copy(s).start()
        full[self.at(self.chip, self.me), :] = cut[self.me]
        all_ids[self.ids_at(self.me), :] = ids[...]

    def send_block(self, s):
        m = self.me if s == 0 else self.source(s)
        if s > 0:
            self.block_copy(s).wait_recv()
        if self.chips == 4:
            for kind in (0, 1) if s % 2 == 0 else (1, 0):
                self.square_copy(kind, s).start()
            if s >= 2:
                self.pass_block(s - 2)
            return
        for step in range(1, self.chips):
            self.chip_copy(step, m).start()

    def pass_block(self, s):
        self.square_copy(s % 2, s).wait_recv()
        self.square_copy(2, s).start()

    def tick(self, t):
        @pl.when(t == 0)
        def _():
            for s in range(self.members):
                self.send_block(s)
            if self.chips == 4:
                for s in range(self.members - 2, self.members):
                    self.pass_block(s)

    def finish(self, ticks):
        full, all_ids = self.held[:2]
        for s in range(1, self.members):
            self.ids_copy(s).wait_recv()
            self.block_copy(s).wait_send()
            self.ids_copy(s).wait_send()

        if self.chips == 4:
            for s in range(self.members):
                for kind in range(3):
                    self.square_copy(kind, s).wait_send()
                    if kind != s % 2:
                        self.square_copy(kind, s).wait_recv()
        else:

            @pl.loop(0, self.members)
            def _(m):
                for s in range(1, self.chips):
                    self.chip_copy(s, m).wait()

        self.outs[0][...] = full[...]
        self.outs[1][...] = all_ids[...]


class QkvGrads(Extra):
    n_in, n_out = 3, 3
    met = True

    def __init__(self, spans, chips, members, grads, sums, out_grads):
        self.spans, self.chips, self.members = spans, chips, members
        self.out_rows = out_grads.shape[0] // chips
        self.block, self.columns = grads.shape[0] // (chips * members), grads.shape[1]
        self.part = self.columns // 3
        self.width = self.part * members
        self.own_rows = self.part // 128
        self.sum_rows = sums.shape[0]
        vmem = pl.BlockSpec(memory_space=pltpu.VMEM)
        self.out_shapes = [
            jax.ShapeDtypeStruct((self.block, 3 * self.width), F32),
            jax.ShapeDtypeStruct((4, self.width // 128, 128), F32),
            jax.ShapeDtypeStruct((self.out_rows, self.width), F32),
        ]
        self.out_specs = [vmem] * 3

    def scratch(self):
        sems = pltpu.SemaphoreType.DMA((self.members,))
        chip_sems = pltpu.SemaphoreType.DMA((self.chips,))
        cross = pltpu.SemaphoreType.DMA((self.chips, self.members))
        return [
            pltpu.VMEM((self.chips, self.members, self.block, self.columns), BF16),
            pltpu.VMEM((self.members, self.block, self.columns), BF16),
            pltpu.VMEM((self.members, self.block, self.columns), BF16),
            pltpu.VMEM((self.members, self.block, self.columns), BF16),
            pltpu.VMEM((self.chips, self.sum_rows, 128), F32),
            pltpu.VMEM((self.sum_rows, 128), F32),
            pltpu.VMEM((self.members, self.sum_rows, 128), F32),
            pltpu.VMEM((self.chips, self.out_rows, self.width), BF16),
            pltpu.VMEM((self.out_rows, self.width), BF16),
            pltpu.VMEM((self.out_rows, self.width), BF16),
        ] + [cross] * 2 + [sems] * 2 + [chip_sems] * 2 + [sems] * 2 + [chip_sems] * 2 + [pltpu.SemaphoreType.DMA] * 2

    def at(self, chip, m):
        return pl.ds(pl.multiple_of((chip * self.members + m) * self.block, self.block), self.block)

    def chip_copy(self, s, m):
        other = lax.rem(self.chip + s, self.chips)
        return self.remote(
            self.ins[0].at[self.at(other, m)], self.arrived.at[s, m],
            self.cross_send.at[s, m], self.cross_recv.at[s, m], chip=other,
        )

    def member_copy(self, s):
        core, place = step_member(self.core, self.place, s, self.spans)
        return self.remote(
            self.summed.at[core * self.spans + place], self.columns_in.at[self.me],
            self.member_send.at[s], self.member_recv.at[s], core=core, ctx=place,
        )

    def sums_chip(self, s):
        return self.remote(
            self.ins[1], self.sums_in.at[s], self.sums_send.at[s], self.sums_recv.at[s],
            chip=lax.rem(self.chip + s, self.chips),
        )

    def sums_member(self, s):
        core, place = step_member(self.core, self.place, s, self.spans)
        return self.remote(
            self.sums_chips, self.sums_members.at[self.me], self.last_send.at[s], self.last_recv.at[s],
            core=core, ctx=place,
        )

    def out_copy(self, s):
        other = lax.rem(self.chip + s, self.chips)
        rows = pl.ds(pl.multiple_of(other * self.out_rows, self.out_rows), self.out_rows)
        return self.remote(
            self.ins[2].at[rows], self.out_in.at[s], self.out_send.at[s], self.out_recv.at[s], chip=other
        )

    def move_copy(self):
        chip, core, place = owner_of(self.chip, self.core, self.place, self.spans)
        return self.remote(
            self.out_sum, self.out_final, self.move_send, self.move_recv, chip=chip, core=core, ctx=place
        )

    def square_copy(self, kind, i):
        along_x, along_y, across = square(self.chip)
        m = self.nth(i)
        first, second = (along_x, along_y) if i % 2 == 0 else (along_y, along_x)
        if kind == 2:
            src, to = self.passing.at[m], second
        else:
            src, to = self.ins[0].at[self.at((across, first)[kind], m)], first
        return self.remote(
            src, self.arrived.at[kind, m], self.cross_send.at[kind, m], self.cross_recv.at[kind, m], chip=to
        )

    def nth(self, i):
        return lax.rem(self.me + 1 + i, self.members)

    def pass_blocks(self):
        along_x, along_y, _ = square(self.chip)
        for i in range(self.members):
            m = self.nth(i)
            self.square_copy(0, i).wait_recv()
            mine = self.ins[0][self.at(along_y if i % 2 == 0 else along_x, m), :]
            self.passing[m] = (mine.astype(F32) + self.arrived[0, m].astype(F32)).astype(BF16)
            self.square_copy(2, i).start()

    def begin(self):
        self.locate()
        (
            self.arrived, self.passing, self.summed, self.columns_in, self.sums_in, self.sums_chips, self.sums_members,
            self.out_in, self.out_sum, self.out_final,
            self.cross_send, self.cross_recv, self.member_send, self.member_recv,
            self.sums_send, self.sums_recv, self.last_send, self.last_recv,
            self.out_send, self.out_recv, self.move_send, self.move_recv,
        ) = self.held
        for s in range(1, self.chips):
            self.out_copy(s).start()

    def start(self):
        for s in range(1, self.chips):
            self.sums_chip(s).start()

    def send_shares(self):
        if self.chips == 4:
            for i in range(self.members):
                self.square_copy(0, i).start()
                self.square_copy(1, i).start()
            return

        @pl.loop(0, self.members)
        def _(i):
            m = lax.rem(self.me + 1 + i, self.members)
            for s in range(1, self.chips):
                self.chip_copy(s, m).start()

    def add_block(self, m):
        total = self.ins[0][self.at(self.chip, m), :].astype(F32)
        for s in range(1, 3 if self.chips == 4 else self.chips):
            self.chip_copy(s, m).wait_recv()
            total = total + self.arrived[s, m].astype(F32)
        self.summed[m] = total.astype(BF16)

    def send_blocks(self, first, last):
        for s in range(first, last):
            core, place = step_member(self.core, self.place, s, self.spans)
            self.add_block(core * self.spans + place)
            self.member_copy(s).start()

    def tick(self, t):
        @pl.when(t == 0)
        def _():
            self.work()
            self.send_shares()

        @pl.when(t == LATE_TICK)
        def _():
            self.late()

        if self.chips == 4:

            @pl.when(t == PASS_TICK)
            def _():
                self.pass_blocks()

        @pl.when(t == 1)
        def _():
            total = self.ins[1][...]
            for s in range(1, self.chips):
                self.sums_chip(s).wait_recv()
                total = total + self.sums_in[s]
            self.sums_chips[...] = total
            self.sums_members[self.me] = total
            for s in range(1, self.members):
                self.sums_member(s).start()

        @pl.when(t == 2)
        def _():
            rows = pl.ds(pl.multiple_of(self.chip * self.out_rows, self.out_rows), self.out_rows)
            total = self.ins[2][rows, :].astype(F32)
            for s in range(1, self.chips):
                self.out_copy(s).wait_recv()
                total = total + self.out_in[s].astype(F32)
            self.out_sum[...] = total.astype(BF16)

            @pl.when(stays(self.chip, self.core, self.place, self.spans))
            def _():
                self.out_final[...] = total.astype(BF16)

            @pl.when(jnp.logical_not(stays(self.chip, self.core, self.place, self.spans)))
            def _():
                self.move_copy().start()

    def finish(self, ticks):
        self.send_blocks(1, self.members)
        self.add_block(self.me)
        self.columns_in[self.me] = self.summed[self.me]
        for s in range(1, self.members):
            self.sums_member(s).wait()
        wide = self.width // 128
        for i in range(2):
            total = self.sums_members[0, i * wide : (i + 1) * wide, :]
            for m in range(1, self.members):
                total = total + self.sums_members[m, i * wide : (i + 1) * wide, :]
            self.outs[1][2 + i] = total
            base = 2 * wide + i * self.own_rows
            for m in range(self.members):
                self.outs[1][i, m * self.own_rows : (m + 1) * self.own_rows, :] = self.sums_members[
                    m, base : base + self.own_rows, :
                ]
        for s in range(1, self.members):
            self.member_copy(s).wait()
        for m in range(self.members):
            for i in range(3):
                self.outs[0][:, i * self.width + m * self.part : i * self.width + (m + 1) * self.part] = (
                    self.columns_in[m, :, i * self.part : (i + 1) * self.part].astype(F32)
                )
        @pl.when(jnp.logical_not(stays(self.chip, self.core, self.place, self.spans)))
        def _():
            self.move_copy().wait()

        self.outs[2][...] = self.out_final[...].astype(F32)
        for s in range(1, self.chips):
            self.sums_chip(s).wait_send()
            self.out_copy(s).wait_send()

        @pl.loop(0, self.members)
        def _(m):
            for s in range(3) if self.chips == 4 else range(1, self.chips):
                self.chip_copy(s, m).wait_send()


def rope_tables(positions):
    half = HEAD_DIM // 2
    frequency = ROPE_BASE ** (-(jnp.arange(half, dtype=F32) * 2.0 / HEAD_DIM))
    angles = positions[:, None] * frequency[None, :]
    cosine = jnp.cos(angles)
    sine = jnp.sin(angles)
    return (jnp.concatenate([cosine, cosine], 1), jnp.concatenate([sine, sine], 1))


def dot(left, right):
    return jnp.dot(left, right, preferred_element_type=F32)


def dot_rows(left, right):
    return lax.dot_general(left, right, (((1,), (1,)), ((), ())), preferred_element_type=F32)


def dot_first(left, right):
    return lax.dot_general(left, right, (((0,), (0,)), ((), ())), preferred_element_type=F32)


def gather(values, axes):
    return lax.all_gather(values, axes, axis=0, tiled=True)


def scatter_sum(values, axes):
    return lax.psum_scatter(values, axes, scatter_dimension=0, tiled=True)


FF_TILE = 512
SUM_TILE = 1024
BATCH_PIECE = 16
GRAD_TILE = 256


def square(chip):
    along_x = chip + 1 - 2 * lax.rem(chip, 2)
    return along_x, lax.rem(chip + 2, 4), lax.rem(along_x + 2, 4)


class SquareSum:
    def __init__(self, chip, block, landing, send, recv):
        self.chip, self.block, self.landing, self.send, self.recv = chip, block, landing, send, recv
        self.x, self.y, self.across = square(chip)

    def copy(self, i):
        owner = (self.across, self.across, self.x, self.y, self.y, self.x)[i]
        half = (0, 1, 0, 1, 0, 1)[i]
        to = (self.x, self.y, self.x, self.y, self.y, self.x)[i]
        return pltpu.make_async_remote_copy(
            src_ref=self.block(owner, half), dst_ref=self.landing.at[i], send_sem=self.send.at[i],
            recv_sem=self.recv.at[i], device_id={"chip": to}, device_id_type=MESH_ID,
        )

    def begin(self, first):
        self.copy(first).start()
        self.copy(first + 1).start()

    def relay(self):
        for i, owner, half in ((0, self.y, 0), (1, self.x, 1)):
            self.copy(i).wait_recv()
            ref = self.block(owner, half)
            ref[...] = (ref[...].astype(F32) + self.landing[i].astype(F32)).astype(BF16)
        self.begin(4)

    def finish(self, half):
        for i in (2 + half, 4 + half):
            self.copy(i).wait_recv()
        for i in (0 + half, 2 + half, 4 + half):
            self.copy(i).wait_send()
        total = self.block(self.chip, half)[...].astype(F32)
        return total + self.landing[2 + half].astype(F32) + self.landing[4 + half].astype(F32)


class Middle:
    def __init__(self, spans, rows, width, hidden, piece):
        self.spans, self.rows, self.width, self.hidden, self.piece = spans, rows, width, hidden, piece
        self.count = rows // piece
        self.block = spans * piece
        self.batch = 2 * self.block

    def body(
        self, chips, partial, tokens, cotangent, gains, gate_up_w, down,
        output, residual_grad, gain_feed, gain_attn, down_sum, gate_sum, residual_all, feed_grad_all, gate_part, up_part, projected_all,
        residual, projected, own, near, from_left, from_right, held, wide, act, back, up_weights, down_weights, slices, given, landed,
        load_sem, weight_sem, store_sem, slice_sem, part_sem, free_sem, near_send, near_recv, right_send, right_recv, left_send, left_recv,
        fwd_send, fwd_recv, bwd_send, bwd_recv, side_send, side_recv, down_send, down_recv, give_send, give_recv, take_send, take_recv,
    ):
        spans, rows, piece, count = self.spans, self.rows, self.piece, self.count
        width, hidden, block, batch = self.width, self.hidden, self.block, self.batch
        core = lax.axis_index("core")
        place = lax.axis_index("ctx")
        other = 1 - core
        last = spans - 1
        has_left = place > 0
        has_right = place < last

        def turn_of(o):
            return jnp.maximum(o, last - o)

        def at(d, k):
            return pl.ds(pl.multiple_of((k * spans + d) * piece, piece), piece)

        def at_seq(seq, d, k):
            return pl.ds(pl.multiple_of(((k * 2 + seq) * spans + d) * piece, piece), piece)

        def batch_at(k):
            return pl.ds(pl.multiple_of(k * batch, batch), batch)

        def natural(seq, d, k):
            return pl.ds(pl.multiple_of((seq * spans + d) * rows + k * piece, piece), piece)

        def remote(src, dst, send, recv, **device):
            return pltpu.make_async_remote_copy(
                src_ref=src, dst_ref=dst, send_sem=send, recv_sem=recv, device_id=device, device_id_type=MESH_ID
            )

        barrier = pltpu.get_barrier_semaphore()
        pl.semaphore_signal(barrier, 1, device_id={"core": other}, device_id_type=MESH_ID)

        @pl.when(has_left)
        def _():
            pl.semaphore_signal(barrier, 1, device_id={"ctx": place - 1}, device_id_type=MESH_ID)

        @pl.when(has_right)
        def _():
            pl.semaphore_signal(barrier, 1, device_id={"ctx": place + 1}, device_id_type=MESH_ID)

        def near_copy(e, d, k):
            src = partial.at[natural(other, d, k)] if e == 0 else own.at[at_seq(other, d, k)]
            return remote(src, near.at[at(d, k)], near_send.at[d, k], near_recv.at[d, k], core=other)

        def right_copy(d, k):
            return remote(
                own.at[at_seq(core, d, k)], from_left.at[at(d, k)], right_send.at[d, k], right_recv.at[d, k],
                ctx=place + 1,
            )

        def left_copy(d, k):
            return remote(
                own.at[at_seq(core, d, k)], from_right.at[at(d, k)], left_send.at[d, k], left_recv.at[d, k],
                ctx=place - 1,
            )

        def spread_copy(o, k, send, recv, **device):
            where = held.at[at_seq(core, o, k)]
            return remote(where, where, send.at[o, k], recv.at[o, k], **device)

        def fwd_copy(o, k):
            return spread_copy(o, k, fwd_send, fwd_recv, ctx=place + 1)

        def bwd_copy(o, k):
            return spread_copy(o, k, bwd_send, bwd_recv, ctx=place - 1)

        def side_copy(o, k):
            return spread_copy(o, k, side_send, side_recv, core=other)

        def load_own(d, k):
            return pltpu.make_async_copy(
                partial.at[natural(core, d, k)], own.at[at_seq(core, d, k)], load_sem.at[d, k]
            )

        @pl.loop(0, count)
        def _(k):
            for d in range(spans):
                load_own(d, k).start()

        load_up = pltpu.make_async_copy(gate_up_w, up_weights, weight_sem.at[0])
        chip = lax.axis_index("chip")
        shard = down.shape[0]
        here = pl.ds(pl.multiple_of(chip * shard, shard), shard)
        load_down = pltpu.make_async_copy(down, down_weights.at[here], weight_sem.at[1])

        if chips == 4:
            along_x, along_y, across = square(chip)

        def down_copy(s):
            if chips != 4:
                return remote(
                    down, down_weights.at[here], down_send.at[s], down_recv.at[s], chip=lax.rem(chip + s, chips)
                )
            half = (0, 1, 1, 0, 0, 1)[s]
            to = (along_x, along_y, along_x, along_y, along_y, along_x)[s]
            size = shard // 2
            if s < 4:
                src = down.at[half * size : (half + 1) * size]
                at_chip = chip
            else:
                at_chip = (along_x, along_y)[s - 4]
            dst = down_weights.at[pl.ds(pl.multiple_of(at_chip * shard + half * size, size), size)]
            return remote(src if s < 4 else dst, dst, down_send.at[s], down_recv.at[s], chip=to)

        def relay_down():
            for s in range(2):
                down_copy(s).wait_recv()
                down_copy(4 + s).start()

        load_up.start()
        load_down.start()
        gain_feed[...] = jnp.zeros_like(gain_feed)
        gain_attn[...] = jnp.zeros_like(gain_attn)
        for s in range(1, chips):
            pl.semaphore_signal(
                barrier, 1, device_id={"chip": lax.rem(chip + s, chips)}, device_id_type=MESH_ID
            )
        pl.semaphore_wait(barrier, chips + has_left.astype(jnp.int32) + has_right.astype(jnp.int32))
        for s in range(4) if chips == 4 else range(1, chips):
            down_copy(s).start()

        @pl.loop(0, count)
        def _(k):
            for d in range(spans):
                near_copy(0, d, k).start()

        def base(e, d, k):
            near_copy(e, d, k).wait_recv()
            if e == 0:
                load_own(d, k).wait()
            return own[at_seq(core, d, k), :].astype(F32) + near[at(d, k), :].astype(F32)

        def pass_on(e, d, k, arrived, copy, later):
            value = base(e, d, k)

            @pl.when(later)
            def _():
                copy(d, k).wait_recv()

            before = arrived[at(d, k), :].astype(F32)
            value = value + jnp.where(later, before, jnp.zeros_like(before))
            own[at_seq(core, d, k), :] = value.astype(BF16)
            copy(d, k).start()

        def pass_right(e, k):
            for d in range(last, 0, -1):

                @pl.when(d > place)
                def _():
                    pass_on(e, d, k, from_left, right_copy, has_left)

        def pass_left(e, k):
            for d in range(last):

                @pl.when(d < place)
                def _():
                    pass_on(e, d, k, from_right, left_copy, has_right)

        def finish(e, k):
            total = base(e, place, k)

            @pl.when(has_left)
            def _():
                right_copy(place, k).wait_recv()

            @pl.when(has_right)
            def _():
                left_copy(place, k).wait_recv()

            zero = jnp.zeros_like(total)
            total = total + jnp.where(has_left, from_left[at(place, k), :].astype(F32), zero)
            total = total + jnp.where(has_right, from_right[at(place, k), :].astype(F32), zero)
            mine = pl.ds(pl.multiple_of(k * piece, piece), piece)
            if e == 0:
                result = after_projected(total, (tokens, gains), (residual, projected), mine)
            elif e == 1:
                result = after_feed(total, (residual, cotangent, gains), (output, gain_feed), mine)
            else:
                result = after_back(total, (projected, cotangent, gains), (residual_grad, gain_attn), mine)
            held[at_seq(core, place, k), :] = result.astype(BF16)

            @pl.when(has_right)
            def _():
                fwd_copy(place, k).start()

            @pl.when(has_left)
            def _():
                bwd_copy(place, k).start()

            side_copy(place, k).start()

        def relay_right(o, k):
            fwd_copy(o, k).wait_recv()

            @pl.when(has_right)
            def _():
                fwd_copy(o, k).start()

            side_copy(o, k).start()

        def relay_left(o, k):
            bwd_copy(o, k).wait_recv()

            @pl.when(has_left)
            def _():
                bwd_copy(o, k).start()

            side_copy(o, k).start()

        def gathered(k):
            for o in range(spans):
                side_copy(o, k).wait_recv()

        def sums_sent(e, k):
            for d in range(spans):
                near_copy(e, d, k).wait_send()

                @pl.when(d > place)
                def _():
                    right_copy(d, k).wait_send()

                @pl.when(d < place)
                def _():
                    left_copy(d, k).wait_send()

        def spread_sent(k):
            for o in range(spans):
                side_copy(o, k).wait_send()

                @pl.when(jnp.logical_and(o <= place, has_right))
                def _():
                    fwd_copy(o, k).wait_send()

                @pl.when(jnp.logical_and(o >= place, has_left))
                def _():
                    bwd_copy(o, k).wait_send()

        def store(src, dst, k, sem):
            return pltpu.make_async_copy(src, dst.at[batch_at(k)], sem)

        def forward(k):
            @pl.when(k == 0)
            def _():
                load_up.wait()
                load_down.wait()
                for s in range(1, chips) if chips != 4 else range(6):
                    down_copy(s).wait_send()
                    if chips != 4 or s >= 2:
                        down_copy(s).wait_recv()

            gathered(k)
            keep = store(held.at[batch_at(k)], residual_all, k, store_sem.at[0])
            keep.start()

            @pl.loop(0, hidden // FF_TILE)
            def _(n):
                low = pl.ds(pl.multiple_of(n * FF_TILE, FF_TILE), FF_TILE)
                high = pl.ds(pl.multiple_of(hidden + n * FF_TILE, FF_TILE), FF_TILE)
                gate = dot(held[batch_at(k), :], up_weights[:, low])
                up = dot(held[batch_at(k), :], up_weights[:, high])
                wide[batch_at(k), low] = gate
                wide[batch_at(k), high] = up
                act[batch_at(k), low] = (gate * (1.0 / (1.0 + jnp.exp(-gate))) * up).astype(BF16)

            sums_sent(0, k)

            @pl.loop(0, width // SUM_TILE)
            def _(n):
                columns = pl.ds(pl.multiple_of(n * SUM_TILE, SUM_TILE), SUM_TILE)
                own[batch_at(k), columns] = dot_rows(act[batch_at(k), :], down_weights[columns, :]).astype(BF16)

            keep.wait()
            spread_sent(k)
            for d in range(spans):
                near_copy(1, d, k).start()

        down_tiles = width // GRAD_TILE
        per_chip = shard // GRAD_TILE

        def tile_rows(n):
            return pl.ds(pl.multiple_of(n * GRAD_TILE, GRAD_TILE), GRAD_TILE)

        if chips == 4:
            assert per_chip == 2
            turns = [(across, 0), (across, 1), (along_x, 0), (along_y, 1), (along_y, 0), (along_x, 1), (chip, 0), (chip, 1)]
            order = [owner * per_chip + half for owner, half in turns]
        else:
            order = [lax.rem(chip + 1 + j // per_chip, chips) * per_chip + j % per_chip for j in range(down_tiles)]
        tiles = [(m, order[j] if m < 2 else j) for m in range(3) for j in range(down_tiles)]

        def load_slice(j):
            m, n = tiles[j]
            source = feed_grad_all if m == 0 else residual_all
            return pltpu.make_async_copy(source.at[:, tile_rows(n)], slices.at[j % 4], slice_sem.at[j % 4])

        def half_at(owner, half):
            return pl.ds(pl.multiple_of((owner * per_chip + half) * GRAD_TILE, GRAD_TILE), GRAD_TILE)

        if chips == 4:
            sums = [
                SquareSum(
                    chip, lambda owner, half: given.at[half_at(owner, half)], landed.at[0], give_send, give_recv
                ),
                SquareSum(
                    chip, lambda owner, half: up_weights.at[half_at(owner, half), :hidden], landed.at[1], take_send, take_recv
                ),
            ]

        def give_copy(s):
            theirs = pl.ds(pl.multiple_of(lax.rem(chip + s, chips) * shard, shard), shard)
            return remote(
                given.at[theirs], down_weights.at[s * shard : (s + 1) * shard], give_send.at[s], give_recv.at[s],
                chip=lax.rem(chip + s, chips),
            )

        def part_copy(n, m):
            half = slice((m - 1) * hidden, m * hidden)
            return pltpu.make_async_copy(
                up_weights.at[tile_rows(n), half], (gate_part, up_part)[m - 1].at[tile_rows(n)], part_sem.at[m - 1, n]
            )

        def work_out(j):
            if j + 2 < len(tiles):
                load_slice(j + 2).start()
            load_slice(j).wait()
            m, n = tiles[j]
            if m == 0:
                given[tile_rows(n), :] = dot_first(slices[j % 4], act[...]).astype(BF16)
            else:
                half = slice((m - 1) * hidden, m * hidden)
                up_weights[tile_rows(n), half] = dot_first(slices[j % 4], back[:, half]).astype(BF16)

        def weight_grads(q):
            if chips == 4:
                m, r = q // 4, q % 4
                if m < 2:
                    for j in range(m * down_tiles + 2 * r, m * down_tiles + 2 * r + 2):
                        work_out(j)
                    if r < 2:
                        sums[m].begin(2 * r)
                    elif r == 2:
                        sums[m].relay()
                else:
                    for j in range(2 * down_tiles, 3 * down_tiles):
                        work_out(j)
                        part_copy(tiles[j][1], 2).start()
                return
            if q < chips:
                for j in range(q * per_chip, (q + 1) * per_chip):
                    work_out(j)
                if q == 0:
                    pl.semaphore_wait(free_sem, chips - 1)
                if q < chips - 1:
                    give_copy(q + 1).start()
                return
            first = down_tiles + 4 * (q - chips)
            for j in range(first, min(first + 4, len(tiles))):
                work_out(j)
                part_copy(tiles[j][1], tiles[j][0]).start()

        def backward(k):
            gathered(k)
            keep = store(held.at[batch_at(k)], feed_grad_all, k, store_sem.at[0])
            keep.start()

            @pl.loop(0, hidden // FF_TILE)
            def _(n):
                low = pl.ds(pl.multiple_of(n * FF_TILE, FF_TILE), FF_TILE)
                high = pl.ds(pl.multiple_of(hidden + n * FF_TILE, FF_TILE), FF_TILE)
                act_grad = dot(held[batch_at(k), :], down_weights[:, low])
                gate = wide[batch_at(k), low]
                up = wide[batch_at(k), high]
                sigmoid = 1.0 / (1.0 + jnp.exp(-gate))
                back[batch_at(k), low] = (act_grad * up * sigmoid * (1.0 + gate * (1.0 - sigmoid))).astype(BF16)
                back[batch_at(k), high] = (act_grad * (gate * sigmoid)).astype(BF16)

            sums_sent(1, k)

            @pl.loop(0, width // SUM_TILE)
            def _(n):
                columns = pl.ds(pl.multiple_of(n * SUM_TILE, SUM_TILE), SUM_TILE)
                own[batch_at(k), columns] = dot_rows(back[batch_at(k), :], up_weights[columns, :]).astype(BF16)

            keep.wait()
            spread_sent(k)
            for d in range(spans):
                near_copy(2, d, k).start()

            @pl.when(k == count - 1)
            def _():
                for s in range(1, chips) if chips != 4 else ():
                    pl.semaphore_signal(
                        free_sem, 1, device_id={"chip": lax.rem(chip + s, chips)}, device_id_type=MESH_ID
                    )
                load_slice(0).start()
                load_slice(1).start()

        def give(seq, d, k):
            return pltpu.make_async_copy(
                held.at[at_seq(seq, d, k)], projected_all.at[natural(seq, d, k)], load_sem.at[d, k]
            )

        def hand_out(k):
            gathered(k)
            sums_sent(2, k)
            for seq in range(2):
                for d in range(spans):
                    give(seq, d, k).start()
                for d in range(spans):
                    give(seq, d, k).wait()
            spread_sent(k)

        step = 2 * last + 2
        last_steps = 9 if chips == 4 else chips + down_tiles // 2
        assert last_steps <= step + 1

        def due(t, run):
            @pl.when(jnp.logical_and(t >= 0, t < count))
            def _():
                run(t)

        @pl.loop(0, 3 * step + count - 1)
        def _(t):
            for e in range(2, -1, -1):
                now = t - e * step
                for j in range(1, spans):
                    o = place - j

                    @pl.when(o >= 0)
                    def _():
                        due(now - turn_of(o) - j, functools.partial(relay_right, o))

                    p = place + j

                    @pl.when(p < spans)
                    def _():
                        due(now - turn_of(p) - j, functools.partial(relay_left, p))

                due(now - place, functools.partial(pass_right, e))
                due(now - (last - place), functools.partial(pass_left, e))
                due(now - turn_of(place), functools.partial(finish, e))
            if chips == 4:

                @pl.when(t == 2 * last - 2)
                def _():
                    relay_down()

            for e, run in ((2, hand_out), (1, backward), (0, forward)):
                due(t - e * step - 2 * last, run)
            for q in range(last_steps):

                @pl.when(t == count + step + 2 * last + q)
                def _():
                    weight_grads(q)

        if chips == 4:
            for group, out in zip(sums, (down_sum, gate_sum)):
                for half in range(2):
                    out[half * GRAD_TILE : (half + 1) * GRAD_TILE, :] = group.finish(half).astype(BF16)
            for n in range(down_tiles):
                part_copy(n, 2).wait()
            return
        total = given[here, :].astype(F32)
        for s in range(1, chips):
            give_copy(s).wait()
            total = total + down_weights[s * shard : (s + 1) * shard, :].astype(F32)
        down_sum[...] = total.astype(BF16)
        gate_sum[...] = jnp.zeros_like(gate_sum)
        for n in range(down_tiles):
            part_copy(n, 1).wait()
            part_copy(n, 2).wait()

    def call(self, chips, partial, tokens, cotangent, gains, gate_up_w, down):
        spans, rows, width, hidden, count = self.spans, self.rows, self.width, self.hidden, self.count
        total = 2 * spans * rows
        vmem = pl.BlockSpec(memory_space=pltpu.VMEM)
        hbm = pl.BlockSpec(memory_space=pl.ANY)
        shape = jax.ShapeDtypeStruct
        sems = pltpu.SemaphoreType.DMA((spans, count))
        two = pltpu.SemaphoreType.DMA((2,))
        return pl.pallas_call(
            functools.partial(self.body, chips),
            out_shape=[
                shape((rows, width), BF16),
                shape((rows, width), F32),
                shape((1, width), F32),
                shape((1, width), F32),
                shape(down.shape, BF16),
                shape(down.shape, BF16),
                shape((total, width), BF16),
                shape((total, width), BF16),
                shape((16, 128) if chips == 4 else (width, hidden), BF16),
                shape((width, hidden), BF16),
                shape((total, width), BF16),
            ],
            in_specs=[hbm, vmem, vmem, vmem, hbm, hbm],
            out_specs=[vmem] * 6 + [hbm] * 5,
            scratch_shapes=[
                pltpu.VMEM((rows, width), F32),
                pltpu.VMEM((rows, width), F32),
                pltpu.VMEM((total, width), BF16),
                pltpu.VMEM((total // 2, width), BF16),
                pltpu.VMEM((total // 2, width), BF16),
                pltpu.VMEM((total // 2, width), BF16),
                pltpu.VMEM((total, width), BF16),
                pltpu.VMEM((total, 2 * hidden), F32),
                pltpu.VMEM((total, hidden), BF16),
                pltpu.VMEM((total, 2 * hidden), BF16),
                pltpu.VMEM((width, 2 * hidden), BF16),
                pltpu.VMEM((width, hidden), BF16),
                pltpu.VMEM((4, total, GRAD_TILE), BF16),
                pltpu.VMEM((width, hidden), BF16),
                pltpu.VMEM((2, 6, GRAD_TILE, hidden) if chips == 4 else (2, 6, 16, 128), BF16),
                sems,
                two,
                two,
                pltpu.SemaphoreType.DMA((4,)),
                pltpu.SemaphoreType.DMA((2, width // GRAD_TILE)),
                pltpu.SemaphoreType.REGULAR,
            ]
            + [sems] * 12
            + [pltpu.SemaphoreType.DMA((max(chips, 6),))] * 6,
            compiler_params=pltpu.CompilerParams(
                collective_id=2, has_side_effects=True, vmem_limit_bytes=62 << 20
            ),
            cost_estimate=pl.CostEstimate(
                flops=36 * rows * spans * width * hidden, bytes_accessed=100 * width * width, transcendentals=0
            ),
            name="feed_forward",
        )(partial, tokens, cotangent, gains, gate_up_w, down)


def turn(values, cosine, sine):
    return values * cosine + pltpu.roll(values, HEAD_DIM // 2, 1) * sine


def row_sums(values):
    total = values[:, :128]
    for first in range(128, values.shape[1], 128):
        total = total + values[:, first : first + 128]
    return jnp.sum(jnp.transpose(total), axis=0, keepdims=True)


def down_rows(row):
    return jnp.transpose(jnp.broadcast_to(row, (128, row.shape[1])))


class Stats:
    def __init__(self, spans, own, arrived, send, recv):
        self.spans, self.own, self.arrived, self.send, self.recv = spans, own, arrived, send, recv
        self.core, self.place = lax.axis_index("core"), lax.axis_index("ctx")
        self.me = self.core * spans + self.place

    def member(self, s):
        core, place = step_member(self.core, self.place, s, self.spans)
        return {"core": core, "ctx": place}

    def greet(self):
        for s in range(1, 2 * self.spans):
            pl.semaphore_signal(
                pltpu.get_barrier_semaphore(), 1, device_id=self.member(s), device_id_type=MESH_ID
            )

    def meet(self):
        pl.semaphore_wait(pltpu.get_barrier_semaphore(), 2 * self.spans - 1)

    def copy(self, s):
        return pltpu.make_async_remote_copy(
            src_ref=self.own, dst_ref=self.arrived.at[s], send_sem=self.send.at[s], recv_sem=self.recv.at[s],
            device_id=self.member(s), device_id_type=MESH_ID,
        )

    def start(self):
        for s in range(1, 2 * self.spans):
            self.copy(s).start()

    def total(self):
        total = self.own[...]
        for s in range(1, 2 * self.spans):
            self.copy(s).wait()
            total = total + self.arrived[s]
        return total


def stats_scratch(spans, total_rows):
    sems = pltpu.SemaphoreType.DMA((2 * spans,))
    return [
        pltpu.VMEM((8, total_rows), F32),
        pltpu.VMEM((2 * spans, 8, total_rows), F32),
        sems,
        sems,
    ]


def allowed_at(ids, seq, block, count, spans):
    rows = ids.shape[1]
    per = block // rows
    ids_of = lambda z: ids[(seq * spans + z) * 8 : (seq * spans + z) * 8 + 8, :].astype(F32)
    first = count * per
    keys = jnp.concatenate([ids_of(z)[:1] for z in range(first + per)], 1)
    queries = jnp.concatenate([jnp.transpose(ids_of(z))[:, :1] for z in range(first, first + per)], 0)
    shape = (block, (count + 1) * block)
    query_at = lax.broadcasted_iota(jnp.int32, shape, 0) + count * block
    key_at = lax.broadcasted_iota(jnp.int32, shape, 1)
    same = queries == keys
    seen = jnp.logical_and(same, key_at <= query_at)
    return jnp.logical_and(seen, jnp.logical_or(keys != 0.0, key_at == query_at))


def softmax_parts(query, key, allowed):
    scores = jnp.where(allowed, dot_rows(query, key) * HEAD_DIM ** (-0.5), -1e30)
    weights = jnp.exp(scores - jnp.max(scores, axis=1, keepdims=True))
    return weights / jnp.sum(weights, axis=1, keepdims=True)


QUERY_BLOCK = 256
ROW_TILE = 256


def attend_body(
    spans, chips, tokens, weights, out_rows, gains, ids, cosine, sine,
    partial_out, out_w_out, query_out, key_out, value_out, normed_out, factor_out, attended_out,
    held, held_w, raw, given, out_w, own, arrived, load_sem, store_sem, chip_send, chip_recv, send, recv,
):
    part = out_w.shape[0]
    total_rows = raw.shape[0]
    length = total_rows // 2
    width = tokens.shape[1]
    tiles = total_rows // ROW_TILE
    stats = Stats(spans, own, arrived, send, recv)
    stats.greet()
    chip = lax.axis_index("chip")
    shard = out_rows.shape[0]
    here = pl.ds(pl.multiple_of(chip * shard, shard), shard)

    def chip_copy(s):
        return pltpu.make_async_remote_copy(
            src_ref=out_rows, dst_ref=out_w.at[here], send_sem=chip_send.at[s], recv_sem=chip_recv.at[s],
            device_id={"chip": lax.rem(chip + s, chips)}, device_id_type=MESH_ID,
        )

    for s in range(1, chips):
        pl.semaphore_signal(
            pltpu.get_barrier_semaphore(), 1, device_id={"chip": lax.rem(chip + s, chips)}, device_id_type=MESH_ID
        )
    out_w[here, :] = out_rows[...]

    def at(i):
        return pl.ds(pl.multiple_of(i * ROW_TILE, ROW_TILE), ROW_TILE)

    def load_rows(i):
        return pltpu.make_async_copy(tokens.at[at(i)], held.at[at(i)], load_sem.at[i])

    own[...] = jnp.zeros_like(own)
    load_w = pltpu.make_async_copy(weights, held_w, load_sem.at[tiles])
    load_w.start()

    @pl.loop(0, tiles)
    def _(i):
        load_rows(i).start()

    pl.semaphore_wait(pltpu.get_barrier_semaphore(), 2 * spans - 1 + chips - 1)
    for s in range(1, chips):
        chip_copy(s).start()
    load_w.wait()

    @pl.loop(0, tiles)
    def _(i):
        load_rows(i).wait()
        values = dot(held[at(i), :], held_w[...])
        raw[at(i), :] = values
        for n in range(2):
            some = values[:, n * part : (n + 1) * part]
            own[n : n + 1, at(i)] = row_sums(some * some)

    stats.start()

    @pl.loop(0, tiles)
    def _(i):
        value_out[at(i), :] = raw[at(i), 2 * part :].astype(BF16)

    factor_out[...] = lax.rsqrt(stats.total() / width + EPS)
    me = stats.me
    columns = pl.ds(pl.multiple_of(me * part, part), part)
    gain = jnp.concatenate([gains[0:1, columns], gains[1:2, columns]], 1)

    @pl.loop(0, tiles)
    def _(i):
        by_query, by_key = down_rows(factor_out[0:1, at(i)]), down_rows(factor_out[1:2, at(i)])
        place = pl.ds(pl.multiple_of(lax.rem(i, length // ROW_TILE) * ROW_TILE, ROW_TILE), ROW_TILE)
        for h in range(part // HEAD_DIM):
            head = slice(h * HEAD_DIM, (h + 1) * HEAD_DIM)
            low = slice(part + h * HEAD_DIM, part + (h + 1) * HEAD_DIM)
            for out, by, where in ((query_out, by_query, head), (key_out, by_key, low)):
                normed = raw[at(i), where] * by
                normed_out[at(i), where] = normed
                out[at(i), head] = turn(normed * gain[:, where], cosine[place, :], sine[place, :]).astype(BF16)

    for s in range(1, chips):
        chip_copy(s).wait()
    out_w_out[...] = out_w[...]
    block = QUERY_BLOCK
    for seq in range(2):
        for count in range(length // block):
            allowed = allowed_at(ids, seq, block, count, spans)
            rows = slice(seq * length + count * block, seq * length + (count + 1) * block)
            keys = slice(seq * length, seq * length + (count + 1) * block)
            for h in range(part // HEAD_DIM):
                head = slice(h * HEAD_DIM, (h + 1) * HEAD_DIM)
                shares = softmax_parts(query_out[rows, head], key_out[keys, head], allowed)
                attended_out[rows, head] = dot(shares.astype(BF16), value_out[keys, head]).astype(BF16)
            i = rows.start // ROW_TILE
            if i >= 2:
                pltpu.make_async_copy(given.at[i % 2], partial_out.at[at(i - 2)], store_sem.at[i - 2]).wait()
            given[i % 2] = dot(attended_out[rows, :], out_w[...]).astype(BF16)
            pltpu.make_async_copy(given.at[i % 2], partial_out.at[at(i)], store_sem.at[i]).start()
    for i in range(tiles - 2, tiles):
        pltpu.make_async_copy(given.at[i % 2], partial_out.at[at(i)], store_sem.at[i]).wait()


def attend(spans, chips, tokens, weights, out_rows, gains, ids, cosine, sine):
    total_rows, width = tokens.shape
    part = out_rows.shape[0] * chips
    tiles = total_rows // ROW_TILE
    vmem = pl.BlockSpec(memory_space=pltpu.VMEM)
    hbm = pl.BlockSpec(memory_space=pl.ANY)
    shape = jax.ShapeDtypeStruct
    return pl.pallas_call(
        functools.partial(attend_body, spans, chips),
        out_shape=[
            shape((total_rows, width), BF16),
            shape((part, width), BF16),
            shape((total_rows, part), BF16),
            shape((total_rows, part), BF16),
            shape((total_rows, part), BF16),
            shape((total_rows, 2 * part), F32),
            shape((8, total_rows), F32),
            shape((total_rows, part), BF16),
        ],
        in_specs=[hbm, hbm] + [vmem] * 5,
        out_specs=[hbm] + [vmem] * 7,
        scratch_shapes=[
            pltpu.VMEM((total_rows, width), BF16),
            pltpu.VMEM(weights.shape, BF16),
            pltpu.VMEM((total_rows, 3 * part), F32),
            pltpu.VMEM((2, ROW_TILE, width), BF16),
            pltpu.VMEM((part, width), BF16),
            *stats_scratch(spans, total_rows)[:2],
            pltpu.SemaphoreType.DMA((tiles + 1,)),
            pltpu.SemaphoreType.DMA((tiles,)),
            pltpu.SemaphoreType.DMA((chips,)),
            pltpu.SemaphoreType.DMA((chips,)),
            *stats_scratch(spans, total_rows)[2:],
        ],
        compiler_params=pltpu.CompilerParams(collective_id=8, has_side_effects=True, vmem_limit_bytes=56 << 20),
        cost_estimate=pl.CostEstimate(flops=2 * total_rows * width * 5 * part, bytes_accessed=0, transcendentals=0),
        name="attend",
    )(tokens, weights, out_rows, gains, ids, cosine, sine)


def attend_back_body(
    spans, chips, exchange, extra, n_scratch,
    grads, tokens, weights, up_part, out_w, gains, ids, cosine, sine, residual_grad, gain_attn, gain_feed,
    query, key, value, normed, factor, attended,
    input_grad, grad_qkv, grad_gains, grad_out, up_sum,
    held, held_tokens, held_w, raw, mixed, attended_grad, own, arrived, load_sem, send, recv,
    qkv_part, out_part, sums, up_held, up_landed, up_send, up_recv, *rest,
):
    part = out_w.shape[0]
    total_rows = raw.shape[0]
    length = total_rows // 2
    width = grads.shape[1]
    tiles = total_rows // ROW_TILE
    scale = HEAD_DIM ** (-0.5)
    stats = Stats(spans, own, arrived, send, recv)
    greet_all(spans, True)

    def at(i):
        return pl.ds(pl.multiple_of(i * ROW_TILE, ROW_TILE), ROW_TILE)

    def load_rows(i):
        return pltpu.make_async_copy(grads.at[at(i)], held.at[at(i)], load_sem.at[i])

    @pl.loop(0, tiles)
    def _(i):
        load_rows(i).start()

    own[...] = jnp.zeros_like(own)
    load_w = pltpu.make_async_copy(weights, held_w, load_sem.at[tiles])
    load_tokens = pltpu.make_async_copy(tokens, held_tokens, load_sem.at[tiles + 1])
    load_w.start()
    load_tokens.start()
    if chips == 4:
        load_up = pltpu.make_async_copy(up_part, up_held, load_sem.at[tiles + 2])
        load_up.start()
    me = stats.me
    columns = pl.ds(pl.multiple_of(me * part, part), part)
    gain = jnp.concatenate([gains[0:1, columns], gains[1:2, columns]], 1)

    @pl.loop(0, tiles)
    def _(i):
        load_rows(i).wait()
        attended_grad[at(i), :] = dot_rows(held[at(i), :], out_w[...]).astype(BF16)

    out_part[...] = dot_first(attended[...], held[...]).astype(BF16)
    wait_all(spans, True)
    extra.ins = [qkv_part, sums, out_part]
    extra.held = list(rest[n_scratch:])
    extra.begin()
    if chips == 4:
        load_up.wait()
        half_rows = width // 8
        up_sums = SquareSum(
            lax.axis_index("chip"),
            lambda owner, half: up_held.at[
                pl.ds(pl.multiple_of((owner * 2 + half) * half_rows, half_rows), half_rows)
            ],
            up_landed, up_send, up_recv,
        )
        up_sums.begin(0)
        up_sums.begin(2)
    block = QUERY_BLOCK
    blocks = length // block
    for seq in range(2):
        for h in range(part // HEAD_DIM):
            head = slice(h * HEAD_DIM, (h + 1) * HEAD_DIM)
            key_at = slice(part + h * HEAD_DIM, part + (h + 1) * HEAD_DIM)
            value_at = slice(2 * part + h * HEAD_DIM, 2 * part + (h + 1) * HEAD_DIM)
            for count in reversed(range(blocks)):
                allowed = allowed_at(ids, seq, block, count, spans)
                rows = slice(seq * length + count * block, seq * length + (count + 1) * block)
                keys = slice(seq * length, seq * length + (count + 1) * block)
                shares = softmax_parts(query[rows, head], key[keys, head], allowed)
                share_grad = dot_rows(attended_grad[rows, head], value[keys, head])
                inner = jnp.sum(shares * share_grad, axis=1, keepdims=True)
                score_grad = (shares * (share_grad - inner)).astype(BF16)
                raw[rows, head] = dot(score_grad, key[keys, head]) * scale
                key_grad = dot_first(score_grad, query[rows, head]) * scale
                value_grad = dot_first(shares.astype(BF16), attended_grad[rows, head])
                if count == blocks - 1:
                    raw[keys, key_at] = key_grad
                    raw[keys, value_at] = value_grad
                else:
                    raw[keys, key_at] += key_grad
                    raw[keys, value_at] += value_grad

    gain_rows = jnp.zeros((1, 2 * part), F32)

    for i in range(tiles):
        place = slice(i * ROW_TILE % length, i * ROW_TILE % length + ROW_TILE)
        for h in range(2 * part // HEAD_DIM):
            head = slice(h * HEAD_DIM, (h + 1) * HEAD_DIM)
            raw[at(i), head] = turn(raw[at(i), head], cosine[place, :], -sine[place, :])
        terms = raw[at(i), : 2 * part] * normed[at(i), :]
        gain_rows = gain_rows + jnp.sum(terms, axis=0, keepdims=True)
        for n in range(2):
            own[n : n + 1, at(i)] = row_sums((terms * gain)[:, n * part : (n + 1) * part])
        mixed[at(i), 2 * part :] = raw[at(i), 2 * part :].astype(BF16)

    stats.start()
    wide = width // 128
    for n in range(wide):
        column = slice(n * 128, (n + 1) * 128)
        sums[n : n + 1, :] = gain_attn[:, column]
        sums[wide + n : wide + n + 1, :] = gain_feed[:, column]
    for n in range(2 * part // 128):
        sums[2 * wide + n : 2 * wide + n + 1, :] = gain_rows[:, n * 128 : (n + 1) * 128]
    own[...] = stats.total() / width

    @pl.loop(0, tiles)
    def _(i):
        for n in range(2):
            mean, by = down_rows(own[n : n + 1, at(i)]), down_rows(factor[n : n + 1, at(i)])
            for first in range(n * part, (n + 1) * part, 128):
                where = slice(first, first + 128)
                back = gain[:, where] * raw[at(i), where] - normed[at(i), where] * mean
                mixed[at(i), where] = (by * back).astype(BF16)

    load_w.wait()

    @pl.loop(0, tiles)
    def _(i):
        held[at(i), :] = dot_rows(mixed[at(i), :], held_w[...]).astype(BF16)

    load_tokens.wait()

    def work():
        @pl.loop(0, width // ROW_TILE)
        def _(i):
            qkv_part[at(i), :] = dot_first(held_tokens[:, at(i)], mixed[...]).astype(BF16)

    extra.work = work
    extra.late = up_sums.relay if chips == 4 else (lambda: None)
    exchange.body(
        held, residual_grad, qkv_part, sums, out_part, input_grad, grad_qkv, grad_gains, grad_out, *rest
    )
    if chips == 4:
        for half in range(2):
            up_sum[half * half_rows : (half + 1) * half_rows, :] = up_sums.finish(half).astype(BF16)


def attend_back(
    spans, chips, rows, grads, tokens, weights, up_part, out_w, gains, ids, cosine, sine, residual_grad, gain_attn,
    gain_feed, saved,
):
    total_rows, width = tokens.shape
    part = out_w.shape[0]
    members = width // part
    hidden = up_part.shape[1]
    tiles = total_rows // ROW_TILE
    vmem = pl.BlockSpec(memory_space=pltpu.VMEM)
    hbm = pl.BlockSpec(memory_space=pl.ANY)
    shape = jax.ShapeDtypeStruct
    sum_rows = (2 * width + 2 * part) // 128
    sum_rows += -sum_rows % 8
    extra = QkvGrads(
        spans, chips, members, shape((width, 3 * part), BF16), shape((sum_rows, 128), F32), shape((part, width), BF16)
    )
    exchange = Exchange(spans, rows, width, SUM_PIECE, True, False, after_input, 1, 1, None, extra)
    scratch = exchange.scratch()
    square_in = chips == 4
    return pl.pallas_call(
        functools.partial(attend_back_body, spans, chips, exchange, extra, len(scratch) - len(extra.scratch())),
        out_shape=[
            shape((rows, width), F32),
            *extra.out_shapes,
            shape((width // chips, hidden) if square_in else (16, 128), BF16),
        ],
        in_specs=[hbm] * 4 + [vmem] * (8 + len(saved)),
        out_specs=[vmem] * 5,
        scratch_shapes=[
            pltpu.VMEM((total_rows, width), BF16),
            pltpu.VMEM((total_rows, width), BF16),
            pltpu.VMEM(weights.shape, BF16),
            pltpu.VMEM((total_rows, 3 * part), F32),
            pltpu.VMEM((total_rows, 3 * part), BF16),
            pltpu.VMEM((total_rows, part), BF16),
            *stats_scratch(spans, total_rows)[:2],
            pltpu.SemaphoreType.DMA((tiles + 3,)),
            *stats_scratch(spans, total_rows)[2:],
            pltpu.VMEM((width, 3 * part), BF16),
            pltpu.VMEM((part, width), BF16),
            pltpu.VMEM((sum_rows, 128), F32),
            pltpu.VMEM((width, hidden) if square_in else (16, 128), BF16),
            pltpu.VMEM((6, width // 8, hidden) if square_in else (6, 16, 128), BF16),
            pltpu.SemaphoreType.DMA((6,)),
            pltpu.SemaphoreType.DMA((6,)),
            *scratch,
        ],
        compiler_params=pltpu.CompilerParams(collective_id=9, has_side_effects=True, vmem_limit_bytes=62 << 20),
        cost_estimate=pl.CostEstimate(
            flops=2 * total_rows * width * 8 * part, bytes_accessed=50 * width * width, transcendentals=0
        ),
        name="attend_back",
    )(
        grads, tokens, weights, up_part, out_w, gains, ids, cosine, sine, residual_grad, gain_attn, gain_feed, *saved
    )


def per_device(inputs, segment, w_qkv, w_out, w_gate, w_up, w_down_t, gains, cotangent):
    rows, width = inputs.shape[1:]
    cores = lax.axis_size("core")
    spans = lax.axis_size("ctx")
    members = cores * spans
    length = rows * spans
    part = width // members
    tokens = inputs[0]

    qkv_rows = w_qkv.shape[0]
    qkv_cut = w_qkv.reshape(qkv_rows, 3, members, part).transpose(2, 0, 1, 3)
    qkv_cut = qkv_cut.reshape(members, qkv_rows, 3 * part)
    chips = lax.axis_size("chip")
    assert chips == spans
    qkv_w, ids, tokens_all = Exchange(
        spans, rows, width, PIECE, False, True, pass_tokens, 1, 0, None,
        QkvWeights(spans, chips, qkv_cut, jnp.broadcast_to(segment, (8, rows))),
    ).call("gather_tokens", 1, None, [tokens], [])
    swaps = [
        (m * spans + a, a * members + m) for m in range(members) for a in range(chips)
    ]
    out_rows = lax.ppermute(w_out, ALL, swaps)

    gate_up, down = split_columns(w_gate, w_up, w_down_t)
    gate_up_w = gather(gate_up, "chip")

    cosine, sine = rope_tables(jnp.arange(length, dtype=F32))
    half = jnp.arange(HEAD_DIM) < HEAD_DIM // 2
    sine = jnp.where(half[None, :], -sine, sine)
    out_part, out_w, *saved = attend(spans, chips, tokens_all, qkv_w, out_rows, gains, ids, cosine, sine)
    (
        output, residual_grad, gain_feed, gain_attn, down_sum, gate_sum, _, _, gate_part, up_part, projected_all
    ) = Middle(spans, rows, width, w_gate.shape[1] // cores, BATCH_PIECE).call(
        chips, out_part, tokens, cotangent[0], gains, gate_up_w, down
    )
    input_grad, grad_qkv, grad_gains, grad_out, up_sum = attend_back(
        spans, chips, rows, projected_all, tokens_all, qkv_w, up_part, out_w, gains, ids, cosine, sine, residual_grad,
        gain_attn, gain_feed, saved,
    )
    if chips != 4:
        gate_sum, up_sum = scatter_sum(gate_part, "chip"), scatter_sum(up_part, "chip")
    grad_gate, grad_up, grad_down = join_columns(gate_sum, up_sum, down_sum)
    return (
        output[None],
        input_grad[None],
        grad_qkv,
        grad_out,
        grad_gate,
        grad_up,
        grad_down,
        grad_gains.reshape(4, width),
    )


def solution(mesh):
    cores = 2
    chips = mesh.shape["dp"] // cores
    split = Mesh(mesh.devices.reshape(chips, cores, mesh.shape["ctx"]), ALL)
    dp = ("chip", "core")
    every = P((*dp, "ctx"), None)
    in_specs = (
        P(dp, "ctx", None),
        P(dp, "ctx"),
        every,
        every,
        P(dp, "ctx"),
        P(dp, "ctx"),
        P(dp, "ctx"),
        P(),
        P(dp, "ctx", None),
    )
    out_specs = (
        P(dp, "ctx", None),
        P(dp, "ctx", None),
        every,
        every,
        P(dp, "ctx"),
        P(dp, "ctx"),
        P(dp, "ctx"),
        P(),
    )
    return jax.shard_map(
        per_device, mesh=split, in_specs=in_specs, out_specs=out_specs, check_vma=False
    )
```

```python
import functools

import jax
import jax.numpy as jnp
from jax import lax
from jax.experimental import pallas as pl
from jax.experimental.pallas import tpu as pltpu
from jax.sharding import Mesh
from jax.sharding import PartitionSpec as P

HEAD_DIM = 128
EPS = 1e-06
ROPE_BASE = 500000.0
F32 = jnp.float32
BF16 = jnp.bfloat16
GROUP = ("core", "ctx")
ALL = ("chip", "core", "ctx")


PIECE = 32
SUM_PIECE = 32
PASS_AT = 1
LATE_TICK = 2
PASS_TICK = 4
LAGJ = 1
MESH_ID = pl.DeviceIdType.MESH


def row_factor(values):
    return lax.rsqrt(jnp.mean(values * values, axis=-1, keepdims=True) + EPS)


def row_norm_back(values, gain, grad):
    factor = row_factor(values)
    normed = values * factor
    scaled = gain * grad
    back = factor * (scaled - normed * jnp.mean(scaled * normed, axis=-1, keepdims=True))
    return back, jnp.sum(grad * normed, axis=0, keepdims=True)


def after_projected(total, ins, outs, rows):
    tokens, gains = ins
    residual_out, projected_out = outs
    projected_out[rows, :] = total
    gain = gains[2:3, :]
    residual = tokens[rows, :].astype(F32) + total * row_factor(total) * gain
    residual_out[rows, :] = residual
    return residual


def after_feed(total, ins, outs, rows):
    residual, cotangent, gains = ins
    output, gain_out = outs
    gain = gains[3:4, :]
    normed = total * row_factor(total) * gain
    output[rows, :] = (residual[rows, :] + normed).astype(BF16)
    back, term = row_norm_back(total, gain, cotangent[rows, :].astype(F32))
    gain_out[...] += term
    return back


def after_back(total, ins, outs, rows):
    projected, cotangent, gains = ins
    grad_out, gain_out = outs
    grad = cotangent[rows, :].astype(F32) + total
    grad_out[rows, :] = grad
    back, term = row_norm_back(projected[rows, :], gains[2:3, :], grad)
    gain_out[...] += term
    return back


def after_input(total, ins, outs, rows):
    (grad,), (result,) = ins, outs
    result[rows, :] = grad[rows, :] + total
    return None


def pass_tokens(total, ins, outs, rows):
    return ins[0][rows, :]


class Exchange:
    def __init__(self, spans, rows, width, piece, reduce, spread, row_fn, n_in, n_out, gain, extra=None):
        self.extra = extra
        self.spans, self.rows, self.width, self.piece = spans, rows, width, piece
        self.reduce, self.spread, self.row_fn = reduce, spread, row_fn
        self.n_in, self.n_out, self.gain = n_in, n_out, gain
        self.count = rows // piece

    def scratch(self):
        spans, count = self.spans, self.count
        block = pltpu.VMEM((spans * self.rows, self.width), BF16)
        sems = pltpu.SemaphoreType.DMA((spans, count))
        items = []
        if self.reduce:
            items += [block] * 4 + [pltpu.SemaphoreType.DMA] + [sems] * 6
        if self.spread:
            items += [pltpu.VMEM((2 * spans * self.rows, self.width), BF16)]
            items += [sems] * 7 + [pltpu.SemaphoreType.DMA]
        if self.extra is not None:
            items += self.extra.scratch()
        return items

    def body(self, *refs):
        spans, rows, piece, count = self.spans, self.rows, self.piece, self.count
        refs = list(refs)
        take = lambda n: [refs.pop(0) for _ in range(n)]
        partial = take(1)[0] if self.reduce else None
        ins = take(self.n_in)
        extra = self.extra
        if extra is not None:
            extra.ins = take(extra.n_in)
        outs = take(self.n_out)
        if extra is not None:
            extra.outs = take(extra.n_out)
        gathered = take(1)[0] if self.spread else None
        if self.reduce:
            own, near, from_left, from_right = take(4)
            (load_sem,) = take(1)
            near_send, near_recv, right_send, right_recv, left_send, left_recv = take(6)
        if self.spread:
            (held,) = take(1)
            fwd_send, fwd_recv, bwd_send, bwd_recv, own_send, side_send, side_recv = take(7)
            (store_sem,) = take(1)
        if extra is not None:
            extra.held = refs
        core = lax.axis_index("core")
        place = lax.axis_index("ctx")
        other = 1 - core
        has_left = place > 0
        has_right = place < spans - 1

        def at(block, k):
            return pl.ds(pl.multiple_of(block * rows + k * piece, piece), piece)

        def held_at(seq, block, k):
            return pl.ds(pl.multiple_of((seq * spans + block) * rows + k * piece, piece), piece)

        def remote(src, dst, send, recv, **device):
            return pltpu.make_async_remote_copy(
                src_ref=src, dst_ref=dst, send_sem=send, recv_sem=recv,
                device_id=device, device_id_type=MESH_ID,
            )

        barrier = pltpu.get_barrier_semaphore()
        if extra is not None:
            if not extra.met:
                meet_all(spans)
        else:
            pl.semaphore_signal(barrier, 1, device_id={"core": other}, device_id_type=MESH_ID)

            @pl.when(has_left)
            def _():
                pl.semaphore_signal(barrier, 1, device_id={"ctx": place - 1}, device_id_type=MESH_ID)

            @pl.when(has_right)
            def _():
                pl.semaphore_signal(barrier, 1, device_id={"ctx": place + 1}, device_id_type=MESH_ID)

            pl.semaphore_wait(barrier, 1 + has_left.astype(jnp.int32) + has_right.astype(jnp.int32))

        if self.gain is not None:
            outs[self.gain][...] = jnp.zeros_like(outs[self.gain])

        def near_copy(d, k):
            return remote(
                partial.at[held_at(other, d, k)], near.at[at(d, k)],
                near_send.at[d, k], near_recv.at[d, k], core=other,
            )

        def right_copy(d, k):
            return remote(
                own.at[at(d, k)], from_left.at[at(d, k)],
                right_send.at[d, k], right_recv.at[d, k], ctx=place + 1,
            )

        def left_copy(d, k):
            return remote(
                own.at[at(d, k)], from_right.at[at(d, k)],
                left_send.at[d, k], left_recv.at[d, k], ctx=place - 1,
            )

        def fwd_copy(o, k, send):
            where = held_at(core, o, k)
            return remote(held.at[where], held.at[where], send, fwd_recv.at[o, k], ctx=place + 1)

        def bwd_copy(o, k, send):
            where = held_at(core, o, k)
            return remote(held.at[where], held.at[where], send, bwd_recv.at[o, k], ctx=place - 1)

        def side_copy(o, k):
            where = held_at(core, o, k)
            return remote(held.at[where], held.at[where], side_send.at[o, k], side_recv.at[o, k], core=other)

        if extra is not None:
            extra.start()
        if self.reduce:
            load = pltpu.make_async_copy(
                partial.at[pl.ds(pl.multiple_of(core * spans * rows, rows), spans * rows)], own, load_sem
            )
            load.start()

            @pl.loop(0, count)
            def _(k):
                for j in range(spans):
                    near_copy(j, k).start()

            load.wait()

        def base(d, k):
            near_copy(d, k).wait_recv()
            return own[at(d, k), :].astype(F32) + near[at(d, k), :].astype(F32)

        def pass_on(d, k, arrived, copy, later):
            value = base(d, k)

            @pl.when(later)
            def _():
                copy(d, k).wait_recv()

            before = arrived[at(d, k), :].astype(F32)
            value = value + jnp.where(later, before, jnp.zeros_like(before))
            own[at(d, k), :] = value.astype(BF16)
            copy(d, k).start()

        def pass_right(k):
            for d in range(spans - 1, 0, -1):

                @pl.when(d > place)
                def _():
                    pass_on(d, k, from_left, right_copy, has_left)

        def pass_left(k):
            for d in range(spans - 1):

                @pl.when(d < place)
                def _():
                    pass_on(d, k, from_right, left_copy, has_right)

        def finish_step(k):
            total = None
            if self.reduce:
                total = base(place, k)

                @pl.when(has_left)
                def _():
                    right_copy(place, k).wait_recv()

                @pl.when(has_right)
                def _():
                    left_copy(place, k).wait_recv()

                zero = jnp.zeros_like(total)
                total = total + jnp.where(has_left, from_left[at(place, k), :].astype(F32), zero)
                total = total + jnp.where(has_right, from_right[at(place, k), :].astype(F32), zero)
            own_rows = pl.ds(pl.multiple_of(k * piece, piece), piece)
            result = self.row_fn(total, ins, outs, own_rows)
            if self.spread:
                held[held_at(core, place, k), :] = result.astype(BF16)

                @pl.when(has_right)
                def _():
                    fwd_copy(place, k, fwd_send.at[place, k]).start()

                @pl.when(has_left)
                def _():
                    bwd_copy(place, k, bwd_send.at[place, k]).start()

                side_copy(place, k).start()

        def relay_step(k, j):
            if True:

                @pl.when(place - j >= 0)
                def _():
                    fwd_copy(place - j, k, fwd_send.at[place - j, k]).wait_recv()

                    @pl.when(has_right)
                    def _():
                        fwd_copy(place - j, k, fwd_send.at[place - j, k]).start()

                    side_copy(place - j, k).start()

                @pl.when(place + j < spans)
                def _():
                    bwd_copy(place + j, k, bwd_send.at[place + j, k]).wait_recv()

                    @pl.when(has_left)
                    def _():
                        bwd_copy(place + j, k, bwd_send.at[place + j, k]).start()

                    side_copy(place + j, k).start()

        lag = spans - 1 if self.reduce else 0

        def due(k, run):
            @pl.when(jnp.logical_and(k >= 0, k < count))
            def _():
                run(k)

        @pl.loop(0, count + lag + (LAGJ * (spans - 1) if self.spread else 0))
        def _(t):
            if self.reduce:
                due(t - place, pass_right)
                due(t - (spans - 1 - place), pass_left)
                due(t - jnp.maximum(place, spans - 1 - place), finish_step)
            else:

                @pl.when(t == 0)
                def _():
                    for k in range(count):
                        finish_step(k)

            if self.spread:
                for j in range(1, spans):
                    after = t - lag - j * LAGJ

                    @pl.when(jnp.logical_and(after >= 0, after < count))
                    def _():
                        relay_step(after, j)
            if extra is not None:
                extra.tick(t)

        if extra is not None:
            extra.finish(count + lag + (LAGJ * (spans - 1) if self.spread else 0))
        if self.spread:

            @pl.loop(0, count)
            def _(k):
                for o in range(spans):
                    side_copy(o, k).wait_recv()

            store = pltpu.make_async_copy(held, gathered, store_sem)
            store.start()

        @pl.loop(0, count)
        def _(k):
            for d in range(spans):
                if self.reduce:
                    near_copy(d, k).wait_send()

                    @pl.when(d > place)
                    def _():
                        right_copy(d, k).wait_send()

                    @pl.when(d < place)
                    def _():
                        left_copy(d, k).wait_send()

                if self.spread:
                    side_copy(d, k).wait_send()

                    @pl.when(jnp.logical_and(d <= place, has_right))
                    def _():
                        fwd_copy(d, k, fwd_send.at[d, k]).wait_send()

                    @pl.when(jnp.logical_and(d >= place, has_left))
                    def _():
                        bwd_copy(d, k, bwd_send.at[d, k]).wait_send()

        if self.spread:
            store.wait()


def owner_of(chip, core, place, spans):
    member = core * spans + place
    return member // 2, lax.rem(member, 2), chip


def summer_of(chip, core, place, spans):
    member = chip * 2 + core
    return place, member // spans, lax.rem(member, spans)


def stays(chip, core, place, spans):
    to_chip, to_core, to_place = owner_of(chip, core, place, spans)
    return jnp.logical_and(to_chip == chip, jnp.logical_and(to_core == core, to_place == place))


def meet_all(spans):
    greet_all(spans, False)
    wait_all(spans, False)


def greet_all(spans, moves):
    chips = lax.axis_size("chip")
    barrier = pltpu.get_barrier_semaphore()
    chip = lax.axis_index("chip")
    core = lax.axis_index("core")
    place = lax.axis_index("ctx")
    for s in range(1, chips):
        pl.semaphore_signal(
            barrier, 1, device_id={"chip": lax.rem(chip + s, chips)}, device_id_type=MESH_ID
        )
    for s in range(1, 2 * spans):
        to_core, to_place = step_member(core, place, s, spans)
        pl.semaphore_signal(
            barrier, 1, device_id={"core": to_core, "ctx": to_place}, device_id_type=MESH_ID
        )
    if moves:

        @pl.when(jnp.logical_not(stays(chip, core, place, spans)))
        def _():
            for find in (owner_of, summer_of):
                to_chip, to_core, to_place = find(chip, core, place, spans)
                pl.semaphore_signal(
                    barrier, 1, device_id={"chip": to_chip, "core": to_core, "ctx": to_place}, device_id_type=MESH_ID
                )


def wait_all(spans, moves):
    count = lax.axis_size("chip") - 1 + 2 * spans - 1
    if moves:
        here = stays(lax.axis_index("chip"), lax.axis_index("core"), lax.axis_index("ctx"), spans)
        count = count + 2 * jnp.logical_not(here).astype(jnp.int32)
    pl.semaphore_wait(pltpu.get_barrier_semaphore(), count)


def step_member(core, place, s, spans):
    return lax.rem(core + s % 2, 2), lax.rem(place + s // 2, spans)


def meet_other_core():
    barrier = pltpu.get_barrier_semaphore()
    other = 1 - lax.axis_index("core")
    pl.semaphore_signal(barrier, 1, device_id={"core": other}, device_id_type=MESH_ID)
    pl.semaphore_wait(barrier, 1)


def split_body(gate, up, down, gate_up_out, down_out, held, load_sem, store_sem, send_sem, recv_sem):
    core = lax.axis_index("core")
    other = 1 - core
    rows, width = gate.shape
    half = width // 2
    where = pl.ds(pl.multiple_of(core * rows, rows), rows)
    places = [gate_up_out.at[where, :half], gate_up_out.at[where, half:], down_out.at[where, :]]
    mine = pl.ds(pl.multiple_of(core * half, half), half)
    theirs = pl.ds(pl.multiple_of(other * half, half), half)
    loads = [
        pltpu.make_async_copy(a.at[:, mine], held.at[i], load_sem.at[i]) for i, a in enumerate((gate, up, down))
    ]
    for load in loads:
        load.start()
    meet_other_core()
    sends = [
        pltpu.make_async_remote_copy(
            src_ref=a.at[:, theirs], dst_ref=places[i], send_sem=send_sem.at[i], recv_sem=recv_sem.at[i],
            device_id={"core": other}, device_id_type=MESH_ID,
        )
        for i, a in enumerate((gate, up, down))
    ]
    for send in sends:
        send.start()
    stores = [pltpu.make_async_copy(held.at[i], places[i], store_sem.at[i]) for i in range(3)]
    for load, store in zip(loads, stores):
        load.wait()
        store.start()
    for store, send in zip(stores, sends):
        store.wait()
        send.wait()


def split_columns(gate, up, down):
    rows, width = gate.shape
    hbm = pl.BlockSpec(memory_space=pl.ANY)
    three = pltpu.SemaphoreType.DMA((3,))
    return pl.pallas_call(
        split_body,
        out_shape=[
            jax.ShapeDtypeStruct((2 * rows, width), BF16),
            jax.ShapeDtypeStruct((2 * rows, width // 2), BF16),
        ],
        in_specs=[hbm] * 3,
        out_specs=[hbm] * 2,
        scratch_shapes=[pltpu.VMEM((3, rows, width // 2), BF16)] + [three] * 4,
        compiler_params=pltpu.CompilerParams(collective_id=6, has_side_effects=True, vmem_limit_bytes=8 << 20),
        name="split_columns",
    )(gate, up, down)


def join_body(gate, up, down, gate_out, up_out, down_out, arrived, send_sem, recv_sem):
    core = lax.axis_index("core")
    other = 1 - core
    rows, width = gate_out.shape
    half = width // 2
    meet_other_core()
    theirs = pl.ds(pl.multiple_of(other * rows, rows), rows)
    pairs = ((gate, gate_out), (up, up_out), (down, down_out))
    sends = [
        pltpu.make_async_remote_copy(
            src_ref=a.at[theirs], dst_ref=arrived.at[i], send_sem=send_sem.at[i], recv_sem=recv_sem.at[i],
            device_id={"core": other}, device_id_type=MESH_ID,
        )
        for i, (a, _) in enumerate(pairs)
    ]
    for send in sends:
        send.start()
    mine = pl.ds(pl.multiple_of(core * half, half), half)
    far = pl.ds(pl.multiple_of(other * half, half), half)
    step = 16

    def rows_at(i, base):
        return pl.ds(pl.multiple_of(base + i * step, step), step)

    @pl.loop(0, rows // step)
    def _(i):
        for a, b in pairs:
            b[rows_at(i, 0), mine] = a[rows_at(i, core * rows), :].astype(F32)

    for send in sends:
        send.wait()

    @pl.loop(0, rows // step)
    def _(i):
        for n, (_, b) in enumerate(pairs):
            b[rows_at(i, 0), far] = arrived[n, rows_at(i, 0), :].astype(F32)


def join_columns(gate, up, down):
    rows, half = gate.shape[0] // 2, gate.shape[1]
    vmem = pl.BlockSpec(memory_space=pltpu.VMEM)
    three = pltpu.SemaphoreType.DMA((3,))
    return pl.pallas_call(
        join_body,
        out_shape=[jax.ShapeDtypeStruct((rows, 2 * half), F32)] * 3,
        in_specs=[vmem] * 3,
        out_specs=[vmem] * 3,
        scratch_shapes=[pltpu.VMEM((3, rows, half), BF16), three, three],
        compiler_params=pltpu.CompilerParams(collective_id=7, has_side_effects=True, vmem_limit_bytes=32 << 20),
        name="join_columns",
    )(gate, up, down)


class Extra:
    met = False

    def remote(self, src, dst, send, recv, **device):
        return pltpu.make_async_remote_copy(
            src_ref=src, dst_ref=dst, send_sem=send, recv_sem=recv,
            device_id=device, device_id_type=MESH_ID,
        )

    def locate(self):
        self.chip = lax.axis_index("chip")
        self.core = lax.axis_index("core")
        self.place = lax.axis_index("ctx")
        self.me = self.core * self.spans + self.place


class QkvWeights(Extra):
    n_in, n_out = 2, 2
    met = True

    def __init__(self, spans, chips, cut, ids):
        self.spans, self.chips = spans, chips
        self.members, self.block, self.columns = cut.shape
        self.ids_shape = ids.shape
        vmem = pl.BlockSpec(memory_space=pltpu.VMEM)
        self.out_shapes = [
            jax.ShapeDtypeStruct((chips * self.members * self.block, self.columns), BF16),
            jax.ShapeDtypeStruct((self.members * ids.shape[0], ids.shape[1]), jnp.int32),
        ]
        self.out_specs = [vmem, vmem]

    def scratch(self):
        rows = self.chips * self.members * self.block
        sems = pltpu.SemaphoreType.DMA((self.members,))
        cross = pltpu.SemaphoreType.DMA((self.chips, self.members))
        ids = (self.members * self.ids_shape[0], self.ids_shape[1])
        return [pltpu.VMEM((rows, self.columns), BF16), pltpu.VMEM(ids, jnp.int32)] + [sems] * 4 + [cross] * 2

    def at(self, chip, m):
        return pl.ds(pl.multiple_of((chip * self.members + m) * self.block, self.block), self.block)

    def ids_at(self, m):
        return pl.ds(pl.multiple_of(m * self.ids_shape[0], self.ids_shape[0]), self.ids_shape[0])

    def block_copy(self, s):
        full, _, send, recv = self.held[:4]
        core, place = step_member(self.core, self.place, s, self.spans)
        return self.remote(
            self.ins[0].at[core * self.spans + place], full.at[self.at(self.chip, self.me)],
            send.at[s], recv.at[s], core=core, ctx=place,
        )

    def ids_copy(self, s):
        all_ids, send, recv = self.held[1], self.held[4], self.held[5]
        core, place = step_member(self.core, self.place, s, self.spans)
        return self.remote(
            self.ins[1], all_ids.at[self.ids_at(self.me)], send.at[s], recv.at[s], core=core, ctx=place
        )

    def source(self, s):
        core = lax.rem(self.core + s % 2, 2)
        return core * self.spans + lax.rem(self.place + self.spans - s // 2, self.spans)

    def chip_copy(self, s, m):
        full, _, _, _, _, _, send, recv = self.held
        where = self.at(self.chip, m)
        return self.remote(
            full.at[where], full.at[where], send.at[s, m], recv.at[s, m], chip=lax.rem(self.chip + s, self.chips)
        )

    def square_copy(self, kind, s):
        full, _, _, _, _, _, send, recv = self.held
        along_x, along_y, _ = square(self.chip)
        m = self.me if s == 0 else self.source(s)
        owner = self.chip if kind < 2 else (along_x if s % 2 == 0 else along_y)
        to = (along_x, along_y, along_y if s % 2 == 0 else along_x)[kind]
        where = self.at(owner, m)
        return self.remote(full.at[where], full.at[where], send.at[kind, s], recv.at[kind, s], chip=to)

    def start(self):
        self.locate()
        cut, ids = self.ins
        full, all_ids = self.held[:2]
        for s in range(1, self.members):
            self.block_copy(s).start()
        for s in range(1, self.members):
            self.ids_copy(s).start()
        full[self.at(self.chip, self.me), :] = cut[self.me]
        all_ids[self.ids_at(self.me), :] = ids[...]

    def send_block(self, s):
        m = self.me if s == 0 else self.source(s)
        if s > 0:
            self.block_copy(s).wait_recv()
        if self.chips == 4:
            for kind in (0, 1) if s % 2 == 0 else (1, 0):
                self.square_copy(kind, s).start()
            return
        for step in range(1, self.chips):
            self.chip_copy(step, m).start()

    def pass_block(self, s):
        self.square_copy(s % 2, s).wait_recv()
        self.square_copy(2, s).start()

    def tick(self, t):
        @pl.when(t == 0)
        def _():
            for s in range(self.members):
                self.send_block(s)

        half = self.members // 2
        for n in range(2):

            @pl.when(t == PASS_AT + n)
            def _():
                if self.chips == 4:
                    for s in range(n * half, (n + 1) * half):
                        self.pass_block(s)
                if n == 1:
                    self.after_blocks()

    def finish(self, ticks):
        full, all_ids = self.held[:2]
        for s in range(1, self.members):
            self.ids_copy(s).wait_recv()
            self.block_copy(s).wait_send()
            self.ids_copy(s).wait_send()

        if self.chips == 4:
            for s in range(self.members):
                for kind in range(3):
                    self.square_copy(kind, s).wait_send()
                    if kind != s % 2:
                        self.square_copy(kind, s).wait_recv()
        else:

            @pl.loop(0, self.members)
            def _(m):
                for s in range(1, self.chips):
                    self.chip_copy(s, m).wait()

        self.outs[0][...] = full[...]
        self.outs[1][...] = all_ids[...]


class QkvGrads(Extra):
    n_in, n_out = 3, 3
    met = True

    def __init__(self, spans, chips, members, grads, sums, out_grads):
        self.spans, self.chips, self.members = spans, chips, members
        self.out_rows = out_grads.shape[0] // chips
        self.block, self.columns = grads.shape[0] // (chips * members), grads.shape[1]
        self.part = self.columns // 3
        self.width = self.part * members
        self.own_rows = self.part // 128
        self.sum_rows = sums.shape[0]
        vmem = pl.BlockSpec(memory_space=pltpu.VMEM)
        self.out_shapes = [
            jax.ShapeDtypeStruct((self.block, 3 * self.width), F32),
            jax.ShapeDtypeStruct((4, self.width // 128, 128), F32),
            jax.ShapeDtypeStruct((self.out_rows, self.width), F32),
        ]
        self.out_specs = [vmem] * 3

    def scratch(self):
        sems = pltpu.SemaphoreType.DMA((self.members,))
        chip_sems = pltpu.SemaphoreType.DMA((self.chips,))
        cross = pltpu.SemaphoreType.DMA((self.chips, self.members))
        return [
            pltpu.VMEM((self.chips, self.members, self.block, self.columns), BF16),
            pltpu.VMEM((self.members, self.block, self.columns), BF16),
            pltpu.VMEM((self.members, self.block, self.columns), BF16),
            pltpu.VMEM((self.members, self.block, self.columns), BF16),
            pltpu.VMEM((self.chips, self.sum_rows, 128), F32),
            pltpu.VMEM((self.sum_rows, 128), F32),
            pltpu.VMEM((self.members, self.sum_rows, 128), F32),
            pltpu.VMEM((self.chips, self.out_rows, self.width), BF16),
            pltpu.VMEM((self.out_rows, self.width), BF16),
            pltpu.VMEM((self.out_rows, self.width), BF16),
        ] + [cross] * 2 + [sems] * 2 + [chip_sems] * 2 + [sems] * 2 + [chip_sems] * 2 + [pltpu.SemaphoreType.DMA] * 2

    def at(self, chip, m):
        return pl.ds(pl.multiple_of((chip * self.members + m) * self.block, self.block), self.block)

    def chip_copy(self, s, m):
        other = lax.rem(self.chip + s, self.chips)
        return self.remote(
            self.ins[0].at[self.at(other, m)], self.arrived.at[s, m],
            self.cross_send.at[s, m], self.cross_recv.at[s, m], chip=other,
        )

    def member_copy(self, s):
        core, place = step_member(self.core, self.place, s, self.spans)
        return self.remote(
            self.summed.at[core * self.spans + place], self.columns_in.at[self.me],
            self.member_send.at[s], self.member_recv.at[s], core=core, ctx=place,
        )

    def sums_chip(self, s):
        return self.remote(
            self.ins[1], self.sums_in.at[s], self.sums_send.at[s], self.sums_recv.at[s],
            chip=lax.rem(self.chip + s, self.chips),
        )

    def sums_member(self, s):
        core, place = step_member(self.core, self.place, s, self.spans)
        return self.remote(
            self.sums_chips, self.sums_members.at[self.me], self.last_send.at[s], self.last_recv.at[s],
            core=core, ctx=place,
        )

    def out_copy(self, s):
        other = lax.rem(self.chip + s, self.chips)
        rows = pl.ds(pl.multiple_of(other * self.out_rows, self.out_rows), self.out_rows)
        return self.remote(
            self.ins[2].at[rows], self.out_in.at[s], self.out_send.at[s], self.out_recv.at[s], chip=other
        )

    def move_copy(self):
        chip, core, place = owner_of(self.chip, self.core, self.place, self.spans)
        return self.remote(
            self.out_sum, self.out_final, self.move_send, self.move_recv, chip=chip, core=core, ctx=place
        )

    def square_copy(self, kind, i):
        along_x, along_y, across = square(self.chip)
        m = self.nth(i)
        first, second = (along_x, along_y) if i % 2 == 0 else (along_y, along_x)
        if kind == 2:
            src, to = self.passing.at[m], second
        else:
            src, to = self.ins[0].at[self.at((across, first)[kind], m)], first
        return self.remote(
            src, self.arrived.at[kind, m], self.cross_send.at[kind, m], self.cross_recv.at[kind, m], chip=to
        )

    def nth(self, i):
        return lax.rem(self.me + 1 + i, self.members)

    def pass_blocks(self):
        along_x, along_y, _ = square(self.chip)
        for i in range(self.members):
            m = self.nth(i)
            self.square_copy(0, i).wait_recv()
            mine = self.ins[0][self.at(along_y if i % 2 == 0 else along_x, m), :]
            self.passing[m] = (mine.astype(F32) + self.arrived[0, m].astype(F32)).astype(BF16)
            self.square_copy(2, i).start()

    def begin(self):
        self.locate()
        (
            self.arrived, self.passing, self.summed, self.columns_in, self.sums_in, self.sums_chips, self.sums_members,
            self.out_in, self.out_sum, self.out_final,
            self.cross_send, self.cross_recv, self.member_send, self.member_recv,
            self.sums_send, self.sums_recv, self.last_send, self.last_recv,
            self.out_send, self.out_recv, self.move_send, self.move_recv,
        ) = self.held
        for s in range(1, self.chips):
            self.out_copy(s).start()

    def start(self):
        for s in range(1, self.chips):
            self.sums_chip(s).start()

    def send_shares(self):
        if self.chips == 4:
            for i in range(self.members):
                self.square_copy(0, i).start()
                self.square_copy(1, i).start()
            return

        @pl.loop(0, self.members)
        def _(i):
            m = lax.rem(self.me + 1 + i, self.members)
            for s in range(1, self.chips):
                self.chip_copy(s, m).start()

    def add_block(self, m):
        total = self.ins[0][self.at(self.chip, m), :].astype(F32)
        for s in range(1, 3 if self.chips == 4 else self.chips):
            self.chip_copy(s, m).wait_recv()
            total = total + self.arrived[s, m].astype(F32)
        self.summed[m] = total.astype(BF16)

    def send_blocks(self, first, last):
        for s in range(first, last):
            core, place = step_member(self.core, self.place, s, self.spans)
            self.add_block(core * self.spans + place)
            self.member_copy(s).start()

    def tick(self, t):
        @pl.when(t == 0)
        def _():
            self.work()
            self.send_shares()

        @pl.when(t == LATE_TICK)
        def _():
            self.late()

        if self.chips == 4:

            @pl.when(t == PASS_TICK)
            def _():
                self.pass_blocks()

        @pl.when(t == 1)
        def _():
            total = self.ins[1][...]
            for s in range(1, self.chips):
                self.sums_chip(s).wait_recv()
                total = total + self.sums_in[s]
            self.sums_chips[...] = total
            self.sums_members[self.me] = total
            for s in range(1, self.members):
                self.sums_member(s).start()

        @pl.when(t == 2)
        def _():
            rows = pl.ds(pl.multiple_of(self.chip * self.out_rows, self.out_rows), self.out_rows)
            total = self.ins[2][rows, :].astype(F32)
            for s in range(1, self.chips):
                self.out_copy(s).wait_recv()
                total = total + self.out_in[s].astype(F32)
            self.out_sum[...] = total.astype(BF16)

            @pl.when(stays(self.chip, self.core, self.place, self.spans))
            def _():
                self.out_final[...] = total.astype(BF16)

            @pl.when(jnp.logical_not(stays(self.chip, self.core, self.place, self.spans)))
            def _():
                self.move_copy().start()

    def finish(self, ticks):
        self.send_blocks(1, self.members)
        self.add_block(self.me)
        self.columns_in[self.me] = self.summed[self.me]
        for s in range(1, self.members):
            self.sums_member(s).wait()
        wide = self.width // 128
        for i in range(2):
            total = self.sums_members[0, i * wide : (i + 1) * wide, :]
            for m in range(1, self.members):
                total = total + self.sums_members[m, i * wide : (i + 1) * wide, :]
            self.outs[1][2 + i] = total
            base = 2 * wide + i * self.own_rows
            for m in range(self.members):
                self.outs[1][i, m * self.own_rows : (m + 1) * self.own_rows, :] = self.sums_members[
                    m, base : base + self.own_rows, :
                ]
        for s in range(1, self.members):
            self.member_copy(s).wait()
        for m in range(self.members):
            for i in range(3):
                self.outs[0][:, i * self.width + m * self.part : i * self.width + (m + 1) * self.part] = (
                    self.columns_in[m, :, i * self.part : (i + 1) * self.part].astype(F32)
                )
        @pl.when(jnp.logical_not(stays(self.chip, self.core, self.place, self.spans)))
        def _():
            self.move_copy().wait()

        self.outs[2][...] = self.out_final[...].astype(F32)
        for s in range(1, self.chips):
            self.sums_chip(s).wait_send()
            self.out_copy(s).wait_send()

        @pl.loop(0, self.members)
        def _(m):
            for s in range(3) if self.chips == 4 else range(1, self.chips):
                self.chip_copy(s, m).wait_send()


def rope_tables(positions):
    half = HEAD_DIM // 2
    frequency = ROPE_BASE ** (-(jnp.arange(half, dtype=F32) * 2.0 / HEAD_DIM))
    angles = positions[:, None] * frequency[None, :]
    cosine = jnp.cos(angles)
    sine = jnp.sin(angles)
    return (jnp.concatenate([cosine, cosine], 1), jnp.concatenate([sine, sine], 1))


def dot(left, right):
    return jnp.dot(left, right, preferred_element_type=F32)


def dot_rows(left, right):
    return lax.dot_general(left, right, (((1,), (1,)), ((), ())), preferred_element_type=F32)


def dot_first(left, right):
    return lax.dot_general(left, right, (((0,), (0,)), ((), ())), preferred_element_type=F32)


def gather(values, axes):
    return lax.all_gather(values, axes, axis=0, tiled=True)


def scatter_sum(values, axes):
    return lax.psum_scatter(values, axes, scatter_dimension=0, tiled=True)


FF_TILE = 512
SUM_TILE = 1024
BATCH_PIECE = 16
DOWN_TICK = 6
GRAD_TILE = 256


def square(chip):
    along_x = chip + 1 - 2 * lax.rem(chip, 2)
    return along_x, lax.rem(chip + 2, 4), lax.rem(along_x + 2, 4)


class SquareSum:
    def __init__(self, chip, block, landing, send, recv):
        self.chip, self.block, self.landing, self.send, self.recv = chip, block, landing, send, recv
        self.x, self.y, self.across = square(chip)

    def copy(self, i):
        owner = (self.across, self.across, self.x, self.y, self.y, self.x)[i]
        half = (0, 1, 0, 1, 0, 1)[i]
        to = (self.x, self.y, self.x, self.y, self.y, self.x)[i]
        return pltpu.make_async_remote_copy(
            src_ref=self.block(owner, half), dst_ref=self.landing.at[i], send_sem=self.send.at[i],
            recv_sem=self.recv.at[i], device_id={"chip": to}, device_id_type=MESH_ID,
        )

    def begin(self, first):
        self.copy(first).start()
        self.copy(first + 1).start()

    def relay(self):
        for i, owner, half in ((0, self.y, 0), (1, self.x, 1)):
            self.copy(i).wait_recv()
            ref = self.block(owner, half)
            ref[...] = (ref[...].astype(F32) + self.landing[i].astype(F32)).astype(BF16)
        self.begin(4)

    def finish(self, half):
        for i in (2 + half, 4 + half):
            self.copy(i).wait_recv()
        for i in (0 + half, 2 + half, 4 + half):
            self.copy(i).wait_send()
        total = self.block(self.chip, half)[...].astype(F32)
        return total + self.landing[2 + half].astype(F32) + self.landing[4 + half].astype(F32)


class Middle:
    def __init__(self, spans, rows, width, hidden, piece):
        self.spans, self.rows, self.width, self.hidden, self.piece = spans, rows, width, hidden, piece
        self.count = rows // piece
        self.block = spans * piece
        self.batch = 2 * self.block

    def body(
        self, chips, partial, tokens, cotangent, gains, gate_up, gate_up_w, down,
        output, residual_grad, gain_feed, gain_attn, down_sum, gate_sum, residual_all, feed_grad_all, gate_part, up_part, projected_all,
        residual, projected, own, near, from_left, from_right, held, wide, act, back, up_weights, down_weights, slices, given, landed,
        load_sem, weight_sem, store_sem, slice_sem, part_sem, free_sem, near_send, near_recv, right_send, right_recv, left_send, left_recv,
        fwd_send, fwd_recv, bwd_send, bwd_recv, side_send, side_recv, down_send, down_recv, give_send, give_recv, take_send, take_recv, pass_send, pass_recv,
    ):
        spans, rows, piece, count = self.spans, self.rows, self.piece, self.count
        width, hidden, block, batch = self.width, self.hidden, self.block, self.batch
        core = lax.axis_index("core")
        place = lax.axis_index("ctx")
        other = 1 - core
        last = spans - 1
        has_left = place > 0
        has_right = place < last

        def turn_of(o):
            return jnp.maximum(o, last - o)

        def at(d, k):
            return pl.ds(pl.multiple_of((k * spans + d) * piece, piece), piece)

        def at_seq(seq, d, k):
            return pl.ds(pl.multiple_of(((k * 2 + seq) * spans + d) * piece, piece), piece)

        def batch_at(k):
            return pl.ds(pl.multiple_of(k * batch, batch), batch)

        def natural(seq, d, k):
            return pl.ds(pl.multiple_of((seq * spans + d) * rows + k * piece, piece), piece)

        def remote(src, dst, send, recv, **device):
            return pltpu.make_async_remote_copy(
                src_ref=src, dst_ref=dst, send_sem=send, recv_sem=recv, device_id=device, device_id_type=MESH_ID
            )

        barrier = pltpu.get_barrier_semaphore()
        pl.semaphore_signal(barrier, 1, device_id={"core": other}, device_id_type=MESH_ID)

        @pl.when(has_left)
        def _():
            pl.semaphore_signal(barrier, 1, device_id={"ctx": place - 1}, device_id_type=MESH_ID)

        @pl.when(has_right)
        def _():
            pl.semaphore_signal(barrier, 1, device_id={"ctx": place + 1}, device_id_type=MESH_ID)

        def near_copy(e, d, k):
            src = partial.at[natural(other, d, k)] if e == 0 else own.at[at_seq(other, d, k)]
            return remote(src, near.at[at(d, k)], near_send.at[d, k], near_recv.at[d, k], core=other)

        def right_copy(d, k):
            return remote(
                own.at[at_seq(core, d, k)], from_left.at[at(d, k)], right_send.at[d, k], right_recv.at[d, k],
                ctx=place + 1,
            )

        def left_copy(d, k):
            return remote(
                own.at[at_seq(core, d, k)], from_right.at[at(d, k)], left_send.at[d, k], left_recv.at[d, k],
                ctx=place - 1,
            )

        def spread_copy(o, k, send, recv, **device):
            where = held.at[at_seq(core, o, k)]
            return remote(where, where, send.at[o, k], recv.at[o, k], **device)

        def fwd_copy(o, k):
            return spread_copy(o, k, fwd_send, fwd_recv, ctx=place + 1)

        def bwd_copy(o, k):
            return spread_copy(o, k, bwd_send, bwd_recv, ctx=place - 1)

        def side_copy(o, k):
            return spread_copy(o, k, side_send, side_recv, core=other)

        def load_own(d, k):
            return pltpu.make_async_copy(
                partial.at[natural(core, d, k)], own.at[at_seq(core, d, k)], load_sem.at[d, k]
            )

        @pl.loop(0, count)
        def _(k):
            for d in range(spans):
                load_own(d, k).start()

        chip = lax.axis_index("chip")
        shard = down.shape[0]
        here = pl.ds(pl.multiple_of(chip * shard, shard), shard)
        load_down = pltpu.make_async_copy(down, down_weights.at[here], weight_sem.at[chips])

        if chips == 4:
            along_x, along_y, across = square(chip)

        def load_up(s):
            if s == 0:
                return pltpu.make_async_copy(gate_up, up_weights.at[here], weight_sem.at[0])
            source = (along_x, along_y)[s - 1] if chips == 4 else lax.rem(chip + s, chips)
            there = pl.ds(pl.multiple_of(source * shard, shard), shard)
            return pltpu.make_async_copy(gate_up_w.at[there], up_weights.at[there], weight_sem.at[s])


        loads = 3 if chips == 4 else chips

        def up_copy(i):
            size = shard // 2
            source, to = ((along_x, along_y), (along_y, along_x))[i]
            where = pl.ds(pl.multiple_of(source * shard + i * size, size), size)
            return remote(gate_up_w.at[where], up_weights.at[where], pass_send.at[i], pass_recv.at[i], chip=to)

        def down_copy(s):
            if chips != 4:
                return remote(
                    down, down_weights.at[here], down_send.at[s], down_recv.at[s], chip=lax.rem(chip + s, chips)
                )
            half = (0, 1, 1, 0, 0, 1)[s]
            to = (along_x, along_y, along_x, along_y, along_y, along_x)[s]
            size = shard // 2
            if s < 4:
                src = down.at[half * size : (half + 1) * size]
                at_chip = chip
            else:
                at_chip = (along_x, along_y)[s - 4]
            dst = down_weights.at[pl.ds(pl.multiple_of(at_chip * shard + half * size, size), size)]
            return remote(src if s < 4 else dst, dst, down_send.at[s], down_recv.at[s], chip=to)

        def relay_down():
            for s in range(2):
                down_copy(s).wait_recv()
                down_copy(4 + s).start()

        for s in range(loads):
            load_up(s).start()
        load_down.start()
        gain_feed[...] = jnp.zeros_like(gain_feed)
        gain_attn[...] = jnp.zeros_like(gain_attn)
        for s in range(1, chips):
            pl.semaphore_signal(
                barrier, 1, device_id={"chip": lax.rem(chip + s, chips)}, device_id_type=MESH_ID
            )
        pl.semaphore_wait(barrier, chips + has_left.astype(jnp.int32) + has_right.astype(jnp.int32))
        if chips == 4:
            for i in range(2):
                up_copy(i).start()
        for s in range(4) if chips == 4 else range(1, chips):
            down_copy(s).start()

        @pl.loop(0, count)
        def _(k):
            for d in range(spans):
                near_copy(0, d, k).start()

        def base(e, d, k):
            near_copy(e, d, k).wait_recv()
            if e == 0:
                load_own(d, k).wait()
            return own[at_seq(core, d, k), :].astype(F32) + near[at(d, k), :].astype(F32)

        def pass_on(e, d, k, arrived, copy, later):
            value = base(e, d, k)

            @pl.when(later)
            def _():
                copy(d, k).wait_recv()

            before = arrived[at(d, k), :].astype(F32)
            value = value + jnp.where(later, before, jnp.zeros_like(before))
            own[at_seq(core, d, k), :] = value.astype(BF16)
            copy(d, k).start()

        def pass_right(e, k):
            for d in range(last, 0, -1):

                @pl.when(d > place)
                def _():
                    pass_on(e, d, k, from_left, right_copy, has_left)

        def pass_left(e, k):
            for d in range(last):

                @pl.when(d < place)
                def _():
                    pass_on(e, d, k, from_right, left_copy, has_right)

        def finish(e, k):
            total = base(e, place, k)

            @pl.when(has_left)
            def _():
                right_copy(place, k).wait_recv()

            @pl.when(has_right)
            def _():
                left_copy(place, k).wait_recv()

            zero = jnp.zeros_like(total)
            total = total + jnp.where(has_left, from_left[at(place, k), :].astype(F32), zero)
            total = total + jnp.where(has_right, from_right[at(place, k), :].astype(F32), zero)
            mine = pl.ds(pl.multiple_of(k * piece, piece), piece)
            if e == 0:
                result = after_projected(total, (tokens, gains), (residual, projected), mine)
            elif e == 1:
                result = after_feed(total, (residual, cotangent, gains), (output, gain_feed), mine)
            else:
                result = after_back(total, (projected, cotangent, gains), (residual_grad, gain_attn), mine)
            held[at_seq(core, place, k), :] = result.astype(BF16)

            @pl.when(has_right)
            def _():
                fwd_copy(place, k).start()

            @pl.when(has_left)
            def _():
                bwd_copy(place, k).start()

            side_copy(place, k).start()

        def relay_right(o, k):
            fwd_copy(o, k).wait_recv()

            @pl.when(has_right)
            def _():
                fwd_copy(o, k).start()

            side_copy(o, k).start()

        def relay_left(o, k):
            bwd_copy(o, k).wait_recv()

            @pl.when(has_left)
            def _():
                bwd_copy(o, k).start()

            side_copy(o, k).start()

        def gathered(k):
            for o in range(spans):
                side_copy(o, k).wait_recv()

        def sums_sent(e, k):
            for d in range(spans):
                near_copy(e, d, k).wait_send()

                @pl.when(d > place)
                def _():
                    right_copy(d, k).wait_send()

                @pl.when(d < place)
                def _():
                    left_copy(d, k).wait_send()

        def spread_sent(k):
            for o in range(spans):
                side_copy(o, k).wait_send()

                @pl.when(jnp.logical_and(o <= place, has_right))
                def _():
                    fwd_copy(o, k).wait_send()

                @pl.when(jnp.logical_and(o >= place, has_left))
                def _():
                    bwd_copy(o, k).wait_send()

        def store(src, dst, k, sem):
            return pltpu.make_async_copy(src, dst.at[batch_at(k)], sem)

        def forward(k):
            @pl.when(k == 0)
            def _():
                for s in range(loads):
                    load_up(s).wait()
                if chips == 4:
                    for i in range(2):
                        up_copy(i).wait()

            gathered(k)
            keep = store(held.at[batch_at(k)], residual_all, k, store_sem.at[0])
            keep.start()

            @pl.loop(0, hidden // FF_TILE)
            def _(n):
                low = pl.ds(pl.multiple_of(n * FF_TILE, FF_TILE), FF_TILE)
                high = pl.ds(pl.multiple_of(hidden + n * FF_TILE, FF_TILE), FF_TILE)
                gate = dot(held[batch_at(k), :], up_weights[:, low])
                up = dot(held[batch_at(k), :], up_weights[:, high])
                wide[batch_at(k), low] = gate
                wide[batch_at(k), high] = up
                act[batch_at(k), low] = (gate * (1.0 / (1.0 + jnp.exp(-gate))) * up).astype(BF16)

            sums_sent(0, k)

            @pl.when(k == 0)
            def _():
                load_down.wait()
                for s in range(1, chips) if chips != 4 else range(6):
                    down_copy(s).wait_send()
                    if chips != 4 or s >= 2:
                        down_copy(s).wait_recv()

            @pl.loop(0, width // SUM_TILE)
            def _(n):
                columns = pl.ds(pl.multiple_of(n * SUM_TILE, SUM_TILE), SUM_TILE)
                own[batch_at(k), columns] = dot_rows(act[batch_at(k), :], down_weights[columns, :]).astype(BF16)

            keep.wait()
            spread_sent(k)
            for d in range(spans):
                near_copy(1, d, k).start()

        down_tiles = width // GRAD_TILE
        per_chip = shard // GRAD_TILE

        def tile_rows(n):
            return pl.ds(pl.multiple_of(n * GRAD_TILE, GRAD_TILE), GRAD_TILE)

        if chips == 4:
            assert per_chip == 2
            turns = [(across, 0), (across, 1), (along_x, 0), (along_y, 1), (along_y, 0), (along_x, 1), (chip, 0), (chip, 1)]
            order = [owner * per_chip + half for owner, half in turns]
        else:
            order = [lax.rem(chip + 1 + j // per_chip, chips) * per_chip + j % per_chip for j in range(down_tiles)]
        tiles = [(m, order[j] if m < 2 else j) for m in range(3) for j in range(down_tiles)]

        def load_slice(j):
            m, n = tiles[j]
            source = feed_grad_all if m == 0 else residual_all
            return pltpu.make_async_copy(source.at[:, tile_rows(n)], slices.at[j % 4], slice_sem.at[j % 4])

        def half_at(owner, half):
            return pl.ds(pl.multiple_of((owner * per_chip + half) * GRAD_TILE, GRAD_TILE), GRAD_TILE)

        if chips == 4:
            sums = [
                SquareSum(
                    chip, lambda owner, half: given.at[half_at(owner, half)], landed.at[0], give_send, give_recv
                ),
                SquareSum(
                    chip, lambda owner, half: up_weights.at[half_at(owner, half), :hidden], landed.at[1], take_send, take_recv
                ),
            ]

        def give_copy(s):
            theirs = pl.ds(pl.multiple_of(lax.rem(chip + s, chips) * shard, shard), shard)
            return remote(
                given.at[theirs], down_weights.at[s * shard : (s + 1) * shard], give_send.at[s], give_recv.at[s],
                chip=lax.rem(chip + s, chips),
            )

        def part_copy(n, m):
            half = slice((m - 1) * hidden, m * hidden)
            return pltpu.make_async_copy(
                up_weights.at[tile_rows(n), half], (gate_part, up_part)[m - 1].at[tile_rows(n)], part_sem.at[m - 1, n]
            )

        def work_out(j):
            if j + 2 < len(tiles):
                load_slice(j + 2).start()
            load_slice(j).wait()
            m, n = tiles[j]
            if m == 0:
                given[tile_rows(n), :] = dot_first(slices[j % 4], act[...]).astype(BF16)
            else:
                half = slice((m - 1) * hidden, m * hidden)
                up_weights[tile_rows(n), half] = dot_first(slices[j % 4], back[:, half]).astype(BF16)

        def weight_grads(q):
            if chips == 4:
                m, r = q // 4, q % 4
                if m < 2:
                    for j in range(m * down_tiles + 2 * r, m * down_tiles + 2 * r + 2):
                        work_out(j)
                    if r < 2:
                        sums[m].begin(2 * r)
                    elif r == 2:
                        sums[m].relay()
                else:
                    for j in range(2 * down_tiles, 3 * down_tiles):
                        work_out(j)
                        part_copy(tiles[j][1], 2).start()
                return
            if q < chips:
                for j in range(q * per_chip, (q + 1) * per_chip):
                    work_out(j)
                if q == 0:
                    pl.semaphore_wait(free_sem, chips - 1)
                if q < chips - 1:
                    give_copy(q + 1).start()
                return
            first = down_tiles + 4 * (q - chips)
            for j in range(first, min(first + 4, len(tiles))):
                work_out(j)
                part_copy(tiles[j][1], tiles[j][0]).start()

        def backward(k):
            gathered(k)
            keep = store(held.at[batch_at(k)], feed_grad_all, k, store_sem.at[0])
            keep.start()

            @pl.loop(0, hidden // FF_TILE)
            def _(n):
                low = pl.ds(pl.multiple_of(n * FF_TILE, FF_TILE), FF_TILE)
                high = pl.ds(pl.multiple_of(hidden + n * FF_TILE, FF_TILE), FF_TILE)
                act_grad = dot(held[batch_at(k), :], down_weights[:, low])
                gate = wide[batch_at(k), low]
                up = wide[batch_at(k), high]
                sigmoid = 1.0 / (1.0 + jnp.exp(-gate))
                back[batch_at(k), low] = (act_grad * up * sigmoid * (1.0 + gate * (1.0 - sigmoid))).astype(BF16)
                back[batch_at(k), high] = (act_grad * (gate * sigmoid)).astype(BF16)

            sums_sent(1, k)

            @pl.loop(0, width // SUM_TILE)
            def _(n):
                columns = pl.ds(pl.multiple_of(n * SUM_TILE, SUM_TILE), SUM_TILE)
                own[batch_at(k), columns] = dot_rows(back[batch_at(k), :], up_weights[columns, :]).astype(BF16)

            keep.wait()
            spread_sent(k)
            for d in range(spans):
                near_copy(2, d, k).start()

            @pl.when(k == count - 1)
            def _():
                for s in range(1, chips) if chips != 4 else ():
                    pl.semaphore_signal(
                        free_sem, 1, device_id={"chip": lax.rem(chip + s, chips)}, device_id_type=MESH_ID
                    )
                load_slice(0).start()
                load_slice(1).start()

        def give(seq, d, k):
            return pltpu.make_async_copy(
                held.at[at_seq(seq, d, k)], projected_all.at[natural(seq, d, k)], load_sem.at[d, k]
            )

        def hand_out(k):
            gathered(k)
            sums_sent(2, k)
            for seq in range(2):
                for d in range(spans):
                    give(seq, d, k).start()
                for d in range(spans):
                    give(seq, d, k).wait()
            spread_sent(k)

        step = 2 * last + 2
        last_steps = 9 if chips == 4 else chips + down_tiles // 2
        assert last_steps <= step + 1

        def due(t, run):
            @pl.when(jnp.logical_and(t >= 0, t < count))
            def _():
                run(t)

        @pl.loop(0, 3 * step + count - 1)
        def _(t):
            for e in range(2, -1, -1):
                now = t - e * step
                for j in range(1, spans):
                    o = place - j

                    @pl.when(o >= 0)
                    def _():
                        due(now - turn_of(o) - j, functools.partial(relay_right, o))

                    p = place + j

                    @pl.when(p < spans)
                    def _():
                        due(now - turn_of(p) - j, functools.partial(relay_left, p))

                due(now - place, functools.partial(pass_right, e))
                due(now - (last - place), functools.partial(pass_left, e))
                due(now - turn_of(place), functools.partial(finish, e))
            if chips == 4:

                @pl.when(t == DOWN_TICK)
                def _():
                    relay_down()

            for e, run in ((2, hand_out), (1, backward), (0, forward)):
                due(t - e * step - 2 * last, run)
            for q in range(last_steps):

                @pl.when(t == count + step + 2 * last + q)
                def _():
                    weight_grads(q)

        if chips == 4:
            for group, out in zip(sums, (down_sum, gate_sum)):
                for half in range(2):
                    out[half * GRAD_TILE : (half + 1) * GRAD_TILE, :] = group.finish(half).astype(BF16)
            for n in range(down_tiles):
                part_copy(n, 2).wait()
            return
        total = given[here, :].astype(F32)
        for s in range(1, chips):
            give_copy(s).wait()
            total = total + down_weights[s * shard : (s + 1) * shard, :].astype(F32)
        down_sum[...] = total.astype(BF16)
        gate_sum[...] = jnp.zeros_like(gate_sum)
        for n in range(down_tiles):
            part_copy(n, 1).wait()
            part_copy(n, 2).wait()

    def call(self, chips, partial, tokens, cotangent, gains, gate_up, gate_up_w, down):
        spans, rows, width, hidden, count = self.spans, self.rows, self.width, self.hidden, self.count
        total = 2 * spans * rows
        vmem = pl.BlockSpec(memory_space=pltpu.VMEM)
        hbm = pl.BlockSpec(memory_space=pl.ANY)
        shape = jax.ShapeDtypeStruct
        sems = pltpu.SemaphoreType.DMA((spans, count))
        two = pltpu.SemaphoreType.DMA((2,))
        return pl.pallas_call(
            functools.partial(self.body, chips),
            out_shape=[
                shape((rows, width), BF16),
                shape((rows, width), F32),
                shape((1, width), F32),
                shape((1, width), F32),
                shape(down.shape, BF16),
                shape(down.shape, BF16),
                shape((total, width), BF16),
                shape((total, width), BF16),
                shape((16, 128) if chips == 4 else (width, hidden), BF16),
                shape((width, hidden), BF16),
                shape((total, width), BF16),
            ],
            in_specs=[hbm, vmem, vmem, vmem, hbm, hbm, hbm],
            out_specs=[vmem] * 6 + [hbm] * 5,
            scratch_shapes=[
                pltpu.VMEM((rows, width), F32),
                pltpu.VMEM((rows, width), F32),
                pltpu.VMEM((total, width), BF16),
                pltpu.VMEM((total // 2, width), BF16),
                pltpu.VMEM((total // 2, width), BF16),
                pltpu.VMEM((total // 2, width), BF16),
                pltpu.VMEM((total, width), BF16),
                pltpu.VMEM((total, 2 * hidden), F32),
                pltpu.VMEM((total, hidden), BF16),
                pltpu.VMEM((total, 2 * hidden), BF16),
                pltpu.VMEM((width, 2 * hidden), BF16),
                pltpu.VMEM((width, hidden), BF16),
                pltpu.VMEM((4, total, GRAD_TILE), BF16),
                pltpu.VMEM((width, hidden), BF16),
                pltpu.VMEM((2, 6, GRAD_TILE, hidden) if chips == 4 else (2, 6, 16, 128), BF16),
                sems,
                pltpu.SemaphoreType.DMA((chips + 1,)),
                two,
                pltpu.SemaphoreType.DMA((4,)),
                pltpu.SemaphoreType.DMA((2, width // GRAD_TILE)),
                pltpu.SemaphoreType.REGULAR,
            ]
            + [sems] * 12
            + [pltpu.SemaphoreType.DMA((max(chips, 6),))] * 8,
            compiler_params=pltpu.CompilerParams(
                collective_id=2, has_side_effects=True, vmem_limit_bytes=62 << 20
            ),
            cost_estimate=pl.CostEstimate(
                flops=36 * rows * spans * width * hidden, bytes_accessed=100 * width * width, transcendentals=0
            ),
            name="feed_forward",
        )(partial, tokens, cotangent, gains, gate_up, gate_up_w, down)


def turn(values, cosine, sine):
    return values * cosine + pltpu.roll(values, HEAD_DIM // 2, 1) * sine


def row_sums(values):
    total = values[:, :128]
    for first in range(128, values.shape[1], 128):
        total = total + values[:, first : first + 128]
    return jnp.sum(jnp.transpose(total), axis=0, keepdims=True)


def down_rows(row):
    return jnp.transpose(jnp.broadcast_to(row, (128, row.shape[1])))


class Stats:
    def __init__(self, spans, own, arrived, send, recv):
        self.spans, self.own, self.arrived, self.send, self.recv = spans, own, arrived, send, recv
        self.core, self.place = lax.axis_index("core"), lax.axis_index("ctx")
        self.me = self.core * spans + self.place

    def member(self, s):
        core, place = step_member(self.core, self.place, s, self.spans)
        return {"core": core, "ctx": place}

    def greet(self):
        for s in range(1, 2 * self.spans):
            pl.semaphore_signal(
                pltpu.get_barrier_semaphore(), 1, device_id=self.member(s), device_id_type=MESH_ID
            )

    def meet(self):
        pl.semaphore_wait(pltpu.get_barrier_semaphore(), 2 * self.spans - 1)

    def copy(self, s):
        return pltpu.make_async_remote_copy(
            src_ref=self.own, dst_ref=self.arrived.at[s], send_sem=self.send.at[s], recv_sem=self.recv.at[s],
            device_id=self.member(s), device_id_type=MESH_ID,
        )

    def start(self):
        for s in range(1, 2 * self.spans):
            self.copy(s).start()

    def total(self):
        total = self.own[...]
        for s in range(1, 2 * self.spans):
            self.copy(s).wait()
            total = total + self.arrived[s]
        return total


def stats_scratch(spans, total_rows):
    sems = pltpu.SemaphoreType.DMA((2 * spans,))
    return [
        pltpu.VMEM((8, total_rows), F32),
        pltpu.VMEM((2 * spans, 8, total_rows), F32),
        sems,
        sems,
    ]


def allowed_at(ids, seq, block, count, spans):
    rows = ids.shape[1]
    per = block // rows
    ids_of = lambda z: ids[(seq * spans + z) * 8 : (seq * spans + z) * 8 + 8, :].astype(F32)
    first = count * per
    keys = jnp.concatenate([ids_of(z)[:1] for z in range(first + per)], 1)
    queries = jnp.concatenate([jnp.transpose(ids_of(z))[:, :1] for z in range(first, first + per)], 0)
    shape = (block, (count + 1) * block)
    query_at = lax.broadcasted_iota(jnp.int32, shape, 0) + count * block
    key_at = lax.broadcasted_iota(jnp.int32, shape, 1)
    same = queries == keys
    seen = jnp.logical_and(same, key_at <= query_at)
    return jnp.logical_and(seen, jnp.logical_or(keys != 0.0, key_at == query_at))


def softmax_parts(query, key, allowed):
    scores = jnp.where(allowed, dot_rows(query, key) * HEAD_DIM ** (-0.5), -1e30)
    weights = jnp.exp(scores - jnp.max(scores, axis=1, keepdims=True))
    return weights / jnp.sum(weights, axis=1, keepdims=True)


QUERY_BLOCK = 256
ROW_TILE = 256


class Neighbours:
    pieces = 4

    def __init__(self, chip, shard, full, send, recv):
        self.chip, self.shard, self.full, self.send, self.recv = chip, shard, full, send, recv
        self.to = square(chip)[:2]

    def copy(self, i, n):
        size = self.shard.shape[0] // self.pieces
        where = self.full.at[pl.ds(pl.multiple_of(self.chip * self.shard.shape[0] + n * size, size), size)]
        return pltpu.make_async_remote_copy(
            src_ref=self.shard.at[n * size : (n + 1) * size], dst_ref=where,
            send_sem=self.send.at[i, n], recv_sem=self.recv.at[i, n],
            device_id={"chip": self.to[i]}, device_id_type=MESH_ID,
        )

    def begin(self):
        for n in range(self.pieces):
            for i in range(2):
                self.copy(i, n).start()

    def finish(self):
        for n in range(self.pieces):
            for i in range(2):
                self.copy(i, n).wait()


def attend_body(
    spans, chips, exchange, extra, n_scratch,
    tokens, cut, own_ids, w_out, gate_up, gains, cosine, sine,
    weights_out, ids, tokens_all, gate_up_w,
    partial_out, out_w_out, query_out, key_out, value_out, normed_out, factor_out, attended_out,
    raw, given, out_w, moved, own, arrived, store_sem, chip_send, chip_recv, send, recv, move_send, move_recv,
    up_send, up_recv, *rest,
):
    part = out_w.shape[0]
    total_rows = raw.shape[0]
    length = total_rows // 2
    width = tokens.shape[1]
    tiles = total_rows // ROW_TILE
    held, held_w = rest[0], rest[n_scratch]
    stats = Stats(spans, own, arrived, send, recv)
    greet_all(spans, True)
    chip, core, place = lax.axis_index("chip"), stats.core, stats.place
    shard = moved.shape[0]
    here = pl.ds(pl.multiple_of(chip * shard, shard), shard)

    def at(i):
        return pl.ds(pl.multiple_of(i * ROW_TILE, ROW_TILE), ROW_TILE)

    def chip_copy(s):
        return pltpu.make_async_remote_copy(
            src_ref=moved, dst_ref=out_w.at[here], send_sem=chip_send.at[s], recv_sem=chip_recv.at[s],
            device_id={"chip": lax.rem(chip + s, chips)}, device_id_type=MESH_ID,
        )

    def move_copy():
        to_chip, to_core, to_place = summer_of(chip, core, place, spans)
        return pltpu.make_async_remote_copy(
            src_ref=w_out, dst_ref=moved, send_sem=move_send, recv_sem=move_recv,
            device_id={"chip": to_chip, "core": to_core, "ctx": to_place}, device_id_type=MESH_ID,
        )

    home = stays(chip, core, place, spans)
    if chips == 4:
        up = Neighbours(chip, gate_up, gate_up_w, up_send, up_recv)
    own[...] = jnp.zeros_like(own)
    wait_all(spans, True)

    @pl.when(home)
    def _():
        moved[...] = w_out[...]

    @pl.when(jnp.logical_not(home))
    def _():
        move_copy().start()

    def after_blocks():
        @pl.when(jnp.logical_not(home))
        def _():
            move_copy().wait()

        for s in range(1, chips):
            chip_copy(s).start()
        out_w[here, :] = moved[...]
        if chips == 4:
            up.begin()

    extra.after_blocks = after_blocks
    exchange.body(tokens, cut, own_ids, weights_out, ids, tokens_all, *rest)

    @pl.loop(0, tiles)
    def _(i):
        values = dot(held[at(i), :], held_w[...])
        raw[at(i), :] = values
        for n in range(2):
            some = values[:, n * part : (n + 1) * part]
            own[n : n + 1, at(i)] = row_sums(some * some)

    stats.start()

    @pl.loop(0, tiles)
    def _(i):
        value_out[at(i), :] = raw[at(i), 2 * part :].astype(BF16)

    factor_out[...] = lax.rsqrt(stats.total() / width + EPS)
    me = stats.me
    columns = pl.ds(pl.multiple_of(me * part, part), part)
    gain = jnp.concatenate([gains[0:1, columns], gains[1:2, columns]], 1)

    @pl.loop(0, tiles)
    def _(i):
        by_query, by_key = down_rows(factor_out[0:1, at(i)]), down_rows(factor_out[1:2, at(i)])
        place = pl.ds(pl.multiple_of(lax.rem(i, length // ROW_TILE) * ROW_TILE, ROW_TILE), ROW_TILE)
        for h in range(part // HEAD_DIM):
            head = slice(h * HEAD_DIM, (h + 1) * HEAD_DIM)
            low = slice(part + h * HEAD_DIM, part + (h + 1) * HEAD_DIM)
            for out, by, where in ((query_out, by_query, head), (key_out, by_key, low)):
                normed = raw[at(i), where] * by
                normed_out[at(i), where] = normed
                out[at(i), head] = turn(normed * gain[:, where], cosine[place, :], sine[place, :]).astype(BF16)

    for s in range(1, chips):
        chip_copy(s).wait()
    out_w_out[...] = out_w[...]
    block = QUERY_BLOCK
    for seq in range(2):
        for count in range(length // block):
            allowed = allowed_at(ids, seq, block, count, spans)
            rows = slice(seq * length + count * block, seq * length + (count + 1) * block)
            keys = slice(seq * length, seq * length + (count + 1) * block)
            for h in range(part // HEAD_DIM):
                head = slice(h * HEAD_DIM, (h + 1) * HEAD_DIM)
                shares = softmax_parts(query_out[rows, head], key_out[keys, head], allowed)
                attended_out[rows, head] = dot(shares.astype(BF16), value_out[keys, head]).astype(BF16)
            i = rows.start // ROW_TILE
            if i >= 2:
                pltpu.make_async_copy(given.at[i % 2], partial_out.at[at(i - 2)], store_sem.at[i - 2]).wait()
            given[i % 2] = dot(attended_out[rows, :], out_w[...]).astype(BF16)
            pltpu.make_async_copy(given.at[i % 2], partial_out.at[at(i)], store_sem.at[i]).start()
    for i in range(tiles - 2, tiles):
        pltpu.make_async_copy(given.at[i % 2], partial_out.at[at(i)], store_sem.at[i]).wait()
    if chips == 4:
        up.finish()


def attend(spans, chips, tokens, cut, ids, w_out, gate_up, gains, cosine, sine):
    rows, width = tokens.shape
    total_rows = 2 * spans * rows
    part = w_out.shape[0] * chips
    tiles = total_rows // ROW_TILE
    vmem = pl.BlockSpec(memory_space=pltpu.VMEM)
    hbm = pl.BlockSpec(memory_space=pl.ANY)
    shape = jax.ShapeDtypeStruct
    extra = QkvWeights(spans, chips, cut, ids)
    exchange = Exchange(spans, rows, width, PIECE, False, True, pass_tokens, 1, 0, None, extra)
    scratch = exchange.scratch()
    return pl.pallas_call(
        functools.partial(attend_body, spans, chips, exchange, extra, len(scratch) - len(extra.scratch())),
        out_shape=[
            *extra.out_shapes,
            shape((total_rows, width), BF16),
            shape((chips * gate_up.shape[0] if chips == 4 else 16, gate_up.shape[1]), BF16),
            shape((total_rows, width), BF16),
            shape((part, width), BF16),
            shape((total_rows, part), BF16),
            shape((total_rows, part), BF16),
            shape((total_rows, part), BF16),
            shape((total_rows, 2 * part), F32),
            shape((8, total_rows), F32),
            shape((total_rows, part), BF16),
        ],
        in_specs=[vmem] * 4 + [hbm] + [vmem] * 3,
        out_specs=[vmem] * 2 + [hbm] * 3 + [vmem] * 7,
        scratch_shapes=[
            pltpu.VMEM((total_rows, 3 * part), F32),
            pltpu.VMEM((2, ROW_TILE, width), BF16),
            pltpu.VMEM((part, width), BF16),
            pltpu.VMEM(w_out.shape, BF16),
            *stats_scratch(spans, total_rows)[:2],
            pltpu.SemaphoreType.DMA((tiles,)),
            pltpu.SemaphoreType.DMA((chips,)),
            pltpu.SemaphoreType.DMA((chips,)),
            *stats_scratch(spans, total_rows)[2:],
            pltpu.SemaphoreType.DMA,
            pltpu.SemaphoreType.DMA,
            pltpu.SemaphoreType.DMA((2, Neighbours.pieces)),
            pltpu.SemaphoreType.DMA((2, Neighbours.pieces)),
            *scratch,
        ],
        compiler_params=pltpu.CompilerParams(collective_id=1, has_side_effects=True, vmem_limit_bytes=58 << 20),
        cost_estimate=pl.CostEstimate(
            flops=2 * total_rows * width * 5 * part, bytes_accessed=50 * width * width, transcendentals=0
        ),
        name="attend",
    )(tokens, cut, ids, w_out, gate_up, gains, cosine, sine)


def attend_back_body(
    spans, chips, exchange, extra, n_scratch,
    grads, tokens, weights, up_part, out_w, gains, ids, cosine, sine, residual_grad, gain_attn, gain_feed,
    query, key, value, normed, factor, attended,
    input_grad, grad_qkv, grad_gains, grad_out, up_sum,
    held, held_tokens, held_w, raw, mixed, attended_grad, own, arrived, load_sem, send, recv,
    qkv_part, out_part, sums, up_held, up_landed, up_send, up_recv, *rest,
):
    part = out_w.shape[0]
    total_rows = raw.shape[0]
    length = total_rows // 2
    width = grads.shape[1]
    tiles = total_rows // ROW_TILE
    scale = HEAD_DIM ** (-0.5)
    stats = Stats(spans, own, arrived, send, recv)
    greet_all(spans, True)

    def at(i):
        return pl.ds(pl.multiple_of(i * ROW_TILE, ROW_TILE), ROW_TILE)

    def load_rows(i):
        return pltpu.make_async_copy(grads.at[at(i)], held.at[at(i)], load_sem.at[i])

    @pl.loop(0, tiles)
    def _(i):
        load_rows(i).start()

    own[...] = jnp.zeros_like(own)
    load_w = pltpu.make_async_copy(weights, held_w, load_sem.at[tiles])
    load_tokens = pltpu.make_async_copy(tokens, held_tokens, load_sem.at[tiles + 1])
    load_w.start()
    load_tokens.start()
    if chips == 4:
        load_up = pltpu.make_async_copy(up_part, up_held, load_sem.at[tiles + 2])
        load_up.start()
    me = stats.me
    columns = pl.ds(pl.multiple_of(me * part, part), part)
    gain = jnp.concatenate([gains[0:1, columns], gains[1:2, columns]], 1)

    @pl.loop(0, tiles)
    def _(i):
        load_rows(i).wait()
        attended_grad[at(i), :] = dot_rows(held[at(i), :], out_w[...]).astype(BF16)

    out_part[...] = dot_first(attended[...], held[...]).astype(BF16)
    wait_all(spans, True)
    extra.ins = [qkv_part, sums, out_part]
    extra.held = list(rest[n_scratch:])
    extra.begin()
    if chips == 4:
        load_up.wait()
        half_rows = width // 8
        up_sums = SquareSum(
            lax.axis_index("chip"),
            lambda owner, half: up_held.at[
                pl.ds(pl.multiple_of((owner * 2 + half) * half_rows, half_rows), half_rows)
            ],
            up_landed, up_send, up_recv,
        )
        up_sums.begin(0)
        up_sums.begin(2)
    block = QUERY_BLOCK
    blocks = length // block
    for seq in range(2):
        for h in range(part // HEAD_DIM):
            head = slice(h * HEAD_DIM, (h + 1) * HEAD_DIM)
            key_at = slice(part + h * HEAD_DIM, part + (h + 1) * HEAD_DIM)
            value_at = slice(2 * part + h * HEAD_DIM, 2 * part + (h + 1) * HEAD_DIM)
            for count in reversed(range(blocks)):
                allowed = allowed_at(ids, seq, block, count, spans)
                rows = slice(seq * length + count * block, seq * length + (count + 1) * block)
                keys = slice(seq * length, seq * length + (count + 1) * block)
                shares = softmax_parts(query[rows, head], key[keys, head], allowed)
                share_grad = dot_rows(attended_grad[rows, head], value[keys, head])
                inner = jnp.sum(shares * share_grad, axis=1, keepdims=True)
                score_grad = (shares * (share_grad - inner)).astype(BF16)
                raw[rows, head] = dot(score_grad, key[keys, head]) * scale
                key_grad = dot_first(score_grad, query[rows, head]) * scale
                value_grad = dot_first(shares.astype(BF16), attended_grad[rows, head])
                if count == blocks - 1:
                    raw[keys, key_at] = key_grad
                    raw[keys, value_at] = value_grad
                else:
                    raw[keys, key_at] += key_grad
                    raw[keys, value_at] += value_grad

    gain_rows = jnp.zeros((1, 2 * part), F32)

    for i in range(tiles):
        place = slice(i * ROW_TILE % length, i * ROW_TILE % length + ROW_TILE)
        for h in range(2 * part // HEAD_DIM):
            head = slice(h * HEAD_DIM, (h + 1) * HEAD_DIM)
            raw[at(i), head] = turn(raw[at(i), head], cosine[place, :], -sine[place, :])
        terms = raw[at(i), : 2 * part] * normed[at(i), :]
        gain_rows = gain_rows + jnp.sum(terms, axis=0, keepdims=True)
        for n in range(2):
            own[n : n + 1, at(i)] = row_sums((terms * gain)[:, n * part : (n + 1) * part])
        mixed[at(i), 2 * part :] = raw[at(i), 2 * part :].astype(BF16)

    stats.start()
    wide = width // 128
    for n in range(wide):
        column = slice(n * 128, (n + 1) * 128)
        sums[n : n + 1, :] = gain_attn[:, column]
        sums[wide + n : wide + n + 1, :] = gain_feed[:, column]
    for n in range(2 * part // 128):
        sums[2 * wide + n : 2 * wide + n + 1, :] = gain_rows[:, n * 128 : (n + 1) * 128]
    own[...] = stats.total() / width

    @pl.loop(0, tiles)
    def _(i):
        for n in range(2):
            mean, by = down_rows(own[n : n + 1, at(i)]), down_rows(factor[n : n + 1, at(i)])
            for first in range(n * part, (n + 1) * part, 128):
                where = slice(first, first + 128)
                back = gain[:, where] * raw[at(i), where] - normed[at(i), where] * mean
                mixed[at(i), where] = (by * back).astype(BF16)

    load_w.wait()

    @pl.loop(0, tiles)
    def _(i):
        held[at(i), :] = dot_rows(mixed[at(i), :], held_w[...]).astype(BF16)

    load_tokens.wait()

    def work():
        @pl.loop(0, width // ROW_TILE)
        def _(i):
            qkv_part[at(i), :] = dot_first(held_tokens[:, at(i)], mixed[...]).astype(BF16)

    extra.work = work
    extra.late = up_sums.relay if chips == 4 else (lambda: None)
    exchange.body(
        held, residual_grad, qkv_part, sums, out_part, input_grad, grad_qkv, grad_gains, grad_out, *rest
    )
    if chips == 4:
        for half in range(2):
            up_sum[half * half_rows : (half + 1) * half_rows, :] = up_sums.finish(half).astype(BF16)


def attend_back(
    spans, chips, rows, grads, tokens, weights, up_part, out_w, gains, ids, cosine, sine, residual_grad, gain_attn,
    gain_feed, saved,
):
    total_rows, width = tokens.shape
    part = out_w.shape[0]
    members = width // part
    hidden = up_part.shape[1]
    tiles = total_rows // ROW_TILE
    vmem = pl.BlockSpec(memory_space=pltpu.VMEM)
    hbm = pl.BlockSpec(memory_space=pl.ANY)
    shape = jax.ShapeDtypeStruct
    sum_rows = (2 * width + 2 * part) // 128
    sum_rows += -sum_rows % 8
    extra = QkvGrads(
        spans, chips, members, shape((width, 3 * part), BF16), shape((sum_rows, 128), F32), shape((part, width), BF16)
    )
    exchange = Exchange(spans, rows, width, SUM_PIECE, True, False, after_input, 1, 1, None, extra)
    scratch = exchange.scratch()
    square_in = chips == 4
    return pl.pallas_call(
        functools.partial(attend_back_body, spans, chips, exchange, extra, len(scratch) - len(extra.scratch())),
        out_shape=[
            shape((rows, width), F32),
            *extra.out_shapes,
            shape((width // chips, hidden) if square_in else (16, 128), BF16),
        ],
        in_specs=[hbm] * 4 + [vmem] * (8 + len(saved)),
        out_specs=[vmem] * 5,
        scratch_shapes=[
            pltpu.VMEM((total_rows, width), BF16),
            pltpu.VMEM((total_rows, width), BF16),
            pltpu.VMEM(weights.shape, BF16),
            pltpu.VMEM((total_rows, 3 * part), F32),
            pltpu.VMEM((total_rows, 3 * part), BF16),
            pltpu.VMEM((total_rows, part), BF16),
            *stats_scratch(spans, total_rows)[:2],
            pltpu.SemaphoreType.DMA((tiles + 3,)),
            *stats_scratch(spans, total_rows)[2:],
            pltpu.VMEM((width, 3 * part), BF16),
            pltpu.VMEM((part, width), BF16),
            pltpu.VMEM((sum_rows, 128), F32),
            pltpu.VMEM((width, hidden) if square_in else (16, 128), BF16),
            pltpu.VMEM((6, width // 8, hidden) if square_in else (6, 16, 128), BF16),
            pltpu.SemaphoreType.DMA((6,)),
            pltpu.SemaphoreType.DMA((6,)),
            *scratch,
        ],
        compiler_params=pltpu.CompilerParams(collective_id=9, has_side_effects=True, vmem_limit_bytes=62 << 20),
        cost_estimate=pl.CostEstimate(
            flops=2 * total_rows * width * 8 * part, bytes_accessed=50 * width * width, transcendentals=0
        ),
        name="attend_back",
    )(
        grads, tokens, weights, up_part, out_w, gains, ids, cosine, sine, residual_grad, gain_attn, gain_feed, *saved
    )


def per_device(inputs, segment, w_qkv, w_out, w_gate, w_up, w_down_t, gains, cotangent):
    rows, width = inputs.shape[1:]
    cores = lax.axis_size("core")
    spans = lax.axis_size("ctx")
    members = cores * spans
    length = rows * spans
    part = width // members
    tokens = inputs[0]

    qkv_rows = w_qkv.shape[0]
    qkv_cut = w_qkv.reshape(qkv_rows, 3, members, part).transpose(2, 0, 1, 3)
    qkv_cut = qkv_cut.reshape(members, qkv_rows, 3 * part)
    chips = lax.axis_size("chip")
    assert chips == spans
    gate_up, down = split_columns(w_gate, w_up, w_down_t)
    cosine, sine = rope_tables(jnp.arange(length, dtype=F32))
    half = jnp.arange(HEAD_DIM) < HEAD_DIM // 2
    sine = jnp.where(half[None, :], -sine, sine)
    qkv_w, ids, tokens_all, gate_up_w, out_part, out_w, *saved = attend(
        spans, chips, tokens, qkv_cut, jnp.broadcast_to(segment, (8, rows)), w_out, gate_up, gains, cosine, sine
    )
    if chips != 4:
        gate_up_w = gather(gate_up, "chip")
    (
        output, residual_grad, gain_feed, gain_attn, down_sum, gate_sum, _, _, gate_part, up_part, projected_all
    ) = Middle(spans, rows, width, w_gate.shape[1] // cores, BATCH_PIECE).call(
        chips, out_part, tokens, cotangent[0], gains, gate_up, gate_up_w, down
    )
    input_grad, grad_qkv, grad_gains, grad_out, up_sum = attend_back(
        spans, chips, rows, projected_all, tokens_all, qkv_w, up_part, out_w, gains, ids, cosine, sine, residual_grad,
        gain_attn, gain_feed, saved,
    )
    if chips != 4:
        gate_sum, up_sum = scatter_sum(gate_part, "chip"), scatter_sum(up_part, "chip")
    grad_gate, grad_up, grad_down = join_columns(gate_sum, up_sum, down_sum)
    return (
        output[None],
        input_grad[None],
        grad_qkv,
        grad_out,
        grad_gate,
        grad_up,
        grad_down,
        grad_gains.reshape(4, width),
    )


def solution(mesh):
    cores = 2
    chips = mesh.shape["dp"] // cores
    split = Mesh(mesh.devices.reshape(chips, cores, mesh.shape["ctx"]), ALL)
    dp = ("chip", "core")
    every = P((*dp, "ctx"), None)
    in_specs = (
        P(dp, "ctx", None),
        P(dp, "ctx"),
        every,
        every,
        P(dp, "ctx"),
        P(dp, "ctx"),
        P(dp, "ctx"),
        P(),
        P(dp, "ctx", None),
    )
    out_specs = (
        P(dp, "ctx", None),
        P(dp, "ctx", None),
        every,
        every,
        P(dp, "ctx"),
        P(dp, "ctx"),
        P(dp, "ctx"),
        P(),
    )
    return jax.shard_map(
        per_device, mesh=split, in_specs=in_specs, out_specs=out_specs, check_vma=False
    )
```

```python
import functools

import jax
import jax.numpy as jnp
from jax import lax
from jax.experimental import pallas as pl
from jax.experimental.pallas import tpu as pltpu
from jax.sharding import Mesh
from jax.sharding import PartitionSpec as P

HEAD_DIM = 128
EPS = 1e-06
ROPE_BASE = 500000.0
F32 = jnp.float32
BF16 = jnp.bfloat16
GROUP = ("core", "ctx")
ALL = ("chip", "core", "ctx")


PIECE = 32
SUM_PIECE = 32
PASS_AT = 1
LATE_TICK = 2
PASS_TICK = 4
LAGJ = 1
MESH_ID = pl.DeviceIdType.MESH


def row_factor(values):
    return lax.rsqrt(jnp.mean(values * values, axis=-1, keepdims=True) + EPS)


def row_norm_back(values, gain, grad):
    factor = row_factor(values)
    normed = values * factor
    scaled = gain * grad
    back = factor * (scaled - normed * jnp.mean(scaled * normed, axis=-1, keepdims=True))
    return back, jnp.sum(grad * normed, axis=0, keepdims=True)


def after_projected(total, ins, outs, rows):
    tokens, gains = ins
    residual_out, projected_out = outs
    projected_out[rows, :] = total
    gain = gains[2:3, :]
    residual = tokens[rows, :].astype(F32) + total * row_factor(total) * gain
    residual_out[rows, :] = residual
    return residual


def after_feed(total, ins, outs, rows):
    residual, cotangent, gains = ins
    output, gain_out = outs
    gain = gains[3:4, :]
    normed = total * row_factor(total) * gain
    output[rows, :] = (residual[rows, :] + normed).astype(BF16)
    back, term = row_norm_back(total, gain, cotangent[rows, :].astype(F32))
    gain_out[...] += term
    return back


def after_back(total, ins, outs, rows):
    projected, cotangent, gains = ins
    grad_out, gain_out = outs
    grad = cotangent[rows, :].astype(F32) + total
    grad_out[rows, :] = grad
    back, term = row_norm_back(projected[rows, :], gains[2:3, :], grad)
    gain_out[...] += term
    return back


def after_input(total, ins, outs, rows):
    (grad,), (result,) = ins, outs
    result[rows, :] = grad[rows, :] + total
    return None


def pass_tokens(total, ins, outs, rows):
    return ins[0][rows, :]


class Exchange:
    def __init__(self, spans, rows, width, piece, reduce, spread, row_fn, n_in, n_out, gain, extra=None):
        self.extra = extra
        self.spans, self.rows, self.width, self.piece = spans, rows, width, piece
        self.reduce, self.spread, self.row_fn = reduce, spread, row_fn
        self.n_in, self.n_out, self.gain = n_in, n_out, gain
        self.count = rows // piece

    def scratch(self):
        spans, count = self.spans, self.count
        block = pltpu.VMEM((spans * self.rows, self.width), BF16)
        sems = pltpu.SemaphoreType.DMA((spans, count))
        items = []
        if self.reduce:
            items += [block] * 4 + [pltpu.SemaphoreType.DMA] + [sems] * 6
        if self.spread:
            items += [pltpu.VMEM((2 * spans * self.rows, self.width), BF16)]
            items += [sems] * 7 + [pltpu.SemaphoreType.DMA]
        if self.extra is not None:
            items += self.extra.scratch()
        return items

    def body(self, *refs):
        spans, rows, piece, count = self.spans, self.rows, self.piece, self.count
        refs = list(refs)
        take = lambda n: [refs.pop(0) for _ in range(n)]
        partial = take(1)[0] if self.reduce else None
        ins = take(self.n_in)
        extra = self.extra
        if extra is not None:
            extra.ins = take(extra.n_in)
        outs = take(self.n_out)
        if extra is not None:
            extra.outs = take(extra.n_out)
        gathered = take(1)[0] if self.spread else None
        if self.reduce:
            own, near, from_left, from_right = take(4)
            (load_sem,) = take(1)
            near_send, near_recv, right_send, right_recv, left_send, left_recv = take(6)
        if self.spread:
            (held,) = take(1)
            fwd_send, fwd_recv, bwd_send, bwd_recv, own_send, side_send, side_recv = take(7)
            (store_sem,) = take(1)
        if extra is not None:
            extra.held = refs
        core = lax.axis_index("core")
        place = lax.axis_index("ctx")
        other = 1 - core
        has_left = place > 0
        has_right = place < spans - 1

        def at(block, k):
            return pl.ds(pl.multiple_of(block * rows + k * piece, piece), piece)

        def held_at(seq, block, k):
            return pl.ds(pl.multiple_of((seq * spans + block) * rows + k * piece, piece), piece)

        def remote(src, dst, send, recv, **device):
            return pltpu.make_async_remote_copy(
                src_ref=src, dst_ref=dst, send_sem=send, recv_sem=recv,
                device_id=device, device_id_type=MESH_ID,
            )

        barrier = pltpu.get_barrier_semaphore()
        if extra is not None:
            if not extra.met:
                meet_all(spans)
        else:
            pl.semaphore_signal(barrier, 1, device_id={"core": other}, device_id_type=MESH_ID)

            @pl.when(has_left)
            def _():
                pl.semaphore_signal(barrier, 1, device_id={"ctx": place - 1}, device_id_type=MESH_ID)

            @pl.when(has_right)
            def _():
                pl.semaphore_signal(barrier, 1, device_id={"ctx": place + 1}, device_id_type=MESH_ID)

            pl.semaphore_wait(barrier, 1 + has_left.astype(jnp.int32) + has_right.astype(jnp.int32))

        if self.gain is not None:
            outs[self.gain][...] = jnp.zeros_like(outs[self.gain])

        def near_copy(d, k):
            return remote(
                partial.at[held_at(other, d, k)], near.at[at(d, k)],
                near_send.at[d, k], near_recv.at[d, k], core=other,
            )

        def right_copy(d, k):
            return remote(
                own.at[at(d, k)], from_left.at[at(d, k)],
                right_send.at[d, k], right_recv.at[d, k], ctx=place + 1,
            )

        def left_copy(d, k):
            return remote(
                own.at[at(d, k)], from_right.at[at(d, k)],
                left_send.at[d, k], left_recv.at[d, k], ctx=place - 1,
            )

        def fwd_copy(o, k, send):
            where = held_at(core, o, k)
            return remote(held.at[where], held.at[where], send, fwd_recv.at[o, k], ctx=place + 1)

        def bwd_copy(o, k, send):
            where = held_at(core, o, k)
            return remote(held.at[where], held.at[where], send, bwd_recv.at[o, k], ctx=place - 1)

        def side_copy(o, k):
            where = held_at(core, o, k)
            return remote(held.at[where], held.at[where], side_send.at[o, k], side_recv.at[o, k], core=other)

        if extra is not None:
            extra.start()
        if self.reduce:
            load = pltpu.make_async_copy(
                partial.at[pl.ds(pl.multiple_of(core * spans * rows, rows), spans * rows)], own, load_sem
            )
            load.start()

            @pl.loop(0, count)
            def _(k):
                for j in range(spans):
                    near_copy(j, k).start()

            load.wait()

        def base(d, k):
            near_copy(d, k).wait_recv()
            return own[at(d, k), :].astype(F32) + near[at(d, k), :].astype(F32)

        def pass_on(d, k, arrived, copy, later):
            value = base(d, k)

            @pl.when(later)
            def _():
                copy(d, k).wait_recv()

            before = arrived[at(d, k), :].astype(F32)
            value = value + jnp.where(later, before, jnp.zeros_like(before))
            own[at(d, k), :] = value.astype(BF16)
            copy(d, k).start()

        def pass_right(k):
            for d in range(spans - 1, 0, -1):

                @pl.when(d > place)
                def _():
                    pass_on(d, k, from_left, right_copy, has_left)

        def pass_left(k):
            for d in range(spans - 1):

                @pl.when(d < place)
                def _():
                    pass_on(d, k, from_right, left_copy, has_right)

        def finish_step(k):
            total = None
            if self.reduce:
                total = base(place, k)

                @pl.when(has_left)
                def _():
                    right_copy(place, k).wait_recv()

                @pl.when(has_right)
                def _():
                    left_copy(place, k).wait_recv()

                zero = jnp.zeros_like(total)
                total = total + jnp.where(has_left, from_left[at(place, k), :].astype(F32), zero)
                total = total + jnp.where(has_right, from_right[at(place, k), :].astype(F32), zero)
            own_rows = pl.ds(pl.multiple_of(k * piece, piece), piece)
            result = self.row_fn(total, ins, outs, own_rows)
            if self.spread:
                held[held_at(core, place, k), :] = result.astype(BF16)

                @pl.when(has_right)
                def _():
                    fwd_copy(place, k, fwd_send.at[place, k]).start()

                @pl.when(has_left)
                def _():
                    bwd_copy(place, k, bwd_send.at[place, k]).start()

                side_copy(place, k).start()

        def relay_step(k, j):
            if True:

                @pl.when(place - j >= 0)
                def _():
                    fwd_copy(place - j, k, fwd_send.at[place - j, k]).wait_recv()

                    @pl.when(has_right)
                    def _():
                        fwd_copy(place - j, k, fwd_send.at[place - j, k]).start()

                    side_copy(place - j, k).start()

                @pl.when(place + j < spans)
                def _():
                    bwd_copy(place + j, k, bwd_send.at[place + j, k]).wait_recv()

                    @pl.when(has_left)
                    def _():
                        bwd_copy(place + j, k, bwd_send.at[place + j, k]).start()

                    side_copy(place + j, k).start()

        lag = spans - 1 if self.reduce else 0

        def due(k, run):
            @pl.when(jnp.logical_and(k >= 0, k < count))
            def _():
                run(k)

        @pl.loop(0, count + lag + (LAGJ * (spans - 1) if self.spread else 0))
        def _(t):
            if self.reduce:
                due(t - place, pass_right)
                due(t - (spans - 1 - place), pass_left)
                due(t - jnp.maximum(place, spans - 1 - place), finish_step)
            else:

                @pl.when(t == 0)
                def _():
                    for k in range(count):
                        finish_step(k)

            if self.spread:
                for j in range(1, spans):
                    after = t - lag - j * LAGJ

                    @pl.when(jnp.logical_and(after >= 0, after < count))
                    def _():
                        relay_step(after, j)
            if extra is not None:
                extra.tick(t)

        if extra is not None:
            extra.finish(count + lag + (LAGJ * (spans - 1) if self.spread else 0))
        if self.spread:

            @pl.loop(0, count)
            def _(k):
                for o in range(spans):
                    side_copy(o, k).wait_recv()

            store = pltpu.make_async_copy(held, gathered, store_sem)
            store.start()

        @pl.loop(0, count)
        def _(k):
            for d in range(spans):
                if self.reduce:
                    near_copy(d, k).wait_send()

                    @pl.when(d > place)
                    def _():
                        right_copy(d, k).wait_send()

                    @pl.when(d < place)
                    def _():
                        left_copy(d, k).wait_send()

                if self.spread:
                    side_copy(d, k).wait_send()

                    @pl.when(jnp.logical_and(d <= place, has_right))
                    def _():
                        fwd_copy(d, k, fwd_send.at[d, k]).wait_send()

                    @pl.when(jnp.logical_and(d >= place, has_left))
                    def _():
                        bwd_copy(d, k, bwd_send.at[d, k]).wait_send()

        if self.spread:
            store.wait()


def owner_of(chip, core, place, spans):
    member = core * spans + place
    return member // 2, lax.rem(member, 2), chip


def summer_of(chip, core, place, spans):
    member = chip * 2 + core
    return place, member // spans, lax.rem(member, spans)


def stays(chip, core, place, spans):
    to_chip, to_core, to_place = owner_of(chip, core, place, spans)
    return jnp.logical_and(to_chip == chip, jnp.logical_and(to_core == core, to_place == place))


def meet_all(spans):
    greet_all(spans, False)
    wait_all(spans, False)


def greet_all(spans, moves):
    chips = lax.axis_size("chip")
    barrier = pltpu.get_barrier_semaphore()
    chip = lax.axis_index("chip")
    core = lax.axis_index("core")
    place = lax.axis_index("ctx")
    for s in range(1, chips):
        pl.semaphore_signal(
            barrier, 1, device_id={"chip": lax.rem(chip + s, chips)}, device_id_type=MESH_ID
        )
    for s in range(1, 2 * spans):
        to_core, to_place = step_member(core, place, s, spans)
        pl.semaphore_signal(
            barrier, 1, device_id={"core": to_core, "ctx": to_place}, device_id_type=MESH_ID
        )
    if moves:

        @pl.when(jnp.logical_not(stays(chip, core, place, spans)))
        def _():
            for find in (owner_of, summer_of):
                to_chip, to_core, to_place = find(chip, core, place, spans)
                pl.semaphore_signal(
                    barrier, 1, device_id={"chip": to_chip, "core": to_core, "ctx": to_place}, device_id_type=MESH_ID
                )


def wait_all(spans, moves):
    count = lax.axis_size("chip") - 1 + 2 * spans - 1
    if moves:
        here = stays(lax.axis_index("chip"), lax.axis_index("core"), lax.axis_index("ctx"), spans)
        count = count + 2 * jnp.logical_not(here).astype(jnp.int32)
    pl.semaphore_wait(pltpu.get_barrier_semaphore(), count)


def step_member(core, place, s, spans):
    return lax.rem(core + s % 2, 2), lax.rem(place + s // 2, spans)


def meet_other_core():
    barrier = pltpu.get_barrier_semaphore()
    other = 1 - lax.axis_index("core")
    pl.semaphore_signal(barrier, 1, device_id={"core": other}, device_id_type=MESH_ID)
    pl.semaphore_wait(barrier, 1)


def split_copies(gate, up, down, gate_up_out, down_out, held, load_sem, store_sem, send_sem, recv_sem):
    core = lax.axis_index("core")
    other = 1 - core
    rows, width = gate.shape
    half = width // 2
    where = pl.ds(pl.multiple_of(core * rows, rows), rows)
    places = [gate_up_out.at[where, :half], gate_up_out.at[where, half:], down_out.at[where, :]]
    mine = pl.ds(pl.multiple_of(core * half, half), half)
    theirs = pl.ds(pl.multiple_of(other * half, half), half)
    arrays = list(enumerate((gate, up, down)))
    loads = [pltpu.make_async_copy(a.at[:, mine], held.at[i], load_sem.at[i]) for i, a in arrays]
    sends = [
        pltpu.make_async_remote_copy(
            src_ref=a.at[:, theirs], dst_ref=places[i], send_sem=send_sem.at[i], recv_sem=recv_sem.at[i],
            device_id={"core": other}, device_id_type=MESH_ID,
        )
        for i, a in arrays
    ]
    stores = [pltpu.make_async_copy(held.at[i], places[i], store_sem.at[i]) for i in range(3)]
    return loads, sends, stores


def join_body(gate, up, down, gate_out, up_out, down_out, arrived, send_sem, recv_sem):
    core = lax.axis_index("core")
    other = 1 - core
    rows, width = gate_out.shape
    half = width // 2
    meet_other_core()
    theirs = pl.ds(pl.multiple_of(other * rows, rows), rows)
    pairs = ((gate, gate_out), (up, up_out), (down, down_out))
    sends = [
        pltpu.make_async_remote_copy(
            src_ref=a.at[theirs], dst_ref=arrived.at[i], send_sem=send_sem.at[i], recv_sem=recv_sem.at[i],
            device_id={"core": other}, device_id_type=MESH_ID,
        )
        for i, (a, _) in enumerate(pairs)
    ]
    for send in sends:
        send.start()
    mine = pl.ds(pl.multiple_of(core * half, half), half)
    far = pl.ds(pl.multiple_of(other * half, half), half)
    step = 16

    def rows_at(i, base):
        return pl.ds(pl.multiple_of(base + i * step, step), step)

    @pl.loop(0, rows // step)
    def _(i):
        for a, b in pairs:
            b[rows_at(i, 0), mine] = a[rows_at(i, core * rows), :].astype(F32)

    for send in sends:
        send.wait()

    @pl.loop(0, rows // step)
    def _(i):
        for n, (_, b) in enumerate(pairs):
            b[rows_at(i, 0), far] = arrived[n, rows_at(i, 0), :].astype(F32)


def join_columns(gate, up, down):
    rows, half = gate.shape[0] // 2, gate.shape[1]
    vmem = pl.BlockSpec(memory_space=pltpu.VMEM)
    three = pltpu.SemaphoreType.DMA((3,))
    return pl.pallas_call(
        join_body,
        out_shape=[jax.ShapeDtypeStruct((rows, 2 * half), F32)] * 3,
        in_specs=[vmem] * 3,
        out_specs=[vmem] * 3,
        scratch_shapes=[pltpu.VMEM((3, rows, half), BF16), three, three],
        compiler_params=pltpu.CompilerParams(collective_id=7, has_side_effects=True, vmem_limit_bytes=32 << 20),
        name="join_columns",
    )(gate, up, down)


class Extra:
    met = False

    def remote(self, src, dst, send, recv, **device):
        return pltpu.make_async_remote_copy(
            src_ref=src, dst_ref=dst, send_sem=send, recv_sem=recv,
            device_id=device, device_id_type=MESH_ID,
        )

    def locate(self):
        self.chip = lax.axis_index("chip")
        self.core = lax.axis_index("core")
        self.place = lax.axis_index("ctx")
        self.me = self.core * self.spans + self.place


class QkvWeights(Extra):
    n_in, n_out = 2, 2
    met = True

    def __init__(self, spans, chips, cut, ids):
        self.spans, self.chips = spans, chips
        self.members, self.block, self.columns = cut.shape
        self.ids_shape = ids.shape
        vmem = pl.BlockSpec(memory_space=pltpu.VMEM)
        self.out_shapes = [
            jax.ShapeDtypeStruct((chips * self.members * self.block, self.columns), BF16),
            jax.ShapeDtypeStruct((self.members * ids.shape[0], ids.shape[1]), jnp.int32),
        ]
        self.out_specs = [vmem, vmem]

    def scratch(self):
        rows = self.chips * self.members * self.block
        sems = pltpu.SemaphoreType.DMA((self.members,))
        cross = pltpu.SemaphoreType.DMA((self.chips, self.members))
        ids = (self.members * self.ids_shape[0], self.ids_shape[1])
        return [pltpu.VMEM((rows, self.columns), BF16), pltpu.VMEM(ids, jnp.int32)] + [sems] * 4 + [cross] * 2

    def at(self, chip, m):
        return pl.ds(pl.multiple_of((chip * self.members + m) * self.block, self.block), self.block)

    def ids_at(self, m):
        return pl.ds(pl.multiple_of(m * self.ids_shape[0], self.ids_shape[0]), self.ids_shape[0])

    def block_copy(self, s):
        full, _, send, recv = self.held[:4]
        core, place = step_member(self.core, self.place, s, self.spans)
        return self.remote(
            self.ins[0].at[core * self.spans + place], full.at[self.at(self.chip, self.me)],
            send.at[s], recv.at[s], core=core, ctx=place,
        )

    def ids_copy(self, s):
        all_ids, send, recv = self.held[1], self.held[4], self.held[5]
        core, place = step_member(self.core, self.place, s, self.spans)
        return self.remote(
            self.ins[1], all_ids.at[self.ids_at(self.me)], send.at[s], recv.at[s], core=core, ctx=place
        )

    def source(self, s):
        core = lax.rem(self.core + s % 2, 2)
        return core * self.spans + lax.rem(self.place + self.spans - s // 2, self.spans)

    def chip_copy(self, s, m):
        full, _, _, _, _, _, send, recv = self.held
        where = self.at(self.chip, m)
        return self.remote(
            full.at[where], full.at[where], send.at[s, m], recv.at[s, m], chip=lax.rem(self.chip + s, self.chips)
        )

    def square_copy(self, kind, s):
        full, _, _, _, _, _, send, recv = self.held
        along_x, along_y, _ = square(self.chip)
        m = self.me if s == 0 else self.source(s)
        owner = self.chip if kind < 2 else (along_x if s % 2 == 0 else along_y)
        to = (along_x, along_y, along_y if s % 2 == 0 else along_x)[kind]
        where = self.at(owner, m)
        return self.remote(full.at[where], full.at[where], send.at[kind, s], recv.at[kind, s], chip=to)

    def start(self):
        self.locate()
        cut, ids = self.ins
        full, all_ids = self.held[:2]
        for s in range(1, self.members):
            self.block_copy(s).start()
        for s in range(1, self.members):
            self.ids_copy(s).start()
        full[self.at(self.chip, self.me), :] = cut[self.me]
        all_ids[self.ids_at(self.me), :] = ids[...]

    def send_block(self, s):
        m = self.me if s == 0 else self.source(s)
        if s > 0:
            self.block_copy(s).wait_recv()
        if self.chips == 4:
            for kind in (0, 1) if s % 2 == 0 else (1, 0):
                self.square_copy(kind, s).start()
            return
        for step in range(1, self.chips):
            self.chip_copy(step, m).start()

    def pass_block(self, s):
        self.square_copy(s % 2, s).wait_recv()
        self.square_copy(2, s).start()

    def tick(self, t):
        @pl.when(t == 0)
        def _():
            for s in range(self.members):
                self.send_block(s)

        half = self.members // 2
        for n in range(2):

            @pl.when(t == PASS_AT + n)
            def _():
                if self.chips == 4:
                    for s in range(n * half, (n + 1) * half):
                        self.pass_block(s)
                if n == 1:
                    self.after_blocks()

    def finish(self, ticks):
        full, all_ids = self.held[:2]
        for s in range(1, self.members):
            self.ids_copy(s).wait_recv()
            self.block_copy(s).wait_send()
            self.ids_copy(s).wait_send()

        if self.chips == 4:
            for s in range(self.members):
                for kind in range(3):
                    self.square_copy(kind, s).wait_send()
                    if kind != s % 2:
                        self.square_copy(kind, s).wait_recv()
        else:

            @pl.loop(0, self.members)
            def _(m):
                for s in range(1, self.chips):
                    self.chip_copy(s, m).wait()

        self.outs[0][...] = full[...]
        self.outs[1][...] = all_ids[...]


class QkvGrads(Extra):
    n_in, n_out = 3, 3
    met = True

    def __init__(self, spans, chips, members, grads, sums, out_grads):
        self.spans, self.chips, self.members = spans, chips, members
        self.out_rows = out_grads.shape[0] // chips
        self.block, self.columns = grads.shape[0] // (chips * members), grads.shape[1]
        self.part = self.columns // 3
        self.width = self.part * members
        self.own_rows = self.part // 128
        self.sum_rows = sums.shape[0]
        vmem = pl.BlockSpec(memory_space=pltpu.VMEM)
        self.out_shapes = [
            jax.ShapeDtypeStruct((self.block, 3 * self.width), BF16),
            jax.ShapeDtypeStruct((4, self.width // 128, 128), F32),
            jax.ShapeDtypeStruct((self.out_rows, self.width), BF16),
        ]
        self.out_specs = [vmem] * 3

    def scratch(self):
        sems = pltpu.SemaphoreType.DMA((self.members,))
        chip_sems = pltpu.SemaphoreType.DMA((self.chips,))
        cross = pltpu.SemaphoreType.DMA((self.chips, self.members))
        return [
            pltpu.VMEM((3 if self.chips == 4 else self.chips, self.members, self.block, self.columns), BF16),
            pltpu.VMEM((self.members, self.block, self.columns), BF16),
            pltpu.VMEM((self.members, self.block, self.columns), BF16),
            pltpu.VMEM((self.members, self.block, self.columns), BF16),
            pltpu.VMEM((self.chips, self.sum_rows, 128), F32),
            pltpu.VMEM((self.sum_rows, 128), F32),
            pltpu.VMEM((self.members, self.sum_rows, 128), F32),
            pltpu.VMEM((self.chips, self.out_rows, self.width), BF16),
            pltpu.VMEM((self.out_rows, self.width), BF16),
            pltpu.VMEM((self.out_rows, self.width), BF16),
        ] + [cross] * 2 + [sems] * 2 + [chip_sems] * 2 + [sems] * 2 + [chip_sems] * 2 + [pltpu.SemaphoreType.DMA] * 2

    def at(self, chip, m):
        return pl.ds(pl.multiple_of((chip * self.members + m) * self.block, self.block), self.block)

    def chip_copy(self, s, m):
        other = lax.rem(self.chip + s, self.chips)
        return self.remote(
            self.ins[0].at[self.at(other, m)], self.arrived.at[s, m],
            self.cross_send.at[s, m], self.cross_recv.at[s, m], chip=other,
        )

    def member_copy(self, s):
        core, place = step_member(self.core, self.place, s, self.spans)
        return self.remote(
            self.summed.at[core * self.spans + place], self.columns_in.at[self.me],
            self.member_send.at[s], self.member_recv.at[s], core=core, ctx=place,
        )

    def sums_chip(self, s):
        return self.remote(
            self.ins[1], self.sums_in.at[s], self.sums_send.at[s], self.sums_recv.at[s],
            chip=lax.rem(self.chip + s, self.chips),
        )

    def sums_member(self, s):
        core, place = step_member(self.core, self.place, s, self.spans)
        return self.remote(
            self.sums_chips, self.sums_members.at[self.me], self.last_send.at[s], self.last_recv.at[s],
            core=core, ctx=place,
        )

    def out_copy(self, s):
        other = lax.rem(self.chip + s, self.chips)
        rows = pl.ds(pl.multiple_of(other * self.out_rows, self.out_rows), self.out_rows)
        return self.remote(
            self.ins[2].at[rows], self.out_in.at[s], self.out_send.at[s], self.out_recv.at[s], chip=other
        )

    def move_copy(self):
        chip, core, place = owner_of(self.chip, self.core, self.place, self.spans)
        return self.remote(
            self.out_sum, self.out_final, self.move_send, self.move_recv, chip=chip, core=core, ctx=place
        )

    def square_copy(self, kind, i):
        along_x, along_y, across = square(self.chip)
        m = self.nth(i)
        first, second = (along_x, along_y) if i % 2 == 0 else (along_y, along_x)
        if kind == 2:
            src, to = self.passing.at[m], second
        else:
            src, to = self.ins[0].at[self.at((across, first)[kind], m)], first
        return self.remote(
            src, self.arrived.at[kind, m], self.cross_send.at[kind, m], self.cross_recv.at[kind, m], chip=to
        )

    def nth(self, i):
        return lax.rem(self.me + 1 + i, self.members)

    def pass_blocks(self):
        along_x, along_y, _ = square(self.chip)
        for i in range(self.members):
            m = self.nth(i)
            self.square_copy(0, i).wait_recv()
            mine = self.ins[0][self.at(along_y if i % 2 == 0 else along_x, m), :]
            self.passing[m] = (mine.astype(F32) + self.arrived[0, m].astype(F32)).astype(BF16)
            self.square_copy(2, i).start()

    def begin(self):
        self.locate()
        (
            self.arrived, self.passing, self.summed, self.columns_in, self.sums_in, self.sums_chips, self.sums_members,
            self.out_in, self.out_sum, self.out_final,
            self.cross_send, self.cross_recv, self.member_send, self.member_recv,
            self.sums_send, self.sums_recv, self.last_send, self.last_recv,
            self.out_send, self.out_recv, self.move_send, self.move_recv,
        ) = self.held
        for s in range(1, self.chips):
            self.out_copy(s).start()

    def start(self):
        for s in range(1, self.chips):
            self.sums_chip(s).start()

    def send_shares(self):
        if self.chips == 4:
            for i in range(self.members):
                self.square_copy(0, i).start()
                self.square_copy(1, i).start()
            return

        @pl.loop(0, self.members)
        def _(i):
            m = lax.rem(self.me + 1 + i, self.members)
            for s in range(1, self.chips):
                self.chip_copy(s, m).start()

    def add_block(self, m):
        total = self.ins[0][self.at(self.chip, m), :].astype(F32)
        for s in range(1, 3 if self.chips == 4 else self.chips):
            self.chip_copy(s, m).wait_recv()
            total = total + self.arrived[s, m].astype(F32)
        self.summed[m] = total.astype(BF16)

    def send_blocks(self, first, last):
        for s in range(first, last):
            core, place = step_member(self.core, self.place, s, self.spans)
            self.add_block(core * self.spans + place)
            self.member_copy(s).start()

    def tick(self, t):
        @pl.when(t == 0)
        def _():
            self.work()
            self.send_shares()

        @pl.when(t == LATE_TICK)
        def _():
            self.late()

        if self.chips == 4:

            @pl.when(t == PASS_TICK)
            def _():
                self.pass_blocks()

        @pl.when(t == 1)
        def _():
            total = self.ins[1][...]
            for s in range(1, self.chips):
                self.sums_chip(s).wait_recv()
                total = total + self.sums_in[s]
            self.sums_chips[...] = total
            self.sums_members[self.me] = total
            for s in range(1, self.members):
                self.sums_member(s).start()

        @pl.when(t == 2)
        def _():
            rows = pl.ds(pl.multiple_of(self.chip * self.out_rows, self.out_rows), self.out_rows)
            total = self.ins[2][rows, :].astype(F32)
            for s in range(1, self.chips):
                self.out_copy(s).wait_recv()
                total = total + self.out_in[s].astype(F32)
            self.out_sum[...] = total.astype(BF16)

            @pl.when(stays(self.chip, self.core, self.place, self.spans))
            def _():
                self.out_final[...] = total.astype(BF16)

            @pl.when(jnp.logical_not(stays(self.chip, self.core, self.place, self.spans)))
            def _():
                self.move_copy().start()

    def finish(self, ticks):
        self.send_blocks(1, self.members)
        self.add_block(self.me)
        self.columns_in[self.me] = self.summed[self.me]
        for s in range(1, self.members):
            self.sums_member(s).wait()
        wide = self.width // 128
        for i in range(2):
            total = self.sums_members[0, i * wide : (i + 1) * wide, :]
            for m in range(1, self.members):
                total = total + self.sums_members[m, i * wide : (i + 1) * wide, :]
            self.outs[1][2 + i] = total
            base = 2 * wide + i * self.own_rows
            for m in range(self.members):
                self.outs[1][i, m * self.own_rows : (m + 1) * self.own_rows, :] = self.sums_members[
                    m, base : base + self.own_rows, :
                ]
        for s in range(1, self.members):
            self.member_copy(s).wait()
        for m in range(self.members):
            for i in range(3):
                self.outs[0][:, i * self.width + m * self.part : i * self.width + (m + 1) * self.part] = (
                    self.columns_in[m, :, i * self.part : (i + 1) * self.part]
                )
        @pl.when(jnp.logical_not(stays(self.chip, self.core, self.place, self.spans)))
        def _():
            self.move_copy().wait()

        self.outs[2][...] = self.out_final[...]
        for s in range(1, self.chips):
            self.sums_chip(s).wait_send()
            self.out_copy(s).wait_send()

        @pl.loop(0, self.members)
        def _(m):
            for s in range(3) if self.chips == 4 else range(1, self.chips):
                self.chip_copy(s, m).wait_send()


def rope_tables(positions):
    half = HEAD_DIM // 2
    frequency = ROPE_BASE ** (-(jnp.arange(half, dtype=F32) * 2.0 / HEAD_DIM))
    angles = positions[:, None] * frequency[None, :]
    cosine = jnp.cos(angles)
    sine = jnp.sin(angles)
    return (jnp.concatenate([cosine, cosine], 1), jnp.concatenate([sine, sine], 1))


def dot(left, right):
    return jnp.dot(left, right, preferred_element_type=F32)


def dot_rows(left, right):
    return lax.dot_general(left, right, (((1,), (1,)), ((), ())), preferred_element_type=F32)


def dot_first(left, right):
    return lax.dot_general(left, right, (((0,), (0,)), ((), ())), preferred_element_type=F32)


def gather(values, axes):
    return lax.all_gather(values, axes, axis=0, tiled=True)


def scatter_sum(values, axes):
    return lax.psum_scatter(values, axes, scatter_dimension=0, tiled=True)


FF_TILE = 512
SUM_TILE = 1024
BATCH_PIECE = 16
DOWN_TICK = 6
GRAD_TILE = 256


def square(chip):
    along_x = chip + 1 - 2 * lax.rem(chip, 2)
    return along_x, lax.rem(chip + 2, 4), lax.rem(along_x + 2, 4)


class SquareSum:
    def __init__(self, chip, block, landing, send, recv):
        self.chip, self.block, self.landing, self.send, self.recv = chip, block, landing, send, recv
        self.x, self.y, self.across = square(chip)

    def copy(self, i):
        owner = (self.across, self.across, self.x, self.y, self.y, self.x)[i]
        half = (0, 1, 0, 1, 0, 1)[i]
        to = (self.x, self.y, self.x, self.y, self.y, self.x)[i]
        return pltpu.make_async_remote_copy(
            src_ref=self.block(owner, half), dst_ref=self.landing.at[i], send_sem=self.send.at[i],
            recv_sem=self.recv.at[i], device_id={"chip": to}, device_id_type=MESH_ID,
        )

    def begin(self, first):
        self.copy(first).start()
        self.copy(first + 1).start()

    def relay(self):
        for i, owner, half in ((0, self.y, 0), (1, self.x, 1)):
            self.copy(i).wait_recv()
            ref = self.block(owner, half)
            ref[...] = (ref[...].astype(F32) + self.landing[i].astype(F32)).astype(BF16)
        self.begin(4)

    def finish(self, half):
        for i in (2 + half, 4 + half):
            self.copy(i).wait_recv()
        for i in (0 + half, 2 + half, 4 + half):
            self.copy(i).wait_send()
        total = self.block(self.chip, half)[...].astype(F32)
        return total + self.landing[2 + half].astype(F32) + self.landing[4 + half].astype(F32)


class Middle:
    def __init__(self, spans, rows, width, hidden, piece):
        self.spans, self.rows, self.width, self.hidden, self.piece = spans, rows, width, hidden, piece
        self.count = rows // piece
        self.block = spans * piece
        self.batch = 2 * self.block

    def body(
        self, chips, partial, tokens, cotangent, gains, gate_up, gate_up_w, down,
        output, residual_grad, gain_feed, gain_attn, down_sum, gate_sum, residual_all, feed_grad_all, gate_part, up_part, projected_all,
        residual, projected, own, near, from_left, from_right, held, wide, act, back, up_weights, down_weights, slices, given, landed,
        load_sem, weight_sem, store_sem, slice_sem, part_sem, free_sem, near_send, near_recv, right_send, right_recv, left_send, left_recv,
        fwd_send, fwd_recv, bwd_send, bwd_recv, side_send, side_recv, down_send, down_recv, give_send, give_recv, take_send, take_recv, pass_send, pass_recv,
    ):
        spans, rows, piece, count = self.spans, self.rows, self.piece, self.count
        width, hidden, block, batch = self.width, self.hidden, self.block, self.batch
        core = lax.axis_index("core")
        place = lax.axis_index("ctx")
        other = 1 - core
        last = spans - 1
        has_left = place > 0
        has_right = place < last

        def turn_of(o):
            return jnp.maximum(o, last - o)

        def at(d, k):
            return pl.ds(pl.multiple_of((k * spans + d) * piece, piece), piece)

        def at_seq(seq, d, k):
            return pl.ds(pl.multiple_of(((k * 2 + seq) * spans + d) * piece, piece), piece)

        def batch_at(k):
            return pl.ds(pl.multiple_of(k * batch, batch), batch)

        def natural(seq, d, k):
            return pl.ds(pl.multiple_of((seq * spans + d) * rows + k * piece, piece), piece)

        def remote(src, dst, send, recv, **device):
            return pltpu.make_async_remote_copy(
                src_ref=src, dst_ref=dst, send_sem=send, recv_sem=recv, device_id=device, device_id_type=MESH_ID
            )

        barrier = pltpu.get_barrier_semaphore()
        pl.semaphore_signal(barrier, 1, device_id={"core": other}, device_id_type=MESH_ID)

        @pl.when(has_left)
        def _():
            pl.semaphore_signal(barrier, 1, device_id={"ctx": place - 1}, device_id_type=MESH_ID)

        @pl.when(has_right)
        def _():
            pl.semaphore_signal(barrier, 1, device_id={"ctx": place + 1}, device_id_type=MESH_ID)

        def near_copy(e, d, k):
            src = partial.at[natural(other, d, k)] if e == 0 else own.at[at_seq(other, d, k)]
            return remote(src, near.at[at(d, k)], near_send.at[d, k], near_recv.at[d, k], core=other)

        def right_copy(d, k):
            return remote(
                own.at[at_seq(core, d, k)], from_left.at[at(d, k)], right_send.at[d, k], right_recv.at[d, k],
                ctx=place + 1,
            )

        def left_copy(d, k):
            return remote(
                own.at[at_seq(core, d, k)], from_right.at[at(d, k)], left_send.at[d, k], left_recv.at[d, k],
                ctx=place - 1,
            )

        def spread_copy(o, k, send, recv, **device):
            where = held.at[at_seq(core, o, k)]
            return remote(where, where, send.at[o, k], recv.at[o, k], **device)

        def fwd_copy(o, k):
            return spread_copy(o, k, fwd_send, fwd_recv, ctx=place + 1)

        def bwd_copy(o, k):
            return spread_copy(o, k, bwd_send, bwd_recv, ctx=place - 1)

        def side_copy(o, k):
            return spread_copy(o, k, side_send, side_recv, core=other)

        def load_own(d, k):
            return pltpu.make_async_copy(
                partial.at[natural(core, d, k)], own.at[at_seq(core, d, k)], load_sem.at[d, k]
            )

        @pl.loop(0, count)
        def _(k):
            for d in range(spans):
                load_own(d, k).start()

        chip = lax.axis_index("chip")
        shard = down.shape[0]
        here = pl.ds(pl.multiple_of(chip * shard, shard), shard)
        load_down = pltpu.make_async_copy(down, down_weights.at[here], weight_sem.at[chips])

        if chips == 4:
            along_x, along_y, across = square(chip)

        def load_up(s):
            if s == 0:
                return pltpu.make_async_copy(gate_up, up_weights.at[here], weight_sem.at[0])
            source = (along_x, along_y)[s - 1] if chips == 4 else lax.rem(chip + s, chips)
            there = pl.ds(pl.multiple_of(source * shard, shard), shard)
            return pltpu.make_async_copy(gate_up_w.at[there], up_weights.at[there], weight_sem.at[s])


        loads = 3 if chips == 4 else chips

        def up_copy(i):
            size = shard // 2
            source, to = ((along_x, along_y), (along_y, along_x))[i]
            where = pl.ds(pl.multiple_of(source * shard + i * size, size), size)
            return remote(gate_up_w.at[where], up_weights.at[where], pass_send.at[i], pass_recv.at[i], chip=to)

        def down_copy(s):
            if chips != 4:
                return remote(
                    down, down_weights.at[here], down_send.at[s], down_recv.at[s], chip=lax.rem(chip + s, chips)
                )
            half = (0, 1, 1, 0, 0, 1)[s]
            to = (along_x, along_y, along_x, along_y, along_y, along_x)[s]
            size = shard // 2
            if s < 4:
                src = down.at[half * size : (half + 1) * size]
                at_chip = chip
            else:
                at_chip = (along_x, along_y)[s - 4]
            dst = down_weights.at[pl.ds(pl.multiple_of(at_chip * shard + half * size, size), size)]
            return remote(src if s < 4 else dst, dst, down_send.at[s], down_recv.at[s], chip=to)

        def relay_down():
            for s in range(2):
                down_copy(s).wait_recv()
                down_copy(4 + s).start()

        for s in range(loads):
            load_up(s).start()
        load_down.start()
        gain_feed[...] = jnp.zeros_like(gain_feed)
        gain_attn[...] = jnp.zeros_like(gain_attn)
        for s in range(1, chips):
            pl.semaphore_signal(
                barrier, 1, device_id={"chip": lax.rem(chip + s, chips)}, device_id_type=MESH_ID
            )
        pl.semaphore_wait(barrier, chips + has_left.astype(jnp.int32) + has_right.astype(jnp.int32))
        if chips == 4:
            for i in range(2):
                up_copy(i).start()
        for s in range(4) if chips == 4 else range(1, chips):
            down_copy(s).start()

        @pl.loop(0, count)
        def _(k):
            for d in range(spans):
                near_copy(0, d, k).start()

        def base(e, d, k):
            near_copy(e, d, k).wait_recv()
            if e == 0:
                load_own(d, k).wait()
            return own[at_seq(core, d, k), :].astype(F32) + near[at(d, k), :].astype(F32)

        def pass_on(e, d, k, arrived, copy, later):
            value = base(e, d, k)

            @pl.when(later)
            def _():
                copy(d, k).wait_recv()

            before = arrived[at(d, k), :].astype(F32)
            value = value + jnp.where(later, before, jnp.zeros_like(before))
            own[at_seq(core, d, k), :] = value.astype(BF16)
            copy(d, k).start()

        def pass_right(e, k):
            for d in range(last, 0, -1):

                @pl.when(d > place)
                def _():
                    pass_on(e, d, k, from_left, right_copy, has_left)

        def pass_left(e, k):
            for d in range(last):

                @pl.when(d < place)
                def _():
                    pass_on(e, d, k, from_right, left_copy, has_right)

        def finish(e, k):
            total = base(e, place, k)

            @pl.when(has_left)
            def _():
                right_copy(place, k).wait_recv()

            @pl.when(has_right)
            def _():
                left_copy(place, k).wait_recv()

            zero = jnp.zeros_like(total)
            total = total + jnp.where(has_left, from_left[at(place, k), :].astype(F32), zero)
            total = total + jnp.where(has_right, from_right[at(place, k), :].astype(F32), zero)
            mine = pl.ds(pl.multiple_of(k * piece, piece), piece)
            if e == 0:
                result = after_projected(total, (tokens, gains), (residual, projected), mine)
            elif e == 1:
                result = after_feed(total, (residual, cotangent, gains), (output, gain_feed), mine)
            else:
                result = after_back(total, (projected, cotangent, gains), (residual_grad, gain_attn), mine)
            held[at_seq(core, place, k), :] = result.astype(BF16)

            @pl.when(has_right)
            def _():
                fwd_copy(place, k).start()

            @pl.when(has_left)
            def _():
                bwd_copy(place, k).start()

            side_copy(place, k).start()

        def relay_right(o, k):
            fwd_copy(o, k).wait_recv()

            @pl.when(has_right)
            def _():
                fwd_copy(o, k).start()

            side_copy(o, k).start()

        def relay_left(o, k):
            bwd_copy(o, k).wait_recv()

            @pl.when(has_left)
            def _():
                bwd_copy(o, k).start()

            side_copy(o, k).start()

        def gathered(k):
            for o in range(spans):
                side_copy(o, k).wait_recv()

        def sums_sent(e, k):
            for d in range(spans):
                near_copy(e, d, k).wait_send()

                @pl.when(d > place)
                def _():
                    right_copy(d, k).wait_send()

                @pl.when(d < place)
                def _():
                    left_copy(d, k).wait_send()

        def spread_sent(k):
            for o in range(spans):
                side_copy(o, k).wait_send()

                @pl.when(jnp.logical_and(o <= place, has_right))
                def _():
                    fwd_copy(o, k).wait_send()

                @pl.when(jnp.logical_and(o >= place, has_left))
                def _():
                    bwd_copy(o, k).wait_send()

        def store(src, dst, k, sem):
            return pltpu.make_async_copy(src, dst.at[batch_at(k)], sem)

        def forward(k):
            @pl.when(k == 0)
            def _():
                for s in range(loads):
                    load_up(s).wait()
                if chips == 4:
                    for i in range(2):
                        up_copy(i).wait()

            gathered(k)
            keep = store(held.at[batch_at(k)], residual_all, k, store_sem.at[0])
            keep.start()

            @pl.loop(0, hidden // FF_TILE)
            def _(n):
                low = pl.ds(pl.multiple_of(n * FF_TILE, FF_TILE), FF_TILE)
                high = pl.ds(pl.multiple_of(hidden + n * FF_TILE, FF_TILE), FF_TILE)
                gate = dot(held[batch_at(k), :], up_weights[:, low])
                up = dot(held[batch_at(k), :], up_weights[:, high])
                wide[batch_at(k), low] = gate
                wide[batch_at(k), high] = up
                act[batch_at(k), low] = (gate * (1.0 / (1.0 + jnp.exp(-gate))) * up).astype(BF16)

            sums_sent(0, k)

            @pl.when(k == 0)
            def _():
                load_down.wait()
                for s in range(1, chips) if chips != 4 else range(6):
                    down_copy(s).wait_send()
                    if chips != 4 or s >= 2:
                        down_copy(s).wait_recv()

            @pl.loop(0, width // SUM_TILE)
            def _(n):
                columns = pl.ds(pl.multiple_of(n * SUM_TILE, SUM_TILE), SUM_TILE)
                own[batch_at(k), columns] = dot_rows(act[batch_at(k), :], down_weights[columns, :]).astype(BF16)

            keep.wait()
            spread_sent(k)
            for d in range(spans):
                near_copy(1, d, k).start()

        down_tiles = width // GRAD_TILE
        per_chip = shard // GRAD_TILE

        def tile_rows(n):
            return pl.ds(pl.multiple_of(n * GRAD_TILE, GRAD_TILE), GRAD_TILE)

        if chips == 4:
            assert per_chip == 2
            turns = [(across, 0), (across, 1), (along_x, 0), (along_y, 1), (along_y, 0), (along_x, 1), (chip, 0), (chip, 1)]
            order = [owner * per_chip + half for owner, half in turns]
        else:
            order = [lax.rem(chip + 1 + j // per_chip, chips) * per_chip + j % per_chip for j in range(down_tiles)]
        tiles = [(m, order[j] if m < 2 else j) for m in range(3) for j in range(down_tiles)]

        def load_slice(j):
            m, n = tiles[j]
            source = feed_grad_all if m == 0 else residual_all
            return pltpu.make_async_copy(source.at[:, tile_rows(n)], slices.at[j % 4], slice_sem.at[j % 4])

        def half_at(owner, half):
            return pl.ds(pl.multiple_of((owner * per_chip + half) * GRAD_TILE, GRAD_TILE), GRAD_TILE)

        if chips == 4:
            sums = [
                SquareSum(
                    chip, lambda owner, half: given.at[half_at(owner, half)], landed.at[0], give_send, give_recv
                ),
                SquareSum(
                    chip, lambda owner, half: up_weights.at[half_at(owner, half), :hidden], landed.at[1], take_send, take_recv
                ),
            ]

        def give_copy(s):
            theirs = pl.ds(pl.multiple_of(lax.rem(chip + s, chips) * shard, shard), shard)
            return remote(
                given.at[theirs], down_weights.at[s * shard : (s + 1) * shard], give_send.at[s], give_recv.at[s],
                chip=lax.rem(chip + s, chips),
            )

        def part_copy(n, m):
            half = slice((m - 1) * hidden, m * hidden)
            return pltpu.make_async_copy(
                up_weights.at[tile_rows(n), half], (gate_part, up_part)[m - 1].at[tile_rows(n)], part_sem.at[m - 1, n]
            )

        def work_out(j):
            if j + 2 < len(tiles):
                load_slice(j + 2).start()
            load_slice(j).wait()
            m, n = tiles[j]
            if m == 0:
                given[tile_rows(n), :] = dot_first(slices[j % 4], act[...]).astype(BF16)
            else:
                half = slice((m - 1) * hidden, m * hidden)
                up_weights[tile_rows(n), half] = dot_first(slices[j % 4], back[:, half]).astype(BF16)

        def weight_grads(q):
            if chips == 4:
                m, r = q // 4, q % 4
                if m < 2:
                    for j in range(m * down_tiles + 2 * r, m * down_tiles + 2 * r + 2):
                        work_out(j)
                    if r < 2:
                        sums[m].begin(2 * r)
                    elif r == 2:
                        sums[m].relay()
                else:
                    for j in range(2 * down_tiles, 3 * down_tiles):
                        work_out(j)
                        part_copy(tiles[j][1], 2).start()
                return
            if q < chips:
                for j in range(q * per_chip, (q + 1) * per_chip):
                    work_out(j)
                if q == 0:
                    pl.semaphore_wait(free_sem, chips - 1)
                if q < chips - 1:
                    give_copy(q + 1).start()
                return
            first = down_tiles + 4 * (q - chips)
            for j in range(first, min(first + 4, len(tiles))):
                work_out(j)
                part_copy(tiles[j][1], tiles[j][0]).start()

        def backward(k):
            gathered(k)
            keep = store(held.at[batch_at(k)], feed_grad_all, k, store_sem.at[0])
            keep.start()

            @pl.loop(0, hidden // FF_TILE)
            def _(n):
                low = pl.ds(pl.multiple_of(n * FF_TILE, FF_TILE), FF_TILE)
                high = pl.ds(pl.multiple_of(hidden + n * FF_TILE, FF_TILE), FF_TILE)
                act_grad = dot(held[batch_at(k), :], down_weights[:, low])
                gate = wide[batch_at(k), low]
                up = wide[batch_at(k), high]
                sigmoid = 1.0 / (1.0 + jnp.exp(-gate))
                back[batch_at(k), low] = (act_grad * up * sigmoid * (1.0 + gate * (1.0 - sigmoid))).astype(BF16)
                back[batch_at(k), high] = (act_grad * (gate * sigmoid)).astype(BF16)

            sums_sent(1, k)

            @pl.loop(0, width // SUM_TILE)
            def _(n):
                columns = pl.ds(pl.multiple_of(n * SUM_TILE, SUM_TILE), SUM_TILE)
                own[batch_at(k), columns] = dot_rows(back[batch_at(k), :], up_weights[columns, :]).astype(BF16)

            keep.wait()
            spread_sent(k)
            for d in range(spans):
                near_copy(2, d, k).start()

            @pl.when(k == count - 1)
            def _():
                for s in range(1, chips) if chips != 4 else ():
                    pl.semaphore_signal(
                        free_sem, 1, device_id={"chip": lax.rem(chip + s, chips)}, device_id_type=MESH_ID
                    )
                load_slice(0).start()
                load_slice(1).start()

        def give(seq, d, k):
            return pltpu.make_async_copy(
                held.at[at_seq(seq, d, k)], projected_all.at[natural(seq, d, k)], load_sem.at[d, k]
            )

        def hand_out(k):
            gathered(k)
            sums_sent(2, k)
            for seq in range(2):
                for d in range(spans):
                    give(seq, d, k).start()
                for d in range(spans):
                    give(seq, d, k).wait()
            spread_sent(k)

        step = 2 * last + 2
        last_steps = 9 if chips == 4 else chips + down_tiles // 2
        assert last_steps <= step + 1

        def due(t, run):
            @pl.when(jnp.logical_and(t >= 0, t < count))
            def _():
                run(t)

        @pl.loop(0, 3 * step + count - 1)
        def _(t):
            for e in range(2, -1, -1):
                now = t - e * step
                for j in range(1, spans):
                    o = place - j

                    @pl.when(o >= 0)
                    def _():
                        due(now - turn_of(o) - j, functools.partial(relay_right, o))

                    p = place + j

                    @pl.when(p < spans)
                    def _():
                        due(now - turn_of(p) - j, functools.partial(relay_left, p))

                due(now - place, functools.partial(pass_right, e))
                due(now - (last - place), functools.partial(pass_left, e))
                due(now - turn_of(place), functools.partial(finish, e))
            if chips == 4:

                @pl.when(t == DOWN_TICK)
                def _():
                    relay_down()

            for e, run in ((2, hand_out), (1, backward), (0, forward)):
                due(t - e * step - 2 * last, run)
            for q in range(last_steps):

                @pl.when(t == count + step + 2 * last + q)
                def _():
                    weight_grads(q)

        if chips == 4:
            for group, out in zip(sums, (down_sum, gate_sum)):
                for half in range(2):
                    out[half * GRAD_TILE : (half + 1) * GRAD_TILE, :] = group.finish(half).astype(BF16)
            for n in range(down_tiles):
                part_copy(n, 2).wait()
            return
        total = given[here, :].astype(F32)
        for s in range(1, chips):
            give_copy(s).wait()
            total = total + down_weights[s * shard : (s + 1) * shard, :].astype(F32)
        down_sum[...] = total.astype(BF16)
        gate_sum[...] = jnp.zeros_like(gate_sum)
        for n in range(down_tiles):
            part_copy(n, 1).wait()
            part_copy(n, 2).wait()

    def call(self, chips, partial, tokens, cotangent, gains, gate_up, gate_up_w, down):
        spans, rows, width, hidden, count = self.spans, self.rows, self.width, self.hidden, self.count
        total = 2 * spans * rows
        vmem = pl.BlockSpec(memory_space=pltpu.VMEM)
        hbm = pl.BlockSpec(memory_space=pl.ANY)
        shape = jax.ShapeDtypeStruct
        sems = pltpu.SemaphoreType.DMA((spans, count))
        two = pltpu.SemaphoreType.DMA((2,))
        return pl.pallas_call(
            functools.partial(self.body, chips),
            out_shape=[
                shape((rows, width), BF16),
                shape((rows, width), F32),
                shape((1, width), F32),
                shape((1, width), F32),
                shape(down.shape, BF16),
                shape(down.shape, BF16),
                shape((total, width), BF16),
                shape((total, width), BF16),
                shape((16, 128) if chips == 4 else (width, hidden), BF16),
                shape((width, hidden), BF16),
                shape((total, width), BF16),
            ],
            in_specs=[hbm, vmem, vmem, vmem, hbm, hbm, hbm],
            out_specs=[vmem] * 6 + [hbm] * 5,
            scratch_shapes=[
                pltpu.VMEM((rows, width), F32),
                pltpu.VMEM((rows, width), F32),
                pltpu.VMEM((total, width), BF16),
                pltpu.VMEM((total // 2, width), BF16),
                pltpu.VMEM((total // 2, width), BF16),
                pltpu.VMEM((total // 2, width), BF16),
                pltpu.VMEM((total, width), BF16),
                pltpu.VMEM((total, 2 * hidden), F32),
                pltpu.VMEM((total, hidden), BF16),
                pltpu.VMEM((total, 2 * hidden), BF16),
                pltpu.VMEM((width, 2 * hidden), BF16),
                pltpu.VMEM((width, hidden), BF16),
                pltpu.VMEM((4, total, GRAD_TILE), BF16),
                pltpu.VMEM((width, hidden), BF16),
                pltpu.VMEM((2, 6, GRAD_TILE, hidden) if chips == 4 else (2, 6, 16, 128), BF16),
                sems,
                pltpu.SemaphoreType.DMA((chips + 1,)),
                two,
                pltpu.SemaphoreType.DMA((4,)),
                pltpu.SemaphoreType.DMA((2, width // GRAD_TILE)),
                pltpu.SemaphoreType.REGULAR,
            ]
            + [sems] * 12
            + [pltpu.SemaphoreType.DMA((max(chips, 6),))] * 8,
            compiler_params=pltpu.CompilerParams(
                collective_id=2, has_side_effects=True, vmem_limit_bytes=62 << 20
            ),
            cost_estimate=pl.CostEstimate(
                flops=36 * rows * spans * width * hidden, bytes_accessed=100 * width * width, transcendentals=0
            ),
            name="feed_forward",
        )(partial, tokens, cotangent, gains, gate_up, gate_up_w, down)


def turn(values, cosine, sine):
    return values * cosine + pltpu.roll(values, HEAD_DIM // 2, 1) * sine


def row_sums(values):
    total = values[:, :128]
    for first in range(128, values.shape[1], 128):
        total = total + values[:, first : first + 128]
    return jnp.sum(jnp.transpose(total), axis=0, keepdims=True)


def down_rows(row):
    return jnp.transpose(jnp.broadcast_to(row, (128, row.shape[1])))


class Stats:
    def __init__(self, spans, own, arrived, send, recv):
        self.spans, self.own, self.arrived, self.send, self.recv = spans, own, arrived, send, recv
        self.core, self.place = lax.axis_index("core"), lax.axis_index("ctx")
        self.me = self.core * spans + self.place

    def member(self, s):
        core, place = step_member(self.core, self.place, s, self.spans)
        return {"core": core, "ctx": place}

    def greet(self):
        for s in range(1, 2 * self.spans):
            pl.semaphore_signal(
                pltpu.get_barrier_semaphore(), 1, device_id=self.member(s), device_id_type=MESH_ID
            )

    def meet(self):
        pl.semaphore_wait(pltpu.get_barrier_semaphore(), 2 * self.spans - 1)

    def copy(self, s):
        return pltpu.make_async_remote_copy(
            src_ref=self.own, dst_ref=self.arrived.at[s], send_sem=self.send.at[s], recv_sem=self.recv.at[s],
            device_id=self.member(s), device_id_type=MESH_ID,
        )

    def start(self):
        for s in range(1, 2 * self.spans):
            self.copy(s).start()

    def total(self):
        total = self.own[...]
        for s in range(1, 2 * self.spans):
            self.copy(s).wait()
            total = total + self.arrived[s]
        return total


def stats_scratch(spans, total_rows):
    sems = pltpu.SemaphoreType.DMA((2 * spans,))
    return [
        pltpu.VMEM((8, total_rows), F32),
        pltpu.VMEM((2 * spans, 8, total_rows), F32),
        sems,
        sems,
    ]


def allowed_at(ids, seq, block, count, spans):
    rows = ids.shape[1]
    per = block // rows
    ids_of = lambda z: ids[(seq * spans + z) * 8 : (seq * spans + z) * 8 + 8, :].astype(F32)
    first = count * per
    keys = jnp.concatenate([ids_of(z)[:1] for z in range(first + per)], 1)
    queries = jnp.concatenate([jnp.transpose(ids_of(z))[:, :1] for z in range(first, first + per)], 0)
    shape = (block, (count + 1) * block)
    query_at = lax.broadcasted_iota(jnp.int32, shape, 0) + count * block
    key_at = lax.broadcasted_iota(jnp.int32, shape, 1)
    same = queries == keys
    seen = jnp.logical_and(same, key_at <= query_at)
    return jnp.logical_and(seen, jnp.logical_or(keys != 0.0, key_at == query_at))


def softmax_parts(query, key, allowed):
    scores = jnp.where(allowed, dot_rows(query, key) * HEAD_DIM ** (-0.5), -1e30)
    weights = jnp.exp(scores - jnp.max(scores, axis=1, keepdims=True))
    return weights / jnp.sum(weights, axis=1, keepdims=True)


QUERY_BLOCK = 256
ROW_TILE = 256


class Neighbours:
    pieces = 4

    def __init__(self, chip, shard, full, send, recv):
        self.chip, self.shard, self.full, self.send, self.recv = chip, shard, full, send, recv
        self.to = square(chip)[:2]

    def copy(self, i, n):
        size = self.shard.shape[0] // self.pieces
        where = self.full.at[pl.ds(pl.multiple_of(self.chip * self.shard.shape[0] + n * size, size), size)]
        return pltpu.make_async_remote_copy(
            src_ref=self.shard.at[n * size : (n + 1) * size], dst_ref=where,
            send_sem=self.send.at[i, n], recv_sem=self.recv.at[i, n],
            device_id={"chip": self.to[i]}, device_id_type=MESH_ID,
        )

    def begin(self):
        for n in range(self.pieces):
            for i in range(2):
                self.copy(i, n).start()

    def finish(self):
        for n in range(self.pieces):
            for i in range(2):
                self.copy(i, n).wait()


def attend_body(
    spans, chips, exchange, extra, n_scratch,
    tokens, w_qkv, segment, w_out, w_gate, w_up, w_down, gains, cosine, sine,
    gate_up, down, weights_out, ids, tokens_all, gate_up_w,
    partial_out, out_w_out, query_out, key_out, value_out, normed_out, factor_out, attended_out,
    cut, own_ids, split, split_sems, raw, given, out_w, moved, own, arrived, store_sem, chip_send, chip_recv, send, recv, move_send, move_recv,
    up_send, up_recv, *rest,
):
    part = out_w.shape[0]
    total_rows = raw.shape[0]
    length = total_rows // 2
    width = tokens.shape[1]
    tiles = total_rows // ROW_TILE
    held, held_w = rest[0], rest[n_scratch]
    stats = Stats(spans, own, arrived, send, recv)
    greet_all(spans, True)
    chip, core, place = lax.axis_index("chip"), stats.core, stats.place
    shard = moved.shape[0]
    here = pl.ds(pl.multiple_of(chip * shard, shard), shard)

    def at(i):
        return pl.ds(pl.multiple_of(i * ROW_TILE, ROW_TILE), ROW_TILE)

    def chip_copy(s):
        return pltpu.make_async_remote_copy(
            src_ref=moved, dst_ref=out_w.at[here], send_sem=chip_send.at[s], recv_sem=chip_recv.at[s],
            device_id={"chip": lax.rem(chip + s, chips)}, device_id_type=MESH_ID,
        )

    def move_copy():
        to_chip, to_core, to_place = summer_of(chip, core, place, spans)
        return pltpu.make_async_remote_copy(
            src_ref=w_out, dst_ref=moved, send_sem=move_send, recv_sem=move_recv,
            device_id={"chip": to_chip, "core": to_core, "ctx": to_place}, device_id_type=MESH_ID,
        )

    home = stays(chip, core, place, spans)
    if chips == 4:
        up = Neighbours(chip, gate_up, gate_up_w, up_send, up_recv)
    own[...] = jnp.zeros_like(own)
    loads, sends, stores = split_copies(w_gate, w_up, w_down, gate_up, down, split, *(split_sems.at[n] for n in range(4)))
    for load in loads:
        load.start()
    for m in range(2 * spans):
        for i in range(3):
            column = i * width + m * part
            cut[m, :, i * part : (i + 1) * part] = w_qkv[:, column : column + part]
    own_ids[...] = jnp.broadcast_to(segment[...], own_ids.shape)
    wait_all(spans, True)
    for load, store, other in zip(loads, stores, sends):
        other.start()
        load.wait()
        store.start()

    @pl.when(home)
    def _():
        moved[...] = w_out[...]

    @pl.when(jnp.logical_not(home))
    def _():
        move_copy().start()

    def after_blocks():
        @pl.when(jnp.logical_not(home))
        def _():
            move_copy().wait()

        for s in range(1, chips):
            chip_copy(s).start()
        out_w[here, :] = moved[...]
        for store, other in zip(stores, sends):
            store.wait()
            other.wait()
        if chips == 4:
            up.begin()

    extra.after_blocks = after_blocks
    exchange.body(tokens, cut, own_ids, weights_out, ids, tokens_all, *rest)

    @pl.loop(0, tiles)
    def _(i):
        values = dot(held[at(i), :], held_w[...])
        raw[at(i), :] = values
        for n in range(2):
            some = values[:, n * part : (n + 1) * part]
            own[n : n + 1, at(i)] = row_sums(some * some)

    stats.start()

    @pl.loop(0, tiles)
    def _(i):
        value_out[at(i), :] = raw[at(i), 2 * part :].astype(BF16)

    factor_out[...] = lax.rsqrt(stats.total() / width + EPS)
    me = stats.me
    columns = pl.ds(pl.multiple_of(me * part, part), part)
    gain = jnp.concatenate([gains[0:1, columns], gains[1:2, columns]], 1)

    @pl.loop(0, tiles)
    def _(i):
        by_query, by_key = down_rows(factor_out[0:1, at(i)]), down_rows(factor_out[1:2, at(i)])
        place = pl.ds(pl.multiple_of(lax.rem(i, length // ROW_TILE) * ROW_TILE, ROW_TILE), ROW_TILE)
        for h in range(part // HEAD_DIM):
            head = slice(h * HEAD_DIM, (h + 1) * HEAD_DIM)
            low = slice(part + h * HEAD_DIM, part + (h + 1) * HEAD_DIM)
            for out, by, where in ((query_out, by_query, head), (key_out, by_key, low)):
                normed = raw[at(i), where] * by
                normed_out[at(i), where] = normed
                out[at(i), head] = turn(normed * gain[:, where], cosine[place, :], sine[place, :]).astype(BF16)

    for s in range(1, chips):
        chip_copy(s).wait()
    out_w_out[...] = out_w[...]
    block = QUERY_BLOCK
    for seq in range(2):
        for count in range(length // block):
            allowed = allowed_at(ids, seq, block, count, spans)
            rows = slice(seq * length + count * block, seq * length + (count + 1) * block)
            keys = slice(seq * length, seq * length + (count + 1) * block)
            for h in range(part // HEAD_DIM):
                head = slice(h * HEAD_DIM, (h + 1) * HEAD_DIM)
                shares = softmax_parts(query_out[rows, head], key_out[keys, head], allowed)
                attended_out[rows, head] = dot(shares.astype(BF16), value_out[keys, head]).astype(BF16)
            i = rows.start // ROW_TILE
            if i >= 2:
                pltpu.make_async_copy(given.at[i % 2], partial_out.at[at(i - 2)], store_sem.at[i - 2]).wait()
            given[i % 2] = dot(attended_out[rows, :], out_w[...]).astype(BF16)
            pltpu.make_async_copy(given.at[i % 2], partial_out.at[at(i)], store_sem.at[i]).start()
    for i in range(tiles - 2, tiles):
        pltpu.make_async_copy(given.at[i % 2], partial_out.at[at(i)], store_sem.at[i]).wait()
    if chips == 4:
        up.finish()


def attend(spans, chips, tokens, w_qkv, segment, w_out, w_gate, w_up, w_down, gains, cosine, sine):
    rows, width = tokens.shape
    total_rows = 2 * spans * rows
    part = w_out.shape[0] * chips
    tiles = total_rows // ROW_TILE
    vmem = pl.BlockSpec(memory_space=pltpu.VMEM)
    hbm = pl.BlockSpec(memory_space=pl.ANY)
    shape = jax.ShapeDtypeStruct
    cut = shape((2 * spans, w_qkv.shape[0], 3 * part), BF16)
    extra = QkvWeights(spans, chips, cut, shape((8, rows), jnp.int32))
    slab, columns = w_gate.shape
    exchange = Exchange(spans, rows, width, PIECE, False, True, pass_tokens, 1, 0, None, extra)
    scratch = exchange.scratch()
    return pl.pallas_call(
        functools.partial(attend_body, spans, chips, exchange, extra, len(scratch) - len(extra.scratch())),
        out_shape=[
            shape((2 * slab, columns), BF16),
            shape((2 * slab, columns // 2), BF16),
            *extra.out_shapes,
            shape((total_rows, width), BF16),
            shape((chips * 2 * slab if chips == 4 else 16, columns), BF16),
            shape((total_rows, width), BF16),
            shape((part, width), BF16),
            shape((total_rows, part), BF16),
            shape((total_rows, part), BF16),
            shape((total_rows, part), BF16),
            shape((total_rows, 2 * part), F32),
            shape((8, total_rows), F32),
            shape((total_rows, part), BF16),
        ],
        in_specs=[vmem] * 4 + [hbm] * 3 + [vmem] * 3,
        out_specs=[hbm] * 2 + [vmem] * 2 + [hbm] * 3 + [vmem] * 7,
        scratch_shapes=[
            pltpu.VMEM(cut.shape, BF16),
            pltpu.VMEM((8, rows), jnp.int32),
            pltpu.VMEM((3, slab, columns // 2), BF16),
            pltpu.SemaphoreType.DMA((4, 3)),
            pltpu.VMEM((total_rows, 3 * part), F32),
            pltpu.VMEM((2, ROW_TILE, width), BF16),
            pltpu.VMEM((part, width), BF16),
            pltpu.VMEM(w_out.shape, BF16),
            *stats_scratch(spans, total_rows)[:2],
            pltpu.SemaphoreType.DMA((tiles,)),
            pltpu.SemaphoreType.DMA((chips,)),
            pltpu.SemaphoreType.DMA((chips,)),
            *stats_scratch(spans, total_rows)[2:],
            pltpu.SemaphoreType.DMA,
            pltpu.SemaphoreType.DMA,
            pltpu.SemaphoreType.DMA((2, Neighbours.pieces)),
            pltpu.SemaphoreType.DMA((2, Neighbours.pieces)),
            *scratch,
        ],
        compiler_params=pltpu.CompilerParams(collective_id=1, has_side_effects=True, vmem_limit_bytes=58 << 20),
        cost_estimate=pl.CostEstimate(
            flops=2 * total_rows * width * 5 * part, bytes_accessed=50 * width * width, transcendentals=0
        ),
        name="attend",
    )(tokens, w_qkv, segment, w_out, w_gate, w_up, w_down, gains, cosine, sine)


def attend_back_body(
    spans, chips, exchange, extra, n_scratch,
    grads, tokens, weights, up_part, gate_sum, down_sum, out_w, gains, ids, cosine, sine, residual_grad, gain_attn, gain_feed,
    query, key, value, normed, factor, attended,
    input_grad, grad_qkv, grad_gains, grad_out, grad_gate, grad_down, grad_up,
    held, held_tokens, held_w, raw, mixed, attended_grad, own, arrived, load_sem, send, recv,
    qkv_part, out_part, sums, up_held, up_landed, up_send, up_recv, joined, join_send, join_recv, *rest,
):
    part = out_w.shape[0]
    total_rows = raw.shape[0]
    length = total_rows // 2
    width = grads.shape[1]
    tiles = total_rows // ROW_TILE
    scale = HEAD_DIM ** (-0.5)
    stats = Stats(spans, own, arrived, send, recv)
    greet_all(spans, True)

    def at(i):
        return pl.ds(pl.multiple_of(i * ROW_TILE, ROW_TILE), ROW_TILE)

    def load_rows(i):
        return pltpu.make_async_copy(grads.at[at(i)], held.at[at(i)], load_sem.at[i])

    @pl.loop(0, tiles)
    def _(i):
        load_rows(i).start()

    own[...] = jnp.zeros_like(own)
    load_w = pltpu.make_async_copy(weights, held_w, load_sem.at[tiles])
    load_tokens = pltpu.make_async_copy(tokens, held_tokens, load_sem.at[tiles + 1])
    load_w.start()
    load_tokens.start()
    if chips == 4:
        load_up = pltpu.make_async_copy(up_part, up_held, load_sem.at[tiles + 2])
        load_up.start()
    me = stats.me
    columns = pl.ds(pl.multiple_of(me * part, part), part)
    gain = jnp.concatenate([gains[0:1, columns], gains[1:2, columns]], 1)

    @pl.loop(0, tiles)
    def _(i):
        load_rows(i).wait()
        attended_grad[at(i), :] = dot_rows(held[at(i), :], out_w[...]).astype(BF16)

    out_part[...] = dot_first(attended[...], held[...]).astype(BF16)
    wait_all(spans, True)
    extra.ins = [qkv_part, sums, out_part]
    extra.held = list(rest[n_scratch:])
    extra.begin()
    if chips == 4:
        load_up.wait()
        half_rows = width // 8
        up_sums = SquareSum(
            lax.axis_index("chip"),
            lambda owner, half: up_held.at[
                pl.ds(pl.multiple_of((owner * 2 + half) * half_rows, half_rows), half_rows)
            ],
            up_landed, up_send, up_recv,
        )
        up_sums.begin(0)
        up_sums.begin(2)
        slab = gate_sum.shape[0] // 2
        side = gate_sum.shape[1]
        my_chip = lax.axis_index("chip")
        up_sum = up_held.at[pl.ds(pl.multiple_of(my_chip * 2 * slab, 2 * slab), 2 * slab)]
        pairs = ((gate_sum, grad_gate), (down_sum, grad_down), (up_sum, grad_up))
        theirs = pl.ds(pl.multiple_of((1 - stats.core) * slab, slab), slab)
        near = pl.ds(pl.multiple_of(stats.core * side, side), side)
        far = pl.ds(pl.multiple_of((1 - stats.core) * side, side), side)

        def join_copy(n):
            return pltpu.make_async_remote_copy(
                src_ref=pairs[n][0].at[theirs], dst_ref=joined.at[n], send_sem=join_send.at[n],
                recv_sem=join_recv.at[n], device_id={"core": 1 - stats.core}, device_id_type=MESH_ID,
            )

        def join(n):
            given, out = pairs[n]
            out[:, near] = given[pl.ds(pl.multiple_of(stats.core * slab, slab), slab), :]
            join_copy(n).wait()
            out[:, far] = joined[n]

        join_copy(0).start()
        join_copy(1).start()
    block = QUERY_BLOCK
    blocks = length // block
    for seq in range(2):
        for h in range(part // HEAD_DIM):
            head = slice(h * HEAD_DIM, (h + 1) * HEAD_DIM)
            key_at = slice(part + h * HEAD_DIM, part + (h + 1) * HEAD_DIM)
            value_at = slice(2 * part + h * HEAD_DIM, 2 * part + (h + 1) * HEAD_DIM)
            for count in reversed(range(blocks)):
                allowed = allowed_at(ids, seq, block, count, spans)
                rows = slice(seq * length + count * block, seq * length + (count + 1) * block)
                keys = slice(seq * length, seq * length + (count + 1) * block)
                shares = softmax_parts(query[rows, head], key[keys, head], allowed)
                share_grad = dot_rows(attended_grad[rows, head], value[keys, head])
                inner = jnp.sum(shares * share_grad, axis=1, keepdims=True)
                score_grad = (shares * (share_grad - inner)).astype(BF16)
                raw[rows, head] = dot(score_grad, key[keys, head]) * scale
                key_grad = dot_first(score_grad, query[rows, head]) * scale
                value_grad = dot_first(shares.astype(BF16), attended_grad[rows, head])
                if count == blocks - 1:
                    raw[keys, key_at] = key_grad
                    raw[keys, value_at] = value_grad
                else:
                    raw[keys, key_at] += key_grad
                    raw[keys, value_at] += value_grad

    gain_rows = jnp.zeros((1, 2 * part), F32)

    for i in range(tiles):
        place = slice(i * ROW_TILE % length, i * ROW_TILE % length + ROW_TILE)
        for h in range(2 * part // HEAD_DIM):
            head = slice(h * HEAD_DIM, (h + 1) * HEAD_DIM)
            raw[at(i), head] = turn(raw[at(i), head], cosine[place, :], -sine[place, :])
        terms = raw[at(i), : 2 * part] * normed[at(i), :]
        gain_rows = gain_rows + jnp.sum(terms, axis=0, keepdims=True)
        for n in range(2):
            own[n : n + 1, at(i)] = row_sums((terms * gain)[:, n * part : (n + 1) * part])
        mixed[at(i), 2 * part :] = raw[at(i), 2 * part :].astype(BF16)

    stats.start()
    wide = width // 128
    for n in range(wide):
        column = slice(n * 128, (n + 1) * 128)
        sums[n : n + 1, :] = gain_attn[:, column]
        sums[wide + n : wide + n + 1, :] = gain_feed[:, column]
    for n in range(2 * part // 128):
        sums[2 * wide + n : 2 * wide + n + 1, :] = gain_rows[:, n * 128 : (n + 1) * 128]
    own[...] = stats.total() / width

    @pl.loop(0, tiles)
    def _(i):
        for n in range(2):
            mean, by = down_rows(own[n : n + 1, at(i)]), down_rows(factor[n : n + 1, at(i)])
            for first in range(n * part, (n + 1) * part, 128):
                where = slice(first, first + 128)
                back = gain[:, where] * raw[at(i), where] - normed[at(i), where] * mean
                mixed[at(i), where] = (by * back).astype(BF16)

    load_w.wait()

    @pl.loop(0, tiles)
    def _(i):
        held[at(i), :] = dot_rows(mixed[at(i), :], held_w[...]).astype(BF16)

    load_tokens.wait()

    def work():
        @pl.loop(0, width // ROW_TILE)
        def _(i):
            qkv_part[at(i), :] = dot_first(held_tokens[:, at(i)], mixed[...]).astype(BF16)

    extra.work = work
    extra.late = up_sums.relay if chips == 4 else (lambda: None)
    exchange.body(
        held, residual_grad, qkv_part, sums, out_part, input_grad, grad_qkv, grad_gains, grad_out, *rest
    )
    if chips == 4:
        for half in range(2):
            up_sum[half * half_rows : (half + 1) * half_rows, :] = up_sums.finish(half).astype(BF16)
        join_copy(2).start()
        for n in range(3):
            join(n)


def attend_back(
    spans, chips, rows, grads, tokens, weights, up_part, gate_sum, down_sum, out_w, gains, ids, cosine, sine,
    residual_grad, gain_attn, gain_feed, saved,
):
    total_rows, width = tokens.shape
    part = out_w.shape[0]
    members = width // part
    hidden = up_part.shape[1]
    tiles = total_rows // ROW_TILE
    vmem = pl.BlockSpec(memory_space=pltpu.VMEM)
    hbm = pl.BlockSpec(memory_space=pl.ANY)
    shape = jax.ShapeDtypeStruct
    sum_rows = (2 * width + 2 * part) // 128
    sum_rows += -sum_rows % 8
    extra = QkvGrads(
        spans, chips, members, shape((width, 3 * part), BF16), shape((sum_rows, 128), F32), shape((part, width), BF16)
    )
    exchange = Exchange(spans, rows, width, SUM_PIECE, True, False, after_input, 1, 1, None, extra)
    scratch = exchange.scratch()
    square_in = chips == 4
    return pl.pallas_call(
        functools.partial(attend_back_body, spans, chips, exchange, extra, len(scratch) - len(extra.scratch())),
        out_shape=[
            shape((rows, width), F32),
            *extra.out_shapes,
            *[shape((width // chips // 2, 2 * hidden) if square_in else (16, 128), BF16)] * 3,
        ],
        in_specs=[hbm] * 4 + [vmem] * (10 + len(saved)),
        out_specs=[vmem] * 7,
        scratch_shapes=[
            pltpu.VMEM((total_rows, width), BF16),
            pltpu.VMEM((total_rows, width), BF16),
            pltpu.VMEM(weights.shape, BF16),
            pltpu.VMEM((total_rows, 3 * part), F32),
            pltpu.VMEM((total_rows, 3 * part), BF16),
            pltpu.VMEM((total_rows, part), BF16),
            *stats_scratch(spans, total_rows)[:2],
            pltpu.SemaphoreType.DMA((tiles + 3,)),
            *stats_scratch(spans, total_rows)[2:],
            pltpu.VMEM((width, 3 * part), BF16),
            pltpu.VMEM((part, width), BF16),
            pltpu.VMEM((sum_rows, 128), F32),
            pltpu.VMEM((width, hidden) if square_in else (16, 128), BF16),
            pltpu.VMEM((6, width // 8, hidden) if square_in else (6, 16, 128), BF16),
            pltpu.SemaphoreType.DMA((6,)),
            pltpu.SemaphoreType.DMA((6,)),
            pltpu.VMEM((3, width // chips // 2, hidden) if square_in else (3, 16, 128), BF16),
            pltpu.SemaphoreType.DMA((3,)),
            pltpu.SemaphoreType.DMA((3,)),
            *scratch,
        ],
        compiler_params=pltpu.CompilerParams(collective_id=9, has_side_effects=True, vmem_limit_bytes=62 << 20),
        cost_estimate=pl.CostEstimate(
            flops=2 * total_rows * width * 8 * part, bytes_accessed=50 * width * width, transcendentals=0
        ),
        name="attend_back",
    )(
        grads, tokens, weights, up_part, gate_sum, down_sum, out_w, gains, ids, cosine, sine, residual_grad, gain_attn,
        gain_feed, *saved,
    )


def per_device(inputs, segment, w_qkv, w_out, w_gate, w_up, w_down_t, gains, cotangent):
    rows, width = inputs.shape[1:]
    cores = lax.axis_size("core")
    spans = lax.axis_size("ctx")
    members = cores * spans
    length = rows * spans
    part = width // members
    tokens = inputs[0]

    chips = lax.axis_size("chip")
    assert chips == spans
    cosine, sine = rope_tables(jnp.arange(length, dtype=F32))
    half = jnp.arange(HEAD_DIM) < HEAD_DIM // 2
    sine = jnp.where(half[None, :], -sine, sine)
    gate_up, down, qkv_w, ids, tokens_all, gate_up_w, out_part, out_w, *saved = attend(
        spans, chips, tokens, w_qkv, segment, w_out, w_gate, w_up, w_down_t, gains, cosine, sine
    )
    if chips != 4:
        gate_up_w = gather(gate_up, "chip")
    (
        output, residual_grad, gain_feed, gain_attn, down_sum, gate_sum, _, _, gate_part, up_part, projected_all
    ) = Middle(spans, rows, width, w_gate.shape[1] // cores, BATCH_PIECE).call(
        chips, out_part, tokens, cotangent[0], gains, gate_up, gate_up_w, down
    )
    input_grad, grad_qkv, grad_gains, grad_out, grad_gate, grad_down, grad_up = attend_back(
        spans, chips, rows, projected_all, tokens_all, qkv_w, up_part, gate_sum, down_sum, out_w, gains, ids, cosine, sine, residual_grad,
        gain_attn, gain_feed, saved,
    )
    if chips != 4:
        gate_sum, up_sum = scatter_sum(gate_part, "chip"), scatter_sum(up_part, "chip")
        grad_gate, grad_up, grad_down = join_columns(gate_sum, up_sum, down_sum)
    return (
        output[None],
        input_grad[None],
        grad_qkv.astype(F32),
        grad_out.astype(F32),
        grad_gate.astype(F32),
        grad_up.astype(F32),
        grad_down.astype(F32),
        grad_gains.reshape(4, width),
    )


def solution(mesh):
    cores = 2
    chips = mesh.shape["dp"] // cores
    split = Mesh(mesh.devices.reshape(chips, cores, mesh.shape["ctx"]), ALL)
    dp = ("chip", "core")
    every = P((*dp, "ctx"), None)
    in_specs = (
        P(dp, "ctx", None),
        P(dp, "ctx"),
        every,
        every,
        P(dp, "ctx"),
        P(dp, "ctx"),
        P(dp, "ctx"),
        P(),
        P(dp, "ctx", None),
    )
    out_specs = (
        P(dp, "ctx", None),
        P(dp, "ctx", None),
        every,
        every,
        P(dp, "ctx"),
        P(dp, "ctx"),
        P(dp, "ctx"),
        P(),
    )
    return jax.shard_map(
        per_device, mesh=split, in_specs=in_specs, out_specs=out_specs, check_vma=False
    )
```

```python
import functools

import jax
import jax.numpy as jnp
from jax import lax
from jax.experimental import pallas as pl
from jax.experimental.pallas import tpu as pltpu
from jax.sharding import Mesh
from jax.sharding import PartitionSpec as P

HEAD_DIM = 128
EPS = 1e-06
ROPE_BASE = 500000.0
F32 = jnp.float32
BF16 = jnp.bfloat16
GROUP = ("core", "ctx")
ALL = ("chip", "core", "ctx")


PIECE = 32
SUM_PIECE = 32
PASS_AT = 1
LATE_TICK = 2
PASS_TICK = 4
LAGJ = 1
MESH_ID = pl.DeviceIdType.MESH


def row_factor(values):
    return lax.rsqrt(jnp.mean(values * values, axis=-1, keepdims=True) + EPS)


def row_norm_back(values, gain, grad):
    factor = row_factor(values)
    normed = values * factor
    scaled = gain * grad
    back = factor * (scaled - normed * jnp.mean(scaled * normed, axis=-1, keepdims=True))
    return back, jnp.sum(grad * normed, axis=0, keepdims=True)


def after_projected(total, ins, outs, rows):
    tokens, gains = ins
    residual_out, projected_out = outs
    projected_out[rows, :] = total
    gain = gains[2:3, :]
    residual = tokens[rows, :].astype(F32) + total * row_factor(total) * gain
    residual_out[rows, :] = residual
    return residual


def after_feed(total, ins, outs, rows):
    residual, cotangent, gains = ins
    output, gain_out = outs
    gain = gains[3:4, :]
    normed = total * row_factor(total) * gain
    output[rows, :] = (residual[rows, :] + normed).astype(BF16)
    back, term = row_norm_back(total, gain, cotangent[rows, :].astype(F32))
    gain_out[...] += term
    return back


def after_back(total, ins, outs, rows):
    projected, cotangent, gains = ins
    grad_out, gain_out = outs
    grad = cotangent[rows, :].astype(F32) + total
    grad_out[rows, :] = grad
    back, term = row_norm_back(projected[rows, :], gains[2:3, :], grad)
    gain_out[...] += term
    return back


def after_input(total, ins, outs, rows):
    (grad,), (result,) = ins, outs
    result[rows, :] = grad[rows, :] + total
    return None


def pass_tokens(total, ins, outs, rows):
    return ins[0][rows, :]


class Exchange:
    def __init__(self, spans, rows, width, piece, reduce, spread, row_fn, n_in, n_out, gain, extra=None):
        self.extra = extra
        self.spans, self.rows, self.width, self.piece = spans, rows, width, piece
        self.reduce, self.spread, self.row_fn = reduce, spread, row_fn
        self.n_in, self.n_out, self.gain = n_in, n_out, gain
        self.count = rows // piece

    def scratch(self):
        spans, count = self.spans, self.count
        block = pltpu.VMEM((spans * self.rows, self.width), BF16)
        sems = pltpu.SemaphoreType.DMA((spans, count))
        items = []
        if self.reduce:
            items += [block] * 4 + [pltpu.SemaphoreType.DMA] + [sems] * 6
        if self.spread:
            items += [pltpu.VMEM((2 * spans * self.rows, self.width), BF16)]
            items += [sems] * 7 + [pltpu.SemaphoreType.DMA]
        if self.extra is not None:
            items += self.extra.scratch()
        return items

    def body(self, *refs):
        spans, rows, piece, count = self.spans, self.rows, self.piece, self.count
        refs = list(refs)
        take = lambda n: [refs.pop(0) for _ in range(n)]
        partial = take(1)[0] if self.reduce else None
        ins = take(self.n_in)
        extra = self.extra
        if extra is not None:
            extra.ins = take(extra.n_in)
        outs = take(self.n_out)
        if extra is not None:
            extra.outs = take(extra.n_out)
        gathered = take(1)[0] if self.spread else None
        if self.reduce:
            own, near, from_left, from_right = take(4)
            (load_sem,) = take(1)
            near_send, near_recv, right_send, right_recv, left_send, left_recv = take(6)
        if self.spread:
            (held,) = take(1)
            fwd_send, fwd_recv, bwd_send, bwd_recv, own_send, side_send, side_recv = take(7)
            (store_sem,) = take(1)
        if extra is not None:
            extra.held = refs
        core = lax.axis_index("core")
        place = lax.axis_index("ctx")
        other = 1 - core
        has_left = place > 0
        has_right = place < spans - 1

        def at(block, k):
            return pl.ds(pl.multiple_of(block * rows + k * piece, piece), piece)

        def held_at(seq, block, k):
            return pl.ds(pl.multiple_of((seq * spans + block) * rows + k * piece, piece), piece)

        def remote(src, dst, send, recv, **device):
            return pltpu.make_async_remote_copy(
                src_ref=src, dst_ref=dst, send_sem=send, recv_sem=recv,
                device_id=device, device_id_type=MESH_ID,
            )

        barrier = pltpu.get_barrier_semaphore()
        if extra is not None:
            if not extra.met:
                meet_all(spans)
        else:
            pl.semaphore_signal(barrier, 1, device_id={"core": other}, device_id_type=MESH_ID)

            @pl.when(has_left)
            def _():
                pl.semaphore_signal(barrier, 1, device_id={"ctx": place - 1}, device_id_type=MESH_ID)

            @pl.when(has_right)
            def _():
                pl.semaphore_signal(barrier, 1, device_id={"ctx": place + 1}, device_id_type=MESH_ID)

            pl.semaphore_wait(barrier, 1 + has_left.astype(jnp.int32) + has_right.astype(jnp.int32))

        if self.gain is not None:
            outs[self.gain][...] = jnp.zeros_like(outs[self.gain])

        def near_copy(d, k):
            return remote(
                partial.at[held_at(other, d, k)], near.at[at(d, k)],
                near_send.at[d, k], near_recv.at[d, k], core=other,
            )

        def right_copy(d, k):
            return remote(
                own.at[at(d, k)], from_left.at[at(d, k)],
                right_send.at[d, k], right_recv.at[d, k], ctx=place + 1,
            )

        def left_copy(d, k):
            return remote(
                own.at[at(d, k)], from_right.at[at(d, k)],
                left_send.at[d, k], left_recv.at[d, k], ctx=place - 1,
            )

        def fwd_copy(o, k, send):
            where = held_at(core, o, k)
            return remote(held.at[where], held.at[where], send, fwd_recv.at[o, k], ctx=place + 1)

        def bwd_copy(o, k, send):
            where = held_at(core, o, k)
            return remote(held.at[where], held.at[where], send, bwd_recv.at[o, k], ctx=place - 1)

        def side_copy(o, k):
            where = held_at(core, o, k)
            return remote(held.at[where], held.at[where], side_send.at[o, k], side_recv.at[o, k], core=other)

        if extra is not None:
            extra.start()
        if self.reduce:
            load = pltpu.make_async_copy(
                partial.at[pl.ds(pl.multiple_of(core * spans * rows, rows), spans * rows)], own, load_sem
            )
            load.start()

            @pl.loop(0, count)
            def _(k):
                for j in range(spans):
                    near_copy(j, k).start()

            load.wait()

        def base(d, k):
            near_copy(d, k).wait_recv()
            return own[at(d, k), :].astype(F32) + near[at(d, k), :].astype(F32)

        def pass_on(d, k, arrived, copy, later):
            value = base(d, k)

            @pl.when(later)
            def _():
                copy(d, k).wait_recv()

            before = arrived[at(d, k), :].astype(F32)
            value = value + jnp.where(later, before, jnp.zeros_like(before))
            own[at(d, k), :] = value.astype(BF16)
            copy(d, k).start()

        def pass_right(k):
            for d in range(spans - 1, 0, -1):

                @pl.when(d > place)
                def _():
                    pass_on(d, k, from_left, right_copy, has_left)

        def pass_left(k):
            for d in range(spans - 1):

                @pl.when(d < place)
                def _():
                    pass_on(d, k, from_right, left_copy, has_right)

        def finish_step(k):
            total = None
            if self.reduce:
                total = base(place, k)

                @pl.when(has_left)
                def _():
                    right_copy(place, k).wait_recv()

                @pl.when(has_right)
                def _():
                    left_copy(place, k).wait_recv()

                zero = jnp.zeros_like(total)
                total = total + jnp.where(has_left, from_left[at(place, k), :].astype(F32), zero)
                total = total + jnp.where(has_right, from_right[at(place, k), :].astype(F32), zero)
            own_rows = pl.ds(pl.multiple_of(k * piece, piece), piece)
            result = self.row_fn(total, ins, outs, own_rows)
            if self.spread:
                held[held_at(core, place, k), :] = result.astype(BF16)

                @pl.when(has_right)
                def _():
                    fwd_copy(place, k, fwd_send.at[place, k]).start()

                @pl.when(has_left)
                def _():
                    bwd_copy(place, k, bwd_send.at[place, k]).start()

                side_copy(place, k).start()

        def relay_step(k, j):
            if True:

                @pl.when(place - j >= 0)
                def _():
                    fwd_copy(place - j, k, fwd_send.at[place - j, k]).wait_recv()

                    @pl.when(has_right)
                    def _():
                        fwd_copy(place - j, k, fwd_send.at[place - j, k]).start()

                    side_copy(place - j, k).start()

                @pl.when(place + j < spans)
                def _():
                    bwd_copy(place + j, k, bwd_send.at[place + j, k]).wait_recv()

                    @pl.when(has_left)
                    def _():
                        bwd_copy(place + j, k, bwd_send.at[place + j, k]).start()

                    side_copy(place + j, k).start()

        lag = spans - 1 if self.reduce else 0

        def due(k, run):
            @pl.when(jnp.logical_and(k >= 0, k < count))
            def _():
                run(k)

        @pl.loop(0, count + lag + (LAGJ * (spans - 1) if self.spread else 0))
        def _(t):
            if self.reduce:
                due(t - place, pass_right)
                due(t - (spans - 1 - place), pass_left)
                due(t - jnp.maximum(place, spans - 1 - place), finish_step)
            else:

                @pl.when(t == 0)
                def _():
                    for k in range(count):
                        finish_step(k)

            if self.spread:
                for j in range(1, spans):
                    after = t - lag - j * LAGJ

                    @pl.when(jnp.logical_and(after >= 0, after < count))
                    def _():
                        relay_step(after, j)
            if extra is not None:
                extra.tick(t)

        if extra is not None:
            extra.finish(count + lag + (LAGJ * (spans - 1) if self.spread else 0))
        if self.spread:

            @pl.loop(0, count)
            def _(k):
                for o in range(spans):
                    side_copy(o, k).wait_recv()

            store = pltpu.make_async_copy(held, gathered, store_sem)
            store.start()

        @pl.loop(0, count)
        def _(k):
            for d in range(spans):
                if self.reduce:
                    near_copy(d, k).wait_send()

                    @pl.when(d > place)
                    def _():
                        right_copy(d, k).wait_send()

                    @pl.when(d < place)
                    def _():
                        left_copy(d, k).wait_send()

                if self.spread:
                    side_copy(d, k).wait_send()

                    @pl.when(jnp.logical_and(d <= place, has_right))
                    def _():
                        fwd_copy(d, k, fwd_send.at[d, k]).wait_send()

                    @pl.when(jnp.logical_and(d >= place, has_left))
                    def _():
                        bwd_copy(d, k, bwd_send.at[d, k]).wait_send()

        if self.spread:
            store.wait()


def owner_of(chip, core, place, spans):
    member = core * spans + place
    return member // 2, lax.rem(member, 2), chip


def summer_of(chip, core, place, spans):
    member = chip * 2 + core
    return place, member // spans, lax.rem(member, spans)


def stays(chip, core, place, spans):
    to_chip, to_core, to_place = owner_of(chip, core, place, spans)
    return jnp.logical_and(to_chip == chip, jnp.logical_and(to_core == core, to_place == place))


def meet_all(spans):
    greet_all(spans, False)
    wait_all(spans, False)


def greet_all(spans, moves):
    chips = lax.axis_size("chip")
    barrier = pltpu.get_barrier_semaphore()
    chip = lax.axis_index("chip")
    core = lax.axis_index("core")
    place = lax.axis_index("ctx")
    for s in range(1, chips):
        pl.semaphore_signal(
            barrier, 1, device_id={"chip": lax.rem(chip + s, chips)}, device_id_type=MESH_ID
        )
    for s in range(1, 2 * spans):
        to_core, to_place = step_member(core, place, s, spans)
        pl.semaphore_signal(
            barrier, 1, device_id={"core": to_core, "ctx": to_place}, device_id_type=MESH_ID
        )
    if moves:

        @pl.when(jnp.logical_not(stays(chip, core, place, spans)))
        def _():
            for find in (owner_of, summer_of):
                to_chip, to_core, to_place = find(chip, core, place, spans)
                pl.semaphore_signal(
                    barrier, 1, device_id={"chip": to_chip, "core": to_core, "ctx": to_place}, device_id_type=MESH_ID
                )


def wait_all(spans, moves):
    count = lax.axis_size("chip") - 1 + 2 * spans - 1
    if moves:
        here = stays(lax.axis_index("chip"), lax.axis_index("core"), lax.axis_index("ctx"), spans)
        count = count + 2 * jnp.logical_not(here).astype(jnp.int32)
    pl.semaphore_wait(pltpu.get_barrier_semaphore(), count)


def step_member(core, place, s, spans):
    return lax.rem(core + s % 2, 2), lax.rem(place + s // 2, spans)


def meet_other_core():
    barrier = pltpu.get_barrier_semaphore()
    other = 1 - lax.axis_index("core")
    pl.semaphore_signal(barrier, 1, device_id={"core": other}, device_id_type=MESH_ID)
    pl.semaphore_wait(barrier, 1)


def split_copies(gate, up, down, gate_up_out, down_out, held, load_sem, store_sem, send_sem, recv_sem):
    core = lax.axis_index("core")
    other = 1 - core
    rows, width = gate.shape
    half = width // 2
    where = pl.ds(pl.multiple_of(core * rows, rows), rows)
    places = [gate_up_out.at[where, :half], gate_up_out.at[where, half:], down_out.at[where, :]]
    mine = pl.ds(pl.multiple_of(core * half, half), half)
    theirs = pl.ds(pl.multiple_of(other * half, half), half)
    arrays = list(enumerate((gate, up, down)))
    loads = [pltpu.make_async_copy(a.at[:, mine], held.at[i], load_sem.at[i]) for i, a in arrays]
    sends = [
        pltpu.make_async_remote_copy(
            src_ref=a.at[:, theirs], dst_ref=places[i], send_sem=send_sem.at[i], recv_sem=recv_sem.at[i],
            device_id={"core": other}, device_id_type=MESH_ID,
        )
        for i, a in arrays
    ]
    stores = [pltpu.make_async_copy(held.at[i], places[i], store_sem.at[i]) for i in range(3)]
    return loads, sends, stores


def join_body(gate, up, down, gate_out, up_out, down_out, arrived, send_sem, recv_sem):
    core = lax.axis_index("core")
    other = 1 - core
    rows, width = gate_out.shape
    half = width // 2
    meet_other_core()
    theirs = pl.ds(pl.multiple_of(other * rows, rows), rows)
    pairs = ((gate, gate_out), (up, up_out), (down, down_out))
    sends = [
        pltpu.make_async_remote_copy(
            src_ref=a.at[theirs], dst_ref=arrived.at[i], send_sem=send_sem.at[i], recv_sem=recv_sem.at[i],
            device_id={"core": other}, device_id_type=MESH_ID,
        )
        for i, (a, _) in enumerate(pairs)
    ]
    for send in sends:
        send.start()
    mine = pl.ds(pl.multiple_of(core * half, half), half)
    far = pl.ds(pl.multiple_of(other * half, half), half)
    step = 16

    def rows_at(i, base):
        return pl.ds(pl.multiple_of(base + i * step, step), step)

    @pl.loop(0, rows // step)
    def _(i):
        for a, b in pairs:
            b[rows_at(i, 0), mine] = a[rows_at(i, core * rows), :].astype(F32)

    for send in sends:
        send.wait()

    @pl.loop(0, rows // step)
    def _(i):
        for n, (_, b) in enumerate(pairs):
            b[rows_at(i, 0), far] = arrived[n, rows_at(i, 0), :].astype(F32)


def join_columns(gate, up, down):
    rows, half = gate.shape[0] // 2, gate.shape[1]
    vmem = pl.BlockSpec(memory_space=pltpu.VMEM)
    three = pltpu.SemaphoreType.DMA((3,))
    return pl.pallas_call(
        join_body,
        out_shape=[jax.ShapeDtypeStruct((rows, 2 * half), F32)] * 3,
        in_specs=[vmem] * 3,
        out_specs=[vmem] * 3,
        scratch_shapes=[pltpu.VMEM((3, rows, half), BF16), three, three],
        compiler_params=pltpu.CompilerParams(collective_id=7, has_side_effects=True, vmem_limit_bytes=32 << 20),
        name="join_columns",
    )(gate, up, down)


class Extra:
    met = False

    def remote(self, src, dst, send, recv, **device):
        return pltpu.make_async_remote_copy(
            src_ref=src, dst_ref=dst, send_sem=send, recv_sem=recv,
            device_id=device, device_id_type=MESH_ID,
        )

    def locate(self):
        self.chip = lax.axis_index("chip")
        self.core = lax.axis_index("core")
        self.place = lax.axis_index("ctx")
        self.me = self.core * self.spans + self.place


class QkvWeights(Extra):
    n_in, n_out = 2, 2
    met = True

    def __init__(self, spans, chips, cut, ids):
        self.spans, self.chips = spans, chips
        self.members, self.block, self.columns = cut.shape
        self.ids_shape = ids.shape
        vmem = pl.BlockSpec(memory_space=pltpu.VMEM)
        self.out_shapes = [
            jax.ShapeDtypeStruct((chips * self.members * self.block, self.columns), BF16),
            jax.ShapeDtypeStruct((self.members * ids.shape[0], ids.shape[1]), jnp.int32),
        ]
        self.out_specs = [vmem, vmem]

    def scratch(self):
        rows = self.chips * self.members * self.block
        sems = pltpu.SemaphoreType.DMA((self.members,))
        cross = pltpu.SemaphoreType.DMA((self.chips, self.members))
        ids = (self.members * self.ids_shape[0], self.ids_shape[1])
        return [pltpu.VMEM((rows, self.columns), BF16), pltpu.VMEM(ids, jnp.int32)] + [sems] * 4 + [cross] * 2

    def at(self, chip, m):
        return pl.ds(pl.multiple_of((chip * self.members + m) * self.block, self.block), self.block)

    def ids_at(self, m):
        return pl.ds(pl.multiple_of(m * self.ids_shape[0], self.ids_shape[0]), self.ids_shape[0])

    def block_copy(self, s):
        full, _, send, recv = self.held[:4]
        core, place = step_member(self.core, self.place, s, self.spans)
        return self.remote(
            self.ins[0].at[core * self.spans + place], full.at[self.at(self.chip, self.me)],
            send.at[s], recv.at[s], core=core, ctx=place,
        )

    def ids_copy(self, s):
        all_ids, send, recv = self.held[1], self.held[4], self.held[5]
        core, place = step_member(self.core, self.place, s, self.spans)
        return self.remote(
            self.ins[1], all_ids.at[self.ids_at(self.me)], send.at[s], recv.at[s], core=core, ctx=place
        )

    def source(self, s):
        core = lax.rem(self.core + s % 2, 2)
        return core * self.spans + lax.rem(self.place + self.spans - s // 2, self.spans)

    def chip_copy(self, s, m):
        full, _, _, _, _, _, send, recv = self.held
        where = self.at(self.chip, m)
        return self.remote(
            full.at[where], full.at[where], send.at[s, m], recv.at[s, m], chip=lax.rem(self.chip + s, self.chips)
        )

    def square_copy(self, kind, s):
        full, _, _, _, _, _, send, recv = self.held
        along_x, along_y, _ = square(self.chip)
        m = self.me if s == 0 else self.source(s)
        owner = self.chip if kind < 2 else (along_x if s % 2 == 0 else along_y)
        to = (along_x, along_y, along_y if s % 2 == 0 else along_x)[kind]
        where = self.at(owner, m)
        return self.remote(full.at[where], full.at[where], send.at[kind, s], recv.at[kind, s], chip=to)

    def start(self):
        self.locate()
        cut, ids = self.ins
        full, all_ids = self.held[:2]
        for s in range(1, self.members):
            self.block_copy(s).start()
        for s in range(1, self.members):
            self.ids_copy(s).start()
        full[self.at(self.chip, self.me), :] = cut[self.me]
        all_ids[self.ids_at(self.me), :] = ids[...]

    def send_block(self, s):
        m = self.me if s == 0 else self.source(s)
        if s > 0:
            self.block_copy(s).wait_recv()
        if self.chips == 4:
            for kind in (0, 1) if s % 2 == 0 else (1, 0):
                self.square_copy(kind, s).start()
            return
        for step in range(1, self.chips):
            self.chip_copy(step, m).start()

    def pass_block(self, s):
        self.square_copy(s % 2, s).wait_recv()
        self.square_copy(2, s).start()

    def tick(self, t):
        @pl.when(t == 0)
        def _():
            for s in range(self.members):
                self.send_block(s)

        half = self.members // 2
        for n in range(2):

            @pl.when(t == PASS_AT + n)
            def _():
                if self.chips == 4:
                    for s in range(n * half, (n + 1) * half):
                        self.pass_block(s)
                if n == 1:
                    self.after_blocks()

    def finish(self, ticks):
        full, all_ids = self.held[:2]
        for s in range(1, self.members):
            self.ids_copy(s).wait_recv()
            self.block_copy(s).wait_send()
            self.ids_copy(s).wait_send()

        if self.chips == 4:
            for s in range(self.members):
                for kind in range(3):
                    self.square_copy(kind, s).wait_send()
                    if kind != s % 2:
                        self.square_copy(kind, s).wait_recv()
        else:

            @pl.loop(0, self.members)
            def _(m):
                for s in range(1, self.chips):
                    self.chip_copy(s, m).wait()

        self.outs[0][...] = full[...]
        self.outs[1][...] = all_ids[...]


class QkvGrads(Extra):
    n_in, n_out = 3, 3
    met = True

    def __init__(self, spans, chips, members, grads, sums, out_grads):
        self.spans, self.chips, self.members = spans, chips, members
        self.out_rows = out_grads.shape[0] // chips
        self.block, self.columns = grads.shape[0] // (chips * members), grads.shape[1]
        self.part = self.columns // 3
        self.width = self.part * members
        self.own_rows = self.part // 128
        self.sum_rows = sums.shape[0]
        vmem = pl.BlockSpec(memory_space=pltpu.VMEM)
        self.out_shapes = [
            jax.ShapeDtypeStruct((self.block, 3 * self.width), BF16),
            jax.ShapeDtypeStruct((4, self.width // 128, 128), F32),
            jax.ShapeDtypeStruct((self.out_rows, self.width), BF16),
        ]
        self.out_specs = [vmem] * 3

    def scratch(self):
        sems = pltpu.SemaphoreType.DMA((self.members,))
        chip_sems = pltpu.SemaphoreType.DMA((self.chips,))
        cross = pltpu.SemaphoreType.DMA((self.chips, self.members))
        return [
            pltpu.VMEM((3 if self.chips == 4 else self.chips, self.members, self.block, self.columns), BF16),
            pltpu.VMEM((self.members, self.block, self.columns), BF16),
            pltpu.VMEM((self.members, self.block, self.columns), BF16),
            pltpu.VMEM((self.members, self.block, self.columns), BF16),
            pltpu.VMEM((self.chips, self.sum_rows, 128), F32),
            pltpu.VMEM((self.sum_rows, 128), F32),
            pltpu.VMEM((self.members, self.sum_rows, 128), F32),
            pltpu.VMEM((self.chips, self.out_rows, self.width), BF16),
            pltpu.VMEM((self.out_rows, self.width), BF16),
            pltpu.VMEM((self.out_rows, self.width), BF16),
        ] + [cross] * 2 + [sems] * 2 + [chip_sems] * 2 + [sems] * 2 + [chip_sems] * 2 + [pltpu.SemaphoreType.DMA] * 2

    def at(self, chip, m):
        return pl.ds(pl.multiple_of((chip * self.members + m) * self.block, self.block), self.block)

    def chip_copy(self, s, m):
        other = lax.rem(self.chip + s, self.chips)
        return self.remote(
            self.ins[0].at[self.at(other, m)], self.arrived.at[s, m],
            self.cross_send.at[s, m], self.cross_recv.at[s, m], chip=other,
        )

    def member_copy(self, s):
        core, place = step_member(self.core, self.place, s, self.spans)
        return self.remote(
            self.summed.at[core * self.spans + place], self.columns_in.at[self.me],
            self.member_send.at[s], self.member_recv.at[s], core=core, ctx=place,
        )

    def sums_chip(self, s):
        return self.remote(
            self.ins[1], self.sums_in.at[s], self.sums_send.at[s], self.sums_recv.at[s],
            chip=lax.rem(self.chip + s, self.chips),
        )

    def sums_member(self, s):
        core, place = step_member(self.core, self.place, s, self.spans)
        return self.remote(
            self.sums_chips, self.sums_members.at[self.me], self.last_send.at[s], self.last_recv.at[s],
            core=core, ctx=place,
        )

    def out_copy(self, s):
        other = lax.rem(self.chip + s, self.chips)
        rows = pl.ds(pl.multiple_of(other * self.out_rows, self.out_rows), self.out_rows)
        return self.remote(
            self.ins[2].at[rows], self.out_in.at[s], self.out_send.at[s], self.out_recv.at[s], chip=other
        )

    def move_copy(self):
        chip, core, place = owner_of(self.chip, self.core, self.place, self.spans)
        return self.remote(
            self.out_sum, self.out_final, self.move_send, self.move_recv, chip=chip, core=core, ctx=place
        )

    def square_copy(self, kind, i):
        along_x, along_y, across = square(self.chip)
        m = self.nth(i)
        first, second = (along_x, along_y) if i % 2 == 0 else (along_y, along_x)
        if kind == 2:
            src, to = self.passing.at[m], second
        else:
            src, to = self.ins[0].at[self.at((across, first)[kind], m)], first
        return self.remote(
            src, self.arrived.at[kind, m], self.cross_send.at[kind, m], self.cross_recv.at[kind, m], chip=to
        )

    def nth(self, i):
        return lax.rem(self.me + 1 + i, self.members)

    def pass_blocks(self):
        along_x, along_y, _ = square(self.chip)
        for i in range(self.members):
            m = self.nth(i)
            self.square_copy(0, i).wait_recv()
            mine = self.ins[0][self.at(along_y if i % 2 == 0 else along_x, m), :]
            self.passing[m] = (mine.astype(F32) + self.arrived[0, m].astype(F32)).astype(BF16)
            self.square_copy(2, i).start()

    def begin(self):
        self.locate()
        (
            self.arrived, self.passing, self.summed, self.columns_in, self.sums_in, self.sums_chips, self.sums_members,
            self.out_in, self.out_sum, self.out_final,
            self.cross_send, self.cross_recv, self.member_send, self.member_recv,
            self.sums_send, self.sums_recv, self.last_send, self.last_recv,
            self.out_send, self.out_recv, self.move_send, self.move_recv,
        ) = self.held
        for s in range(1, self.chips):
            self.out_copy(s).start()

    def start(self):
        for s in range(1, self.chips):
            self.sums_chip(s).start()

    def send_shares(self):
        if self.chips == 4:
            for i in range(self.members):
                self.square_copy(0, i).start()
                self.square_copy(1, i).start()
            return

        @pl.loop(0, self.members)
        def _(i):
            m = lax.rem(self.me + 1 + i, self.members)
            for s in range(1, self.chips):
                self.chip_copy(s, m).start()

    def add_block(self, m):
        total = self.ins[0][self.at(self.chip, m), :].astype(F32)
        for s in range(1, 3 if self.chips == 4 else self.chips):
            self.chip_copy(s, m).wait_recv()
            total = total + self.arrived[s, m].astype(F32)
        self.summed[m] = total.astype(BF16)

    def send_blocks(self, first, last):
        for s in range(first, last):
            core, place = step_member(self.core, self.place, s, self.spans)
            self.add_block(core * self.spans + place)
            self.member_copy(s).start()

    def tick(self, t):
        @pl.when(t == 0)
        def _():
            self.work()
            self.send_shares()

        @pl.when(t == LATE_TICK)
        def _():
            self.late()

        if self.chips == 4:

            @pl.when(t == PASS_TICK)
            def _():
                self.pass_blocks()

        @pl.when(t == 1)
        def _():
            total = self.ins[1][...]
            for s in range(1, self.chips):
                self.sums_chip(s).wait_recv()
                total = total + self.sums_in[s]
            self.sums_chips[...] = total
            self.sums_members[self.me] = total
            for s in range(1, self.members):
                self.sums_member(s).start()

        @pl.when(t == 2)
        def _():
            rows = pl.ds(pl.multiple_of(self.chip * self.out_rows, self.out_rows), self.out_rows)
            total = self.ins[2][rows, :].astype(F32)
            for s in range(1, self.chips):
                self.out_copy(s).wait_recv()
                total = total + self.out_in[s].astype(F32)
            self.out_sum[...] = total.astype(BF16)

            @pl.when(stays(self.chip, self.core, self.place, self.spans))
            def _():
                self.out_final[...] = total.astype(BF16)

            @pl.when(jnp.logical_not(stays(self.chip, self.core, self.place, self.spans)))
            def _():
                self.move_copy().start()

    def finish(self, ticks):
        self.send_blocks(1, self.members)
        self.add_block(self.me)
        self.columns_in[self.me] = self.summed[self.me]
        for s in range(1, self.members):
            self.sums_member(s).wait()
        wide = self.width // 128
        for i in range(2):
            total = self.sums_members[0, i * wide : (i + 1) * wide, :]
            for m in range(1, self.members):
                total = total + self.sums_members[m, i * wide : (i + 1) * wide, :]
            self.outs[1][2 + i] = total
            base = 2 * wide + i * self.own_rows
            for m in range(self.members):
                self.outs[1][i, m * self.own_rows : (m + 1) * self.own_rows, :] = self.sums_members[
                    m, base : base + self.own_rows, :
                ]
        for s in range(1, self.members):
            self.member_copy(s).wait()
        for m in range(self.members):
            for i in range(3):
                self.outs[0][:, i * self.width + m * self.part : i * self.width + (m + 1) * self.part] = (
                    self.columns_in[m, :, i * self.part : (i + 1) * self.part]
                )
        @pl.when(jnp.logical_not(stays(self.chip, self.core, self.place, self.spans)))
        def _():
            self.move_copy().wait()

        self.outs[2][...] = self.out_final[...]
        for s in range(1, self.chips):
            self.sums_chip(s).wait_send()
            self.out_copy(s).wait_send()

        @pl.loop(0, self.members)
        def _(m):
            for s in range(3) if self.chips == 4 else range(1, self.chips):
                self.chip_copy(s, m).wait_send()


def rope_tables(positions):
    half = HEAD_DIM // 2
    frequency = ROPE_BASE ** (-(jnp.arange(half, dtype=F32) * 2.0 / HEAD_DIM))
    angles = positions[:, None] * frequency[None, :]
    cosine = jnp.cos(angles)
    sine = jnp.sin(angles)
    return (jnp.concatenate([cosine, cosine], 1), jnp.concatenate([sine, sine], 1))


def dot(left, right):
    return jnp.dot(left, right, preferred_element_type=F32)


def dot_rows(left, right):
    return lax.dot_general(left, right, (((1,), (1,)), ((), ())), preferred_element_type=F32)


def dot_first(left, right):
    return lax.dot_general(left, right, (((0,), (0,)), ((), ())), preferred_element_type=F32)


def gather(values, axes):
    return lax.all_gather(values, axes, axis=0, tiled=True)


def scatter_sum(values, axes):
    return lax.psum_scatter(values, axes, scatter_dimension=0, tiled=True)


FF_TILE = 512
SUM_TILE = 1024
BATCH_PIECE = 16
DOWN_TICK = 6
GRAD_TILE = 256


def square(chip):
    along_x = chip + 1 - 2 * lax.rem(chip, 2)
    return along_x, lax.rem(chip + 2, 4), lax.rem(along_x + 2, 4)


class SquareSum:
    def __init__(self, chip, block, landing, send, recv):
        self.chip, self.block, self.landing, self.send, self.recv = chip, block, landing, send, recv
        self.x, self.y, self.across = square(chip)

    def copy(self, i):
        owner = (self.across, self.across, self.x, self.y, self.y, self.x)[i]
        half = (0, 1, 0, 1, 0, 1)[i]
        to = (self.x, self.y, self.x, self.y, self.y, self.x)[i]
        return pltpu.make_async_remote_copy(
            src_ref=self.block(owner, half), dst_ref=self.landing.at[i], send_sem=self.send.at[i],
            recv_sem=self.recv.at[i], device_id={"chip": to}, device_id_type=MESH_ID,
        )

    def begin(self, first):
        self.copy(first).start()
        self.copy(first + 1).start()

    def relay(self):
        for i, owner, half in ((0, self.y, 0), (1, self.x, 1)):
            self.copy(i).wait_recv()
            ref = self.block(owner, half)
            ref[...] = (ref[...].astype(F32) + self.landing[i].astype(F32)).astype(BF16)
        self.begin(4)

    def finish(self, half):
        for i in (2 + half, 4 + half):
            self.copy(i).wait_recv()
        for i in (0 + half, 2 + half, 4 + half):
            self.copy(i).wait_send()
        total = self.block(self.chip, half)[...].astype(F32)
        return total + self.landing[2 + half].astype(F32) + self.landing[4 + half].astype(F32)


class Middle:
    def __init__(self, spans, rows, width, hidden, piece):
        self.spans, self.rows, self.width, self.hidden, self.piece = spans, rows, width, hidden, piece
        self.count = rows // piece
        self.block = spans * piece
        self.batch = 2 * self.block

    def body(
        self, chips, partial, tokens, cotangent, gains, gate_up, gate_up_w, down,
        output, residual_grad, gain_feed, gain_attn, down_sum, gate_sum, residual_all, feed_grad_all, gate_part, up_part, projected_all,
        residual, projected, own, near, from_left, from_right, held, wide, act, back, up_weights, down_weights, slices, given, landed,
        load_sem, weight_sem, store_sem, slice_sem, part_sem, free_sem, near_send, near_recv, right_send, right_recv, left_send, left_recv,
        fwd_send, fwd_recv, bwd_send, bwd_recv, side_send, side_recv, down_send, down_recv, give_send, give_recv, take_send, take_recv, pass_send, pass_recv,
    ):
        spans, rows, piece, count = self.spans, self.rows, self.piece, self.count
        width, hidden, block, batch = self.width, self.hidden, self.block, self.batch
        core = lax.axis_index("core")
        place = lax.axis_index("ctx")
        other = 1 - core
        last = spans - 1
        has_left = place > 0
        has_right = place < last

        def turn_of(o):
            return jnp.maximum(o, last - o)

        def at(d, k):
            return pl.ds(pl.multiple_of((k * spans + d) * piece, piece), piece)

        def at_seq(seq, d, k):
            return pl.ds(pl.multiple_of(((k * 2 + seq) * spans + d) * piece, piece), piece)

        def batch_at(k):
            return pl.ds(pl.multiple_of(k * batch, batch), batch)

        def natural(seq, d, k):
            return pl.ds(pl.multiple_of((seq * spans + d) * rows + k * piece, piece), piece)

        def remote(src, dst, send, recv, **device):
            return pltpu.make_async_remote_copy(
                src_ref=src, dst_ref=dst, send_sem=send, recv_sem=recv, device_id=device, device_id_type=MESH_ID
            )

        barrier = pltpu.get_barrier_semaphore()
        pl.semaphore_signal(barrier, 1, device_id={"core": other}, device_id_type=MESH_ID)

        @pl.when(has_left)
        def _():
            pl.semaphore_signal(barrier, 1, device_id={"ctx": place - 1}, device_id_type=MESH_ID)

        @pl.when(has_right)
        def _():
            pl.semaphore_signal(barrier, 1, device_id={"ctx": place + 1}, device_id_type=MESH_ID)

        def near_copy(e, d, k):
            src = partial.at[natural(other, d, k)] if e == 0 else own.at[at_seq(other, d, k)]
            return remote(src, near.at[at(d, k)], near_send.at[d, k], near_recv.at[d, k], core=other)

        def right_copy(d, k):
            return remote(
                own.at[at_seq(core, d, k)], from_left.at[at(d, k)], right_send.at[d, k], right_recv.at[d, k],
                ctx=place + 1,
            )

        def left_copy(d, k):
            return remote(
                own.at[at_seq(core, d, k)], from_right.at[at(d, k)], left_send.at[d, k], left_recv.at[d, k],
                ctx=place - 1,
            )

        def spread_copy(o, k, send, recv, **device):
            where = held.at[at_seq(core, o, k)]
            return remote(where, where, send.at[o, k], recv.at[o, k], **device)

        def fwd_copy(o, k):
            return spread_copy(o, k, fwd_send, fwd_recv, ctx=place + 1)

        def bwd_copy(o, k):
            return spread_copy(o, k, bwd_send, bwd_recv, ctx=place - 1)

        def side_copy(o, k):
            return spread_copy(o, k, side_send, side_recv, core=other)

        def load_own(d, k):
            return pltpu.make_async_copy(
                partial.at[natural(core, d, k)], own.at[at_seq(core, d, k)], load_sem.at[d, k]
            )

        @pl.loop(0, count)
        def _(k):
            for d in range(spans):
                load_own(d, k).start()

        chip = lax.axis_index("chip")
        shard = down.shape[0]
        here = pl.ds(pl.multiple_of(chip * shard, shard), shard)
        load_down = pltpu.make_async_copy(down, down_weights.at[here], weight_sem.at[chips])

        if chips == 4:
            along_x, along_y, across = square(chip)

        def load_up(s):
            if s == 0:
                return pltpu.make_async_copy(gate_up, up_weights.at[here], weight_sem.at[0])
            source = (along_x, along_y)[s - 1] if chips == 4 else lax.rem(chip + s, chips)
            there = pl.ds(pl.multiple_of(source * shard, shard), shard)
            return pltpu.make_async_copy(gate_up_w.at[there], up_weights.at[there], weight_sem.at[s])


        loads = 3 if chips == 4 else chips

        def up_copy(i):
            size = shard // 2
            source, to = ((along_x, along_y), (along_y, along_x))[i]
            where = pl.ds(pl.multiple_of(source * shard + i * size, size), size)
            return remote(gate_up_w.at[where], up_weights.at[where], pass_send.at[i], pass_recv.at[i], chip=to)

        def down_copy(s):
            if chips != 4:
                return remote(
                    down, down_weights.at[here], down_send.at[s], down_recv.at[s], chip=lax.rem(chip + s, chips)
                )
            half = (0, 1, 1, 0, 0, 1)[s]
            to = (along_x, along_y, along_x, along_y, along_y, along_x)[s]
            size = shard // 2
            if s < 4:
                src = down.at[half * size : (half + 1) * size]
                at_chip = chip
            else:
                at_chip = (along_x, along_y)[s - 4]
            dst = down_weights.at[pl.ds(pl.multiple_of(at_chip * shard + half * size, size), size)]
            return remote(src if s < 4 else dst, dst, down_send.at[s], down_recv.at[s], chip=to)

        def relay_down():
            for s in range(2):
                down_copy(s).wait_recv()
                down_copy(4 + s).start()

        for s in range(loads):
            load_up(s).start()
        load_down.start()
        gain_feed[...] = jnp.zeros_like(gain_feed)
        gain_attn[...] = jnp.zeros_like(gain_attn)
        for s in range(1, chips):
            pl.semaphore_signal(
                barrier, 1, device_id={"chip": lax.rem(chip + s, chips)}, device_id_type=MESH_ID
            )
        pl.semaphore_wait(barrier, chips + has_left.astype(jnp.int32) + has_right.astype(jnp.int32))
        if chips == 4:
            for i in range(2):
                up_copy(i).start()
        for s in range(4) if chips == 4 else range(1, chips):
            down_copy(s).start()

        @pl.loop(0, count)
        def _(k):
            for d in range(spans):
                near_copy(0, d, k).start()

        def base(e, d, k):
            near_copy(e, d, k).wait_recv()
            if e == 0:
                load_own(d, k).wait()
            return own[at_seq(core, d, k), :].astype(F32) + near[at(d, k), :].astype(F32)

        def pass_on(e, d, k, arrived, copy, later):
            value = base(e, d, k)

            @pl.when(later)
            def _():
                copy(d, k).wait_recv()

            before = arrived[at(d, k), :].astype(F32)
            value = value + jnp.where(later, before, jnp.zeros_like(before))
            own[at_seq(core, d, k), :] = value.astype(BF16)
            copy(d, k).start()

        def pass_right(e, k):
            for d in range(last, 0, -1):

                @pl.when(d > place)
                def _():
                    pass_on(e, d, k, from_left, right_copy, has_left)

        def pass_left(e, k):
            for d in range(last):

                @pl.when(d < place)
                def _():
                    pass_on(e, d, k, from_right, left_copy, has_right)

        def finish(e, k):
            total = base(e, place, k)

            @pl.when(has_left)
            def _():
                right_copy(place, k).wait_recv()

            @pl.when(has_right)
            def _():
                left_copy(place, k).wait_recv()

            zero = jnp.zeros_like(total)
            total = total + jnp.where(has_left, from_left[at(place, k), :].astype(F32), zero)
            total = total + jnp.where(has_right, from_right[at(place, k), :].astype(F32), zero)
            mine = pl.ds(pl.multiple_of(k * piece, piece), piece)
            if e == 0:
                result = after_projected(total, (tokens, gains), (residual, projected), mine)
            elif e == 1:
                result = after_feed(total, (residual, cotangent, gains), (output, gain_feed), mine)
            else:
                result = after_back(total, (projected, cotangent, gains), (residual_grad, gain_attn), mine)
            held[at_seq(core, place, k), :] = result.astype(BF16)

            @pl.when(has_right)
            def _():
                fwd_copy(place, k).start()

            @pl.when(has_left)
            def _():
                bwd_copy(place, k).start()

            side_copy(place, k).start()

        def relay_right(o, k):
            fwd_copy(o, k).wait_recv()

            @pl.when(has_right)
            def _():
                fwd_copy(o, k).start()

            side_copy(o, k).start()

        def relay_left(o, k):
            bwd_copy(o, k).wait_recv()

            @pl.when(has_left)
            def _():
                bwd_copy(o, k).start()

            side_copy(o, k).start()

        def gathered(k):
            for o in range(spans):
                side_copy(o, k).wait_recv()

        def sums_sent(e, k):
            for d in range(spans):
                near_copy(e, d, k).wait_send()

                @pl.when(d > place)
                def _():
                    right_copy(d, k).wait_send()

                @pl.when(d < place)
                def _():
                    left_copy(d, k).wait_send()

        def spread_sent(k):
            for o in range(spans):
                side_copy(o, k).wait_send()

                @pl.when(jnp.logical_and(o <= place, has_right))
                def _():
                    fwd_copy(o, k).wait_send()

                @pl.when(jnp.logical_and(o >= place, has_left))
                def _():
                    bwd_copy(o, k).wait_send()

        def store(src, dst, k, sem):
            return pltpu.make_async_copy(src, dst.at[batch_at(k)], sem)

        def forward(k):
            @pl.when(k == 0)
            def _():
                for s in range(loads):
                    load_up(s).wait()
                if chips == 4:
                    for i in range(2):
                        up_copy(i).wait()

            gathered(k)
            keep = store(held.at[batch_at(k)], residual_all, k, store_sem.at[0])
            keep.start()

            @pl.loop(0, hidden // FF_TILE)
            def _(n):
                low = pl.ds(pl.multiple_of(n * FF_TILE, FF_TILE), FF_TILE)
                high = pl.ds(pl.multiple_of(hidden + n * FF_TILE, FF_TILE), FF_TILE)
                gate = dot(held[batch_at(k), :], up_weights[:, low])
                up = dot(held[batch_at(k), :], up_weights[:, high])
                wide[batch_at(k), low] = gate
                wide[batch_at(k), high] = up
                act[batch_at(k), low] = (gate * (1.0 / (1.0 + jnp.exp(-gate))) * up).astype(BF16)

            sums_sent(0, k)

            @pl.when(k == 0)
            def _():
                load_down.wait()
                for s in range(1, chips) if chips != 4 else range(6):
                    down_copy(s).wait_send()
                    if chips != 4 or s >= 2:
                        down_copy(s).wait_recv()

            @pl.loop(0, width // SUM_TILE)
            def _(n):
                columns = pl.ds(pl.multiple_of(n * SUM_TILE, SUM_TILE), SUM_TILE)
                own[batch_at(k), columns] = dot_rows(act[batch_at(k), :], down_weights[columns, :]).astype(BF16)

            keep.wait()
            spread_sent(k)
            for d in range(spans):
                near_copy(1, d, k).start()

        down_tiles = width // GRAD_TILE
        per_chip = shard // GRAD_TILE

        def tile_rows(n):
            return pl.ds(pl.multiple_of(n * GRAD_TILE, GRAD_TILE), GRAD_TILE)

        if chips == 4:
            assert per_chip == 2
            turns = [(across, 0), (across, 1), (along_x, 0), (along_y, 1), (along_y, 0), (along_x, 1), (chip, 0), (chip, 1)]
            order = [owner * per_chip + half for owner, half in turns]
        else:
            order = [lax.rem(chip + 1 + j // per_chip, chips) * per_chip + j % per_chip for j in range(down_tiles)]
        tiles = [(m, order[j] if m < 2 else j) for m in range(3) for j in range(down_tiles)]

        def load_slice(j):
            m, n = tiles[j]
            source = feed_grad_all if m == 0 else residual_all
            return pltpu.make_async_copy(source.at[:, tile_rows(n)], slices.at[j % 4], slice_sem.at[j % 4])

        def half_at(owner, half):
            return pl.ds(pl.multiple_of((owner * per_chip + half) * GRAD_TILE, GRAD_TILE), GRAD_TILE)

        if chips == 4:
            sums = [
                SquareSum(
                    chip, lambda owner, half: given.at[half_at(owner, half)], landed.at[0], give_send, give_recv
                ),
                SquareSum(
                    chip, lambda owner, half: up_weights.at[half_at(owner, half), :hidden], landed.at[1], take_send, take_recv
                ),
            ]

        def give_copy(s):
            theirs = pl.ds(pl.multiple_of(lax.rem(chip + s, chips) * shard, shard), shard)
            return remote(
                given.at[theirs], down_weights.at[s * shard : (s + 1) * shard], give_send.at[s], give_recv.at[s],
                chip=lax.rem(chip + s, chips),
            )

        def part_copy(n, m):
            half = slice((m - 1) * hidden, m * hidden)
            return pltpu.make_async_copy(
                up_weights.at[tile_rows(n), half], (gate_part, up_part)[m - 1].at[tile_rows(n)], part_sem.at[m - 1, n]
            )

        def work_out(j):
            if j + 2 < len(tiles):
                load_slice(j + 2).start()
            load_slice(j).wait()
            m, n = tiles[j]
            if m == 0:
                given[tile_rows(n), :] = dot_first(slices[j % 4], act[...]).astype(BF16)
            else:
                half = slice((m - 1) * hidden, m * hidden)
                up_weights[tile_rows(n), half] = dot_first(slices[j % 4], back[:, half]).astype(BF16)

        def weight_grads(q):
            if chips == 4:
                m, r = q // 4, q % 4
                if m < 2:
                    for j in range(m * down_tiles + 2 * r, m * down_tiles + 2 * r + 2):
                        work_out(j)
                    if r < 2:
                        sums[m].begin(2 * r)
                    elif r == 2:
                        sums[m].relay()
                else:
                    for j in range(2 * down_tiles, 3 * down_tiles):
                        work_out(j)
                        part_copy(tiles[j][1], 2).start()
                return
            if q < chips:
                for j in range(q * per_chip, (q + 1) * per_chip):
                    work_out(j)
                if q == 0:
                    pl.semaphore_wait(free_sem, chips - 1)
                if q < chips - 1:
                    give_copy(q + 1).start()
                return
            first = down_tiles + 4 * (q - chips)
            for j in range(first, min(first + 4, len(tiles))):
                work_out(j)
                part_copy(tiles[j][1], tiles[j][0]).start()

        def backward(k):
            gathered(k)
            keep = store(held.at[batch_at(k)], feed_grad_all, k, store_sem.at[0])
            keep.start()

            @pl.loop(0, hidden // FF_TILE)
            def _(n):
                low = pl.ds(pl.multiple_of(n * FF_TILE, FF_TILE), FF_TILE)
                high = pl.ds(pl.multiple_of(hidden + n * FF_TILE, FF_TILE), FF_TILE)
                act_grad = dot(held[batch_at(k), :], down_weights[:, low])
                gate = wide[batch_at(k), low]
                up = wide[batch_at(k), high]
                sigmoid = 1.0 / (1.0 + jnp.exp(-gate))
                back[batch_at(k), low] = (act_grad * up * sigmoid * (1.0 + gate * (1.0 - sigmoid))).astype(BF16)
                back[batch_at(k), high] = (act_grad * (gate * sigmoid)).astype(BF16)

            sums_sent(1, k)

            @pl.loop(0, width // SUM_TILE)
            def _(n):
                columns = pl.ds(pl.multiple_of(n * SUM_TILE, SUM_TILE), SUM_TILE)
                own[batch_at(k), columns] = dot_rows(back[batch_at(k), :], up_weights[columns, :]).astype(BF16)

            keep.wait()
            spread_sent(k)
            for d in range(spans):
                near_copy(2, d, k).start()

            @pl.when(k == count - 1)
            def _():
                for s in range(1, chips) if chips != 4 else ():
                    pl.semaphore_signal(
                        free_sem, 1, device_id={"chip": lax.rem(chip + s, chips)}, device_id_type=MESH_ID
                    )
                load_slice(0).start()
                load_slice(1).start()

        def give(seq, d, k):
            return pltpu.make_async_copy(
                held.at[at_seq(seq, d, k)], projected_all.at[natural(seq, d, k)], load_sem.at[d, k]
            )

        def hand_out(k):
            gathered(k)
            sums_sent(2, k)
            for seq in range(2):
                for d in range(spans):
                    give(seq, d, k).start()
                for d in range(spans):
                    give(seq, d, k).wait()
            spread_sent(k)

        step = 2 * last + 3
        last_steps = 9 if chips == 4 else chips + down_tiles // 2
        assert last_steps <= step + 1

        def due(t, run):
            @pl.when(jnp.logical_and(t >= 0, t < count))
            def _():
                run(t)

        @pl.loop(0, 3 * step + count - 1)
        def _(t):
            for e in range(2, -1, -1):
                now = t - e * step
                for j in range(1, spans):
                    o = place - j

                    @pl.when(o >= 0)
                    def _():
                        due(now - turn_of(o) - j, functools.partial(relay_right, o))

                    p = place + j

                    @pl.when(p < spans)
                    def _():
                        due(now - turn_of(p) - j, functools.partial(relay_left, p))

                due(now - place, functools.partial(pass_right, e))
                due(now - (last - place), functools.partial(pass_left, e))
                due(now - turn_of(place), functools.partial(finish, e))
            if chips == 4:

                @pl.when(t == DOWN_TICK)
                def _():
                    relay_down()

            for e, run in ((2, hand_out), (1, backward), (0, forward)):
                due(t - e * step - 2 * last, run)
            for q in range(last_steps):

                @pl.when(t == count + step + 2 * last + q)
                def _():
                    weight_grads(q)

        if chips == 4:
            for group, out in zip(sums, (down_sum, gate_sum)):
                for half in range(2):
                    out[half * GRAD_TILE : (half + 1) * GRAD_TILE, :] = group.finish(half).astype(BF16)
            for n in range(down_tiles):
                part_copy(n, 2).wait()
            return
        total = given[here, :].astype(F32)
        for s in range(1, chips):
            give_copy(s).wait()
            total = total + down_weights[s * shard : (s + 1) * shard, :].astype(F32)
        down_sum[...] = total.astype(BF16)
        gate_sum[...] = jnp.zeros_like(gate_sum)
        for n in range(down_tiles):
            part_copy(n, 1).wait()
            part_copy(n, 2).wait()

    def call(self, chips, partial, tokens, cotangent, gains, gate_up, gate_up_w, down):
        spans, rows, width, hidden, count = self.spans, self.rows, self.width, self.hidden, self.count
        total = 2 * spans * rows
        vmem = pl.BlockSpec(memory_space=pltpu.VMEM)
        hbm = pl.BlockSpec(memory_space=pl.ANY)
        shape = jax.ShapeDtypeStruct
        sems = pltpu.SemaphoreType.DMA((spans, count))
        two = pltpu.SemaphoreType.DMA((2,))
        return pl.pallas_call(
            functools.partial(self.body, chips),
            out_shape=[
                shape((rows, width), BF16),
                shape((rows, width), F32),
                shape((1, width), F32),
                shape((1, width), F32),
                shape(down.shape, BF16),
                shape(down.shape, BF16),
                shape((total, width), BF16),
                shape((total, width), BF16),
                shape((16, 128) if chips == 4 else (width, hidden), BF16),
                shape((width, hidden), BF16),
                shape((total, width), BF16),
            ],
            in_specs=[hbm, vmem, vmem, vmem, hbm, hbm, hbm],
            out_specs=[vmem] * 6 + [hbm] * 5,
            scratch_shapes=[
                pltpu.VMEM((rows, width), F32),
                pltpu.VMEM((rows, width), F32),
                pltpu.VMEM((total, width), BF16),
                pltpu.VMEM((total // 2, width), BF16),
                pltpu.VMEM((total // 2, width), BF16),
                pltpu.VMEM((total // 2, width), BF16),
                pltpu.VMEM((total, width), BF16),
                pltpu.VMEM((total, 2 * hidden), F32),
                pltpu.VMEM((total, hidden), BF16),
                pltpu.VMEM((total, 2 * hidden), BF16),
                pltpu.VMEM((width, 2 * hidden), BF16),
                pltpu.VMEM((width, hidden), BF16),
                pltpu.VMEM((4, total, GRAD_TILE), BF16),
                pltpu.VMEM((width, hidden), BF16),
                pltpu.VMEM((2, 6, GRAD_TILE, hidden) if chips == 4 else (2, 6, 16, 128), BF16),
                sems,
                pltpu.SemaphoreType.DMA((chips + 1,)),
                two,
                pltpu.SemaphoreType.DMA((4,)),
                pltpu.SemaphoreType.DMA((2, width // GRAD_TILE)),
                pltpu.SemaphoreType.REGULAR,
            ]
            + [sems] * 12
            + [pltpu.SemaphoreType.DMA((max(chips, 6),))] * 8,
            compiler_params=pltpu.CompilerParams(
                collective_id=2, has_side_effects=True, vmem_limit_bytes=62 << 20
            ),
            cost_estimate=pl.CostEstimate(
                flops=36 * rows * spans * width * hidden, bytes_accessed=100 * width * width, transcendentals=0
            ),
            name="feed_forward",
        )(partial, tokens, cotangent, gains, gate_up, gate_up_w, down)


def turn(values, cosine, sine):
    return values * cosine + pltpu.roll(values, HEAD_DIM // 2, 1) * sine


def row_sums(values):
    total = values[:, :128]
    for first in range(128, values.shape[1], 128):
        total = total + values[:, first : first + 128]
    return jnp.sum(jnp.transpose(total), axis=0, keepdims=True)


def down_rows(row):
    return jnp.transpose(jnp.broadcast_to(row, (128, row.shape[1])))


class Stats:
    def __init__(self, spans, own, arrived, send, recv):
        self.spans, self.own, self.arrived, self.send, self.recv = spans, own, arrived, send, recv
        self.core, self.place = lax.axis_index("core"), lax.axis_index("ctx")
        self.me = self.core * spans + self.place

    def member(self, s):
        core, place = step_member(self.core, self.place, s, self.spans)
        return {"core": core, "ctx": place}

    def greet(self):
        for s in range(1, 2 * self.spans):
            pl.semaphore_signal(
                pltpu.get_barrier_semaphore(), 1, device_id=self.member(s), device_id_type=MESH_ID
            )

    def meet(self):
        pl.semaphore_wait(pltpu.get_barrier_semaphore(), 2 * self.spans - 1)

    def copy(self, s):
        return pltpu.make_async_remote_copy(
            src_ref=self.own, dst_ref=self.arrived.at[s], send_sem=self.send.at[s], recv_sem=self.recv.at[s],
            device_id=self.member(s), device_id_type=MESH_ID,
        )

    def start(self):
        for s in range(1, 2 * self.spans):
            self.copy(s).start()

    def total(self):
        total = self.own[...]
        for s in range(1, 2 * self.spans):
            self.copy(s).wait()
            total = total + self.arrived[s]
        return total


def stats_scratch(spans, total_rows):
    sems = pltpu.SemaphoreType.DMA((2 * spans,))
    return [
        pltpu.VMEM((8, total_rows), F32),
        pltpu.VMEM((2 * spans, 8, total_rows), F32),
        sems,
        sems,
    ]


def allowed_at(ids, seq, block, count, spans):
    rows = ids.shape[1]
    per = block // rows
    ids_of = lambda z: ids[(seq * spans + z) * 8 : (seq * spans + z) * 8 + 8, :].astype(F32)
    first = count * per
    keys = jnp.concatenate([ids_of(z)[:1] for z in range(first + per)], 1)
    queries = jnp.concatenate([jnp.transpose(ids_of(z))[:, :1] for z in range(first, first + per)], 0)
    shape = (block, (count + 1) * block)
    query_at = lax.broadcasted_iota(jnp.int32, shape, 0) + count * block
    key_at = lax.broadcasted_iota(jnp.int32, shape, 1)
    same = queries == keys
    seen = jnp.logical_and(same, key_at <= query_at)
    return jnp.logical_and(seen, jnp.logical_or(keys != 0.0, key_at == query_at))


def softmax_parts(query, key, allowed):
    scores = jnp.where(allowed, dot_rows(query, key) * HEAD_DIM ** (-0.5), -1e30)
    weights = jnp.exp(scores - jnp.max(scores, axis=1, keepdims=True))
    return weights / jnp.sum(weights, axis=1, keepdims=True)


QUERY_BLOCK = 256
ROW_TILE = 256


class Neighbours:
    pieces = 4

    def __init__(self, chip, shard, full, send, recv):
        self.chip, self.shard, self.full, self.send, self.recv = chip, shard, full, send, recv
        self.to = square(chip)[:2]

    def copy(self, i, n):
        size = self.shard.shape[0] // self.pieces
        where = self.full.at[pl.ds(pl.multiple_of(self.chip * self.shard.shape[0] + n * size, size), size)]
        return pltpu.make_async_remote_copy(
            src_ref=self.shard.at[n * size : (n + 1) * size], dst_ref=where,
            send_sem=self.send.at[i, n], recv_sem=self.recv.at[i, n],
            device_id={"chip": self.to[i]}, device_id_type=MESH_ID,
        )

    def begin(self):
        for n in range(self.pieces):
            for i in range(2):
                self.copy(i, n).start()

    def finish(self):
        for n in range(self.pieces):
            for i in range(2):
                self.copy(i, n).wait()


def attend_body(
    spans, chips, exchange, extra, n_scratch,
    tokens, w_qkv, segment, w_out, w_gate, w_up, w_down, gains, cosine, sine,
    gate_up, down, weights_out, ids, tokens_all, gate_up_w,
    partial_out, out_w_out, query_out, key_out, value_out, normed_out, factor_out, attended_out,
    cut, own_ids, split, split_sems, raw, given, out_w, moved, own, arrived, store_sem, chip_send, chip_recv, send, recv, move_send, move_recv,
    up_send, up_recv, *rest,
):
    part = out_w.shape[0]
    total_rows = raw.shape[0]
    length = total_rows // 2
    width = tokens.shape[1]
    tiles = total_rows // ROW_TILE
    held, held_w = rest[0], rest[n_scratch]
    stats = Stats(spans, own, arrived, send, recv)
    greet_all(spans, True)
    chip, core, place = lax.axis_index("chip"), stats.core, stats.place
    shard = moved.shape[0]
    here = pl.ds(pl.multiple_of(chip * shard, shard), shard)

    def at(i):
        return pl.ds(pl.multiple_of(i * ROW_TILE, ROW_TILE), ROW_TILE)

    def chip_copy(s):
        return pltpu.make_async_remote_copy(
            src_ref=moved, dst_ref=out_w.at[here], send_sem=chip_send.at[s], recv_sem=chip_recv.at[s],
            device_id={"chip": lax.rem(chip + s, chips)}, device_id_type=MESH_ID,
        )

    def move_copy():
        to_chip, to_core, to_place = summer_of(chip, core, place, spans)
        return pltpu.make_async_remote_copy(
            src_ref=w_out, dst_ref=moved, send_sem=move_send, recv_sem=move_recv,
            device_id={"chip": to_chip, "core": to_core, "ctx": to_place}, device_id_type=MESH_ID,
        )

    home = stays(chip, core, place, spans)
    if chips == 4:
        up = Neighbours(chip, gate_up, gate_up_w, up_send, up_recv)
    own[...] = jnp.zeros_like(own)
    loads, sends, stores = split_copies(w_gate, w_up, w_down, gate_up, down, split, *(split_sems.at[n] for n in range(4)))
    for load in loads:
        load.start()
    for m in range(2 * spans):
        for i in range(3):
            column = i * width + m * part
            cut[m, :, i * part : (i + 1) * part] = w_qkv[:, column : column + part]
    own_ids[...] = jnp.broadcast_to(segment[...], own_ids.shape)
    wait_all(spans, True)
    for load, store, other in zip(loads, stores, sends):
        other.start()
        load.wait()
        store.start()

    @pl.when(home)
    def _():
        moved[...] = w_out[...]

    @pl.when(jnp.logical_not(home))
    def _():
        move_copy().start()

    def after_blocks():
        @pl.when(jnp.logical_not(home))
        def _():
            move_copy().wait()

        for s in range(1, chips):
            chip_copy(s).start()
        out_w[here, :] = moved[...]
        for store, other in zip(stores, sends):
            store.wait()
            other.wait()
        if chips == 4:
            up.begin()

    extra.after_blocks = after_blocks
    exchange.body(tokens, cut, own_ids, weights_out, ids, tokens_all, *rest)

    @pl.loop(0, tiles)
    def _(i):
        values = dot(held[at(i), :], held_w[...])
        raw[at(i), :] = values
        for n in range(2):
            some = values[:, n * part : (n + 1) * part]
            own[n : n + 1, at(i)] = row_sums(some * some)

    stats.start()

    @pl.loop(0, tiles)
    def _(i):
        value_out[at(i), :] = raw[at(i), 2 * part :].astype(BF16)

    factor_out[...] = lax.rsqrt(stats.total() / width + EPS)
    me = stats.me
    columns = pl.ds(pl.multiple_of(me * part, part), part)
    gain = jnp.concatenate([gains[0:1, columns], gains[1:2, columns]], 1)

    @pl.loop(0, tiles)
    def _(i):
        by_query, by_key = down_rows(factor_out[0:1, at(i)]), down_rows(factor_out[1:2, at(i)])
        place = pl.ds(pl.multiple_of(lax.rem(i, length // ROW_TILE) * ROW_TILE, ROW_TILE), ROW_TILE)
        for h in range(part // HEAD_DIM):
            head = slice(h * HEAD_DIM, (h + 1) * HEAD_DIM)
            low = slice(part + h * HEAD_DIM, part + (h + 1) * HEAD_DIM)
            for out, by, where in ((query_out, by_query, head), (key_out, by_key, low)):
                normed = raw[at(i), where] * by
                normed_out[at(i), where] = normed
                out[at(i), head] = turn(normed * gain[:, where], cosine[place, :], sine[place, :]).astype(BF16)

    for s in range(1, chips):
        chip_copy(s).wait()
    out_w_out[...] = out_w[...]
    block = QUERY_BLOCK
    for seq in range(2):
        for count in range(length // block):
            allowed = allowed_at(ids, seq, block, count, spans)
            rows = slice(seq * length + count * block, seq * length + (count + 1) * block)
            keys = slice(seq * length, seq * length + (count + 1) * block)
            for h in range(part // HEAD_DIM):
                head = slice(h * HEAD_DIM, (h + 1) * HEAD_DIM)
                shares = softmax_parts(query_out[rows, head], key_out[keys, head], allowed)
                attended_out[rows, head] = dot(shares.astype(BF16), value_out[keys, head]).astype(BF16)
            i = rows.start // ROW_TILE
            if i >= 2:
                pltpu.make_async_copy(given.at[i % 2], partial_out.at[at(i - 2)], store_sem.at[i - 2]).wait()
            given[i % 2] = dot(attended_out[rows, :], out_w[...]).astype(BF16)
            pltpu.make_async_copy(given.at[i % 2], partial_out.at[at(i)], store_sem.at[i]).start()
    for i in range(tiles - 2, tiles):
        pltpu.make_async_copy(given.at[i % 2], partial_out.at[at(i)], store_sem.at[i]).wait()
    if chips == 4:
        up.finish()


def attend(spans, chips, tokens, w_qkv, segment, w_out, w_gate, w_up, w_down, gains, cosine, sine):
    rows, width = tokens.shape
    total_rows = 2 * spans * rows
    part = w_out.shape[0] * chips
    tiles = total_rows // ROW_TILE
    vmem = pl.BlockSpec(memory_space=pltpu.VMEM)
    hbm = pl.BlockSpec(memory_space=pl.ANY)
    shape = jax.ShapeDtypeStruct
    cut = shape((2 * spans, w_qkv.shape[0], 3 * part), BF16)
    extra = QkvWeights(spans, chips, cut, shape((8, rows), jnp.int32))
    slab, columns = w_gate.shape
    exchange = Exchange(spans, rows, width, PIECE, False, True, pass_tokens, 1, 0, None, extra)
    scratch = exchange.scratch()
    return pl.pallas_call(
        functools.partial(attend_body, spans, chips, exchange, extra, len(scratch) - len(extra.scratch())),
        out_shape=[
            shape((2 * slab, columns), BF16),
            shape((2 * slab, columns // 2), BF16),
            *extra.out_shapes,
            shape((total_rows, width), BF16),
            shape((chips * 2 * slab if chips == 4 else 16, columns), BF16),
            shape((total_rows, width), BF16),
            shape((part, width), BF16),
            shape((total_rows, part), BF16),
            shape((total_rows, part), BF16),
            shape((total_rows, part), BF16),
            shape((total_rows, 2 * part), F32),
            shape((8, total_rows), F32),
            shape((total_rows, part), BF16),
        ],
        in_specs=[vmem] * 4 + [hbm] * 3 + [vmem] * 3,
        out_specs=[hbm] * 2 + [vmem] * 2 + [hbm] * 3 + [vmem] * 7,
        scratch_shapes=[
            pltpu.VMEM(cut.shape, BF16),
            pltpu.VMEM((8, rows), jnp.int32),
            pltpu.VMEM((3, slab, columns // 2), BF16),
            pltpu.SemaphoreType.DMA((4, 3)),
            pltpu.VMEM((total_rows, 3 * part), F32),
            pltpu.VMEM((2, ROW_TILE, width), BF16),
            pltpu.VMEM((part, width), BF16),
            pltpu.VMEM(w_out.shape, BF16),
            *stats_scratch(spans, total_rows)[:2],
            pltpu.SemaphoreType.DMA((tiles,)),
            pltpu.SemaphoreType.DMA((chips,)),
            pltpu.SemaphoreType.DMA((chips,)),
            *stats_scratch(spans, total_rows)[2:],
            pltpu.SemaphoreType.DMA,
            pltpu.SemaphoreType.DMA,
            pltpu.SemaphoreType.DMA((2, Neighbours.pieces)),
            pltpu.SemaphoreType.DMA((2, Neighbours.pieces)),
            *scratch,
        ],
        compiler_params=pltpu.CompilerParams(collective_id=1, has_side_effects=True, vmem_limit_bytes=58 << 20),
        cost_estimate=pl.CostEstimate(
            flops=2 * total_rows * width * 5 * part, bytes_accessed=50 * width * width, transcendentals=0
        ),
        name="attend",
    )(tokens, w_qkv, segment, w_out, w_gate, w_up, w_down, gains, cosine, sine)


def attend_back_body(
    spans, chips, exchange, extra, n_scratch,
    grads, tokens, weights, up_part, gate_sum, down_sum, out_w, gains, ids, cosine, sine, residual_grad, gain_attn, gain_feed,
    query, key, value, normed, factor, attended,
    input_grad, grad_qkv, grad_gains, grad_out, grad_gate, grad_down, grad_up,
    held, held_tokens, held_w, raw, mixed, attended_grad, own, arrived, load_sem, send, recv,
    qkv_part, out_part, sums, up_held, up_landed, up_send, up_recv, joined, join_send, join_recv, *rest,
):
    part = out_w.shape[0]
    total_rows = raw.shape[0]
    length = total_rows // 2
    width = grads.shape[1]
    tiles = total_rows // ROW_TILE
    scale = HEAD_DIM ** (-0.5)
    stats = Stats(spans, own, arrived, send, recv)
    greet_all(spans, True)

    def at(i):
        return pl.ds(pl.multiple_of(i * ROW_TILE, ROW_TILE), ROW_TILE)

    def load_rows(i):
        return pltpu.make_async_copy(grads.at[at(i)], held.at[at(i)], load_sem.at[i])

    @pl.loop(0, tiles)
    def _(i):
        load_rows(i).start()

    own[...] = jnp.zeros_like(own)
    load_w = pltpu.make_async_copy(weights, held_w, load_sem.at[tiles])
    load_tokens = pltpu.make_async_copy(tokens, held_tokens, load_sem.at[tiles + 1])
    load_w.start()
    load_tokens.start()
    if chips == 4:
        load_up = pltpu.make_async_copy(up_part, up_held, load_sem.at[tiles + 2])
        load_up.start()
    me = stats.me
    columns = pl.ds(pl.multiple_of(me * part, part), part)
    gain = jnp.concatenate([gains[0:1, columns], gains[1:2, columns]], 1)

    @pl.loop(0, tiles)
    def _(i):
        load_rows(i).wait()
        attended_grad[at(i), :] = dot_rows(held[at(i), :], out_w[...]).astype(BF16)

    out_part[...] = dot_first(attended[...], held[...]).astype(BF16)
    wait_all(spans, True)
    extra.ins = [qkv_part, sums, out_part]
    extra.held = list(rest[n_scratch:])
    extra.begin()
    if chips == 4:
        load_up.wait()
        half_rows = width // 8
        up_sums = SquareSum(
            lax.axis_index("chip"),
            lambda owner, half: up_held.at[
                pl.ds(pl.multiple_of((owner * 2 + half) * half_rows, half_rows), half_rows)
            ],
            up_landed, up_send, up_recv,
        )
        up_sums.begin(0)
        up_sums.begin(2)
        slab = gate_sum.shape[0] // 2
        side = gate_sum.shape[1]
        my_chip = lax.axis_index("chip")
        up_sum = up_held.at[pl.ds(pl.multiple_of(my_chip * 2 * slab, 2 * slab), 2 * slab)]
        pairs = ((gate_sum, grad_gate), (down_sum, grad_down), (up_sum, grad_up))
        theirs = pl.ds(pl.multiple_of((1 - stats.core) * slab, slab), slab)
        near = pl.ds(pl.multiple_of(stats.core * side, side), side)
        far = pl.ds(pl.multiple_of((1 - stats.core) * side, side), side)

        def join_copy(n):
            return pltpu.make_async_remote_copy(
                src_ref=pairs[n][0].at[theirs], dst_ref=joined.at[n], send_sem=join_send.at[n],
                recv_sem=join_recv.at[n], device_id={"core": 1 - stats.core}, device_id_type=MESH_ID,
            )

        def join(n):
            given, out = pairs[n]
            out[:, near] = given[pl.ds(pl.multiple_of(stats.core * slab, slab), slab), :]
            join_copy(n).wait()
            out[:, far] = joined[n]

        join_copy(0).start()
        join_copy(1).start()
    block = QUERY_BLOCK
    blocks = length // block
    for seq in range(2):
        for h in range(part // HEAD_DIM):
            head = slice(h * HEAD_DIM, (h + 1) * HEAD_DIM)
            key_at = slice(part + h * HEAD_DIM, part + (h + 1) * HEAD_DIM)
            value_at = slice(2 * part + h * HEAD_DIM, 2 * part + (h + 1) * HEAD_DIM)
            for count in reversed(range(blocks)):
                allowed = allowed_at(ids, seq, block, count, spans)
                rows = slice(seq * length + count * block, seq * length + (count + 1) * block)
                keys = slice(seq * length, seq * length + (count + 1) * block)
                shares = softmax_parts(query[rows, head], key[keys, head], allowed)
                share_grad = dot_rows(attended_grad[rows, head], value[keys, head])
                inner = jnp.sum(shares * share_grad, axis=1, keepdims=True)
                score_grad = (shares * (share_grad - inner)).astype(BF16)
                raw[rows, head] = dot(score_grad, key[keys, head]) * scale
                key_grad = dot_first(score_grad, query[rows, head]) * scale
                value_grad = dot_first(shares.astype(BF16), attended_grad[rows, head])
                if count == blocks - 1:
                    raw[keys, key_at] = key_grad
                    raw[keys, value_at] = value_grad
                else:
                    raw[keys, key_at] += key_grad
                    raw[keys, value_at] += value_grad

    gain_rows = jnp.zeros((1, 2 * part), F32)

    for i in range(tiles):
        place = slice(i * ROW_TILE % length, i * ROW_TILE % length + ROW_TILE)
        for h in range(2 * part // HEAD_DIM):
            head = slice(h * HEAD_DIM, (h + 1) * HEAD_DIM)
            raw[at(i), head] = turn(raw[at(i), head], cosine[place, :], -sine[place, :])
        terms = raw[at(i), : 2 * part] * normed[at(i), :]
        gain_rows = gain_rows + jnp.sum(terms, axis=0, keepdims=True)
        for n in range(2):
            own[n : n + 1, at(i)] = row_sums((terms * gain)[:, n * part : (n + 1) * part])
        mixed[at(i), 2 * part :] = raw[at(i), 2 * part :].astype(BF16)

    stats.start()
    wide = width // 128
    for n in range(wide):
        column = slice(n * 128, (n + 1) * 128)
        sums[n : n + 1, :] = gain_attn[:, column]
        sums[wide + n : wide + n + 1, :] = gain_feed[:, column]
    for n in range(2 * part // 128):
        sums[2 * wide + n : 2 * wide + n + 1, :] = gain_rows[:, n * 128 : (n + 1) * 128]
    own[...] = stats.total() / width

    @pl.loop(0, tiles)
    def _(i):
        for n in range(2):
            mean, by = down_rows(own[n : n + 1, at(i)]), down_rows(factor[n : n + 1, at(i)])
            for first in range(n * part, (n + 1) * part, 128):
                where = slice(first, first + 128)
                back = gain[:, where] * raw[at(i), where] - normed[at(i), where] * mean
                mixed[at(i), where] = (by * back).astype(BF16)

    load_w.wait()

    @pl.loop(0, tiles)
    def _(i):
        held[at(i), :] = dot_rows(mixed[at(i), :], held_w[...]).astype(BF16)

    load_tokens.wait()

    def work():
        @pl.loop(0, width // ROW_TILE)
        def _(i):
            qkv_part[at(i), :] = dot_first(held_tokens[:, at(i)], mixed[...]).astype(BF16)

    extra.work = work
    extra.late = up_sums.relay if chips == 4 else (lambda: None)
    exchange.body(
        held, residual_grad, qkv_part, sums, out_part, input_grad, grad_qkv, grad_gains, grad_out, *rest
    )
    if chips == 4:
        for half in range(2):
            up_sum[half * half_rows : (half + 1) * half_rows, :] = up_sums.finish(half).astype(BF16)
        join_copy(2).start()
        for n in range(3):
            join(n)


def attend_back(
    spans, chips, rows, grads, tokens, weights, up_part, gate_sum, down_sum, out_w, gains, ids, cosine, sine,
    residual_grad, gain_attn, gain_feed, saved,
):
    total_rows, width = tokens.shape
    part = out_w.shape[0]
    members = width // part
    hidden = up_part.shape[1]
    tiles = total_rows // ROW_TILE
    vmem = pl.BlockSpec(memory_space=pltpu.VMEM)
    hbm = pl.BlockSpec(memory_space=pl.ANY)
    shape = jax.ShapeDtypeStruct
    sum_rows = (2 * width + 2 * part) // 128
    sum_rows += -sum_rows % 8
    extra = QkvGrads(
        spans, chips, members, shape((width, 3 * part), BF16), shape((sum_rows, 128), F32), shape((part, width), BF16)
    )
    exchange = Exchange(spans, rows, width, SUM_PIECE, True, False, after_input, 1, 1, None, extra)
    scratch = exchange.scratch()
    square_in = chips == 4
    return pl.pallas_call(
        functools.partial(attend_back_body, spans, chips, exchange, extra, len(scratch) - len(extra.scratch())),
        out_shape=[
            shape((rows, width), F32),
            *extra.out_shapes,
            *[shape((width // chips // 2, 2 * hidden) if square_in else (16, 128), BF16)] * 3,
        ],
        in_specs=[hbm] * 4 + [vmem] * (10 + len(saved)),
        out_specs=[vmem] * 7,
        scratch_shapes=[
            pltpu.VMEM((total_rows, width), BF16),
            pltpu.VMEM((total_rows, width), BF16),
            pltpu.VMEM(weights.shape, BF16),
            pltpu.VMEM((total_rows, 3 * part), F32),
            pltpu.VMEM((total_rows, 3 * part), BF16),
            pltpu.VMEM((total_rows, part), BF16),
            *stats_scratch(spans, total_rows)[:2],
            pltpu.SemaphoreType.DMA((tiles + 3,)),
            *stats_scratch(spans, total_rows)[2:],
            pltpu.VMEM((width, 3 * part), BF16),
            pltpu.VMEM((part, width), BF16),
            pltpu.VMEM((sum_rows, 128), F32),
            pltpu.VMEM((width, hidden) if square_in else (16, 128), BF16),
            pltpu.VMEM((6, width // 8, hidden) if square_in else (6, 16, 128), BF16),
            pltpu.SemaphoreType.DMA((6,)),
            pltpu.SemaphoreType.DMA((6,)),
            pltpu.VMEM((3, width // chips // 2, hidden) if square_in else (3, 16, 128), BF16),
            pltpu.SemaphoreType.DMA((3,)),
            pltpu.SemaphoreType.DMA((3,)),
            *scratch,
        ],
        compiler_params=pltpu.CompilerParams(collective_id=9, has_side_effects=True, vmem_limit_bytes=62 << 20),
        cost_estimate=pl.CostEstimate(
            flops=2 * total_rows * width * 8 * part, bytes_accessed=50 * width * width, transcendentals=0
        ),
        name="attend_back",
    )(
        grads, tokens, weights, up_part, gate_sum, down_sum, out_w, gains, ids, cosine, sine, residual_grad, gain_attn,
        gain_feed, *saved,
    )


def per_device(inputs, segment, w_qkv, w_out, w_gate, w_up, w_down_t, gains, cotangent):
    rows, width = inputs.shape[1:]
    cores = lax.axis_size("core")
    spans = lax.axis_size("ctx")
    members = cores * spans
    length = rows * spans
    part = width // members
    tokens = inputs[0]

    chips = lax.axis_size("chip")
    assert chips == spans
    cosine, sine = rope_tables(jnp.arange(length, dtype=F32))
    half = jnp.arange(HEAD_DIM) < HEAD_DIM // 2
    sine = jnp.where(half[None, :], -sine, sine)
    gate_up, down, qkv_w, ids, tokens_all, gate_up_w, out_part, out_w, *saved = attend(
        spans, chips, tokens, w_qkv, segment, w_out, w_gate, w_up, w_down_t, gains, cosine, sine
    )
    if chips != 4:
        gate_up_w = gather(gate_up, "chip")
    (
        output, residual_grad, gain_feed, gain_attn, down_sum, gate_sum, _, _, gate_part, up_part, projected_all
    ) = Middle(spans, rows, width, w_gate.shape[1] // cores, BATCH_PIECE).call(
        chips, out_part, tokens, cotangent[0], gains, gate_up, gate_up_w, down
    )
    input_grad, grad_qkv, grad_gains, grad_out, grad_gate, grad_down, grad_up = attend_back(
        spans, chips, rows, projected_all, tokens_all, qkv_w, up_part, gate_sum, down_sum, out_w, gains, ids, cosine, sine, residual_grad,
        gain_attn, gain_feed, saved,
    )
    if chips != 4:
        gate_sum, up_sum = scatter_sum(gate_part, "chip"), scatter_sum(up_part, "chip")
        grad_gate, grad_up, grad_down = join_columns(gate_sum, up_sum, down_sum)
    return (
        output[None],
        input_grad[None],
        grad_qkv.astype(F32),
        grad_out.astype(F32),
        grad_gate.astype(F32),
        grad_up.astype(F32),
        grad_down.astype(F32),
        grad_gains.reshape(4, width),
    )


def solution(mesh):
    cores = 2
    chips = mesh.shape["dp"] // cores
    split = Mesh(mesh.devices.reshape(chips, cores, mesh.shape["ctx"]), ALL)
    dp = ("chip", "core")
    every = P((*dp, "ctx"), None)
    in_specs = (
        P(dp, "ctx", None),
        P(dp, "ctx"),
        every,
        every,
        P(dp, "ctx"),
        P(dp, "ctx"),
        P(dp, "ctx"),
        P(),
        P(dp, "ctx", None),
    )
    out_specs = (
        P(dp, "ctx", None),
        P(dp, "ctx", None),
        every,
        every,
        P(dp, "ctx"),
        P(dp, "ctx"),
        P(dp, "ctx"),
        P(),
    )
    return jax.shard_map(
        per_device, mesh=split, in_specs=in_specs, out_specs=out_specs, check_vma=False
    )
```
